32 devices in a mesh: seq: 8 (over y, x, core), tp: 4 (over z).
Axes of the slice: x: 2, y: 2, z: 4, core: 2. Of those that a mesh axis runs over, the one named last changes fastest.
Arguments:
- tokens: bfloat16 [1, 4096, 2048], P(None, 'seq'), may hold values from -6 to 6
- gain_attn: float32 [2048], replicated, may hold values from 0.5 to 1.5
- w_query: bfloat16 [2048, 2048], P(None, 'tp'), may hold values from -0.21875 to 0.21875
- w_key: bfloat16 [2048, 2048], P(None, 'tp'), may hold values from -0.21875 to 0.21875
- w_value: bfloat16 [2048, 2048], P(None, 'tp'), may hold values from -0.125 to 0.125
- w_out: bfloat16 [2048, 2048], P('tp'), may hold values from -0.25 to 0.25
- gain_ffn: float32 [2048], replicated, may hold values from 0.5 to 1.5
- w_gate: bfloat16 [2048, 8192], P(None, 'tp'), may hold values from -0.125 to 0.125
- w_up: bfloat16 [2048, 8192], P(None, 'tp'), may hold values from -0.125 to 0.125
- w_down: bfloat16 [8192, 2048], P('tp'), may hold values from -0.0625 to 0.0625
- cotangent: bfloat16 [1, 4096, 2048], P(None, 'seq'), may hold values from -6 to 6
- doc_ids: int32 [1, 4096], replicated, may hold values from 0 to 15, never falling along the last dimension, each value on 1 to 2048 neighbouring positions
- valid: int32 [1, 4096], replicated, may hold values 0 or 1
- group_order: int32 [1, 16], replicated, may hold values from 0 to 15, each once within a row
Outputs:
- layer_out: bfloat16 [1, 4096, 2048], P(None, 'seq')
- grad_tokens: float32 [1, 4096, 2048], P(None, 'seq')
- grad_gain_attn: float32 [2048], P('seq')
- grad_query: float32 [2048, 2048], P('seq', 'tp')
- grad_key: float32 [2048, 2048], P('seq', 'tp')
- grad_value: float32 [2048, 2048], P('seq', 'tp')
- grad_out: float32 [2048, 2048], P('tp', 'seq')
- grad_gain_ffn: float32 [2048], P('seq')
- grad_gate: float32 [2048, 8192], P('seq', 'tp')
- grad_up: float32 [2048, 8192], P('seq', 'tp')
- grad_down: float32 [8192, 2048], P('tp', 'seq')
The draws below stay inside these ranges and needn't reach their ends.
Inputs may be any that keep to these rules, and one draw needn't show every extreme that they name: `doc_ids`: document numbers never fall along a sequence; a document holds 1 to 2048 positions. `group_order`: each row is a permutation; device i of seq stores storage blocks 2 i and 2 i + 1 of every sequence.
All inputs are finite; a program needn't handle non-finite values.
Results may differ from the reference program's by a relative error of at most 0.014.
The reference program's roundings to bfloat16 on the way count: a program that leaves them out, or rounds other values in their place, can miss the bound.
Values may be sent and summed in bfloat16 or wider, within the bound.
No kernel may reach another device: no remote copies, remote signals or barrier semaphores. Data moves between devices by JAX's collectives and lax.ppermute only.
A program may use at most 320 MiB of HBM per device.

```python
import math
import jax
import jax.numpy as jnp
import numpy as np
from jax import lax

D = 2048
HEAD_COUNT = 16
HEAD_WIDTH = 128
FF = 8192
SEQUENCE_LENGTH = 4096
SEQUENCE_COUNT = 1
GROUPS = 16


def plant(values, own_key, least, top_value):
    spot = [jax.random.randint(jax.random.fold_in(own_key, axis), (), 0, length) for axis, length in enumerate(values.shape)]
    widest = values.shape.index(max(values.shape))
    beside = spot[:widest] + [(spot[widest] + 1) % values.shape[widest]] + spot[widest + 1:]
    return values.at[tuple(spot)].set(least).at[tuple(beside)].set(top_value)


def levels(stream_key, shape, cuts, smallest, top_value):
    factor_of, own = 1.0, jax.random.fold_in(stream_key, 6)
    for position, blocks in cuts:
        heights = jnp.exp(jax.random.uniform(jax.random.fold_in(own, position), (blocks,), jnp.float32, smallest / len(cuts), top_value / len(cuts)))
        factor_of = factor_of * jnp.repeat(heights, shape[position] // blocks).reshape([-1 if axis == position else 1 for axis in range(len(shape))])
    return factor_of


def split_up(count, total, limit, lean):
    weights = [(1 << 20) // math.isqrt(rank ** lean) + 1 for rank in range(2, count + 1)]
    rest, holding = total - limit - (count - 1), [1] * (count - 1)
    while rest > 0:
        movable = [i for i in range(count - 1) if holding[i] < limit]
        pool, budget = sum([weights[i] for i in movable]), rest
        for i in movable:
            more = min(limit - holding[i], max(1, budget * weights[i] // pool), rest)
            holding[i] = holding[i] + more
            rest = rest - more
    return np.array([limit] + holding)


def uneven(rng, amount, total, reach, slope):
    if amount == 2:
        one = jax.random.randint(rng, (), max(1, total - reach), min(reach, total - 1) + 1)
        return jnp.stack([one, total - one])
    sizes = jnp.asarray(split_up(amount, total, reach, slope), jnp.int32)
    couples = (amount - 1) // 2
    giver, taker = sizes[1:1 + 2 * couples:2], sizes[2:2 + 2 * couples:2]
    slack = jnp.minimum(giver - 1, reach - taker)
    passed = jax.random.randint(jax.random.fold_in(rng, 1), (couples,), 0, 1 << 20) % (slack + 1)
    sizes = sizes.at[1:1 + 2 * couples:2].set(giver - passed).at[2:2 + 2 * couples:2].set(taker + passed)
    return sizes[jax.random.permutation(jax.random.fold_in(rng, 2), amount)]


def gaussian(own_key, dims, width, most, cuts=(), held_as=jnp.bfloat16):
    level = levels(own_key, dims, cuts, -0.22, 0.18) if cuts else 1.0
    values = jax.random.normal(own_key, dims, jnp.float32) * width * level
    return jnp.minimum(jnp.maximum(values, -most), most).astype(held_as)


def setup_inputs(seed: int = 0) -> dict:
    arg_keys = jax.random.split(jax.random.key(seed), 15)
    tokens = gaussian(arg_keys[0], (SEQUENCE_COUNT, SEQUENCE_LENGTH, D), 1.0, 6.0, ((1, 8),))
    gain_attn = jnp.clip(1.0 + 0.1 * jax.random.normal(arg_keys[1], (D,), jnp.float32), 0.5, 1.5)
    w_query = gaussian(arg_keys[2], (D, HEAD_COUNT * HEAD_WIDTH), (D // 3) ** -0.5, 0.21875, ((1, 4),))
    w_key = gaussian(arg_keys[3], (D, HEAD_COUNT * HEAD_WIDTH), (D // 3) ** -0.5, 0.21875, ((1, 4),))
    w_value = gaussian(arg_keys[4], (D, HEAD_COUNT * HEAD_WIDTH), D ** -0.5, 0.125, ((1, 4),))
    w_out = gaussian(arg_keys[5], (HEAD_COUNT * HEAD_WIDTH, D), (HEAD_COUNT * HEAD_WIDTH // 4) ** -0.5, 0.25, ((0, 4),))
    gain_ffn = jnp.clip(1.0 + 0.1 * jax.random.normal(arg_keys[6], (D,), jnp.float32), 0.5, 1.5)
    w_gate = gaussian(arg_keys[7], (D, FF), D ** -0.5, 0.125, ((1, 4),))
    w_up = gaussian(arg_keys[8], (D, FF), D ** -0.5, 0.125, ((1, 4),))
    w_down = gaussian(arg_keys[9], (FF, D), FF ** -0.5, 0.0625, ((0, 4),))
    cotangent = gaussian(arg_keys[10], (SEQUENCE_COUNT, SEQUENCE_LENGTH, D), 1.0, 6.0, ((1, 8),))
    doc_ids = jax.vmap(lambda own: jnp.searchsorted(jnp.cumsum(uneven(own, max(SEQUENCE_LENGTH // 256, 4), SEQUENCE_LENGTH, SEQUENCE_LENGTH // 2, 2)), jnp.arange(SEQUENCE_LENGTH), side="right"))(jax.random.split(arg_keys[11], SEQUENCE_COUNT)).reshape((SEQUENCE_COUNT, SEQUENCE_LENGTH)).astype(jnp.int32)
    valid = plant((jax.random.randint(arg_keys[12], (SEQUENCE_COUNT, SEQUENCE_LENGTH), 0, 8) < 7).astype(jnp.int32), jax.random.fold_in(arg_keys[12], 1), 0, 1)
    group_order = jax.vmap(lambda own: jax.random.permutation(own, GROUPS))(jax.random.split(arg_keys[13], SEQUENCE_COUNT)).reshape((SEQUENCE_COUNT, GROUPS)).astype(jnp.int32)
    return {"tokens": tokens, "gain_attn": gain_attn, "w_query": w_query, "w_key": w_key, "w_value": w_value, "w_out": w_out, "gain_ffn": gain_ffn, "w_gate": w_gate, "w_up": w_up, "w_down": w_down, "cotangent": cotangent, "doc_ids": doc_ids, "valid": valid, "group_order": group_order}


HIGH_PRECISION = lax.Precision.HIGHEST
norm_eps = 1e-05
rope_base = 10000.0

@jax.custom_vjp
def low(v):
    return lax.optimization_barrier(v.astype(jnp.bfloat16)).astype(jnp.float32)

@jax.custom_vjp
def low_back(v):
    return v

def low_keep(v):
    return (low(v), None)

def low_pass(kept, grad):
    return (grad,)

def back_keep(v):
    return (v, None)

def back_low(kept, grad):
    return (low(grad),)
low.defvjp(low_keep, low_pass)
low_back.defvjp(back_keep, back_low)

def rope_tables(places, head_size):
    half_size = head_size // 2
    freqs = rope_base ** (-jnp.arange(half_size, dtype=jnp.float32) * 2.0 / head_size)
    angles = places.astype(jnp.float32)[..., None] * freqs
    return (jnp.cos(angles), jnp.sin(angles))

def rotate(values, cosine, sine):
    half_size = values.shape[-1] // 2
    first = values[..., :half_size]
    second = values[..., half_size:]
    cos_b = cosine[..., None, :]
    sin_b = sine[..., None, :]
    return jnp.concatenate([first * cos_b - second * sin_b, second * cos_b + first * sin_b], axis=-1)

def visible(place_q, doc_q, place_k, doc_k, live_k):
    allowed = (place_k[None, :] <= place_q[:, None]) & (doc_k[None, :] == doc_q[:, None]) & (live_k[None, :] == 1)
    return allowed.astype(jnp.float32)

def rms_norm(hidden, gain):
    scale = lax.rsqrt(lax.optimization_barrier(jnp.mean(hidden * hidden, axis=-1, keepdims=True)) + norm_eps)
    return hidden * scale * gain

def reference(tokens, gain_attn, w_query, w_key, w_value, w_out, gain_ffn, w_gate, w_up, w_down, cotangent, doc_ids, valid, group_order):
    span = SEQUENCE_LENGTH // GROUPS
    every = jnp.arange(SEQUENCE_LENGTH, dtype=jnp.int32)
    places = (jnp.take(group_order, every // span, axis=1) * span + (every % span)[None, :]).astype(jnp.int32)
    docs = jnp.take_along_axis(doc_ids, places, axis=1)
    lives = jnp.take_along_axis(valid, places, axis=1)
    cosine, sine = rope_tables(places, HEAD_WIDTH)
    seq_index = jnp.repeat(jnp.arange(SEQUENCE_COUNT, dtype=jnp.int32), HEAD_COUNT)

    def one_head(items):
        query_h, key_h, value_h, index = items
        place = places[index]
        mask = visible(place, docs[index], place, docs[index], lives[index])
        scores = low_back(jnp.dot(query_h, key_h.T, precision=HIGH_PRECISION) * (1.0 / math.sqrt(HEAD_WIDTH)) - math.log(SEQUENCE_LENGTH))
        weights = low(jax.nn.sigmoid(scores) * mask)
        return jnp.dot(weights, value_h, precision=HIGH_PRECISION)

    def by_head(values):
        return values.transpose(0, 2, 1, 3).reshape(SEQUENCE_COUNT * HEAD_COUNT, SEQUENCE_LENGTH, HEAD_WIDTH)

    def forward(input_rows, g_attn, wq, wk, wv, output_weight, g_ffn, gate_weight, up_weight, down_weight):
        normalized_rows = low(rms_norm(input_rows, g_attn))

        def project(weight_matrix):
            return low_back(jnp.einsum('cgw,wn->cgn', normalized_rows, weight_matrix, precision=HIGH_PRECISION)).reshape(SEQUENCE_COUNT, SEQUENCE_LENGTH, HEAD_COUNT, HEAD_WIDTH)
        query = low(rotate(project(wq), cosine, sine))
        key = low(rotate(project(wk), cosine, sine))
        value = low(project(wv))
        mixed = lax.map(jax.checkpoint(one_head), (by_head(query), by_head(key), by_head(value), seq_index))
        mixed = mixed.reshape(SEQUENCE_COUNT, HEAD_COUNT, SEQUENCE_LENGTH, HEAD_WIDTH).transpose(0, 2, 1, 3).reshape(SEQUENCE_COUNT, SEQUENCE_LENGTH, HEAD_COUNT * HEAD_WIDTH)
        attention_output = low(low_back(mixed))
        hidden_rows = input_rows + low_back(jnp.einsum('qrx,xg->qrg', attention_output, output_weight, precision=HIGH_PRECISION))
        normalized_feedforward = low(rms_norm(hidden_rows, g_ffn))
        gate_rows = low_back(jnp.einsum('cqu,um->cqm', normalized_feedforward, gate_weight, precision=HIGH_PRECISION))
        up_projected = low_back(jnp.einsum('cqu,um->cqm', normalized_feedforward, up_weight, precision=HIGH_PRECISION))
        activation_rows = low(jax.nn.silu(gate_rows) * up_projected)
        return hidden_rows + low_back(jnp.einsum('vhk,kg->vhg', activation_rows, down_weight, precision=HIGH_PRECISION))
    floats = (tokens.astype(jnp.float32), gain_attn.astype(jnp.float32), w_query.astype(jnp.float32), w_key.astype(jnp.float32), w_value.astype(jnp.float32), w_out.astype(jnp.float32), gain_ffn.astype(jnp.float32), w_gate.astype(jnp.float32), w_up.astype(jnp.float32), w_down.astype(jnp.float32))
    result, pull = jax.vjp(forward, *floats)
    grads = pull(cotangent.astype(jnp.float32))
    return (result.astype(jnp.bfloat16), grads[0], grads[1], grads[2], grads[3], grads[4], grads[5], grads[6], grads[7], grads[8], grads[9])
```

```python
import math

import jax
import jax.numpy as jnp
from jax import lax
from jax.sharding import PartitionSpec as P

HEAD_WIDTH = 128


norm_eps = 1e-05
rope_base = 10000.0


def rope_tables(places, head_size):
    half_size = head_size // 2
    freqs = rope_base ** (-jnp.arange(half_size, dtype=jnp.float32) * 2.0 / head_size)
    angles = places.astype(jnp.float32)[..., None] * freqs
    return (jnp.cos(angles), jnp.sin(angles))


def rotate(values, cosine, sine, forward):
    half_size = values.shape[-1] // 2
    first = values[..., :half_size]
    second = values[..., half_size:]
    cos_b = cosine[..., None, :]
    sin_b = sine[..., None, :]
    if forward:
        return jnp.concatenate(
            [first * cos_b - second * sin_b, second * cos_b + first * sin_b], axis=-1
        )
    return jnp.concatenate(
        [first * cos_b + second * sin_b, second * cos_b - first * sin_b], axis=-1
    )


def visible(place_q, doc_q, place_k, doc_k, live_k):
    allowed = (
        (place_k[None, :] <= place_q[:, None])
        & (doc_k[None, :] == doc_q[:, None])
        & (live_k[None, :] == 1)
    )
    return allowed.astype(jnp.float32)


def score_block(query_heads, key_heads, head_size, length):
    scores = jnp.einsum("qhe,khe->hqk", query_heads, key_heads, preferred_element_type=jnp.float32)
    return scores * (1.0 / math.sqrt(head_size)) - math.log(length)


def score_grads(query_heads, key_heads, value_heads, grad_heads, mask, head_size, length):
    sigma = jax.nn.sigmoid(score_block(query_heads, key_heads, head_size, length))
    weights = (sigma * mask).astype(jnp.bfloat16)
    grad_weights = jnp.einsum(
        "qhe,khe->hqk", grad_heads, value_heads, preferred_element_type=jnp.float32
    )
    grad_scores = (grad_weights * (sigma * (1.0 - sigma)) * mask).astype(jnp.bfloat16)
    return (weights, grad_scores)


def local_general(
    tokens,
    gain_attn,
    w_query,
    w_key,
    w_value,
    w_out,
    gain_ffn,
    w_gate,
    w_up,
    w_down,
    cotangent,
    doc_ids,
    valid,
    group_order,
):
    seq_count, row_count, model_width = tokens.shape
    length = doc_ids.shape[1]
    span = length // group_order.shape[1]
    head_size = HEAD_WIDTH
    local_width = w_query.shape[1]
    local_heads = local_width // head_size
    flat_rows = seq_count * row_count
    factor = 1.0 / math.sqrt(head_size)
    own_rows = lax.axis_index("seq") * row_count + jnp.arange(row_count, dtype=jnp.int32)
    all_rows = jnp.arange(length, dtype=jnp.int32)
    place_all = jnp.take(group_order, all_rows // span, axis=1) * span + (all_rows % span)[None, :]
    place_own = jnp.take(group_order, own_rows // span, axis=1) * span + (own_rows % span)[None, :]
    doc_all = jnp.take_along_axis(doc_ids, place_all, axis=1)
    live_all = jnp.take_along_axis(valid, place_all, axis=1)
    doc_own = jnp.take_along_axis(doc_ids, place_own, axis=1)
    cosine, sine = rope_tables(place_own, head_size)
    input_rows = tokens.astype(jnp.float32).reshape(flat_rows, model_width)
    scale_attn = lax.rsqrt(jnp.mean(input_rows * input_rows, axis=-1, keepdims=True) + norm_eps)
    unit_attn = input_rows * scale_attn
    normed_attn = (unit_attn * gain_attn).astype(jnp.bfloat16)

    def project(weight_matrix):
        return jnp.dot(normed_attn, weight_matrix, preferred_element_type=jnp.float32).reshape(
            seq_count, row_count, local_heads, head_size
        )

    query_rot = (
        rotate(project(w_query), cosine, sine, True)
        .astype(jnp.bfloat16)
        .reshape(seq_count, row_count, local_width)
    )
    key_rot = (
        rotate(project(w_key), cosine, sine, True)
        .astype(jnp.bfloat16)
        .reshape(seq_count, row_count, local_width)
    )
    value_low = (
        jnp.dot(normed_attn, w_value, preferred_element_type=jnp.float32)
        .astype(jnp.bfloat16)
        .reshape(seq_count, row_count, local_width)
    )
    key_all, value_all = (
        lax.all_gather(key_rot, "seq", axis=1, tiled=True),
        lax.all_gather(value_low, "seq", axis=1, tiled=True),
    )

    def attend(items):
        query_seq, key_seq, value_seq, place_q, doc_q, place_k, doc_k, live_k = items
        query_heads = query_seq.reshape(row_count, local_heads, head_size)
        key_heads = key_seq.reshape(length, local_heads, head_size)
        value_heads = value_seq.reshape(length, local_heads, head_size)
        mask = visible(place_q, doc_q, place_k, doc_k, live_k)
        weights = (
            jax.nn.sigmoid(score_block(query_heads, key_heads, head_size, length)) * mask
        ).astype(jnp.bfloat16)
        mixed = jnp.einsum("hqk,khe->qhe", weights, value_heads, preferred_element_type=jnp.float32)
        return mixed.astype(jnp.bfloat16).reshape(row_count, local_width)

    attention_output = lax.map(
        attend, (query_rot, key_all, value_all, place_own, doc_own, place_all, doc_all, live_all)
    )
    attended_flat = attention_output.reshape(flat_rows, local_width)
    branch_attn = lax.psum(jnp.dot(attended_flat, w_out, preferred_element_type=jnp.float32), "tp")
    hidden_rows = input_rows + branch_attn
    scale_ffn = lax.rsqrt(jnp.mean(hidden_rows * hidden_rows, axis=-1, keepdims=True) + norm_eps)
    unit_ffn = hidden_rows * scale_ffn
    normalized_feedforward = (unit_ffn * gain_ffn).astype(jnp.bfloat16)
    gate_rows = jnp.dot(normalized_feedforward, w_gate, preferred_element_type=jnp.float32)
    up_projected = jnp.dot(normalized_feedforward, w_up, preferred_element_type=jnp.float32)
    gate_sig = jax.nn.sigmoid(gate_rows)
    activation_rows = (gate_rows * gate_sig * up_projected).astype(jnp.bfloat16)
    branch_ffn = lax.psum(
        jnp.dot(activation_rows, w_down, preferred_element_type=jnp.float32).astype(jnp.bfloat16),
        "tp",
    ).astype(jnp.float32)
    layer_out = (
        (hidden_rows + branch_ffn).astype(jnp.bfloat16).reshape(seq_count, row_count, model_width)
    )
    upstream = cotangent.astype(jnp.float32).reshape(flat_rows, model_width)
    upstream_low = upstream.astype(jnp.bfloat16)
    grad_down = jnp.einsum(
        "tf,td->fd", activation_rows, upstream_low, preferred_element_type=jnp.float32
    )
    grad_act = jnp.einsum("td,fd->tf", upstream_low, w_down, preferred_element_type=jnp.float32)
    gate_pre = (grad_act * up_projected * (gate_sig * (1.0 + gate_rows * (1.0 - gate_sig)))).astype(
        jnp.bfloat16
    )
    up_pre = (grad_act * (gate_rows * gate_sig)).astype(jnp.bfloat16)
    grad_gate = jnp.einsum(
        "td,tf->df", normalized_feedforward, gate_pre, preferred_element_type=jnp.float32
    )
    grad_up = jnp.einsum(
        "td,tf->df", normalized_feedforward, up_pre, preferred_element_type=jnp.float32
    )
    normed_ffn_part = jnp.einsum(
        "tf,df->td", gate_pre, w_gate, preferred_element_type=jnp.float32
    ) + jnp.einsum("tf,df->td", up_pre, w_up, preferred_element_type=jnp.float32)
    grad_normed_ffn = lax.psum(normed_ffn_part, "tp")
    gain_ffn_part = jnp.sum(grad_normed_ffn * unit_ffn, axis=0)
    back_ffn = grad_normed_ffn * gain_ffn
    grad_middle = upstream + scale_ffn * (
        back_ffn - unit_ffn * jnp.mean(back_ffn * unit_ffn, axis=-1, keepdims=True)
    )
    middle_low = grad_middle.astype(jnp.bfloat16)
    grad_out = jnp.einsum(
        "te,td->ed", attended_flat, middle_low, preferred_element_type=jnp.float32
    )
    grad_attended = (
        jnp.einsum("td,ed->te", middle_low, w_out, preferred_element_type=jnp.float32)
        .astype(jnp.bfloat16)
        .reshape(seq_count, row_count, local_width)
    )
    key_back, value_back = (key_all, value_all)

    def attend_back(items):
        query_seq, key_seq, value_seq, grad_seq, place_q, doc_q, place_k, doc_k, live_k = items
        query_heads = query_seq.reshape(row_count, local_heads, head_size)
        key_heads = key_seq.reshape(length, local_heads, head_size)
        value_heads = value_seq.reshape(length, local_heads, head_size)
        grad_heads = grad_seq.reshape(row_count, local_heads, head_size)
        mask = visible(place_q, doc_q, place_k, doc_k, live_k)
        weights, grad_scores = score_grads(
            query_heads, key_heads, value_heads, grad_heads, mask, head_size, length
        )
        grad_value_seq = jnp.einsum(
            "hqk,qhe->khe", weights, grad_heads, preferred_element_type=jnp.float32
        )
        grad_query_seq = (
            jnp.einsum("hqk,khe->qhe", grad_scores, key_heads, preferred_element_type=jnp.float32)
            * factor
        )
        grad_key_seq = (
            jnp.einsum("hqk,qhe->khe", grad_scores, query_heads, preferred_element_type=jnp.float32)
            * factor
        )
        return (
            grad_query_seq,
            grad_key_seq.reshape(length, local_width),
            grad_value_seq.reshape(length, local_width),
        )

    grad_query_rot, grad_key_all, grad_value_all = lax.map(
        attend_back,
        (
            query_rot,
            key_back,
            value_back,
            grad_attended,
            place_own,
            doc_own,
            place_all,
            doc_all,
            live_all,
        ),
    )
    grad_key_rot, grad_value_own = (
        lax.psum_scatter(grad_key_all, "seq", scatter_dimension=1, tiled=True),
        lax.psum_scatter(grad_value_all, "seq", scatter_dimension=1, tiled=True),
    )
    query_low = (
        rotate(grad_query_rot, cosine, sine, False)
        .astype(jnp.bfloat16)
        .reshape(flat_rows, local_width)
    )
    key_low = (
        rotate(
            grad_key_rot.reshape(seq_count, row_count, local_heads, head_size), cosine, sine, False
        )
        .astype(jnp.bfloat16)
        .reshape(flat_rows, local_width)
    )
    value_grad_low = grad_value_own.astype(jnp.bfloat16).reshape(flat_rows, local_width)
    grad_query = jnp.einsum("td,te->de", normed_attn, query_low, preferred_element_type=jnp.float32)
    grad_key = jnp.einsum("td,te->de", normed_attn, key_low, preferred_element_type=jnp.float32)
    grad_value = jnp.einsum(
        "td,te->de", normed_attn, value_grad_low, preferred_element_type=jnp.float32
    )
    normed_attn_part = (
        jnp.einsum("te,de->td", query_low, w_query, preferred_element_type=jnp.float32)
        + jnp.einsum("te,de->td", key_low, w_key, preferred_element_type=jnp.float32)
        + jnp.einsum("te,de->td", value_grad_low, w_value, preferred_element_type=jnp.float32)
    )
    grad_normed_attn = lax.psum(normed_attn_part, "tp")
    gain_attn_part = jnp.sum(grad_normed_attn * unit_attn, axis=0)
    back_attn = grad_normed_attn * gain_attn
    grad_inputs = grad_middle + scale_attn * (
        back_attn - unit_attn * jnp.mean(back_attn * unit_attn, axis=-1, keepdims=True)
    )
    grad_tokens = grad_inputs.reshape(seq_count, row_count, model_width)
    (
        query_shard,
        key_shard,
        value_shard,
        out_shard,
        gain_attn_shard,
        gate_shard,
        up_shard,
        down_shard,
        gain_ffn_shard,
    ) = (
        lax.psum_scatter(grad_query, "seq", scatter_dimension=0, tiled=True),
        lax.psum_scatter(grad_key, "seq", scatter_dimension=0, tiled=True),
        lax.psum_scatter(grad_value, "seq", scatter_dimension=0, tiled=True),
        lax.psum_scatter(grad_out, "seq", scatter_dimension=1, tiled=True),
        lax.psum_scatter(gain_attn_part, "seq", scatter_dimension=0, tiled=True),
        lax.psum_scatter(grad_gate, "seq", scatter_dimension=0, tiled=True),
        lax.psum_scatter(grad_up, "seq", scatter_dimension=0, tiled=True),
        lax.psum_scatter(grad_down, "seq", scatter_dimension=1, tiled=True),
        lax.psum_scatter(gain_ffn_part, "seq", scatter_dimension=0, tiled=True),
    )
    return (
        layer_out,
        grad_tokens,
        gain_attn_shard,
        query_shard,
        key_shard,
        value_shard,
        out_shard,
        gain_ffn_shard,
        gate_shard,
        up_shard,
        down_shard,
    )


def line_gather(shard, axis, count):
    upward, downward, below, above = shard, shard, {}, {}
    for step in range(1, count):
        upward = lax.ppermute(upward, axis, [(i, i + 1) for i in range(step - 1, count - 1)])
        downward = lax.ppermute(downward, axis, [(i, i - 1) for i in range(1, count - step + 1)])
        below[step], above[step] = upward, downward
    return [shard] + [above[d] + below[count - d] for d in range(1, count)]


def line_scatter_sum(parts, axis, count):
    upward, downward = None, None
    for step in range(1, count):
        up_part, down_part = parts[count - step], parts[step]
        if upward is not None:
            up_part = up_part.astype(jnp.float32) + upward.astype(jnp.float32)
            down_part = down_part.astype(jnp.float32) + downward.astype(jnp.float32)
        upward = lax.ppermute(
            up_part.astype(jnp.bfloat16), axis, [(i, i + 1) for i in range(0, step)]
        )
        downward = lax.ppermute(
            down_part.astype(jnp.bfloat16), axis, [(i, i - 1) for i in range(count - step, count)]
        )
    return parts[0].astype(jnp.float32) + (
        upward.astype(jnp.float32) + downward.astype(jnp.float32)
    )


def dense(left, right):
    return jnp.dot(left, right, preferred_element_type=jnp.float32)


def dense_t(left, right):
    return lax.dot_general(
        left, right, (((1,), (1,)), ((), ())), preferred_element_type=jnp.float32
    )


def local_heads_apart(
    tokens,
    gain_attn,
    w_query,
    w_key,
    w_value,
    w_out,
    gain_ffn,
    w_gate,
    w_up,
    w_down,
    cotangent,
    doc_ids,
    valid,
    group_order,
    *,
    seq_size,
    tp_size,
):
    _, row_count, width = tokens.shape
    length = doc_ids.shape[1]
    groups = group_order.shape[1]
    span = length // groups
    head = HEAD_WIDTH
    heads = w_query.shape[1] // head
    chips = seq_size // 2
    part = row_count // tp_size
    factor = 1.0 / math.sqrt(head)
    bf16, f32 = jnp.bfloat16, jnp.float32
    same_core = [[2 * p + c for p in range(chips)] for c in range(2)]
    other_core = [(i, i ^ 1) for i in range(seq_size)]
    own_seq, own_tp = lax.axis_index("seq"), lax.axis_index("tp")
    core = own_seq % 2
    block = width // seq_size

    def swap(values):
        return lax.ppermute(values, "seq", other_core)

    def to_heads(values):
        return lax.all_to_all(values, "seq", 0, 0, axis_index_groups=same_core, tiled=True)

    w_out_all = lax.all_gather(w_out, "tp", axis=0, tiled=True)

    order = group_order[0]
    per_device = row_count // span

    def blocks_of(which):
        devices = 2 * jnp.arange(chips, dtype=jnp.int32) + which
        storage = (devices[:, None] * per_device + jnp.arange(per_device)[None, :]).reshape(-1)
        return jnp.take(order, storage)

    def places_of(block_ids):
        return (block_ids[:, None] * span + jnp.arange(span, dtype=jnp.int32)[None, :]).reshape(-1)

    own_blocks, other_blocks = blocks_of(core), blocks_of(1 - core)
    key_blocks = jnp.concatenate([own_blocks, other_blocks])
    place_q, place_k = places_of(own_blocks), places_of(key_blocks)
    doc_k = jnp.take(doc_ids.reshape(groups, span), key_blocks, axis=0).reshape(-1)
    live_k = jnp.take(valid.reshape(groups, span), key_blocks, axis=0).reshape(-1)
    doc_q = doc_k[: length // 2]

    own_rows = own_seq * per_device + jnp.arange(per_device, dtype=jnp.int32)
    cosine, sine = rope_tables(places_of(jnp.take(order, own_rows)), head)
    cosine_q, sine_q = rope_tables(place_q, head)

    rows = tokens.astype(f32).reshape(row_count, width)
    scale_attn = lax.rsqrt(jnp.mean(rows * rows, axis=-1, keepdims=True) + norm_eps)
    unit_attn = rows * scale_attn
    normed_attn = (unit_attn * gain_attn).astype(bf16)

    def project(weight):
        return dense(normed_attn, weight).reshape(row_count, heads, head)

    packed = jnp.concatenate(
        [
            rotate(project(w_query), cosine, sine, True).astype(bf16),
            rotate(project(w_key), cosine, sine, True).astype(bf16),
            project(w_value).astype(bf16),
        ],
        axis=-1,
    ).transpose(1, 0, 2)
    mine = to_heads(packed).reshape(chips * row_count, 3 * head)
    query, key_value = mine[:, :head], mine[:, head:]
    key_value = jnp.concatenate([key_value, swap(key_value)], axis=0)
    key, value = key_value[:, :head], key_value[:, head:]

    upstream_low = cotangent.reshape(row_count, width)

    def relative(values):
        twice = jnp.concatenate([values, values], axis=0)
        return lax.dynamic_slice_in_dim(twice, own_tp * part, row_count, 0)

    upstream_rel = relative(upstream_low)
    grad_act = dense_t(upstream_rel, w_down)

    mask = visible(place_q, doc_q, place_k, doc_k, live_k)
    sigma = jax.nn.sigmoid(dense_t(query, key) * factor - math.log(length))
    probs = (sigma * mask).astype(bf16)
    attended = dense(probs, value).astype(bf16)
    attended = to_heads(attended.reshape(chips, row_count, head))
    attended = attended.transpose(1, 0, 2).reshape(row_count, heads * head)
    attended_part = lax.all_to_all(attended, "tp", 0, 0, tiled=True)
    attended_part = (
        attended_part.reshape(tp_size, part, heads * head).transpose(1, 0, 2).reshape(part, -1)
    )

    def own_part(values):
        return lax.dynamic_slice_in_dim(values, own_tp * part, part, 0)

    middle = own_part(rows) + dense(attended_part, w_out_all)
    scale_ffn = lax.rsqrt(jnp.mean(middle * middle, axis=-1, keepdims=True) + norm_eps)
    unit_ffn = middle * scale_ffn
    normed_part = (unit_ffn * gain_ffn).astype(bf16)
    normed_ffn = jnp.concatenate(line_gather(normed_part, "tp", tp_size), axis=0)

    gate = dense(normed_ffn, w_gate)
    up = dense(normed_ffn, w_up)
    gate_sig = jax.nn.sigmoid(gate)
    activated = (gate * gate_sig * up).astype(bf16)
    gate_pre = (grad_act * up * (gate_sig * (1.0 + gate * (1.0 - gate_sig)))).astype(bf16)
    up_pre = (grad_act * (gate * gate_sig)).astype(bf16)
    normed_grad = (dense_t(gate_pre, w_gate) + dense_t(up_pre, w_up)).astype(bf16)

    def relative_parts(values):
        return [values[d * part : (d + 1) * part] for d in range(tp_size)]

    grad_normed = line_scatter_sum(relative_parts(normed_grad), "tp", tp_size)
    gain_ffn_part = jnp.sum(grad_normed * unit_ffn, axis=0)
    back = grad_normed * gain_ffn
    grad_middle = own_part(upstream_low).astype(f32) + scale_ffn * (
        back - unit_ffn * jnp.mean(back * unit_ffn, axis=-1, keepdims=True)
    )
    middle_low = grad_middle.astype(bf16)
    grad_attended = dense_t(middle_low, w_out_all).astype(bf16)
    grad_attended = grad_attended.reshape(part, tp_size, heads * head).transpose(1, 0, 2)
    grad_attended = lax.all_to_all(grad_attended, "tp", 0, 0, tiled=True)
    grad_attended = grad_attended.reshape(row_count, heads, head).transpose(1, 0, 2)
    grad_heads = to_heads(grad_attended).reshape(chips * row_count, head)

    branch = dense(activated, w_down).astype(bf16)
    branch_part = line_scatter_sum(relative_parts(branch), "tp", tp_size)
    layer_part = (middle + branch_part).astype(bf16)
    layer_out = lax.all_gather(layer_part, "tp", axis=0, tiled=True)
    middle_all = lax.all_gather(middle_low, "tp", axis=0, tiled=True)

    grad_value = lax.dot_general(
        probs, grad_heads, (((0,), (0,)), ((), ())), preferred_element_type=f32
    )
    grad_scores = (dense_t(grad_heads, value) * (sigma * (1.0 - sigma)) * mask).astype(bf16)
    grad_query = dense(grad_scores, key) * factor
    grad_key = (
        lax.dot_general(grad_scores, query, (((0,), (0,)), ((), ())), preferred_element_type=f32)
        * factor
    )
    both = jnp.concatenate([grad_key, grad_value], axis=-1)
    half = length // 2
    both = both[:half] + swap(both[half:].astype(bf16)).astype(f32)

    def turn_back(values):
        return rotate(values[:, None, :], cosine_q, sine_q, False)[:, 0, :].astype(bf16)

    packed_back = jnp.concatenate(
        [turn_back(grad_query), turn_back(both[:, :head]), both[:, head:].astype(bf16)], axis=-1
    ).reshape(chips, row_count, 3 * head)
    back_heads = to_heads(packed_back).transpose(1, 0, 2)
    query_low = back_heads[:, :, :head].reshape(row_count, heads * head)
    key_low = back_heads[:, :, head : 2 * head].reshape(row_count, heads * head)
    value_low = back_heads[:, :, 2 * head :].reshape(row_count, heads * head)

    normed_grad1 = dense_t(query_low, w_query) + dense_t(key_low, w_key) + dense_t(
        value_low, w_value
    )
    gain_attn_part = jnp.sum(normed_grad1 * unit_attn, axis=0)
    grad_normed1 = line_scatter_sum(
        relative_parts(relative(normed_grad1.astype(bf16))), "tp", tp_size
    )
    back1 = grad_normed1 * gain_attn
    unit_part = own_part(unit_attn)
    grad_inputs = grad_middle + own_part(scale_attn) * (
        back1 - unit_part * jnp.mean(back1 * unit_part, axis=-1, keepdims=True)
    )
    tokens_rel = jnp.concatenate(
        line_gather(grad_inputs.astype(bf16), "tp", tp_size), axis=0
    )
    twice = jnp.concatenate([tokens_rel, tokens_rel], axis=0)
    grad_tokens = lax.dynamic_slice_in_dim(
        twice, row_count - own_tp * part, row_count, 0
    ).astype(f32)

    def parity(values, which):
        return lax.dynamic_index_in_dim(
            values.reshape(row_count, chips, 2, block), which, 2, keepdims=False
        ).reshape(row_count, chips * block)

    def both_tokens_parity(values):
        return jnp.concatenate([parity(values, core), swap(parity(values, 1 - core))], axis=0)

    def both_tokens(values):
        return jnp.concatenate([values, swap(values)], axis=0)

    def outer(left, right):
        return lax.dot_general(
            left, right, (((0,), (0,)), ((), ())), preferred_element_type=f32
        ).astype(bf16)

    def spread(values):
        return lax.psum_scatter(
            values, "seq", scatter_dimension=0, axis_index_groups=same_core, tiled=True
        )

    upstream_cols = both_tokens_parity(upstream_rel)
    normed2_cols = both_tokens_parity(normed_ffn)
    normed1_cols = both_tokens_parity(normed_attn)
    middle_cols = both_tokens_parity(middle_all)
    ffn_grads = jnp.concatenate(
        [
            outer(normed2_cols, both_tokens(gate_pre)),
            outer(normed2_cols, both_tokens(up_pre)),
            outer(upstream_cols, both_tokens(activated)),
        ],
        axis=1,
    )
    ffn_shard = spread(ffn_grads).astype(f32)
    hidden = w_gate.shape[1]
    attn_grads = jnp.concatenate(
        [
            outer(middle_cols, both_tokens(attended)),
            outer(normed1_cols, both_tokens(query_low)),
            outer(normed1_cols, both_tokens(key_low)),
            outer(normed1_cols, both_tokens(value_low)),
        ],
        axis=1,
    )
    attn_shard = spread(attn_grads).astype(f32)
    own_width = heads * head
    gains = lax.psum(jnp.stack([gain_attn_part, gain_ffn_part]), ("seq", "tp"))
    gains = lax.dynamic_slice_in_dim(gains, own_seq * block, block, 1)
    return (
        layer_out.reshape(1, row_count, width),
        grad_tokens.reshape(1, row_count, width),
        gains[0],
        attn_shard[:, own_width : 2 * own_width],
        attn_shard[:, 2 * own_width : 3 * own_width],
        attn_shard[:, 3 * own_width :],
        attn_shard[:, :own_width].T,
        gains[1],
        ffn_shard[:, :hidden],
        ffn_shard[:, hidden : 2 * hidden],
        ffn_shard[:, 2 * hidden :].T,
    )


def solution(mesh):
    placed = (
        P(None, "seq", None),
        P(),
        P(None, "tp"),
        P(None, "tp"),
        P(None, "tp"),
        P("tp", None),
        P(),
        P(None, "tp"),
        P(None, "tp"),
        P("tp", None),
        P(None, "seq", None),
        P(),
        P(),
        P(),
    )
    seq_size, tp_size = mesh.shape["seq"], mesh.shape["tp"]

    def local(*args):
        heads = args[2].shape[1] // HEAD_WIDTH
        if seq_size == 2 * heads and args[0].shape[0] == 1:
            return local_heads_apart(*args, seq_size=seq_size, tp_size=tp_size)
        return local_general(*args)

    return jax.shard_map(
        local,
        mesh=mesh,
        in_specs=placed,
        out_specs=(
            P(None, "seq", None),
            P(None, "seq", None),
            P("seq"),
            P("seq", "tp"),
            P("seq", "tp"),
            P("seq", "tp"),
            P("tp", "seq"),
            P("seq"),
            P("seq", "tp"),
            P("seq", "tp"),
            P("tp", "seq"),
        ),
        check_vma=False,
    )
```

```python
import functools
import math

import jax
import jax.numpy as jnp
from jax import lax
from jax.experimental import pallas as pl
from jax.experimental.pallas import tpu as pltpu
from jax.sharding import PartitionSpec as P

HEAD_WIDTH = 128


norm_eps = 1e-05
rope_base = 10000.0


def rope_tables(places, head_size):
    half_size = head_size // 2
    freqs = rope_base ** (-jnp.arange(half_size, dtype=jnp.float32) * 2.0 / head_size)
    angles = places.astype(jnp.float32)[..., None] * freqs
    return (jnp.cos(angles), jnp.sin(angles))


def rotate(values, cosine, sine, forward):
    half_size = values.shape[-1] // 2
    first = values[..., :half_size]
    second = values[..., half_size:]
    cos_b = cosine[..., None, :]
    sin_b = sine[..., None, :]
    if forward:
        return jnp.concatenate(
            [first * cos_b - second * sin_b, second * cos_b + first * sin_b], axis=-1
        )
    return jnp.concatenate(
        [first * cos_b + second * sin_b, second * cos_b - first * sin_b], axis=-1
    )


def visible(place_q, doc_q, place_k, doc_k, live_k):
    allowed = (
        (place_k[None, :] <= place_q[:, None])
        & (doc_k[None, :] == doc_q[:, None])
        & (live_k[None, :] == 1)
    )
    return allowed.astype(jnp.float32)


def score_block(query_heads, key_heads, head_size, length):
    scores = jnp.einsum("qhe,khe->hqk", query_heads, key_heads, preferred_element_type=jnp.float32)
    return scores * (1.0 / math.sqrt(head_size)) - math.log(length)


def score_grads(query_heads, key_heads, value_heads, grad_heads, mask, head_size, length):
    sigma = jax.nn.sigmoid(score_block(query_heads, key_heads, head_size, length))
    weights = (sigma * mask).astype(jnp.bfloat16)
    grad_weights = jnp.einsum(
        "qhe,khe->hqk", grad_heads, value_heads, preferred_element_type=jnp.float32
    )
    grad_scores = (grad_weights * (sigma * (1.0 - sigma)) * mask).astype(jnp.bfloat16)
    return (weights, grad_scores)


def local_general(
    tokens,
    gain_attn,
    w_query,
    w_key,
    w_value,
    w_out,
    gain_ffn,
    w_gate,
    w_up,
    w_down,
    cotangent,
    doc_ids,
    valid,
    group_order,
):
    seq_count, row_count, model_width = tokens.shape
    length = doc_ids.shape[1]
    span = length // group_order.shape[1]
    head_size = HEAD_WIDTH
    local_width = w_query.shape[1]
    local_heads = local_width // head_size
    flat_rows = seq_count * row_count
    factor = 1.0 / math.sqrt(head_size)
    own_rows = lax.axis_index("seq") * row_count + jnp.arange(row_count, dtype=jnp.int32)
    all_rows = jnp.arange(length, dtype=jnp.int32)
    place_all = jnp.take(group_order, all_rows // span, axis=1) * span + (all_rows % span)[None, :]
    place_own = jnp.take(group_order, own_rows // span, axis=1) * span + (own_rows % span)[None, :]
    doc_all = jnp.take_along_axis(doc_ids, place_all, axis=1)
    live_all = jnp.take_along_axis(valid, place_all, axis=1)
    doc_own = jnp.take_along_axis(doc_ids, place_own, axis=1)
    cosine, sine = rope_tables(place_own, head_size)
    input_rows = tokens.astype(jnp.float32).reshape(flat_rows, model_width)
    scale_attn = lax.rsqrt(jnp.mean(input_rows * input_rows, axis=-1, keepdims=True) + norm_eps)
    unit_attn = input_rows * scale_attn
    normed_attn = (unit_attn * gain_attn).astype(jnp.bfloat16)

    def project(weight_matrix):
        return jnp.dot(normed_attn, weight_matrix, preferred_element_type=jnp.float32).reshape(
            seq_count, row_count, local_heads, head_size
        )

    query_rot = (
        rotate(project(w_query), cosine, sine, True)
        .astype(jnp.bfloat16)
        .reshape(seq_count, row_count, local_width)
    )
    key_rot = (
        rotate(project(w_key), cosine, sine, True)
        .astype(jnp.bfloat16)
        .reshape(seq_count, row_count, local_width)
    )
    value_low = (
        jnp.dot(normed_attn, w_value, preferred_element_type=jnp.float32)
        .astype(jnp.bfloat16)
        .reshape(seq_count, row_count, local_width)
    )
    key_all, value_all = (
        lax.all_gather(key_rot, "seq", axis=1, tiled=True),
        lax.all_gather(value_low, "seq", axis=1, tiled=True),
    )

    def attend(items):
        query_seq, key_seq, value_seq, place_q, doc_q, place_k, doc_k, live_k = items
        query_heads = query_seq.reshape(row_count, local_heads, head_size)
        key_heads = key_seq.reshape(length, local_heads, head_size)
        value_heads = value_seq.reshape(length, local_heads, head_size)
        mask = visible(place_q, doc_q, place_k, doc_k, live_k)
        weights = (
            jax.nn.sigmoid(score_block(query_heads, key_heads, head_size, length)) * mask
        ).astype(jnp.bfloat16)
        mixed = jnp.einsum("hqk,khe->qhe", weights, value_heads, preferred_element_type=jnp.float32)
        return mixed.astype(jnp.bfloat16).reshape(row_count, local_width)

    attention_output = lax.map(
        attend, (query_rot, key_all, value_all, place_own, doc_own, place_all, doc_all, live_all)
    )
    attended_flat = attention_output.reshape(flat_rows, local_width)
    branch_attn = lax.psum(jnp.dot(attended_flat, w_out, preferred_element_type=jnp.float32), "tp")
    hidden_rows = input_rows + branch_attn
    scale_ffn = lax.rsqrt(jnp.mean(hidden_rows * hidden_rows, axis=-1, keepdims=True) + norm_eps)
    unit_ffn = hidden_rows * scale_ffn
    normalized_feedforward = (unit_ffn * gain_ffn).astype(jnp.bfloat16)
    gate_rows = jnp.dot(normalized_feedforward, w_gate, preferred_element_type=jnp.float32)
    up_projected = jnp.dot(normalized_feedforward, w_up, preferred_element_type=jnp.float32)
    gate_sig = jax.nn.sigmoid(gate_rows)
    activation_rows = (gate_rows * gate_sig * up_projected).astype(jnp.bfloat16)
    branch_ffn = lax.psum(
        jnp.dot(activation_rows, w_down, preferred_element_type=jnp.float32).astype(jnp.bfloat16),
        "tp",
    ).astype(jnp.float32)
    layer_out = (
        (hidden_rows + branch_ffn).astype(jnp.bfloat16).reshape(seq_count, row_count, model_width)
    )
    upstream = cotangent.astype(jnp.float32).reshape(flat_rows, model_width)
    upstream_low = upstream.astype(jnp.bfloat16)
    grad_down = jnp.einsum(
        "tf,td->fd", activation_rows, upstream_low, preferred_element_type=jnp.float32
    )
    grad_act = jnp.einsum("td,fd->tf", upstream_low, w_down, preferred_element_type=jnp.float32)
    gate_pre = (grad_act * up_projected * (gate_sig * (1.0 + gate_rows * (1.0 - gate_sig)))).astype(
        jnp.bfloat16
    )
    up_pre = (grad_act * (gate_rows * gate_sig)).astype(jnp.bfloat16)
    grad_gate = jnp.einsum(
        "td,tf->df", normalized_feedforward, gate_pre, preferred_element_type=jnp.float32
    )
    grad_up = jnp.einsum(
        "td,tf->df", normalized_feedforward, up_pre, preferred_element_type=jnp.float32
    )
    normed_ffn_part = jnp.einsum(
        "tf,df->td", gate_pre, w_gate, preferred_element_type=jnp.float32
    ) + jnp.einsum("tf,df->td", up_pre, w_up, preferred_element_type=jnp.float32)
    grad_normed_ffn = lax.psum(normed_ffn_part, "tp")
    gain_ffn_part = jnp.sum(grad_normed_ffn * unit_ffn, axis=0)
    back_ffn = grad_normed_ffn * gain_ffn
    grad_middle = upstream + scale_ffn * (
        back_ffn - unit_ffn * jnp.mean(back_ffn * unit_ffn, axis=-1, keepdims=True)
    )
    middle_low = grad_middle.astype(jnp.bfloat16)
    grad_out = jnp.einsum(
        "te,td->ed", attended_flat, middle_low, preferred_element_type=jnp.float32
    )
    grad_attended = (
        jnp.einsum("td,ed->te", middle_low, w_out, preferred_element_type=jnp.float32)
        .astype(jnp.bfloat16)
        .reshape(seq_count, row_count, local_width)
    )
    key_back, value_back = (key_all, value_all)

    def attend_back(items):
        query_seq, key_seq, value_seq, grad_seq, place_q, doc_q, place_k, doc_k, live_k = items
        query_heads = query_seq.reshape(row_count, local_heads, head_size)
        key_heads = key_seq.reshape(length, local_heads, head_size)
        value_heads = value_seq.reshape(length, local_heads, head_size)
        grad_heads = grad_seq.reshape(row_count, local_heads, head_size)
        mask = visible(place_q, doc_q, place_k, doc_k, live_k)
        weights, grad_scores = score_grads(
            query_heads, key_heads, value_heads, grad_heads, mask, head_size, length
        )
        grad_value_seq = jnp.einsum(
            "hqk,qhe->khe", weights, grad_heads, preferred_element_type=jnp.float32
        )
        grad_query_seq = (
            jnp.einsum("hqk,khe->qhe", grad_scores, key_heads, preferred_element_type=jnp.float32)
            * factor
        )
        grad_key_seq = (
            jnp.einsum("hqk,qhe->khe", grad_scores, query_heads, preferred_element_type=jnp.float32)
            * factor
        )
        return (
            grad_query_seq,
            grad_key_seq.reshape(length, local_width),
            grad_value_seq.reshape(length, local_width),
        )

    grad_query_rot, grad_key_all, grad_value_all = lax.map(
        attend_back,
        (
            query_rot,
            key_back,
            value_back,
            grad_attended,
            place_own,
            doc_own,
            place_all,
            doc_all,
            live_all,
        ),
    )
    grad_key_rot, grad_value_own = (
        lax.psum_scatter(grad_key_all, "seq", scatter_dimension=1, tiled=True),
        lax.psum_scatter(grad_value_all, "seq", scatter_dimension=1, tiled=True),
    )
    query_low = (
        rotate(grad_query_rot, cosine, sine, False)
        .astype(jnp.bfloat16)
        .reshape(flat_rows, local_width)
    )
    key_low = (
        rotate(
            grad_key_rot.reshape(seq_count, row_count, local_heads, head_size), cosine, sine, False
        )
        .astype(jnp.bfloat16)
        .reshape(flat_rows, local_width)
    )
    value_grad_low = grad_value_own.astype(jnp.bfloat16).reshape(flat_rows, local_width)
    grad_query = jnp.einsum("td,te->de", normed_attn, query_low, preferred_element_type=jnp.float32)
    grad_key = jnp.einsum("td,te->de", normed_attn, key_low, preferred_element_type=jnp.float32)
    grad_value = jnp.einsum(
        "td,te->de", normed_attn, value_grad_low, preferred_element_type=jnp.float32
    )
    normed_attn_part = (
        jnp.einsum("te,de->td", query_low, w_query, preferred_element_type=jnp.float32)
        + jnp.einsum("te,de->td", key_low, w_key, preferred_element_type=jnp.float32)
        + jnp.einsum("te,de->td", value_grad_low, w_value, preferred_element_type=jnp.float32)
    )
    grad_normed_attn = lax.psum(normed_attn_part, "tp")
    gain_attn_part = jnp.sum(grad_normed_attn * unit_attn, axis=0)
    back_attn = grad_normed_attn * gain_attn
    grad_inputs = grad_middle + scale_attn * (
        back_attn - unit_attn * jnp.mean(back_attn * unit_attn, axis=-1, keepdims=True)
    )
    grad_tokens = grad_inputs.reshape(seq_count, row_count, model_width)
    (
        query_shard,
        key_shard,
        value_shard,
        out_shard,
        gain_attn_shard,
        gate_shard,
        up_shard,
        down_shard,
        gain_ffn_shard,
    ) = (
        lax.psum_scatter(grad_query, "seq", scatter_dimension=0, tiled=True),
        lax.psum_scatter(grad_key, "seq", scatter_dimension=0, tiled=True),
        lax.psum_scatter(grad_value, "seq", scatter_dimension=0, tiled=True),
        lax.psum_scatter(grad_out, "seq", scatter_dimension=1, tiled=True),
        lax.psum_scatter(gain_attn_part, "seq", scatter_dimension=0, tiled=True),
        lax.psum_scatter(grad_gate, "seq", scatter_dimension=0, tiled=True),
        lax.psum_scatter(grad_up, "seq", scatter_dimension=0, tiled=True),
        lax.psum_scatter(grad_down, "seq", scatter_dimension=1, tiled=True),
        lax.psum_scatter(gain_ffn_part, "seq", scatter_dimension=0, tiled=True),
    )
    return (
        layer_out,
        grad_tokens,
        gain_attn_shard,
        query_shard,
        key_shard,
        value_shard,
        out_shard,
        gain_ffn_shard,
        gate_shard,
        up_shard,
        down_shard,
    )


def dense(left, right):
    return jnp.dot(left, right, preferred_element_type=jnp.float32)


def dense_t(left, right):
    return lax.dot_general(
        left, right, (((1,), (1,)), ((), ())), preferred_element_type=jnp.float32
    )


def sigma_of(scores, length):
    return 1.0 / (1.0 + jnp.exp(math.log(length) - scores * (1.0 / math.sqrt(HEAD_WIDTH))))


def in_position_order(slot_places, own_ref, other_ref, own_first, span, scratch_refs):
    head = HEAD_WIDTH
    own_slots = own_ref.shape[0] // span
    for slot in range(2 * own_slots):
        source, first = (own_ref, own_first) if slot < own_slots else (other_ref, 0)
        rows = slice((slot % own_slots) * span, (slot % own_slots + 1) * span)
        target = pl.ds(pl.multiple_of(slot_places[slot] * span, span), span)
        for index, scratch in enumerate(scratch_refs):
            columns = slice(first + index * head, first + (index + 1) * head)
            scratch[target, :] = source[rows, columns]
    for scratch in scratch_refs:
        scratch[2 * own_slots * span :, :] = jnp.zeros((span, head), scratch.dtype)


def attend_kernel(
    slot_places, key_low, own_ref, other_ref, start_ref, out_ref, key_ref, value_ref, *, span
):
    head = HEAD_WIDTH
    own_slots = own_ref.shape[0] // span
    length = 2 * own_ref.shape[0]
    in_position_order(slot_places, own_ref, other_ref, head, span, (key_ref, value_ref))
    row = lax.broadcasted_iota(jnp.int32, (span, 2 * span), 0)
    column = lax.broadcasted_iota(jnp.int32, (span, 2 * span), 1)

    def query_block(slot, carry):
        rows = pl.ds(pl.multiple_of(slot * span, span), span)
        place = slot_places[slot]
        low = key_low[slot]
        query = own_ref[rows, :head]
        first = start_ref[rows, :]

        def key_pair(step, total):
            base = pl.multiple_of((low + 2 * step) * span, span)
            keys = pl.ds(base, 2 * span)
            scores = dense_t(query, key_ref[keys, :])
            seen = (column >= first - base) & (column - row <= place * span - base)
            probs = jnp.where(seen, sigma_of(scores, length), 0.0).astype(jnp.bfloat16)
            return total + dense(probs, value_ref[keys, :])

        total = lax.fori_loop(
            0, (place - low) // 2 + 1, key_pair, jnp.zeros((span, head), jnp.float32)
        )
        out_ref[rows, :] = total.astype(jnp.bfloat16)
        return carry

    lax.fori_loop(0, own_slots, query_block, 0)


def attend_back_kernel(
    slot_places,
    key_low,
    own_ref,
    other_ref,
    start_ref,
    grad_ref,
    grad_query_ref,
    grad_own_ref,
    grad_other_ref,
    key_ref,
    value_ref,
    sum_key_ref,
    sum_value_ref,
    *,
    span,
):
    head = HEAD_WIDTH
    own_slots = own_ref.shape[0] // span
    length = 2 * own_ref.shape[0]
    factor = 1.0 / math.sqrt(head)
    in_position_order(slot_places, own_ref, other_ref, head, span, (key_ref, value_ref))
    sum_key_ref[...] = jnp.zeros_like(sum_key_ref)
    sum_value_ref[...] = jnp.zeros_like(sum_value_ref)
    row = lax.broadcasted_iota(jnp.int32, (2 * span, span), 0)
    column = lax.broadcasted_iota(jnp.int32, (2 * span, span), 1)

    def query_block(slot, carry):
        rows = pl.ds(pl.multiple_of(slot * span, span), span)
        place = slot_places[slot]
        low = key_low[slot]
        query = own_ref[rows, :head]
        grad = grad_ref[rows, :]
        first = start_ref[pl.ds(slot, 1), :]

        def key_pair(step, total):
            base = pl.multiple_of((low + 2 * step) * span, span)
            keys = pl.ds(base, 2 * span)
            key = key_ref[keys, :]
            seen = (row >= first - base) & (row - column <= place * span - base)
            sigma = jnp.where(seen, sigma_of(dense_t(key, query), length), 0.0)
            sum_value_ref[keys, :] += dense(sigma.astype(jnp.bfloat16), grad)
            grad_probs = dense_t(value_ref[keys, :], grad)
            grad_scores = (grad_probs * (sigma * (1.0 - sigma))).astype(jnp.bfloat16)
            sum_key_ref[keys, :] += dense(grad_scores, query)
            return total + lax.dot_general(
                grad_scores, key, (((0,), (0,)), ((), ())), preferred_element_type=jnp.float32
            )

        total = lax.fori_loop(
            0, (place - low) // 2 + 1, key_pair, jnp.zeros((span, head), jnp.float32)
        )
        grad_query_ref[rows, :] = total * factor
        return carry

    lax.fori_loop(0, own_slots, query_block, 0)
    for slot in range(2 * own_slots):
        target = grad_own_ref if slot < own_slots else grad_other_ref
        rows = slice((slot % own_slots) * span, (slot % own_slots + 1) * span)
        source = pl.ds(pl.multiple_of(slot_places[slot] * span, span), span)
        target[rows, :head] = (sum_key_ref[source, :] * factor).astype(target.dtype)
        target[rows, head:] = sum_value_ref[source, :].astype(target.dtype)


SHORT = pl.CostEstimate(flops=1, bytes_accessed=1, transcendentals=0)
SMALL = pl.BlockSpec(memory_space=pltpu.SMEM)
WHOLE = pl.BlockSpec(memory_space=pltpu.VMEM)


def attend_call(slot_places, key_low, own, other, start, span):
    rows = own.shape[0]
    return pl.pallas_call(
        functools.partial(attend_kernel, span=span),
        out_shape=jax.ShapeDtypeStruct((rows, HEAD_WIDTH), jnp.bfloat16),
        in_specs=[SMALL, SMALL, WHOLE, WHOLE, WHOLE],
        out_specs=WHOLE,
        scratch_shapes=[pltpu.VMEM((2 * rows + span, HEAD_WIDTH), jnp.bfloat16)] * 2,
        compiler_params=pltpu.CompilerParams(vmem_limit_bytes=8 << 20),
        cost_estimate=SHORT,
        name="attend",
    )(slot_places, key_low, own, other, start)


def attend_back_call(slot_places, key_low, own, other, start, grad, span):
    rows = own.shape[0]
    return pl.pallas_call(
        functools.partial(attend_back_kernel, span=span),
        out_shape=(
            jax.ShapeDtypeStruct((rows, HEAD_WIDTH), jnp.float32),
            jax.ShapeDtypeStruct((rows, 2 * HEAD_WIDTH), jnp.float32),
            jax.ShapeDtypeStruct((rows, 2 * HEAD_WIDTH), jnp.bfloat16),
        ),
        in_specs=[SMALL, SMALL, WHOLE, WHOLE, WHOLE, WHOLE],
        out_specs=(WHOLE, WHOLE, WHOLE),
        scratch_shapes=[pltpu.VMEM((2 * rows + span, HEAD_WIDTH), jnp.bfloat16)] * 2
        + [pltpu.VMEM((2 * rows + span, HEAD_WIDTH), jnp.float32)] * 2,
        compiler_params=pltpu.CompilerParams(vmem_limit_bytes=14 << 20),
        cost_estimate=SHORT,
        name="attend_back",
    )(slot_places, key_low, own, other, start, grad)


def call(kernel, outs, ins, scratch=(), scalars=0, grid=None, in_specs=None, out_specs=None, work=0, name=None, room=12):
    params = pltpu.CompilerParams(vmem_limit_bytes=room << 20)
    if grid is None:
        return pl.pallas_call(
            kernel,
            out_shape=tuple(outs),
            in_specs=[SMALL] * scalars + [WHOLE] * (len(ins) - scalars),
            out_specs=tuple([WHOLE] * len(outs)),
            scratch_shapes=list(scratch),
            compiler_params=params,
            cost_estimate=SHORT,
            name=name,
        )(*ins)
    return pl.pallas_call(
        kernel,
        out_shape=tuple(outs),
        grid_spec=pltpu.PrefetchScalarGridSpec(
            num_scalar_prefetch=scalars,
            grid=grid,
            in_specs=in_specs,
            out_specs=tuple(out_specs),
            scratch_shapes=list(scratch),
        ),
        compiler_params=params,
        cost_estimate=SHORT,
        name=name,
    )(*ins)


def made(shape, dtype):
    return jax.ShapeDtypeStruct(shape, dtype)


def norm_of(values):
    rows = values.astype(jnp.float32)
    scale = lax.rsqrt(jnp.mean(rows * rows, axis=-1, keepdims=True) + norm_eps)
    return scale, rows * scale


def norm_back(grad, gain, scale, unit):
    back = grad * gain
    return scale * (back - unit * jnp.mean(back * unit, axis=-1, keepdims=True))


def project_kernel(
    tokens_ref, gain_ref, live_ref, cosine_ref, sine_ref, query_ref, key_ref, value_ref, packed_ref, normed_ref
):
    head = HEAD_WIDTH
    rows = tokens_ref.shape[0]

    @pl.when(pl.program_id(0) == 0)
    def _():
        step = 128

        def piece(index, carry):
            at = pl.ds(pl.multiple_of(index * step, step), step)
            normed_ref[at, :] = (norm_of(tokens_ref[at, :])[1] * gain_ref[...]).astype(jnp.bfloat16)
            return carry

        lax.fori_loop(0, rows // step, piece, 0)

    normed = normed_ref[...]
    for index, weight in enumerate((query_ref, key_ref, value_ref)):
        both = dense(normed, weight[...])
        for which in range(2):
            values = both[:, which * head : (which + 1) * head]
            if index < 2:
                values = values * cosine_ref[...] + pltpu.roll(values, head // 2, 1) * sine_ref[...]
            else:
                values = jnp.where(live_ref[...] == 1, values, 0.0)
            packed_ref[which, :, index * head : (index + 1) * head] = values.astype(jnp.bfloat16)


def project_call(tokens, gain, live, cosine, sine, w_query, w_key, w_value):
    rows, width = tokens.shape
    heads = w_query.shape[1] // HEAD_WIDTH
    whole = lambda shape: pl.BlockSpec(shape, lambda h: (0, 0))
    weight = pl.BlockSpec((width, 2 * HEAD_WIDTH), lambda h: (0, h))
    w_query, w_key, w_value = [
        pltpu.with_memory_space_constraint(w, pltpu.HBM) for w in (w_query, w_key, w_value)
    ]
    return call(
        project_kernel,
        (made((heads, rows, 3 * HEAD_WIDTH), jnp.bfloat16), made((rows, width), jnp.bfloat16)),
        (tokens, gain, live, cosine, sine, w_query, w_key, w_value),
        grid=(heads // 2,),
        in_specs=[
            whole((rows, width)), whole((1, width)), whole((rows, 1)),
            whole((rows, HEAD_WIDTH)), whole((rows, HEAD_WIDTH)), weight, weight, weight,
        ],
        out_specs=[
            pl.BlockSpec((2, rows, 3 * HEAD_WIDTH), lambda h: (h, 0, 0)), whole((rows, width)),
        ],
        work=6 * rows * width * w_query.shape[1],
        room=32,
        name="project",
    )


def piece_at(own_tp, d, count):
    return lax.rem(own_tp + d, count)


def out_kernel(where_ref, tokens_ref, gain_ref, attended_ref, *refs):
    *weights, middle_ref, normed_ref = refs
    own_tp, core = where_ref[0], where_ref[1]
    count, part, _ = attended_ref.shape
    half = weights[0].shape[0]
    total = tokens_ref[pl.ds(pl.multiple_of(own_tp * part, part), part), :].astype(jnp.float32)
    for d in range(count):
        for which in range(2):
            side = core if which == 0 else 1 - core
            columns = pl.ds(pl.multiple_of(side * half, half), half)
            values = attended_ref[piece_at(own_tp, d, count), :, columns]
            total = total + dense(values, weights[2 * d + which][...])
    middle_ref[...] = total
    normed_ref[...] = (norm_of(total)[1] * gain_ref[...]).astype(jnp.bfloat16)


def ffn_kernel(where_ref, *refs, chunk, sources, first):
    grad_act_ref, gate_ref, up_ref = refs[sources : sources + 3]
    act_ref, gate_pre_ref, up_pre_ref, normed_ref, *grads, total_ref = refs[
        sources + 3 + (0 if first else 4) :
    ]
    own_tp = where_ref[0]
    part = grads[0].shape[0]
    step = pl.program_id(0)

    @pl.when(step == 0)
    def _():
        if first:
            normed_ref[:part, :] = refs[0][...]
            normed_ref[part:, :] = jnp.where(from_above(own_tp, 1), refs[1][...], refs[2][...])
        elif chunk == 2:
            normed_ref[...] = jnp.where(from_above(own_tp, 2), refs[0][...], refs[1][...])
        else:
            inner = jnp.where(own_tp == 1, refs[0][...], refs[1][...])
            ends = jnp.where(own_tp == 0, refs[2][...], refs[3][...])
            normed_ref[...] = jnp.where(is_inner(own_tp), inner, ends)

    normed = normed_ref[...]
    gate = dense(normed, gate_ref[...])
    up = dense(normed, up_ref[...])
    sig = jax.nn.sigmoid(gate)
    grad_act = grad_act_ref[...]
    act_ref[...] = (gate * sig * up).astype(jnp.bfloat16)
    gate_pre = (grad_act * up * (sig * (1.0 + gate * (1.0 - sig)))).astype(jnp.bfloat16)
    up_pre = (grad_act * (gate * sig)).astype(jnp.bfloat16)
    gate_pre_ref[...] = gate_pre
    up_pre_ref[...] = up_pre
    term = dense_t(gate_pre, gate_ref[...]) + dense_t(up_pre, up_ref[...])

    @pl.when(step == 0)
    def _():
        total_ref[...] = term

    @pl.when(step > 0)
    def _():
        total_ref[...] += term

    @pl.when(step == pl.num_programs(0) - 1)
    def _():
        for index, grad_ref in enumerate(grads):
            rows = slice(index * part, (index + 1) * part)
            grad_ref[...] = total_ref[rows, :].astype(jnp.bfloat16)


def from_above(own_tp, chunk):
    return own_tp % (2 * chunk) < chunk


def is_inner(own_tp):
    return (own_tp == 1) | (own_tp == 2)


def ffn_call(where, chunk, sources, grad_act, w_gate, w_up, filled):
    part, width = sources[0].shape
    total, hidden = grad_act.shape
    wide = 512
    count = 2 if filled is None else 1
    rows = count * part
    whole = pl.BlockSpec((part, width), lambda f, w: (0, 0))
    weight = pl.BlockSpec((width, wide), lambda f, w: (0, f))
    block = pl.BlockSpec((rows, wide), lambda f, w: (chunk, f))
    low = made((total, hidden), jnp.bfloat16)
    w_gate, w_up = [pltpu.with_memory_space_constraint(w, pltpu.HBM) for w in (w_gate, w_up)]
    ins = [where, *sources, grad_act, w_gate, w_up]
    specs = [whole] * len(sources) + [block, weight, weight]
    aliases = {}
    if filled is not None:
        aliases = {len(ins) + i: i for i in range(4)}
        ins += list(filled)
        specs += [pl.BlockSpec(memory_space=pl.ANY)] * 4
    outs = pl.pallas_call(
        functools.partial(ffn_kernel, chunk=chunk, sources=len(sources), first=not aliases),
        out_shape=(low, low, low, made((total, width), jnp.bfloat16))
        + (made((part, width), jnp.bfloat16),) * count,
        grid_spec=pltpu.PrefetchScalarGridSpec(
            num_scalar_prefetch=1,
            grid=(hidden // wide,),
            in_specs=specs,
            out_specs=(
                block, block, block, pl.BlockSpec((rows, width), lambda f, w: (chunk, 0)),
            )
            + (whole,) * count,
            scratch_shapes=[pltpu.VMEM((rows, width), jnp.float32)],
        ),
        input_output_aliases=aliases,
        compiler_params=pltpu.CompilerParams(vmem_limit_bytes=28 << 20),
        cost_estimate=SHORT,
        name="ffn",
    )(*ins)
    return outs[:4], outs[4:]


def middle_kernel(where_ref, middle_ref, upstream_ref, gain_ref, *refs):
    terms, refs = refs[: refs[-2].shape[0]], refs[refs[-2].shape[0] :]
    *weights, low_ref, grad_ref, back_ref, gain_grad_ref = refs
    own_tp, core = where_ref[0], where_ref[1]
    count, part, _ = back_ref.shape
    half = weights[0].shape[0]
    scale, unit = norm_of(middle_ref[...])
    grad = sum([t[...].astype(jnp.float32) for t in terms[1:]], terms[0][...].astype(jnp.float32))
    gain_grad_ref[...] = jnp.sum(grad * unit, axis=0, keepdims=True)
    at = pl.ds(pl.multiple_of(own_tp * part, part), part)
    total = upstream_ref[at, :].astype(jnp.float32) + norm_back(grad, gain_ref[...], scale, unit)
    grad_ref[...] = total
    low = total.astype(jnp.bfloat16)
    low_ref[...] = low
    for d in range(count):
        for which in range(2):
            side = core if which == 0 else 1 - core
            columns = pl.ds(pl.multiple_of(side * half, half), half)
            back_ref[piece_at(own_tp, d, count), :, columns] = dense_t(
                low, weights[2 * d + which][...]
            ).astype(jnp.bfloat16)


def back_kernel(where_ref, back_ref, live_ref, tokens_ref, query_ref, key_ref, value_ref, low_ref, gain_ref, *refs):
    *outs, ordered_ref, unit_ref = refs
    head = HEAD_WIDTH
    heads = back_ref.shape[0]
    count = len(outs)
    part = outs[0].shape[0]
    own = heads * head
    step = pl.program_id(0)

    @pl.when(step == 0)
    def _():
        for d in range(count):
            at = pl.ds(pl.multiple_of(piece_at(where_ref[0], d, count) * part, part), part)
            rows = slice(d * part, (d + 1) * part)
            for index in range(3):
                low = jnp.concatenate(
                    [back_ref[h, at, index * head : (index + 1) * head] for h in range(heads)],
                    axis=-1,
                )
                if index == 2:
                    low = jnp.where(live_ref[at, :] == 1, low.astype(jnp.float32), 0.0)
                    low = low.astype(jnp.bfloat16)
                low_ref[at, index * own : (index + 1) * own] = low
                ordered_ref[rows, index * own : (index + 1) * own] = low
            unit = norm_of(tokens_ref[at, :])[1]
            for block in range(unit_ref.shape[0]):
                wide = unit_ref.shape[2]
                unit_ref[block, rows, :] = unit[:, block * wide : (block + 1) * wide]

    total = None
    for index, weight in enumerate((query_ref, key_ref, value_ref)):
        term = dense_t(ordered_ref[:, index * own : (index + 1) * own], weight[...])
        total = term if total is None else total + term
    gain_ref[...] = jnp.sum(total * unit_ref[step], axis=0, keepdims=True)
    for d in range(count):
        outs[d][...] = total[d * part : (d + 1) * part].astype(jnp.bfloat16)


def back_call(where, back_heads, live, tokens, weights, count):
    rows, width = tokens.shape
    own = weights[0].shape[1]
    part = rows // count
    wide = 512
    blocks = width // wide
    weights = [pltpu.with_memory_space_constraint(w, pltpu.HBM) for w in weights]
    whole = lambda x: pl.BlockSpec(x.shape, lambda f, w: (0,) * len(x.shape))
    return pl.pallas_call(
        back_kernel,
        out_shape=(made((rows, 3 * own), jnp.bfloat16), made((1, width), jnp.float32))
        + (made((part, width), jnp.bfloat16),) * count,
        grid_spec=pltpu.PrefetchScalarGridSpec(
            num_scalar_prefetch=1,
            grid=(blocks,),
            in_specs=[whole(back_heads), whole(live), whole(tokens)]
            + [pl.BlockSpec((wide, own), lambda f, w: (f, 0))] * 3,
            out_specs=(
                pl.BlockSpec((rows, 3 * own), lambda f, w: (0, 0)),
                pl.BlockSpec((1, wide), lambda f, w: (0, f)),
            )
            + (pl.BlockSpec((part, wide), lambda f, w: (0, f)),) * count,
            scratch_shapes=[
                pltpu.VMEM((rows, 3 * own), jnp.bfloat16),
                pltpu.VMEM((blocks, rows, wide), jnp.float32),
            ],
        ),
        compiler_params=pltpu.CompilerParams(vmem_limit_bytes=32 << 20),
        cost_estimate=SHORT,
        name="back",
    )(where, back_heads, live, tokens, *weights)


def tokens_kernel(where_ref, tokens_ref, gain_ref, middle_ref, gains_ref, own_ref, below_ref, above_ref, out_ref):
    part = own_ref.shape[0]
    at = pl.ds(pl.multiple_of(where_ref[0] * part, part), part)
    scale, unit = norm_of(tokens_ref[at, :])
    grad = own_ref[...].astype(jnp.float32) + (
        below_ref[...].astype(jnp.float32) + above_ref[...].astype(jnp.float32)
    )
    total = middle_ref[...] + norm_back(grad, gain_ref[...], scale, unit)
    out_ref[:part, :] = total.astype(jnp.bfloat16)
    gains = gains_ref[...]
    high = gains.astype(jnp.bfloat16)
    low = (gains - high.astype(jnp.float32)).astype(jnp.bfloat16)
    wide = gains.shape[1]
    rows = out_ref.shape[0] - part
    for index, values in enumerate((high, low)):
        out_ref[part:, index * wide : (index + 1) * wide] = jnp.broadcast_to(values, (rows, wide))
    out_ref[part:, 2 * wide :] = jnp.zeros((rows, out_ref.shape[1] - 2 * wide), jnp.bfloat16)


def layer_kernel(middle_ref, branch_ref, out_ref):
    out_ref[...] = (middle_ref[...] + branch_ref[...].astype(jnp.float32)).astype(jnp.bfloat16)


def join_kernel(where_ref, own_ref, *refs, relative, part):
    count = (len(refs) - (1 if own_ref.shape[0] == part else 3)) // 2 + 1
    pieces, (out_ref, *rest) = refs[: 2 * count - 2], refs[2 * count - 2 :]
    for d in range(count):
        place = d if relative else piece_at(where_ref[0], d, count)
        values = own_ref[...] if d == 0 else pieces[d - 1][...] + pieces[2 * count - 2 - d][...]
        out_ref[pl.ds(pl.multiple_of(place * part, part), part), :] = values[:part].astype(out_ref.dtype)
        if rest:
            gains_ref, terms_ref = rest
            wide = gains_ref.shape[1]
            row = values[part:].astype(jnp.float32)
            terms_ref[place] = row[:8, :wide] + row[:8, wide : 2 * wide]
    if rest:
        total = terms_ref[0]
        for index in range(1, count):
            total = total + terms_ref[index]
        gains_ref[...] = total[:1]


def join(where, gathered, dtype, relative, gains=0):
    own, above, below = gathered
    count = len(above) + 1
    part, width = own.shape[0] - (16 if gains else 0), own.shape[1]
    outs, scratch = [made((count * part, width), dtype)], []
    if gains:
        outs.append(made((1, gains), jnp.float32))
        scratch.append(pltpu.VMEM((count, 8, gains), jnp.float32))
    return call(
        functools.partial(join_kernel, relative=relative, part=part),
        outs,
        (where, own, *above, *below),
        scratch=scratch,
        scalars=1,
        name="join",
    )


def tie(*values):
    return lax.optimization_barrier(values)


def after(value, *others):
    return lax.optimization_barrier((value, *others))[0]


class Line:
    def __init__(self, axis, count):
        self.axis, self.count, self.at = axis, count, 0
        self.upward, self.downward = None, None

    def tie(self, *others):
        self.upward, self.downward, *others = tie(self.upward, self.downward, *others)
        return others[0] if len(others) == 1 else others

    def send(self, up, down, up_pairs, down_pairs):
        self.upward = lax.ppermute(up, self.axis, up_pairs)
        self.downward = lax.ppermute(down, self.axis, down_pairs)


class Gather(Line):
    def __init__(self, shard, axis, count):
        super().__init__(axis, count)
        self.own, self.above, self.below = shard, [], []

    def step(self):
        if self.at:
            self.keep()
        up, down = (self.upward, self.downward) if self.at else (self.own, self.own)
        self.at += 1
        at, count = self.at, self.count
        self.send(
            up,
            down,
            [(i, i + 1) for i in range(at - 1, count - 1)],
            [(i, i - 1) for i in range(1, count - at + 1)],
        )

    def keep(self):
        self.below.append(self.upward)
        self.above.append(self.downward)

    def result(self):
        while self.at < self.count - 1:
            self.step()
        self.keep()
        return self.own, self.above, self.below


class Sum(Line):
    def __init__(self, parts, axis, count):
        super().__init__(axis, count)
        self.parts = parts

    def step(self):
        f32, bf16 = jnp.float32, jnp.bfloat16
        first = self.at == 0
        self.at += 1
        at, count = self.at, self.count
        up, down = self.parts[count - at], self.parts[at]
        if not first:
            up = (up.astype(f32) + self.upward.astype(f32)).astype(bf16)
            down = (down.astype(f32) + self.downward.astype(f32)).astype(bf16)
        self.send(
            up,
            down,
            [(i, i + 1) for i in range(0, at)],
            [(i, i - 1) for i in range(count - at, count)],
        )

    def result(self):
        while self.at < self.count - 1:
            self.step()
        return self.parts[0], self.upward, self.downward


def outer(left, right):
    return lax.dot_general(
        left, right, (((0,), (0,)), ((), ())), preferred_element_type=jnp.float32
    )


def chip_outer_kernel(where_ref, *refs, sides):
    del where_ref
    keep_x, sent_x, keep_y, sent_y = refs[-4:]
    step = pl.program_id(0)
    values = []
    for side in range(sides):
        left, left_other, right, right_other = refs[4 * side : 4 * side + 4]
        product = outer(left[...], right[...]) + outer(left_other[...], right_other[...])
        values.append(product.astype(jnp.bfloat16))
    values = values[0] if sides == 1 else jnp.concatenate(values, axis=-1)
    half = values.shape[1] // 2

    for target, part, places in (
        (keep_x, 0, (0, 1)),
        (sent_x, 0, (2, 3)),
        (keep_y, 1, (0, 3)),
        (sent_y, 1, (1, 2)),
    ):

        @pl.when((step == places[0]) | (step == places[1]))
        def _(target=target, part=part):
            target[0] = values[:, part * half : (part + 1) * half]


def chip_outer_call(where, pairs, seq_size, name, columns=1, column=0, into=None):
    rows, width = pairs[0][0].shape
    block = width // seq_size
    half = sum(pair[2].shape[1] for pair in pairs) // 2

    def left_index(k, w):
        chip = jnp.where(k == 0, 0, jnp.where(k == 1, 2, jnp.where(k == 2, 3, 1)))
        return 0, 2 * (w[2] ^ chip) + w[1]

    specs, ins = [], []
    for pair in pairs:
        wide = pl.BlockSpec(pair[2].shape, lambda k, w: (0, 0))
        specs += [pl.BlockSpec((rows, block), left_index)] * 2 + [wide, wide]
        ins += list(pair)
    aliases = {}
    if into is not None:
        aliases = {1 + len(ins) + i: i for i in range(4)}
        specs += [pl.BlockSpec(memory_space=pltpu.HBM)] * 4
        ins += list(into)

    def target(place):
        return pl.BlockSpec((1, block, half), lambda k, w: (place(k), 0, column))

    return pl.pallas_call(
        functools.partial(chip_outer_kernel, sides=len(pairs)),
        out_shape=(pltpu.HBM((2, block, columns * half), jnp.bfloat16),) * 4,
        grid_spec=pltpu.PrefetchScalarGridSpec(
            num_scalar_prefetch=1,
            grid=(4,),
            in_specs=specs,
            out_specs=(
                target(lambda k: jnp.minimum(k, 1)),
                target(lambda k: k // 3),
                target(lambda k: k // 3),
                target(lambda k: k // 2),
            ),
        ),
        input_output_aliases=aliases,
        compiler_params=pltpu.CompilerParams(vmem_limit_bytes=24 << 20),
        cost_estimate=SHORT,
        name=name,
    )(where, *ins)


class ChipSum:
    def __init__(self, arrays, seq_size):
        self.arrays, self.size = arrays, seq_size

    def over(self, values, side):
        return lax.ppermute(values, "seq", [(i, i ^ side) for i in range(self.size)])

    def first(self, *earlier):
        _, sent_x, _, sent_y = self.arrays
        if earlier:
            sent_x, sent_y = tie(sent_x, sent_y, *earlier)[:2]
        self.got_x, self.got_y = self.over(sent_x, 2), self.over(sent_y, 4)

    def tie(self, *others):
        self.got_x, self.got_y, *others = tie(self.got_x, self.got_y, *others)
        return others[0] if len(others) == 1 else others

    def second(self, *earlier):
        f32, bf16 = jnp.float32, jnp.bfloat16
        if earlier:
            self.got_x, self.got_y = tie(self.got_x, self.got_y, *earlier)[:2]
        keep_x, _, keep_y, _ = self.arrays
        through_x = (keep_x[1].astype(f32) + self.got_x[0].astype(f32)).astype(bf16)
        through_y = (keep_y[1].astype(f32) + self.got_y[1].astype(f32)).astype(bf16)
        self.last_x, self.last_y = self.over(through_x, 4), self.over(through_y, 2)

    def tie_last(self, *values):
        self.last_x, self.last_y, *values = tie(self.last_x, self.last_y, *values)
        return values

    def terms(self):
        keep_x, _, keep_y, _ = self.arrays
        return (keep_x, self.got_x, self.last_x), (keep_y, self.got_y, self.last_y)


def widen_kernel(*refs, terms, turned):
    f32 = jnp.float32
    values_refs, outs = refs[: len(terms)], refs[len(terms) :]
    column = 0
    for index, out_ref in enumerate(outs):
        wide = out_ref.shape[0] if turned[index] else out_ref.shape[1]
        columns = slice(column, column + wide)
        total = None
        for ref, place in zip(values_refs, terms):
            values = ref[:, columns] if place is None else ref[place, :, columns]
            total = values.astype(f32) if total is None else total + values.astype(f32)
        out_ref[...] = total.T if turned[index] else total
        column += wide


def widen(values, terms, widths, turned, name):
    rows = values[-1].shape[0]
    outs = [made((w, rows) if t else (rows, w), jnp.float32) for w, t in zip(widths, turned)]
    kernel = functools.partial(widen_kernel, terms=terms, turned=turned)
    return call(kernel, outs, tuple(values), name=name, room=24)


def widen_pair_kernel(*refs, turned):
    f32 = jnp.float32
    outs = refs[6:]
    for index, out_ref in enumerate(outs):
        half = (out_ref.shape[0] if turned[index] else out_ref.shape[1]) // 2
        columns = slice(index * half, (index + 1) * half)
        for way, (got_place, keep, got, last) in enumerate(((1, *refs[:3]), (0, *refs[3:6]))):
            total = keep[0, :, columns].astype(f32) + got[got_place, :, columns].astype(f32)
            total = total + last[:, columns].astype(f32)
            target = slice(way * half, (way + 1) * half)
            if turned[index]:
                out_ref[target, :] = total.T
            else:
                out_ref[:, target] = total


def widen_pair(values, width, turned, name):
    rows = values[2].shape[0]
    outs = [made((width, rows) if t else (rows, width), jnp.float32) for t in turned]
    kernel = functools.partial(widen_pair_kernel, turned=turned)
    return call(kernel, outs, tuple(values), name=name, room=24)


def matmul_kernel(where_ref, left_ref, right_ref, out_ref, *, turned, parts):
    product = (dense_t if turned else dense)(left_ref[...], right_ref[...]).astype(out_ref.dtype)
    if parts == 1:
        out_ref[...] = product
    part = product.shape[0] // parts
    for k in range(parts if parts > 1 else 0):
        place = where_ref[0] ^ k
        rows = pl.ds(pl.multiple_of(place * part, part), part)
        out_ref[rows, :] = product[k * part : (k + 1) * part]


def matmul_call(where, left, right, dtype, turned, name, parts=1):
    rows, depth = left.shape
    columns = right.shape[0 if turned else 1]
    wide = 512
    right = pltpu.with_memory_space_constraint(right, pltpu.HBM)
    if turned:
        right_spec = pl.BlockSpec((wide, depth), lambda f, w: (f, 0))
    else:
        right_spec = pl.BlockSpec((depth, wide), lambda f, w: (0, f))
    return pl.pallas_call(
        functools.partial(matmul_kernel, turned=turned, parts=parts),
        out_shape=made((rows, columns), dtype),
        grid_spec=pltpu.PrefetchScalarGridSpec(
            num_scalar_prefetch=1,
            grid=(columns // wide,),
            in_specs=[pl.BlockSpec((rows, depth), lambda f, w: (0, 0)), right_spec],
            out_specs=pl.BlockSpec((rows, wide), lambda f, w: (0, f)),
        ),
        compiler_params=pltpu.CompilerParams(vmem_limit_bytes=20 << 20),
        cost_estimate=SHORT,
        name=name,
    )(where, left, right)


def turn_kernel(query_ref, both_ref, other_ref, cosine_ref, sine_ref, out_ref):
    head = HEAD_WIDTH
    step = 256

    def piece(index, carry):
        rows = pl.ds(pl.multiple_of(index * step, step), step)
        both = both_ref[rows, :] + other_ref[rows, :].astype(jnp.float32)
        cosine, sine = cosine_ref[rows, :], sine_ref[rows, :]
        for place, values in ((0, query_ref[rows, :]), (1, both[:, :head])):
            values = values * cosine - pltpu.roll(values, head // 2, 1) * sine
            out_ref[rows, place * head : (place + 1) * head] = values.astype(jnp.bfloat16)
        out_ref[rows, 2 * head :] = both[:, head:].astype(jnp.bfloat16)
        return carry

    lax.fori_loop(0, query_ref.shape[0] // step, piece, 0)


def local_heads_apart(
    tokens,
    gain_attn,
    w_query,
    w_key,
    w_value,
    w_out,
    gain_ffn,
    w_gate,
    w_up,
    w_down,
    cotangent,
    doc_ids,
    valid,
    group_order,
    *,
    seq_size,
    tp_size,
):
    _, row_count, width = tokens.shape
    length = doc_ids.shape[1]
    groups = group_order.shape[1]
    span = length // groups
    head = HEAD_WIDTH
    heads = w_query.shape[1] // head
    own_width = heads * head
    hidden = w_gate.shape[1]
    chips = seq_size // 2
    part = row_count // tp_size
    block = width // seq_size
    bf16, f32, i32 = jnp.bfloat16, jnp.float32, jnp.int32
    same_core = [[2 * p + c for p in range(chips)] for c in range(2)]
    other_core = [(i, i ^ 1) for i in range(seq_size)]
    own_seq, own_tp = lax.axis_index("seq"), lax.axis_index("tp")
    core = own_seq % 2
    where = jnp.stack([own_tp, core, own_seq // 2]).astype(i32)
    tokens = tokens.reshape(row_count, width)
    upstream = cotangent.reshape(row_count, width)
    gain_attn, gain_ffn = gain_attn.reshape(1, width), gain_ffn.reshape(1, width)

    def swap(values):
        return lax.ppermute(values, "seq", other_core)

    def to_heads(values):
        return lax.all_to_all(values, "seq", 0, 0, axis_index_groups=same_core, tiled=True)

    def part_of(values, place):
        return lax.dynamic_slice_in_dim(values, place * part, part, 0)

    def reordered(values):
        return jnp.concatenate([part_of(values, own_tp ^ k) for k in range(tp_size)], axis=0)

    def across(values, k):
        return lax.ppermute(values, "tp", [(i, i ^ k) for i in range(tp_size)])

    half = own_width // 2
    weight_line = Gather(lax.dynamic_slice_in_dim(w_out, core * half, half, 0), "tp", tp_size)
    weight_line.step()

    order = group_order[0]
    per_device = row_count // span

    def blocks_of(which):
        devices = 2 * jnp.arange(chips, dtype=i32) + which
        storage = (devices[:, None] * per_device + jnp.arange(per_device)[None, :]).reshape(-1)
        return jnp.take(order, storage)

    def places_of(block_ids):
        return (block_ids[:, None] * span + jnp.arange(span, dtype=i32)[None, :]).reshape(-1)

    own_blocks, other_blocks = blocks_of(core), blocks_of(1 - core)
    slot_places = jnp.concatenate([own_blocks, other_blocks])
    docs = doc_ids[0]
    first = jnp.sum(docs[None, :] < docs.reshape(groups, span)[:, :1], axis=1, dtype=i32)
    position = jnp.arange(length, dtype=i32).reshape(groups, span)
    change = jnp.where(docs != jnp.roll(docs, 1), jnp.arange(length, dtype=i32), 0)
    change = change.reshape(groups, span)
    start = jnp.max(
        jnp.where(position[:, None, :] <= position[:, :, None], change[:, None, :], 0), axis=2
    )
    start = jnp.maximum(start, first[:, None])
    start_q = jnp.take(start, own_blocks, axis=0)
    key_low = jnp.take(first, own_blocks) // span
    row_blocks = jnp.take(order, own_seq * per_device + jnp.arange(per_device, dtype=i32))
    live = jnp.take(valid.reshape(groups, span), row_blocks, axis=0).reshape(row_count, 1)
    cosine, sine = rope_tables(places_of(row_blocks), head)
    cosine = jnp.concatenate([cosine, cosine], axis=-1)
    sine = jnp.concatenate([-sine, sine], axis=-1)
    cosine_q, sine_q = rope_tables(places_of(own_blocks), head)
    cosine_q = jnp.concatenate([cosine_q, cosine_q], axis=-1)
    sine_q = jnp.concatenate([-sine_q, sine_q], axis=-1)

    packed, normed_attn = project_call(
        tokens, gain_attn, live, cosine, sine, w_query, w_key, w_value
    )
    mine = to_heads(packed).reshape(chips * row_count, 3 * head)
    upstream_rel = reordered(weight_line.tie(upstream))
    weight_line.step()
    grad_act = matmul_call(where, upstream_rel, w_down, f32, True, "grad_act")
    upstream_pair = (upstream_rel, swap(upstream_rel))
    normed_attn_pair = (normed_attn, swap(normed_attn))
    mine, grad_act = weight_line.tie(mine, grad_act)
    weight_line.step()
    other = swap(mine[:, head:])

    attended = attend_call(slot_places, key_low, mine, other, start_q.reshape(-1, 1), span)
    attended = to_heads(attended.reshape(chips, row_count, head))
    attended = attended.transpose(1, 0, 2).reshape(row_count, own_width)
    attended_part = lax.all_to_all(
        attended.reshape(tp_size, part, own_width), "tp", 0, 0, tiled=True
    )
    weight_line.tie(attended_part)
    own_w, above_w, below_w = weight_line.result()
    out_weights = []
    for d in range(tp_size):
        piece = own_w if d == 0 else above_w[d - 1] + below_w[tp_size - 1 - d]
        out_weights += [piece, swap(piece)]
    middle, normed_part = call(
        out_kernel,
        (made((part, width), f32), made((part, width), bf16)),
        (where, tokens, gain_ffn, attended_part, *out_weights),
        scalars=1,
        work=2 * part * width * width,
        name="out",
    )

    line = Gather(normed_part, "tp", tp_size)
    line.step()
    line.step()
    above_1, below_1 = line.above[0], line.below[0]
    filled, (own_grad, grad_1) = ffn_call(
        where, 0, [normed_part, above_1, below_1], grad_act, w_gate, w_up, None
    )
    filled = line.tie(*filled)
    line.step()
    above_2, below_2 = line.above[1], line.below[1]
    filled, (grad_2,) = ffn_call(where, 2, [above_2, below_2], grad_act, w_gate, w_up, filled)
    *filled, grad_1, grad_2 = line.tie(*filled, grad_1, grad_2)
    grad_1, grad_2 = across(grad_1, 1), across(grad_2, 2)
    _, (_, _, above_3), (_, _, below_3) = line.result()
    filled, (grad_3,) = ffn_call(
        where, 3, [above_1, below_1, above_3, below_3], grad_act, w_gate, w_up, filled
    )
    grad_3 = across(grad_3, 3)
    activated, gate_pre, up_pre, normed_ffn = filled

    normed_pair = (normed_ffn, swap(normed_ffn))
    outer_ffn = functools.partial(
        chip_outer_call, where, seq_size=seq_size, name="ffn_outer"
    )
    gate_quad = (*normed_pair, gate_pre, swap(gate_pre))
    up_quad = (*normed_pair, up_pre, swap(up_pre))
    down_quad = (*upstream_pair, activated, swap(activated))
    *gate_quad, grad_1, grad_2 = tie(*gate_quad, grad_1, grad_2)
    gate_sum = ChipSum(outer_ffn([gate_quad]), seq_size)
    gate_sum.first()
    rest_grads = outer_ffn([up_quad], columns=2, column=0)
    rest_grads = outer_ffn([down_quad], columns=2, column=1, into=rest_grads)
    grad_3, *rest_grads = tie(grad_3, *rest_grads)
    rest_sum = ChipSum(rest_grads, seq_size)
    middle_low, grad_middle, grad_attended, gain_ffn_part = call(
        middle_kernel,
        (
            made((part, width), bf16),
            made((part, width), f32),
            made((tp_size, part, own_width), bf16),
            made((1, width), f32),
        ),
        (where, middle, upstream, gain_ffn, own_grad, grad_1, grad_2, grad_3, *out_weights),
        scalars=1,
        work=2 * part * width * width,
        name="middle",
    )
    grad_attended = lax.all_to_all(grad_attended, "tp", 0, 0, tiled=True)
    branch = matmul_call(where, after(activated, middle_low), w_down, bf16, False, "branch", tp_size)
    grad_attended, branch = gate_sum.tie(grad_attended, branch)
    branch = after(branch, grad_attended)
    branch_part = lax.psum_scatter(branch, "tp", scatter_dimension=0, tiled=True)
    middle_all = lax.all_gather(after(middle_low, grad_attended), "tp", axis=0, tiled=True)
    grad_attended = grad_attended.reshape(row_count, heads, head).transpose(1, 0, 2)
    grad_heads = to_heads(grad_attended).reshape(chips * row_count, head)
    grad_query, both, both_other = attend_back_call(
        slot_places, key_low, mine, other, start_q, grad_heads, span
    )
    other_term = swap(both_other)
    packed_back = call(
        turn_kernel,
        (made((chips * row_count, 3 * head), bf16),),
        (grad_query, both, other_term, cosine_q, sine_q),
        name="turn",
    )[0].reshape(chips, row_count, 3 * head)
    back_heads = to_heads(packed_back)
    rest_sum.first(packed_back)
    attended_pair = (attended, swap(attended))
    back_heads = after(back_heads, attended_pair[1])
    layer_part = call(
        layer_kernel,
        (made((part, width), bf16),),
        (middle, branch_part),
        name="layer",
    )[0]
    layer_out = lax.all_gather(after(layer_part, middle_all), "tp", axis=0, tiled=True)
    low, gain_attn_part, *parts = back_call(
        where, back_heads, live, tokens, (w_query, w_key, w_value), tp_size
    )
    sums = Sum(parts, "tp", tp_size)
    sums.step()
    middle_all = after(middle_all, low)
    middle_pair = (middle_all, swap(middle_all))
    attn_grads = chip_outer_call(
        where,
        [(*middle_pair, *attended_pair), (*normed_attn_pair, low, swap(low))],
        seq_size,
        "attn_outer",
    )
    attn_grads, low = sums.tie(attn_grads, low)
    attn_sum = ChipSum(attn_grads, seq_size)
    attn_sum.first()
    gate_sum.second(low)
    sums.step()
    gains = jnp.concatenate([gain_attn_part, gain_ffn_part], axis=0)
    gains = after(gains.reshape(2, seq_size, block).transpose(1, 0, 2), low)
    gains = jnp.sum(lax.all_to_all(gains, "seq", 0, 0, tiled=True), axis=0).reshape(1, 2 * block)
    low = sums.tie(rest_sum.tie(low))
    rest_sum.second(low)
    sums.step()
    tokens_part = call(
        tokens_kernel,
        (made((part + 16, width), bf16),),
        (where, tokens, gain_attn, grad_middle, gains, *sums.result()),
        scalars=1,
        name="tokens",
    )[0]
    tokens_part, _ = gate_sum.tie_last(*rest_sum.tie_last(attn_sum.tie(after(tokens_part, layer_out)), low))
    token_line = Gather(tokens_part, "tp", tp_size)
    token_line.step()
    attn_sum.second()
    gate_x, gate_y = gate_sum.terms()
    (grad_gate,) = widen_pair([*gate_x, *gate_y], hidden, (False,), "widen_gate")
    rest_x, rest_y = rest_sum.terms()
    grad_up, grad_down = widen_pair([*rest_x, *rest_y], hidden, (False, True), "widen_rest")
    grad_gate = token_line.tie(grad_gate)
    token_line.step()
    terms_x, terms_y = attn_sum.terms()
    grad_out, grad_query = widen(
        terms_x, [0, 1, None], [own_width] * 2, (True, False), "widen_attn"
    )
    grad_key, grad_value = widen(
        terms_y, [0, 0, None], [own_width] * 2, (False, False), "widen_attn"
    )
    grad_out, grad_key = token_line.tie(grad_out, grad_key)
    token_line.step()
    grad_tokens, gains = join(where, token_line.result(), f32, False, 2 * block)
    gains = gains.reshape(2, block)

    return (
        layer_out.reshape(1, row_count, width),
        grad_tokens.reshape(1, row_count, width),
        gains[0],
        grad_query,
        grad_key,
        grad_value,
        grad_out,
        gains[1],
        grad_gate,
        grad_up,
        grad_down,
    )


def solution(mesh):
    placed = (
        P(None, "seq", None),
        P(),
        P(None, "tp"),
        P(None, "tp"),
        P(None, "tp"),
        P("tp", None),
        P(),
        P(None, "tp"),
        P(None, "tp"),
        P("tp", None),
        P(None, "seq", None),
        P(),
        P(),
        P(),
    )
    seq_size, tp_size = mesh.shape["seq"], mesh.shape["tp"]

    def local(*args):
        heads = args[2].shape[1] // HEAD_WIDTH
        if seq_size == 8 and tp_size == 4 and heads == 4 and args[0].shape[0] == 1:
            return local_heads_apart(*args, seq_size=seq_size, tp_size=tp_size)
        return local_general(*args)

    return jax.shard_map(
        local,
        mesh=mesh,
        in_specs=placed,
        out_specs=(
            P(None, "seq", None),
            P(None, "seq", None),
            P("seq"),
            P("seq", "tp"),
            P("seq", "tp"),
            P("seq", "tp"),
            P("tp", "seq"),
            P("seq"),
            P("seq", "tp"),
            P("seq", "tp"),
            P("tp", "seq"),
        ),
        check_vma=False,
    )
```

```python
import functools
import math

import jax
import jax.numpy as jnp
from jax import lax
from jax.experimental import pallas as pl
from jax.experimental.pallas import tpu as pltpu
from jax.sharding import PartitionSpec as P

HEAD_WIDTH = 128


norm_eps = 1e-05
rope_base = 10000.0


def rope_tables(places, head_size):
    half_size = head_size // 2
    freqs = rope_base ** (-jnp.arange(half_size, dtype=jnp.float32) * 2.0 / head_size)
    angles = places.astype(jnp.float32)[..., None] * freqs
    return (jnp.cos(angles), jnp.sin(angles))


def rotate(values, cosine, sine, forward):
    half_size = values.shape[-1] // 2
    first = values[..., :half_size]
    second = values[..., half_size:]
    cos_b = cosine[..., None, :]
    sin_b = sine[..., None, :]
    if forward:
        return jnp.concatenate(
            [first * cos_b - second * sin_b, second * cos_b + first * sin_b], axis=-1
        )
    return jnp.concatenate(
        [first * cos_b + second * sin_b, second * cos_b - first * sin_b], axis=-1
    )


def visible(place_q, doc_q, place_k, doc_k, live_k):
    allowed = (
        (place_k[None, :] <= place_q[:, None])
        & (doc_k[None, :] == doc_q[:, None])
        & (live_k[None, :] == 1)
    )
    return allowed.astype(jnp.float32)


def score_block(query_heads, key_heads, head_size, length):
    scores = jnp.einsum("qhe,khe->hqk", query_heads, key_heads, preferred_element_type=jnp.float32)
    return scores * (1.0 / math.sqrt(head_size)) - math.log(length)


def score_grads(query_heads, key_heads, value_heads, grad_heads, mask, head_size, length):
    sigma = jax.nn.sigmoid(score_block(query_heads, key_heads, head_size, length))
    weights = (sigma * mask).astype(jnp.bfloat16)
    grad_weights = jnp.einsum(
        "qhe,khe->hqk", grad_heads, value_heads, preferred_element_type=jnp.float32
    )
    grad_scores = (grad_weights * (sigma * (1.0 - sigma)) * mask).astype(jnp.bfloat16)
    return (weights, grad_scores)


def local_general(
    tokens,
    gain_attn,
    w_query,
    w_key,
    w_value,
    w_out,
    gain_ffn,
    w_gate,
    w_up,
    w_down,
    cotangent,
    doc_ids,
    valid,
    group_order,
):
    seq_count, row_count, model_width = tokens.shape
    length = doc_ids.shape[1]
    span = length // group_order.shape[1]
    head_size = HEAD_WIDTH
    local_width = w_query.shape[1]
    local_heads = local_width // head_size
    flat_rows = seq_count * row_count
    factor = 1.0 / math.sqrt(head_size)
    own_rows = lax.axis_index("seq") * row_count + jnp.arange(row_count, dtype=jnp.int32)
    all_rows = jnp.arange(length, dtype=jnp.int32)
    place_all = jnp.take(group_order, all_rows // span, axis=1) * span + (all_rows % span)[None, :]
    place_own = jnp.take(group_order, own_rows // span, axis=1) * span + (own_rows % span)[None, :]
    doc_all = jnp.take_along_axis(doc_ids, place_all, axis=1)
    live_all = jnp.take_along_axis(valid, place_all, axis=1)
    doc_own = jnp.take_along_axis(doc_ids, place_own, axis=1)
    cosine, sine = rope_tables(place_own, head_size)
    input_rows = tokens.astype(jnp.float32).reshape(flat_rows, model_width)
    scale_attn = lax.rsqrt(jnp.mean(input_rows * input_rows, axis=-1, keepdims=True) + norm_eps)
    unit_attn = input_rows * scale_attn
    normed_attn = (unit_attn * gain_attn).astype(jnp.bfloat16)

    def project(weight_matrix):
        return jnp.dot(normed_attn, weight_matrix, preferred_element_type=jnp.float32).reshape(
            seq_count, row_count, local_heads, head_size
        )

    query_rot = (
        rotate(project(w_query), cosine, sine, True)
        .astype(jnp.bfloat16)
        .reshape(seq_count, row_count, local_width)
    )
    key_rot = (
        rotate(project(w_key), cosine, sine, True)
        .astype(jnp.bfloat16)
        .reshape(seq_count, row_count, local_width)
    )
    value_low = (
        jnp.dot(normed_attn, w_value, preferred_element_type=jnp.float32)
        .astype(jnp.bfloat16)
        .reshape(seq_count, row_count, local_width)
    )
    key_all, value_all = (
        lax.all_gather(key_rot, "seq", axis=1, tiled=True),
        lax.all_gather(value_low, "seq", axis=1, tiled=True),
    )

    def attend(items):
        query_seq, key_seq, value_seq, place_q, doc_q, place_k, doc_k, live_k = items
        query_heads = query_seq.reshape(row_count, local_heads, head_size)
        key_heads = key_seq.reshape(length, local_heads, head_size)
        value_heads = value_seq.reshape(length, local_heads, head_size)
        mask = visible(place_q, doc_q, place_k, doc_k, live_k)
        weights = (
            jax.nn.sigmoid(score_block(query_heads, key_heads, head_size, length)) * mask
        ).astype(jnp.bfloat16)
        mixed = jnp.einsum("hqk,khe->qhe", weights, value_heads, preferred_element_type=jnp.float32)
        return mixed.astype(jnp.bfloat16).reshape(row_count, local_width)

    attention_output = lax.map(
        attend, (query_rot, key_all, value_all, place_own, doc_own, place_all, doc_all, live_all)
    )
    attended_flat = attention_output.reshape(flat_rows, local_width)
    branch_attn = lax.psum(jnp.dot(attended_flat, w_out, preferred_element_type=jnp.float32), "tp")
    hidden_rows = input_rows + branch_attn
    scale_ffn = lax.rsqrt(jnp.mean(hidden_rows * hidden_rows, axis=-1, keepdims=True) + norm_eps)
    unit_ffn = hidden_rows * scale_ffn
    normalized_feedforward = (unit_ffn * gain_ffn).astype(jnp.bfloat16)
    gate_rows = jnp.dot(normalized_feedforward, w_gate, preferred_element_type=jnp.float32)
    up_projected = jnp.dot(normalized_feedforward, w_up, preferred_element_type=jnp.float32)
    gate_sig = jax.nn.sigmoid(gate_rows)
    activation_rows = (gate_rows * gate_sig * up_projected).astype(jnp.bfloat16)
    branch_ffn = lax.psum(
        jnp.dot(activation_rows, w_down, preferred_element_type=jnp.float32).astype(jnp.bfloat16),
        "tp",
    ).astype(jnp.float32)
    layer_out = (
        (hidden_rows + branch_ffn).astype(jnp.bfloat16).reshape(seq_count, row_count, model_width)
    )
    upstream = cotangent.astype(jnp.float32).reshape(flat_rows, model_width)
    upstream_low = upstream.astype(jnp.bfloat16)
    grad_down = jnp.einsum(
        "tf,td->fd", activation_rows, upstream_low, preferred_element_type=jnp.float32
    )
    grad_act = jnp.einsum("td,fd->tf", upstream_low, w_down, preferred_element_type=jnp.float32)
    gate_pre = (grad_act * up_projected * (gate_sig * (1.0 + gate_rows * (1.0 - gate_sig)))).astype(
        jnp.bfloat16
    )
    up_pre = (grad_act * (gate_rows * gate_sig)).astype(jnp.bfloat16)
    grad_gate = jnp.einsum(
        "td,tf->df", normalized_feedforward, gate_pre, preferred_element_type=jnp.float32
    )
    grad_up = jnp.einsum(
        "td,tf->df", normalized_feedforward, up_pre, preferred_element_type=jnp.float32
    )
    normed_ffn_part = jnp.einsum(
        "tf,df->td", gate_pre, w_gate, preferred_element_type=jnp.float32
    ) + jnp.einsum("tf,df->td", up_pre, w_up, preferred_element_type=jnp.float32)
    grad_normed_ffn = lax.psum(normed_ffn_part, "tp")
    gain_ffn_part = jnp.sum(grad_normed_ffn * unit_ffn, axis=0)
    back_ffn = grad_normed_ffn * gain_ffn
    grad_middle = upstream + scale_ffn * (
        back_ffn - unit_ffn * jnp.mean(back_ffn * unit_ffn, axis=-1, keepdims=True)
    )
    middle_low = grad_middle.astype(jnp.bfloat16)
    grad_out = jnp.einsum(
        "te,td->ed", attended_flat, middle_low, preferred_element_type=jnp.float32
    )
    grad_attended = (
        jnp.einsum("td,ed->te", middle_low, w_out, preferred_element_type=jnp.float32)
        .astype(jnp.bfloat16)
        .reshape(seq_count, row_count, local_width)
    )
    key_back, value_back = (key_all, value_all)

    def attend_back(items):
        query_seq, key_seq, value_seq, grad_seq, place_q, doc_q, place_k, doc_k, live_k = items
        query_heads = query_seq.reshape(row_count, local_heads, head_size)
        key_heads = key_seq.reshape(length, local_heads, head_size)
        value_heads = value_seq.reshape(length, local_heads, head_size)
        grad_heads = grad_seq.reshape(row_count, local_heads, head_size)
        mask = visible(place_q, doc_q, place_k, doc_k, live_k)
        weights, grad_scores = score_grads(
            query_heads, key_heads, value_heads, grad_heads, mask, head_size, length
        )
        grad_value_seq = jnp.einsum(
            "hqk,qhe->khe", weights, grad_heads, preferred_element_type=jnp.float32
        )
        grad_query_seq = (
            jnp.einsum("hqk,khe->qhe", grad_scores, key_heads, preferred_element_type=jnp.float32)
            * factor
        )
        grad_key_seq = (
            jnp.einsum("hqk,qhe->khe", grad_scores, query_heads, preferred_element_type=jnp.float32)
            * factor
        )
        return (
            grad_query_seq,
            grad_key_seq.reshape(length, local_width),
            grad_value_seq.reshape(length, local_width),
        )

    grad_query_rot, grad_key_all, grad_value_all = lax.map(
        attend_back,
        (
            query_rot,
            key_back,
            value_back,
            grad_attended,
            place_own,
            doc_own,
            place_all,
            doc_all,
            live_all,
        ),
    )
    grad_key_rot, grad_value_own = (
        lax.psum_scatter(grad_key_all, "seq", scatter_dimension=1, tiled=True),
        lax.psum_scatter(grad_value_all, "seq", scatter_dimension=1, tiled=True),
    )
    query_low = (
        rotate(grad_query_rot, cosine, sine, False)
        .astype(jnp.bfloat16)
        .reshape(flat_rows, local_width)
    )
    key_low = (
        rotate(
            grad_key_rot.reshape(seq_count, row_count, local_heads, head_size), cosine, sine, False
        )
        .astype(jnp.bfloat16)
        .reshape(flat_rows, local_width)
    )
    value_grad_low = grad_value_own.astype(jnp.bfloat16).reshape(flat_rows, local_width)
    grad_query = jnp.einsum("td,te->de", normed_attn, query_low, preferred_element_type=jnp.float32)
    grad_key = jnp.einsum("td,te->de", normed_attn, key_low, preferred_element_type=jnp.float32)
    grad_value = jnp.einsum(
        "td,te->de", normed_attn, value_grad_low, preferred_element_type=jnp.float32
    )
    normed_attn_part = (
        jnp.einsum("te,de->td", query_low, w_query, preferred_element_type=jnp.float32)
        + jnp.einsum("te,de->td", key_low, w_key, preferred_element_type=jnp.float32)
        + jnp.einsum("te,de->td", value_grad_low, w_value, preferred_element_type=jnp.float32)
    )
    grad_normed_attn = lax.psum(normed_attn_part, "tp")
    gain_attn_part = jnp.sum(grad_normed_attn * unit_attn, axis=0)
    back_attn = grad_normed_attn * gain_attn
    grad_inputs = grad_middle + scale_attn * (
        back_attn - unit_attn * jnp.mean(back_attn * unit_attn, axis=-1, keepdims=True)
    )
    grad_tokens = grad_inputs.reshape(seq_count, row_count, model_width)
    (
        query_shard,
        key_shard,
        value_shard,
        out_shard,
        gain_attn_shard,
        gate_shard,
        up_shard,
        down_shard,
        gain_ffn_shard,
    ) = (
        lax.psum_scatter(grad_query, "seq", scatter_dimension=0, tiled=True),
        lax.psum_scatter(grad_key, "seq", scatter_dimension=0, tiled=True),
        lax.psum_scatter(grad_value, "seq", scatter_dimension=0, tiled=True),
        lax.psum_scatter(grad_out, "seq", scatter_dimension=1, tiled=True),
        lax.psum_scatter(gain_attn_part, "seq", scatter_dimension=0, tiled=True),
        lax.psum_scatter(grad_gate, "seq", scatter_dimension=0, tiled=True),
        lax.psum_scatter(grad_up, "seq", scatter_dimension=0, tiled=True),
        lax.psum_scatter(grad_down, "seq", scatter_dimension=1, tiled=True),
        lax.psum_scatter(gain_ffn_part, "seq", scatter_dimension=0, tiled=True),
    )
    return (
        layer_out,
        grad_tokens,
        gain_attn_shard,
        query_shard,
        key_shard,
        value_shard,
        out_shard,
        gain_ffn_shard,
        gate_shard,
        up_shard,
        down_shard,
    )


def dense(left, right):
    return jnp.dot(left, right, preferred_element_type=jnp.float32)


def dense_t(left, right):
    return lax.dot_general(
        left, right, (((1,), (1,)), ((), ())), preferred_element_type=jnp.float32
    )


def sigma_of(scores, length):
    return 1.0 / (1.0 + jnp.exp(math.log(length) - scores * (1.0 / math.sqrt(HEAD_WIDTH))))


def in_position_order(slot_places, own_ref, other_ref, own_first, span, scratch_refs):
    head = HEAD_WIDTH
    own_slots = own_ref.shape[0] // span
    for slot in range(2 * own_slots):
        source, first = (own_ref, own_first) if slot < own_slots else (other_ref, 0)
        rows = slice((slot % own_slots) * span, (slot % own_slots + 1) * span)
        target = pl.ds(pl.multiple_of(slot_places[slot] * span, span), span)
        for index, scratch in enumerate(scratch_refs):
            columns = slice(first + index * head, first + (index + 1) * head)
            scratch[target, :] = source[rows, columns]
    for scratch in scratch_refs:
        scratch[2 * own_slots * span :, :] = jnp.zeros((span, head), scratch.dtype)


def attend_kernel(
    slot_places, key_low, own_ref, other_ref, start_ref, out_ref, key_ref, value_ref, *, span
):
    head = HEAD_WIDTH
    own_slots = own_ref.shape[0] // span
    length = 2 * own_ref.shape[0]
    in_position_order(slot_places, own_ref, other_ref, head, span, (key_ref, value_ref))
    row = lax.broadcasted_iota(jnp.int32, (span, 2 * span), 0)
    column = lax.broadcasted_iota(jnp.int32, (span, 2 * span), 1)

    def query_block(slot, carry):
        rows = pl.ds(pl.multiple_of(slot * span, span), span)
        place = slot_places[slot]
        low = key_low[slot]
        query = own_ref[rows, :head]
        first = start_ref[rows, :]

        def key_pair(step, total):
            base = pl.multiple_of((low + 2 * step) * span, span)
            keys = pl.ds(base, 2 * span)
            scores = dense_t(query, key_ref[keys, :])
            seen = (column >= first - base) & (column - row <= place * span - base)
            probs = jnp.where(seen, sigma_of(scores, length), 0.0).astype(jnp.bfloat16)
            return total + dense(probs, value_ref[keys, :])

        total = lax.fori_loop(
            0, (place - low) // 2 + 1, key_pair, jnp.zeros((span, head), jnp.float32)
        )
        out_ref[rows, :] = total.astype(jnp.bfloat16)
        return carry

    lax.fori_loop(0, own_slots, query_block, 0)


def attend_back_kernel(
    slot_places,
    key_low,
    own_ref,
    other_ref,
    start_ref,
    grad_ref,
    grad_query_ref,
    grad_own_ref,
    grad_other_ref,
    key_ref,
    value_ref,
    sum_key_ref,
    sum_value_ref,
    *,
    span,
):
    head = HEAD_WIDTH
    own_slots = own_ref.shape[0] // span
    length = 2 * own_ref.shape[0]
    factor = 1.0 / math.sqrt(head)
    in_position_order(slot_places, own_ref, other_ref, head, span, (key_ref, value_ref))
    sum_key_ref[...] = jnp.zeros_like(sum_key_ref)
    sum_value_ref[...] = jnp.zeros_like(sum_value_ref)
    row = lax.broadcasted_iota(jnp.int32, (2 * span, span), 0)
    column = lax.broadcasted_iota(jnp.int32, (2 * span, span), 1)

    def query_block(slot, carry):
        rows = pl.ds(pl.multiple_of(slot * span, span), span)
        place = slot_places[slot]
        low = key_low[slot]
        query = own_ref[rows, :head]
        grad = grad_ref[rows, :]
        first = start_ref[pl.ds(slot, 1), :]

        def key_pair(step, total):
            base = pl.multiple_of((low + 2 * step) * span, span)
            keys = pl.ds(base, 2 * span)
            key = key_ref[keys, :]
            seen = (row >= first - base) & (row - column <= place * span - base)
            sigma = jnp.where(seen, sigma_of(dense_t(key, query), length), 0.0)
            sum_value_ref[keys, :] += dense(sigma.astype(jnp.bfloat16), grad)
            grad_probs = dense_t(value_ref[keys, :], grad)
            grad_scores = (grad_probs * (sigma * (1.0 - sigma))).astype(jnp.bfloat16)
            sum_key_ref[keys, :] += dense(grad_scores, query)
            return total + lax.dot_general(
                grad_scores, key, (((0,), (0,)), ((), ())), preferred_element_type=jnp.float32
            )

        total = lax.fori_loop(
            0, (place - low) // 2 + 1, key_pair, jnp.zeros((span, head), jnp.float32)
        )
        grad_query_ref[rows, :] = total * factor
        return carry

    lax.fori_loop(0, own_slots, query_block, 0)
    for slot in range(2 * own_slots):
        target = grad_own_ref if slot < own_slots else grad_other_ref
        rows = slice((slot % own_slots) * span, (slot % own_slots + 1) * span)
        source = pl.ds(pl.multiple_of(slot_places[slot] * span, span), span)
        target[rows, :head] = (sum_key_ref[source, :] * factor).astype(target.dtype)
        target[rows, head:] = sum_value_ref[source, :].astype(target.dtype)


SHORT = pl.CostEstimate(flops=1, bytes_accessed=1, transcendentals=0)
SMALL = pl.BlockSpec(memory_space=pltpu.SMEM)
WHOLE = pl.BlockSpec(memory_space=pltpu.VMEM)


def attend_call(slot_places, key_low, own, other, start, span):
    rows = own.shape[0]
    return pl.pallas_call(
        functools.partial(attend_kernel, span=span),
        out_shape=jax.ShapeDtypeStruct((rows, HEAD_WIDTH), jnp.bfloat16),
        in_specs=[SMALL, SMALL, WHOLE, WHOLE, WHOLE],
        out_specs=WHOLE,
        scratch_shapes=[pltpu.VMEM((2 * rows + span, HEAD_WIDTH), jnp.bfloat16)] * 2,
        compiler_params=pltpu.CompilerParams(vmem_limit_bytes=8 << 20),
        cost_estimate=SHORT,
        name="attend",
    )(slot_places, key_low, own, other, start)


def attend_back_call(slot_places, key_low, own, other, start, grad, span):
    rows = own.shape[0]
    return pl.pallas_call(
        functools.partial(attend_back_kernel, span=span),
        out_shape=(
            jax.ShapeDtypeStruct((rows, HEAD_WIDTH), jnp.float32),
            jax.ShapeDtypeStruct((rows, 2 * HEAD_WIDTH), jnp.float32),
            jax.ShapeDtypeStruct((rows, 2 * HEAD_WIDTH), jnp.bfloat16),
        ),
        in_specs=[SMALL, SMALL, WHOLE, WHOLE, WHOLE, WHOLE],
        out_specs=(WHOLE, WHOLE, WHOLE),
        scratch_shapes=[pltpu.VMEM((2 * rows + span, HEAD_WIDTH), jnp.bfloat16)] * 2
        + [pltpu.VMEM((2 * rows + span, HEAD_WIDTH), jnp.float32)] * 2,
        compiler_params=pltpu.CompilerParams(vmem_limit_bytes=14 << 20),
        cost_estimate=SHORT,
        name="attend_back",
    )(slot_places, key_low, own, other, start, grad)


def call(kernel, outs, ins, scratch=(), scalars=0, grid=None, in_specs=None, out_specs=None, work=0, name=None, room=12):
    params = pltpu.CompilerParams(vmem_limit_bytes=room << 20)
    if grid is None:
        return pl.pallas_call(
            kernel,
            out_shape=tuple(outs),
            in_specs=[SMALL] * scalars + [WHOLE] * (len(ins) - scalars),
            out_specs=tuple([WHOLE] * len(outs)),
            scratch_shapes=list(scratch),
            compiler_params=params,
            cost_estimate=SHORT,
            name=name,
        )(*ins)
    return pl.pallas_call(
        kernel,
        out_shape=tuple(outs),
        grid_spec=pltpu.PrefetchScalarGridSpec(
            num_scalar_prefetch=scalars,
            grid=grid,
            in_specs=in_specs,
            out_specs=tuple(out_specs),
            scratch_shapes=list(scratch),
        ),
        compiler_params=params,
        cost_estimate=SHORT,
        name=name,
    )(*ins)


def made(shape, dtype):
    return jax.ShapeDtypeStruct(shape, dtype)


def norm_of(values):
    rows = values.astype(jnp.float32)
    scale = lax.rsqrt(jnp.mean(rows * rows, axis=-1, keepdims=True) + norm_eps)
    return scale, rows * scale


def norm_back(grad, gain, scale, unit):
    back = grad * gain
    return scale * (back - unit * jnp.mean(back * unit, axis=-1, keepdims=True))


def project_kernel(
    tokens_ref, gain_ref, live_ref, cosine_ref, sine_ref, query_ref, key_ref, value_ref, packed_ref, normed_ref
):
    head = HEAD_WIDTH
    rows = tokens_ref.shape[0]

    @pl.when(pl.program_id(0) == 0)
    def _():
        step = 128

        def piece(index, carry):
            at = pl.ds(pl.multiple_of(index * step, step), step)
            normed_ref[at, :] = (norm_of(tokens_ref[at, :])[1] * gain_ref[...]).astype(jnp.bfloat16)
            return carry

        lax.fori_loop(0, rows // step, piece, 0)

    normed = normed_ref[...]
    for index, weight in enumerate((query_ref, key_ref, value_ref)):
        both = dense(normed, weight[...])
        for which in range(2):
            values = both[:, which * head : (which + 1) * head]
            if index < 2:
                values = values * cosine_ref[...] + pltpu.roll(values, head // 2, 1) * sine_ref[...]
            else:
                values = jnp.where(live_ref[...] == 1, values, 0.0)
            packed_ref[which, :, index * head : (index + 1) * head] = values.astype(jnp.bfloat16)


def project_call(tokens, gain, live, cosine, sine, w_query, w_key, w_value):
    rows, width = tokens.shape
    heads = w_query.shape[1] // HEAD_WIDTH
    whole = lambda shape: pl.BlockSpec(shape, lambda h: (0, 0))
    weight = pl.BlockSpec((width, 2 * HEAD_WIDTH), lambda h: (0, h))
    w_query, w_key, w_value = [
        pltpu.with_memory_space_constraint(w, pltpu.HBM) for w in (w_query, w_key, w_value)
    ]
    return call(
        project_kernel,
        (made((heads, rows, 3 * HEAD_WIDTH), jnp.bfloat16), made((rows, width), jnp.bfloat16)),
        (tokens, gain, live, cosine, sine, w_query, w_key, w_value),
        grid=(heads // 2,),
        in_specs=[
            whole((rows, width)), whole((1, width)), whole((rows, 1)),
            whole((rows, HEAD_WIDTH)), whole((rows, HEAD_WIDTH)), weight, weight, weight,
        ],
        out_specs=[
            pl.BlockSpec((2, rows, 3 * HEAD_WIDTH), lambda h: (h, 0, 0)), whole((rows, width)),
        ],
        work=6 * rows * width * w_query.shape[1],
        room=32,
        name="project",
    )


def piece_at(own_tp, d, count):
    return lax.rem(own_tp + d, count)


def out_kernel(where_ref, tokens_ref, gain_ref, attended_ref, *refs):
    *weights, middle_ref, normed_ref = refs
    own_tp, core = where_ref[0], where_ref[1]
    count, part, _ = attended_ref.shape
    _, half, wide = weights[0].shape
    starts = (0, wide, middle_ref.shape[1])
    rows = tokens_ref[pl.ds(pl.multiple_of(own_tp * part, part), part), :].astype(jnp.float32)
    for piece in range(2):
        target = slice(starts[piece], starts[piece + 1])
        total = rows[:, target]
        for d in range(count):
            for which in range(2):
                side = core if which == 0 else 1 - core
                columns = pl.ds(pl.multiple_of(side * half, half), half)
                values = attended_ref[d, :, columns]
                total = total + dense(values, weights[2 * piece + which][d])
        middle_ref[:, target] = total
    normed_ref[...] = (norm_of(middle_ref[...])[1] * gain_ref[...]).astype(jnp.bfloat16)


def ffn_kernel(where_ref, *refs, chunk, sources, first):
    grad_act_ref, gate_ref, up_ref = refs[sources : sources + 3]
    act_ref, gate_pre_ref, up_pre_ref, normed_ref, *grads, total_ref = refs[
        sources + 3 + (0 if first else 4) :
    ]
    own_tp = where_ref[0]
    part = grads[0].shape[0]
    step = pl.program_id(0)

    @pl.when(step == 0)
    def _():
        if first:
            normed_ref[:part, :] = refs[0][...]
            normed_ref[part:, :] = jnp.where(from_above(own_tp, 1), refs[1][...], refs[2][...])
        elif chunk == 2:
            normed_ref[...] = jnp.where(from_above(own_tp, 2), refs[0][...], refs[1][...])
        else:
            inner = jnp.where(own_tp == 1, refs[0][...], refs[1][...])
            ends = jnp.where(own_tp == 0, refs[2][...], refs[3][...])
            normed_ref[...] = jnp.where(is_inner(own_tp), inner, ends)

    normed = normed_ref[...]
    gate = dense(normed, gate_ref[...])
    up = dense(normed, up_ref[...])
    sig = jax.nn.sigmoid(gate)
    grad_act = grad_act_ref[...]
    act_ref[...] = (gate * sig * up).astype(jnp.bfloat16)
    gate_pre = (grad_act * up * (sig * (1.0 + gate * (1.0 - sig)))).astype(jnp.bfloat16)
    up_pre = (grad_act * (gate * sig)).astype(jnp.bfloat16)
    gate_pre_ref[...] = gate_pre
    up_pre_ref[...] = up_pre
    term = dense_t(gate_pre, gate_ref[...]) + dense_t(up_pre, up_ref[...])

    @pl.when(step == 0)
    def _():
        total_ref[...] = term

    @pl.when(step > 0)
    def _():
        total_ref[...] += term

    @pl.when(step == pl.num_programs(0) - 1)
    def _():
        for index, grad_ref in enumerate(grads):
            rows = slice(index * part, (index + 1) * part)
            grad_ref[...] = total_ref[rows, :].astype(jnp.bfloat16)


def from_above(own_tp, chunk):
    return own_tp % (2 * chunk) < chunk


def is_inner(own_tp):
    return (own_tp == 1) | (own_tp == 2)


def ffn_call(where, chunk, sources, grad_act, w_gate, w_up, filled):
    part, width = sources[0].shape
    total, hidden = grad_act.shape
    wide = 512
    count = 2 if filled is None else 1
    rows = count * part
    whole = pl.BlockSpec((part, width), lambda f, w: (0, 0))
    weight = pl.BlockSpec((width, wide), lambda f, w: (0, f))
    block = pl.BlockSpec((rows, wide), lambda f, w: (chunk, f))
    low = made((total, hidden), jnp.bfloat16)
    w_gate, w_up = [pltpu.with_memory_space_constraint(w, pltpu.HBM) for w in (w_gate, w_up)]
    ins = [where, *sources, grad_act, w_gate, w_up]
    specs = [whole] * len(sources) + [block, weight, weight]
    aliases = {}
    if filled is not None:
        aliases = {len(ins) + i: i for i in range(4)}
        ins += list(filled)
        specs += [pl.BlockSpec(memory_space=pl.ANY)] * 4
    outs = pl.pallas_call(
        functools.partial(ffn_kernel, chunk=chunk, sources=len(sources), first=not aliases),
        out_shape=(low, low, low, made((total, width), jnp.bfloat16))
        + (made((part, width), jnp.bfloat16),) * count,
        grid_spec=pltpu.PrefetchScalarGridSpec(
            num_scalar_prefetch=1,
            grid=(hidden // wide,),
            in_specs=specs,
            out_specs=(
                block, block, block, pl.BlockSpec((rows, width), lambda f, w: (chunk, 0)),
            )
            + (whole,) * count,
            scratch_shapes=[pltpu.VMEM((rows, width), jnp.float32)],
        ),
        input_output_aliases=aliases,
        compiler_params=pltpu.CompilerParams(vmem_limit_bytes=28 << 20),
        cost_estimate=SHORT,
        name="ffn",
    )(*ins)
    return outs[:4], outs[4:]


def middle_kernel(where_ref, middle_ref, upstream_ref, gain_ref, *refs):
    terms, refs = refs[: refs[-2].shape[0]], refs[refs[-2].shape[0] :]
    *weights, low_ref, grad_ref, back_ref, gain_grad_ref = refs
    own_tp, core = where_ref[0], where_ref[1]
    count, part, _ = back_ref.shape
    _, half, wide = weights[0].shape
    scale, unit = norm_of(middle_ref[...])
    grad = sum([t[...].astype(jnp.float32) for t in terms[1:]], terms[0][...].astype(jnp.float32))
    gain_grad_ref[...] = jnp.sum(grad * unit, axis=0, keepdims=True)
    at = pl.ds(pl.multiple_of(own_tp * part, part), part)
    total = upstream_ref[at, :].astype(jnp.float32) + norm_back(grad, gain_ref[...], scale, unit)
    grad_ref[...] = total
    low = total.astype(jnp.bfloat16)
    low_ref[...] = low
    for d in range(count):
        for which in range(2):
            side = core if which == 0 else 1 - core
            columns = pl.ds(pl.multiple_of(side * half, half), half)
            values = dense_t(low[:, :wide], weights[which][d])
            values = values + dense_t(low[:, wide:], weights[2 + which][d])
            back_ref[d, :, columns] = values.astype(jnp.bfloat16)


def back_kernel(where_ref, back_ref, live_ref, tokens_ref, query_ref, key_ref, value_ref, low_ref, gain_ref, *refs):
    *outs, ordered_ref, unit_ref = refs
    head = HEAD_WIDTH
    heads = back_ref.shape[0]
    count = len(outs)
    part = outs[0].shape[0]
    own = heads * head
    step = pl.program_id(0)

    @pl.when(step == 0)
    def _():
        for d in range(count):
            at = pl.ds(pl.multiple_of(piece_at(where_ref[0], d, count) * part, part), part)
            rows = slice(d * part, (d + 1) * part)
            for index in range(3):
                low = jnp.concatenate(
                    [back_ref[h, at, index * head : (index + 1) * head] for h in range(heads)],
                    axis=-1,
                )
                if index == 2:
                    low = jnp.where(live_ref[at, :] == 1, low.astype(jnp.float32), 0.0)
                    low = low.astype(jnp.bfloat16)
                low_ref[at, index * own : (index + 1) * own] = low
                ordered_ref[rows, index * own : (index + 1) * own] = low
            unit = norm_of(tokens_ref[at, :])[1]
            for block in range(unit_ref.shape[0]):
                wide = unit_ref.shape[2]
                unit_ref[block, rows, :] = unit[:, block * wide : (block + 1) * wide]

    total = None
    for index, weight in enumerate((query_ref, key_ref, value_ref)):
        term = dense_t(ordered_ref[:, index * own : (index + 1) * own], weight[...])
        total = term if total is None else total + term
    gain_ref[...] = jnp.sum(total * unit_ref[step], axis=0, keepdims=True)
    for d in range(count):
        outs[d][...] = total[d * part : (d + 1) * part].astype(jnp.bfloat16)


def back_call(where, back_heads, live, tokens, weights, count):
    rows, width = tokens.shape
    own = weights[0].shape[1]
    part = rows // count
    wide = 512
    blocks = width // wide
    weights = [pltpu.with_memory_space_constraint(w, pltpu.HBM) for w in weights]
    whole = lambda x: pl.BlockSpec(x.shape, lambda f, w: (0,) * len(x.shape))
    return pl.pallas_call(
        back_kernel,
        out_shape=(made((rows, 3 * own), jnp.bfloat16), made((1, width), jnp.float32))
        + (made((part, width), jnp.bfloat16),) * count,
        grid_spec=pltpu.PrefetchScalarGridSpec(
            num_scalar_prefetch=1,
            grid=(blocks,),
            in_specs=[whole(back_heads), whole(live), whole(tokens)]
            + [pl.BlockSpec((wide, own), lambda f, w: (f, 0))] * 3,
            out_specs=(
                pl.BlockSpec((rows, 3 * own), lambda f, w: (0, 0)),
                pl.BlockSpec((1, wide), lambda f, w: (0, f)),
            )
            + (pl.BlockSpec((part, wide), lambda f, w: (0, f)),) * count,
            scratch_shapes=[
                pltpu.VMEM((rows, 3 * own), jnp.bfloat16),
                pltpu.VMEM((blocks, rows, wide), jnp.float32),
            ],
        ),
        compiler_params=pltpu.CompilerParams(vmem_limit_bytes=32 << 20),
        cost_estimate=SHORT,
        name="back",
    )(where, back_heads, live, tokens, *weights)


def tokens_kernel(
    where_ref, tokens_ref, gain_ref, grad_ref, gains_ref, middle_ref, branch_ref, own_ref, below_ref, above_ref, out_ref
):
    part = own_ref.shape[0]
    at = pl.ds(pl.multiple_of(where_ref[0] * part, part), part)
    scale, unit = norm_of(tokens_ref[at, :])
    grad = own_ref[...].astype(jnp.float32) + (
        below_ref[...].astype(jnp.float32) + above_ref[...].astype(jnp.float32)
    )
    total = grad_ref[...] + norm_back(grad, gain_ref[...], scale, unit)
    out_ref[:part, :] = total.astype(jnp.bfloat16)
    gains = gains_ref[...]
    high = gains.astype(jnp.bfloat16)
    low = (gains - high.astype(jnp.float32)).astype(jnp.bfloat16)
    wide = gains.shape[1]
    rows = out_ref.shape[0] - 2 * part
    middle = slice(part, part + rows)
    for index, values in enumerate((high, low)):
        out_ref[middle, index * wide : (index + 1) * wide] = jnp.broadcast_to(values, (rows, wide))
    out_ref[middle, 2 * wide :] = jnp.zeros((rows, out_ref.shape[1] - 2 * wide), jnp.bfloat16)
    layer = middle_ref[...] + branch_ref[...].astype(jnp.float32)
    out_ref[part + rows :, :] = layer.astype(jnp.bfloat16)


def join_kernel(where_ref, own_ref, *refs, part):
    *pieces, out_ref, gains_ref, layer_ref, terms_ref = refs
    count = len(pieces) // 2 + 1
    wide = gains_ref.shape[1]
    for d in range(count):
        place = piece_at(where_ref[0], d, count)
        values = own_ref[...] if d == 0 else pieces[d - 1][...] + pieces[2 * count - 2 - d][...]
        at = pl.ds(pl.multiple_of(place * part, part), part)
        out_ref[at, :] = values[:part].astype(jnp.float32)
        row = values[part : part + 8].astype(jnp.float32)
        terms_ref[place] = row[:, :wide] + row[:, wide : 2 * wide]
        layer_ref[at, :] = values[values.shape[0] - part :]
    total = terms_ref[0]
    for index in range(1, count):
        total = total + terms_ref[index]
    gains_ref[...] = total[:1]


def join(where, gathered, part, gains):
    own, above, below = gathered
    count = len(above) + 1
    width = own.shape[1]
    return call(
        functools.partial(join_kernel, part=part),
        (
            made((count * part, width), jnp.float32),
            made((1, gains), jnp.float32),
            made((count * part, width), jnp.bfloat16),
        ),
        (where, own, *above, *below),
        scratch=[pltpu.VMEM((count, 8, gains), jnp.float32)],
        scalars=1,
        name="join",
    )


def tie(*values):
    return lax.optimization_barrier(values)


def after(value, *others):
    return lax.optimization_barrier((value, *others))[0]


class Line:
    def __init__(self, axis, count):
        self.axis, self.count, self.at = axis, count, 0
        self.upward, self.downward = None, None

    def tie(self, *others):
        self.upward, self.downward, *others = tie(self.upward, self.downward, *others)
        return others[0] if len(others) == 1 else others

    def send(self, up, down, up_pairs, down_pairs):
        self.upward = lax.ppermute(up, self.axis, up_pairs)
        self.downward = lax.ppermute(down, self.axis, down_pairs)


class Gather(Line):
    def __init__(self, shard, axis, count):
        super().__init__(axis, count)
        self.own, self.above, self.below = shard, [], []

    def step(self):
        if self.at:
            self.keep()
        up, down = (self.upward, self.downward) if self.at else (self.own, self.own)
        self.at += 1
        at, count = self.at, self.count
        self.send(
            up,
            down,
            [(i, i + 1) for i in range(at - 1, count - 1)],
            [(i, i - 1) for i in range(1, count - at + 1)],
        )

    def keep(self):
        self.below.append(self.upward)
        self.above.append(self.downward)

    def result(self):
        while self.at < self.count - 1:
            self.step()
        self.keep()
        return self.own, self.above, self.below


def add_kernel(up_ref, got_up_ref, down_ref, got_down_ref, sum_up_ref, sum_down_ref):
    for part, got, total in (
        (up_ref, got_up_ref, sum_up_ref),
        (down_ref, got_down_ref, sum_down_ref),
    ):
        total[...] = (part[...].astype(jnp.float32) + got[...].astype(jnp.float32)).astype(
            jnp.bfloat16
        )


class Sum(Line):
    def __init__(self, parts, axis, count):
        super().__init__(axis, count)
        self.parts = parts

    def step(self):
        first = self.at == 0
        self.at += 1
        at, count = self.at, self.count
        up, down = self.parts[count - at], self.parts[at]
        if not first:
            outs = (made(up.shape, jnp.bfloat16),) * 2
            up, down = call(
                add_kernel, outs, (up, self.upward, down, self.downward), name="add"
            )
        self.send(
            up,
            down,
            [(i, i + 1) for i in range(0, at)],
            [(i, i - 1) for i in range(count - at, count)],
        )

    def result(self):
        while self.at < self.count - 1:
            self.step()
        return self.parts[0], self.upward, self.downward


def outer(left, right):
    return lax.dot_general(
        left, right, (((0,), (0,)), ((), ())), preferred_element_type=jnp.float32
    )


def chip_outer_kernel(where_ref, *refs, sides):
    del where_ref
    keep_x, sent_x, keep_y, sent_y = refs[-4:]
    step = pl.program_id(0)
    values = []
    for side in range(sides):
        left, left_other, right, right_other = refs[4 * side : 4 * side + 4]
        product = outer(left[...], right[...]) + outer(left_other[...], right_other[...])
        values.append(product.astype(jnp.bfloat16))
    values = values[0] if sides == 1 else jnp.concatenate(values, axis=-1)
    half = values.shape[1] // 2

    for target, part, places in (
        (keep_x, 0, (0, 1)),
        (sent_x, 0, (2, 3)),
        (keep_y, 1, (0, 3)),
        (sent_y, 1, (1, 2)),
    ):

        @pl.when((step == places[0]) | (step == places[1]))
        def _(target=target, part=part):
            target[0] = values[:, part * half : (part + 1) * half]


def chip_outer_call(where, pairs, seq_size, name, columns=1, column=0, into=None):
    rows, width = pairs[0][0].shape
    block = width // seq_size
    half = sum(pair[2].shape[1] for pair in pairs) // 2

    def left_index(k, w):
        chip = jnp.where(k == 0, 0, jnp.where(k == 1, 2, jnp.where(k == 2, 3, 1)))
        return 0, 2 * (w[2] ^ chip) + w[1]

    specs, ins = [], []
    for pair in pairs:
        wide = pl.BlockSpec(pair[2].shape, lambda k, w: (0, 0))
        specs += [pl.BlockSpec((rows, block), left_index)] * 2 + [wide, wide]
        ins += list(pair)
    aliases = {}
    if into is not None:
        aliases = {1 + len(ins) + i: i for i in range(4)}
        specs += [pl.BlockSpec(memory_space=pltpu.HBM)] * 4
        ins += list(into)

    def target(place):
        return pl.BlockSpec((1, block, half), lambda k, w: (place(k), 0, column))

    return pl.pallas_call(
        functools.partial(chip_outer_kernel, sides=len(pairs)),
        out_shape=(pltpu.HBM((2, block, columns * half), jnp.bfloat16),) * 4,
        grid_spec=pltpu.PrefetchScalarGridSpec(
            num_scalar_prefetch=1,
            grid=(4,),
            in_specs=specs,
            out_specs=(
                target(lambda k: jnp.minimum(k, 1)),
                target(lambda k: k // 3),
                target(lambda k: k // 3),
                target(lambda k: k // 2),
            ),
        ),
        input_output_aliases=aliases,
        compiler_params=pltpu.CompilerParams(vmem_limit_bytes=24 << 20),
        cost_estimate=SHORT,
        name=name,
    )(where, *ins)


class ChipSum:
    def __init__(self, arrays, seq_size):
        self.arrays, self.size = arrays, seq_size

    def over(self, values, side):
        return lax.ppermute(values, "seq", [(i, i ^ side) for i in range(self.size)])

    def first(self, *earlier):
        _, sent_x, _, sent_y = self.arrays
        if earlier:
            sent_x, sent_y = tie(sent_x, sent_y, *earlier)[:2]
        self.got_x, self.got_y = self.over(sent_x, 2), self.over(sent_y, 4)

    def tie(self, *others):
        self.got_x, self.got_y, *others = tie(self.got_x, self.got_y, *others)
        return others[0] if len(others) == 1 else others

    def second(self, *earlier):
        f32, bf16 = jnp.float32, jnp.bfloat16
        if earlier:
            self.got_x, self.got_y = tie(self.got_x, self.got_y, *earlier)[:2]
        keep_x, _, keep_y, _ = self.arrays
        through_x = (keep_x[1].astype(f32) + self.got_x[0].astype(f32)).astype(bf16)
        through_y = (keep_y[1].astype(f32) + self.got_y[1].astype(f32)).astype(bf16)
        self.last_x, self.last_y = self.over(through_x, 4), self.over(through_y, 2)

    def tie_last(self, *values):
        self.last_x, self.last_y, *values = tie(self.last_x, self.last_y, *values)
        return values

    def terms(self):
        keep_x, _, keep_y, _ = self.arrays
        return (keep_x, self.got_x, self.last_x), (keep_y, self.got_y, self.last_y)


def widen_kernel(*refs, terms, turned):
    f32 = jnp.float32
    values_refs, outs = refs[: len(terms)], refs[len(terms) :]
    column = 0
    for index, out_ref in enumerate(outs):
        wide = out_ref.shape[0] if turned[index] else out_ref.shape[1]
        columns = slice(column, column + wide)
        total = None
        for ref, place in zip(values_refs, terms):
            values = ref[:, columns] if place is None else ref[place, :, columns]
            total = values.astype(f32) if total is None else total + values.astype(f32)
        out_ref[...] = total.T if turned[index] else total
        column += wide


def widen(values, terms, widths, turned, name):
    rows = values[-1].shape[0]
    outs = [made((w, rows) if t else (rows, w), jnp.float32) for w, t in zip(widths, turned)]
    kernel = functools.partial(widen_kernel, terms=terms, turned=turned)
    return call(kernel, outs, tuple(values), name=name, room=24)


def widen_pair_kernel(*refs, turned):
    f32 = jnp.float32
    outs = refs[6:]
    for index, out_ref in enumerate(outs):
        half = (out_ref.shape[0] if turned[index] else out_ref.shape[1]) // 2
        columns = slice(index * half, (index + 1) * half)
        for way, (got_place, keep, got, last) in enumerate(((1, *refs[:3]), (0, *refs[3:6]))):
            total = keep[0, :, columns].astype(f32) + got[got_place, :, columns].astype(f32)
            total = total + last[:, columns].astype(f32)
            target = slice(way * half, (way + 1) * half)
            if turned[index]:
                out_ref[target, :] = total.T
            else:
                out_ref[:, target] = total


def widen_pair(values, width, turned, name):
    rows = values[2].shape[0]
    outs = [made((width, rows) if t else (rows, width), jnp.float32) for t in turned]
    kernel = functools.partial(widen_pair_kernel, turned=turned)
    return call(kernel, outs, tuple(values), name=name, room=24)


def matmul_kernel(where_ref, left_ref, right_ref, out_ref, *, turned, parts):
    product = (dense_t if turned else dense)(left_ref[...], right_ref[...]).astype(out_ref.dtype)
    if parts == 1:
        out_ref[...] = product
    part = product.shape[0] // parts
    for k in range(parts if parts > 1 else 0):
        place = where_ref[0] ^ k
        rows = pl.ds(pl.multiple_of(place * part, part), part)
        out_ref[rows, :] = product[k * part : (k + 1) * part]


def matmul_call(where, left, right, dtype, turned, name, parts=1):
    rows, depth = left.shape
    columns = right.shape[0 if turned else 1]
    wide = 512
    right = pltpu.with_memory_space_constraint(right, pltpu.HBM)
    if turned:
        right_spec = pl.BlockSpec((wide, depth), lambda f, w: (f, 0))
    else:
        right_spec = pl.BlockSpec((depth, wide), lambda f, w: (0, f))
    return pl.pallas_call(
        functools.partial(matmul_kernel, turned=turned, parts=parts),
        out_shape=made((rows, columns), dtype),
        grid_spec=pltpu.PrefetchScalarGridSpec(
            num_scalar_prefetch=1,
            grid=(columns // wide,),
            in_specs=[pl.BlockSpec((rows, depth), lambda f, w: (0, 0)), right_spec],
            out_specs=pl.BlockSpec((rows, wide), lambda f, w: (0, f)),
        ),
        compiler_params=pltpu.CompilerParams(vmem_limit_bytes=20 << 20),
        cost_estimate=SHORT,
        name=name,
    )(where, left, right)


def turn_kernel(query_ref, both_ref, other_ref, cosine_ref, sine_ref, out_ref):
    head = HEAD_WIDTH
    step = 256

    def piece(index, carry):
        rows = pl.ds(pl.multiple_of(index * step, step), step)
        both = both_ref[rows, :] + other_ref[rows, :].astype(jnp.float32)
        cosine, sine = cosine_ref[rows, :], sine_ref[rows, :]
        for place, values in ((0, query_ref[rows, :]), (1, both[:, :head])):
            values = values * cosine - pltpu.roll(values, head // 2, 1) * sine
            out_ref[rows, place * head : (place + 1) * head] = values.astype(jnp.bfloat16)
        out_ref[rows, 2 * head :] = both[:, head:].astype(jnp.bfloat16)
        return carry

    lax.fori_loop(0, query_ref.shape[0] // step, piece, 0)


def local_heads_apart(
    tokens,
    gain_attn,
    w_query,
    w_key,
    w_value,
    w_out,
    gain_ffn,
    w_gate,
    w_up,
    w_down,
    cotangent,
    doc_ids,
    valid,
    group_order,
    *,
    seq_size,
    tp_size,
):
    _, row_count, width = tokens.shape
    length = doc_ids.shape[1]
    groups = group_order.shape[1]
    span = length // groups
    head = HEAD_WIDTH
    heads = w_query.shape[1] // head
    own_width = heads * head
    hidden = w_gate.shape[1]
    chips = seq_size // 2
    part = row_count // tp_size
    block = width // seq_size
    bf16, f32, i32 = jnp.bfloat16, jnp.float32, jnp.int32
    same_core = [[2 * p + c for p in range(chips)] for c in range(2)]
    other_core = [(i, i ^ 1) for i in range(seq_size)]
    own_seq, own_tp = lax.axis_index("seq"), lax.axis_index("tp")
    core = own_seq % 2
    where = jnp.stack([own_tp, core, own_seq // 2]).astype(i32)
    tokens = tokens.reshape(row_count, width)
    upstream = cotangent.reshape(row_count, width)
    gain_attn, gain_ffn = gain_attn.reshape(1, width), gain_ffn.reshape(1, width)

    def swap(values):
        return lax.ppermute(values, "seq", other_core)

    def to_heads(values):
        return lax.all_to_all(values, "seq", 0, 0, axis_index_groups=same_core, tiled=True)

    def part_of(values, place):
        return lax.dynamic_slice_in_dim(values, place * part, part, 0)

    def reordered(values):
        return jnp.concatenate([part_of(values, own_tp ^ k) for k in range(tp_size)], axis=0)

    def across(values, k):
        return lax.ppermute(values, "tp", [(i, i ^ k) for i in range(tp_size)])

    half = own_width // 2
    most = width * 5 // 8
    w_half = lax.dynamic_slice_in_dim(w_out, core * half, half, 0)

    def gathered(columns):
        values = lax.all_gather(columns, "tp", axis=0, tiled=True)
        return values.reshape(tp_size, half, columns.shape[1])

    w_first = gathered(w_half[:, :most])
    w_second = gathered(w_half[:, most:])

    order = group_order[0]
    per_device = row_count // span

    def blocks_of(which):
        devices = 2 * jnp.arange(chips, dtype=i32) + which
        storage = (devices[:, None] * per_device + jnp.arange(per_device)[None, :]).reshape(-1)
        return jnp.take(order, storage)

    def places_of(block_ids):
        return (block_ids[:, None] * span + jnp.arange(span, dtype=i32)[None, :]).reshape(-1)

    own_blocks, other_blocks = blocks_of(core), blocks_of(1 - core)
    slot_places = jnp.concatenate([own_blocks, other_blocks])
    docs = doc_ids[0]
    first = jnp.sum(docs[None, :] < docs.reshape(groups, span)[:, :1], axis=1, dtype=i32)
    position = jnp.arange(length, dtype=i32).reshape(groups, span)
    change = jnp.where(docs != jnp.roll(docs, 1), jnp.arange(length, dtype=i32), 0)
    change = change.reshape(groups, span)
    start = jnp.max(
        jnp.where(position[:, None, :] <= position[:, :, None], change[:, None, :], 0), axis=2
    )
    start = jnp.maximum(start, first[:, None])
    start_q = jnp.take(start, own_blocks, axis=0)
    key_low = jnp.take(first, own_blocks) // span
    row_blocks = jnp.take(order, own_seq * per_device + jnp.arange(per_device, dtype=i32))
    live = jnp.take(valid.reshape(groups, span), row_blocks, axis=0).reshape(row_count, 1)
    cosine, sine = rope_tables(places_of(row_blocks), head)
    cosine = jnp.concatenate([cosine, cosine], axis=-1)
    sine = jnp.concatenate([-sine, sine], axis=-1)
    cosine_q, sine_q = rope_tables(places_of(own_blocks), head)
    cosine_q = jnp.concatenate([cosine_q, cosine_q], axis=-1)
    sine_q = jnp.concatenate([-sine_q, sine_q], axis=-1)

    packed, normed_attn = project_call(
        tokens, gain_attn, live, cosine, sine, w_query, w_key, w_value
    )
    mine = to_heads(packed).reshape(chips * row_count, 3 * head)
    upstream_rel = reordered(upstream)
    grad_act = matmul_call(where, upstream_rel, w_down, f32, True, "grad_act")
    upstream_pair = (upstream_rel, swap(upstream_rel))
    normed_attn_pair = (normed_attn, swap(normed_attn))
    mine, grad_act = tie(mine, grad_act)
    other = swap(mine[:, head:])

    attended = attend_call(slot_places, key_low, mine, other, start_q.reshape(-1, 1), span)
    attended, w_first = tie(attended, w_first)
    attended = to_heads(attended.reshape(chips, row_count, head))
    attended = attended.transpose(1, 0, 2).reshape(row_count, own_width)
    attended_part = lax.all_to_all(
        attended.reshape(tp_size, part, own_width), "tp", 0, 0, tiled=True
    )
    w_second = after(w_second, attended_part)
    out_weights = (w_first, swap(w_first), w_second, swap(w_second))
    middle, normed_part = call(
        out_kernel,
        (made((part, width), f32), made((part, width), bf16)),
        (where, tokens, gain_ffn, attended_part, *out_weights),
        scalars=1,
        work=2 * part * width * width,
        name="out",
    )

    line = Gather(normed_part, "tp", tp_size)
    line.step()
    line.step()
    above_1, below_1 = line.above[0], line.below[0]
    filled, (own_grad, grad_1) = ffn_call(
        where, 0, [normed_part, above_1, below_1], grad_act, w_gate, w_up, None
    )
    filled = line.tie(*filled)
    line.step()
    above_2, below_2 = line.above[1], line.below[1]
    filled, (grad_2,) = ffn_call(where, 2, [above_2, below_2], grad_act, w_gate, w_up, filled)
    *filled, grad_1, grad_2 = line.tie(*filled, grad_1, grad_2)
    grad_1, grad_2 = across(grad_1, 1), across(grad_2, 2)
    _, (_, _, above_3), (_, _, below_3) = line.result()
    filled, (grad_3,) = ffn_call(
        where, 3, [above_1, below_1, above_3, below_3], grad_act, w_gate, w_up, filled
    )
    grad_3 = across(grad_3, 3)
    activated, gate_pre, up_pre, normed_ffn = filled
    gate_pre, grad_1, grad_2 = tie(gate_pre, grad_1, grad_2)

    normed_pair = (normed_ffn, swap(normed_ffn))
    outer_ffn = functools.partial(
        chip_outer_call, where, seq_size=seq_size, name="ffn_outer"
    )
    gate_quad = (*normed_pair, gate_pre, swap(gate_pre))
    up_quad = (*normed_pair, up_pre, swap(up_pre))
    down_quad = (*upstream_pair, activated, swap(activated))
    gate_sum = ChipSum(outer_ffn([gate_quad]), seq_size)
    gate_sum.first()
    up_sum = ChipSum(outer_ffn([up_quad]), seq_size)
    down_sum = ChipSum(outer_ffn([down_quad]), seq_size)
    grad_3, *arrays = tie(grad_3, *up_sum.arrays, *down_sum.arrays)
    up_sum.arrays, down_sum.arrays = arrays[:4], arrays[4:]
    middle_low, grad_middle, grad_attended, gain_ffn_part = call(
        middle_kernel,
        (
            made((part, width), bf16),
            made((part, width), f32),
            made((tp_size, part, own_width), bf16),
            made((1, width), f32),
        ),
        (where, middle, upstream, gain_ffn, own_grad, grad_1, grad_2, grad_3, *out_weights),
        scalars=1,
        work=2 * part * width * width,
        name="middle",
    )
    grad_attended = lax.all_to_all(grad_attended, "tp", 0, 0, tiled=True)
    branch = matmul_call(where, after(activated, middle_low), w_down, bf16, False, "branch", tp_size)
    grad_attended, branch = gate_sum.tie(grad_attended, branch)
    branch = after(branch, grad_attended)
    branch_part = lax.psum_scatter(branch, "tp", scatter_dimension=0, tiled=True)
    grad_attended = grad_attended.reshape(row_count, heads, head).transpose(1, 0, 2)
    grad_heads = to_heads(grad_attended).reshape(chips * row_count, head)
    grad_query, both, both_other = attend_back_call(
        slot_places, key_low, mine, other, start_q, grad_heads, span
    )
    other_term = swap(both_other)
    middle_all = lax.all_gather(after(middle_low, other_term), "tp", axis=0, tiled=True)
    packed_back = call(
        turn_kernel,
        (made((chips * row_count, 3 * head), bf16),),
        (grad_query, both, other_term, cosine_q, sine_q),
        name="turn",
    )[0].reshape(chips, row_count, 3 * head)
    back_heads = to_heads(packed_back)
    attended_pair = (attended, swap(attended))
    back_heads = after(back_heads, attended_pair[1], branch_part)
    low, gain_attn_part, *parts = back_call(
        where, back_heads, live, tokens, (w_query, w_key, w_value), tp_size
    )
    sums = Sum(parts, "tp", tp_size)
    sums.step()
    up_sum.first(low)
    gains = jnp.concatenate([gain_attn_part, gain_ffn_part], axis=0)
    gains = gains.reshape(2, seq_size, block).transpose(1, 0, 2)
    gains = jnp.sum(lax.all_to_all(gains, "seq", 0, 0, tiled=True), axis=0).reshape(1, 2 * block)
    up_sum.got_x, up_sum.got_y, low, gains = sums.tie(up_sum.got_x, up_sum.got_y, low, gains)
    down_sum.first(low)
    sums.step()
    down_sum.got_x, down_sum.got_y, low, middle_all = sums.tie(
        down_sum.got_x, down_sum.got_y, low, middle_all
    )
    up_sum.second(low)
    sums.step()
    middle_pair = (middle_all, swap(middle_all))
    attn_grads = chip_outer_call(
        where,
        [(*middle_pair, *attended_pair), (*normed_attn_pair, low, swap(low))],
        seq_size,
        "attn_outer",
    )
    up_sum.last_x, up_sum.last_y, *attn_grads = sums.tie(
        up_sum.last_x, up_sum.last_y, *attn_grads
    )
    attn_sum = ChipSum(attn_grads, seq_size)
    tokens_part = call(
        tokens_kernel,
        (made((2 * part + 16, width), bf16),),
        (where, tokens, gain_attn, grad_middle, gains, middle, branch_part, *sums.result()),
        scalars=1,
        name="tokens",
    )[0]
    token_line = Gather(tokens_part, "tp", tp_size)
    token_line.step()
    attn_sum.first(tokens_part)
    attn_sum.got_x, attn_sum.got_y, low = token_line.tie(attn_sum.got_x, attn_sum.got_y, low)
    token_line.step()
    down_sum.second(low)
    gate_sum.second(low)
    (*last, low) = token_line.tie(
        down_sum.last_x, down_sum.last_y, gate_sum.last_x, gate_sum.last_y, low
    )
    down_sum.last_x, down_sum.last_y, gate_sum.last_x, gate_sum.last_y = last
    token_line.step()
    attn_sum.second(low)
    up_sum.last_x = after(up_sum.last_x, low)
    up_x, up_y = up_sum.terms()
    (grad_up,) = widen_pair([*up_x, *up_y], hidden, (False,), "widen_up")
    down_x, down_y = down_sum.terms()
    (grad_down,) = widen_pair([*down_x, *down_y], hidden, (True,), "widen_down")
    gate_x, gate_y = gate_sum.terms()
    (grad_gate,) = widen_pair([*gate_x, *gate_y], hidden, (False,), "widen_gate")
    terms_x, terms_y = attn_sum.terms()
    grad_out, grad_query = widen(
        terms_x, [0, 1, None], [own_width] * 2, (True, False), "widen_attn"
    )
    grad_key, grad_value = widen(
        terms_y, [0, 0, None], [own_width] * 2, (False, False), "widen_attn"
    )
    grad_out, grad_key, grad_gate, grad_up = token_line.tie(grad_out, grad_key, grad_gate, grad_up)
    grad_tokens, gains, layer_out = join(where, token_line.result(), part, 2 * block)
    gains = gains.reshape(2, block)

    return (
        layer_out.reshape(1, row_count, width),
        grad_tokens.reshape(1, row_count, width),
        gains[0],
        grad_query,
        grad_key,
        grad_value,
        grad_out,
        gains[1],
        grad_gate,
        grad_up,
        grad_down,
    )


def solution(mesh):
    placed = (
        P(None, "seq", None),
        P(),
        P(None, "tp"),
        P(None, "tp"),
        P(None, "tp"),
        P("tp", None),
        P(),
        P(None, "tp"),
        P(None, "tp"),
        P("tp", None),
        P(None, "seq", None),
        P(),
        P(),
        P(),
    )
    seq_size, tp_size = mesh.shape["seq"], mesh.shape["tp"]

    def local(*args):
        heads = args[2].shape[1] // HEAD_WIDTH
        if seq_size == 8 and tp_size == 4 and heads == 4 and args[0].shape[0] == 1:
            return local_heads_apart(*args, seq_size=seq_size, tp_size=tp_size)
        return local_general(*args)

    return jax.shard_map(
        local,
        mesh=mesh,
        in_specs=placed,
        out_specs=(
            P(None, "seq", None),
            P(None, "seq", None),
            P("seq"),
            P("seq", "tp"),
            P("seq", "tp"),
            P("seq", "tp"),
            P("tp", "seq"),
            P("seq"),
            P("seq", "tp"),
            P("seq", "tp"),
            P("tp", "seq"),
        ),
        check_vma=False,
    )
```

```python
import functools
import math

import jax
import jax.numpy as jnp
from jax import lax
from jax.experimental import pallas as pl
from jax.experimental.pallas import tpu as pltpu
from jax.sharding import PartitionSpec as P

HEAD_WIDTH = 128


norm_eps = 1e-05
rope_base = 10000.0


def rope_tables(places, head_size):
    half_size = head_size // 2
    freqs = rope_base ** (-jnp.arange(half_size, dtype=jnp.float32) * 2.0 / head_size)
    angles = places.astype(jnp.float32)[..., None] * freqs
    return (jnp.cos(angles), jnp.sin(angles))


def rotate(values, cosine, sine, forward):
    half_size = values.shape[-1] // 2
    first = values[..., :half_size]
    second = values[..., half_size:]
    cos_b = cosine[..., None, :]
    sin_b = sine[..., None, :]
    if forward:
        return jnp.concatenate(
            [first * cos_b - second * sin_b, second * cos_b + first * sin_b], axis=-1
        )
    return jnp.concatenate(
        [first * cos_b + second * sin_b, second * cos_b - first * sin_b], axis=-1
    )


def visible(place_q, doc_q, place_k, doc_k, live_k):
    allowed = (
        (place_k[None, :] <= place_q[:, None])
        & (doc_k[None, :] == doc_q[:, None])
        & (live_k[None, :] == 1)
    )
    return allowed.astype(jnp.float32)


def score_block(query_heads, key_heads, head_size, length):
    scores = jnp.einsum("qhe,khe->hqk", query_heads, key_heads, preferred_element_type=jnp.float32)
    return scores * (1.0 / math.sqrt(head_size)) - math.log(length)


def score_grads(query_heads, key_heads, value_heads, grad_heads, mask, head_size, length):
    sigma = jax.nn.sigmoid(score_block(query_heads, key_heads, head_size, length))
    weights = (sigma * mask).astype(jnp.bfloat16)
    grad_weights = jnp.einsum(
        "qhe,khe->hqk", grad_heads, value_heads, preferred_element_type=jnp.float32
    )
    grad_scores = (grad_weights * (sigma * (1.0 - sigma)) * mask).astype(jnp.bfloat16)
    return (weights, grad_scores)


def local_general(
    tokens,
    gain_attn,
    w_query,
    w_key,
    w_value,
    w_out,
    gain_ffn,
    w_gate,
    w_up,
    w_down,
    cotangent,
    doc_ids,
    valid,
    group_order,
):
    seq_count, row_count, model_width = tokens.shape
    length = doc_ids.shape[1]
    span = length // group_order.shape[1]
    head_size = HEAD_WIDTH
    local_width = w_query.shape[1]
    local_heads = local_width // head_size
    flat_rows = seq_count * row_count
    factor = 1.0 / math.sqrt(head_size)
    own_rows = lax.axis_index("seq") * row_count + jnp.arange(row_count, dtype=jnp.int32)
    all_rows = jnp.arange(length, dtype=jnp.int32)
    place_all = jnp.take(group_order, all_rows // span, axis=1) * span + (all_rows % span)[None, :]
    place_own = jnp.take(group_order, own_rows // span, axis=1) * span + (own_rows % span)[None, :]
    doc_all = jnp.take_along_axis(doc_ids, place_all, axis=1)
    live_all = jnp.take_along_axis(valid, place_all, axis=1)
    doc_own = jnp.take_along_axis(doc_ids, place_own, axis=1)
    cosine, sine = rope_tables(place_own, head_size)
    input_rows = tokens.astype(jnp.float32).reshape(flat_rows, model_width)
    scale_attn = lax.rsqrt(jnp.mean(input_rows * input_rows, axis=-1, keepdims=True) + norm_eps)
    unit_attn = input_rows * scale_attn
    normed_attn = (unit_attn * gain_attn).astype(jnp.bfloat16)

    def project(weight_matrix):
        return jnp.dot(normed_attn, weight_matrix, preferred_element_type=jnp.float32).reshape(
            seq_count, row_count, local_heads, head_size
        )

    query_rot = (
        rotate(project(w_query), cosine, sine, True)
        .astype(jnp.bfloat16)
        .reshape(seq_count, row_count, local_width)
    )
    key_rot = (
        rotate(project(w_key), cosine, sine, True)
        .astype(jnp.bfloat16)
        .reshape(seq_count, row_count, local_width)
    )
    value_low = (
        jnp.dot(normed_attn, w_value, preferred_element_type=jnp.float32)
        .astype(jnp.bfloat16)
        .reshape(seq_count, row_count, local_width)
    )
    key_all, value_all = (
        lax.all_gather(key_rot, "seq", axis=1, tiled=True),
        lax.all_gather(value_low, "seq", axis=1, tiled=True),
    )

    def attend(items):
        query_seq, key_seq, value_seq, place_q, doc_q, place_k, doc_k, live_k = items
        query_heads = query_seq.reshape(row_count, local_heads, head_size)
        key_heads = key_seq.reshape(length, local_heads, head_size)
        value_heads = value_seq.reshape(length, local_heads, head_size)
        mask = visible(place_q, doc_q, place_k, doc_k, live_k)
        weights = (
            jax.nn.sigmoid(score_block(query_heads, key_heads, head_size, length)) * mask
        ).astype(jnp.bfloat16)
        mixed = jnp.einsum("hqk,khe->qhe", weights, value_heads, preferred_element_type=jnp.float32)
        return mixed.astype(jnp.bfloat16).reshape(row_count, local_width)

    attention_output = lax.map(
        attend, (query_rot, key_all, value_all, place_own, doc_own, place_all, doc_all, live_all)
    )
    attended_flat = attention_output.reshape(flat_rows, local_width)
    branch_attn = lax.psum(jnp.dot(attended_flat, w_out, preferred_element_type=jnp.float32), "tp")
    hidden_rows = input_rows + branch_attn
    scale_ffn = lax.rsqrt(jnp.mean(hidden_rows * hidden_rows, axis=-1, keepdims=True) + norm_eps)
    unit_ffn = hidden_rows * scale_ffn
    normalized_feedforward = (unit_ffn * gain_ffn).astype(jnp.bfloat16)
    gate_rows = jnp.dot(normalized_feedforward, w_gate, preferred_element_type=jnp.float32)
    up_projected = jnp.dot(normalized_feedforward, w_up, preferred_element_type=jnp.float32)
    gate_sig = jax.nn.sigmoid(gate_rows)
    activation_rows = (gate_rows * gate_sig * up_projected).astype(jnp.bfloat16)
    branch_ffn = lax.psum(
        jnp.dot(activation_rows, w_down, preferred_element_type=jnp.float32).astype(jnp.bfloat16),
        "tp",
    ).astype(jnp.float32)
    layer_out = (
        (hidden_rows + branch_ffn).astype(jnp.bfloat16).reshape(seq_count, row_count, model_width)
    )
    upstream = cotangent.astype(jnp.float32).reshape(flat_rows, model_width)
    upstream_low = upstream.astype(jnp.bfloat16)
    grad_down = jnp.einsum(
        "tf,td->fd", activation_rows, upstream_low, preferred_element_type=jnp.float32
    )
    grad_act = jnp.einsum("td,fd->tf", upstream_low, w_down, preferred_element_type=jnp.float32)
    gate_pre = (grad_act * up_projected * (gate_sig * (1.0 + gate_rows * (1.0 - gate_sig)))).astype(
        jnp.bfloat16
    )
    up_pre = (grad_act * (gate_rows * gate_sig)).astype(jnp.bfloat16)
    grad_gate = jnp.einsum(
        "td,tf->df", normalized_feedforward, gate_pre, preferred_element_type=jnp.float32
    )
    grad_up = jnp.einsum(
        "td,tf->df", normalized_feedforward, up_pre, preferred_element_type=jnp.float32
    )
    normed_ffn_part = jnp.einsum(
        "tf,df->td", gate_pre, w_gate, preferred_element_type=jnp.float32
    ) + jnp.einsum("tf,df->td", up_pre, w_up, preferred_element_type=jnp.float32)
    grad_normed_ffn = lax.psum(normed_ffn_part, "tp")
    gain_ffn_part = jnp.sum(grad_normed_ffn * unit_ffn, axis=0)
    back_ffn = grad_normed_ffn * gain_ffn
    grad_middle = upstream + scale_ffn * (
        back_ffn - unit_ffn * jnp.mean(back_ffn * unit_ffn, axis=-1, keepdims=True)
    )
    middle_low = grad_middle.astype(jnp.bfloat16)
    grad_out = jnp.einsum(
        "te,td->ed", attended_flat, middle_low, preferred_element_type=jnp.float32
    )
    grad_attended = (
        jnp.einsum("td,ed->te", middle_low, w_out, preferred_element_type=jnp.float32)
        .astype(jnp.bfloat16)
        .reshape(seq_count, row_count, local_width)
    )
    key_back, value_back = (key_all, value_all)

    def attend_back(items):
        query_seq, key_seq, value_seq, grad_seq, place_q, doc_q, place_k, doc_k, live_k = items
        query_heads = query_seq.reshape(row_count, local_heads, head_size)
        key_heads = key_seq.reshape(length, local_heads, head_size)
        value_heads = value_seq.reshape(length, local_heads, head_size)
        grad_heads = grad_seq.reshape(row_count, local_heads, head_size)
        mask = visible(place_q, doc_q, place_k, doc_k, live_k)
        weights, grad_scores = score_grads(
            query_heads, key_heads, value_heads, grad_heads, mask, head_size, length
        )
        grad_value_seq = jnp.einsum(
            "hqk,qhe->khe", weights, grad_heads, preferred_element_type=jnp.float32
        )
        grad_query_seq = (
            jnp.einsum("hqk,khe->qhe", grad_scores, key_heads, preferred_element_type=jnp.float32)
            * factor
        )
        grad_key_seq = (
            jnp.einsum("hqk,qhe->khe", grad_scores, query_heads, preferred_element_type=jnp.float32)
            * factor
        )
        return (
            grad_query_seq,
            grad_key_seq.reshape(length, local_width),
            grad_value_seq.reshape(length, local_width),
        )

    grad_query_rot, grad_key_all, grad_value_all = lax.map(
        attend_back,
        (
            query_rot,
            key_back,
            value_back,
            grad_attended,
            place_own,
            doc_own,
            place_all,
            doc_all,
            live_all,
        ),
    )
    grad_key_rot, grad_value_own = (
        lax.psum_scatter(grad_key_all, "seq", scatter_dimension=1, tiled=True),
        lax.psum_scatter(grad_value_all, "seq", scatter_dimension=1, tiled=True),
    )
    query_low = (
        rotate(grad_query_rot, cosine, sine, False)
        .astype(jnp.bfloat16)
        .reshape(flat_rows, local_width)
    )
    key_low = (
        rotate(
            grad_key_rot.reshape(seq_count, row_count, local_heads, head_size), cosine, sine, False
        )
        .astype(jnp.bfloat16)
        .reshape(flat_rows, local_width)
    )
    value_grad_low = grad_value_own.astype(jnp.bfloat16).reshape(flat_rows, local_width)
    grad_query = jnp.einsum("td,te->de", normed_attn, query_low, preferred_element_type=jnp.float32)
    grad_key = jnp.einsum("td,te->de", normed_attn, key_low, preferred_element_type=jnp.float32)
    grad_value = jnp.einsum(
        "td,te->de", normed_attn, value_grad_low, preferred_element_type=jnp.float32
    )
    normed_attn_part = (
        jnp.einsum("te,de->td", query_low, w_query, preferred_element_type=jnp.float32)
        + jnp.einsum("te,de->td", key_low, w_key, preferred_element_type=jnp.float32)
        + jnp.einsum("te,de->td", value_grad_low, w_value, preferred_element_type=jnp.float32)
    )
    grad_normed_attn = lax.psum(normed_attn_part, "tp")
    gain_attn_part = jnp.sum(grad_normed_attn * unit_attn, axis=0)
    back_attn = grad_normed_attn * gain_attn
    grad_inputs = grad_middle + scale_attn * (
        back_attn - unit_attn * jnp.mean(back_attn * unit_attn, axis=-1, keepdims=True)
    )
    grad_tokens = grad_inputs.reshape(seq_count, row_count, model_width)
    (
        query_shard,
        key_shard,
        value_shard,
        out_shard,
        gain_attn_shard,
        gate_shard,
        up_shard,
        down_shard,
        gain_ffn_shard,
    ) = (
        lax.psum_scatter(grad_query, "seq", scatter_dimension=0, tiled=True),
        lax.psum_scatter(grad_key, "seq", scatter_dimension=0, tiled=True),
        lax.psum_scatter(grad_value, "seq", scatter_dimension=0, tiled=True),
        lax.psum_scatter(grad_out, "seq", scatter_dimension=1, tiled=True),
        lax.psum_scatter(gain_attn_part, "seq", scatter_dimension=0, tiled=True),
        lax.psum_scatter(grad_gate, "seq", scatter_dimension=0, tiled=True),
        lax.psum_scatter(grad_up, "seq", scatter_dimension=0, tiled=True),
        lax.psum_scatter(grad_down, "seq", scatter_dimension=1, tiled=True),
        lax.psum_scatter(gain_ffn_part, "seq", scatter_dimension=0, tiled=True),
    )
    return (
        layer_out,
        grad_tokens,
        gain_attn_shard,
        query_shard,
        key_shard,
        value_shard,
        out_shard,
        gain_ffn_shard,
        gate_shard,
        up_shard,
        down_shard,
    )


def dense(left, right):
    return jnp.dot(left, right, preferred_element_type=jnp.float32)


def dense_t(left, right):
    return lax.dot_general(
        left, right, (((1,), (1,)), ((), ())), preferred_element_type=jnp.float32
    )


def sigma_of(scores, length):
    return 1.0 / (1.0 + jnp.exp(math.log(length) - scores * (1.0 / math.sqrt(HEAD_WIDTH))))


def in_position_order(slot_places, own_ref, other_ref, own_first, span, scratch_refs):
    head = HEAD_WIDTH
    own_slots = own_ref.shape[0] // span
    for slot in range(2 * own_slots):
        source, first = (own_ref, own_first) if slot < own_slots else (other_ref, 0)
        rows = slice((slot % own_slots) * span, (slot % own_slots + 1) * span)
        target = pl.ds(pl.multiple_of(slot_places[slot] * span, span), span)
        for index, scratch in enumerate(scratch_refs):
            columns = slice(first + index * head, first + (index + 1) * head)
            scratch[target, :] = source[rows, columns]
    for scratch in scratch_refs:
        scratch[2 * own_slots * span :, :] = jnp.zeros((span, head), scratch.dtype)


def attend_kernel(
    slot_places, key_low, own_ref, other_ref, start_ref, out_ref, key_ref, value_ref, *, span
):
    head = HEAD_WIDTH
    own_slots = own_ref.shape[0] // span
    length = 2 * own_ref.shape[0]
    in_position_order(slot_places, own_ref, other_ref, head, span, (key_ref, value_ref))
    row = lax.broadcasted_iota(jnp.int32, (span, 2 * span), 0)
    column = lax.broadcasted_iota(jnp.int32, (span, 2 * span), 1)

    def query_block(slot, carry):
        rows = pl.ds(pl.multiple_of(slot * span, span), span)
        place = slot_places[slot]
        low = key_low[slot]
        query = own_ref[rows, :head]
        first = start_ref[rows, :]

        def key_pair(step, total):
            base = pl.multiple_of((low + 2 * step) * span, span)
            keys = pl.ds(base, 2 * span)
            scores = dense_t(query, key_ref[keys, :])
            seen = (column >= first - base) & (column - row <= place * span - base)
            probs = jnp.where(seen, sigma_of(scores, length), 0.0).astype(jnp.bfloat16)
            return total + dense(probs, value_ref[keys, :])

        total = lax.fori_loop(
            0, (place - low) // 2 + 1, key_pair, jnp.zeros((span, head), jnp.float32)
        )
        out_ref[rows, :] = total.astype(jnp.bfloat16)
        return carry

    lax.fori_loop(0, own_slots, query_block, 0)


def attend_back_kernel(
    slot_places,
    key_low,
    own_ref,
    other_ref,
    start_ref,
    grad_ref,
    grad_query_ref,
    grad_own_ref,
    grad_other_ref,
    key_ref,
    value_ref,
    sum_key_ref,
    sum_value_ref,
    *,
    span,
):
    head = HEAD_WIDTH
    own_slots = own_ref.shape[0] // span
    length = 2 * own_ref.shape[0]
    factor = 1.0 / math.sqrt(head)
    in_position_order(slot_places, own_ref, other_ref, head, span, (key_ref, value_ref))
    sum_key_ref[...] = jnp.zeros_like(sum_key_ref)
    sum_value_ref[...] = jnp.zeros_like(sum_value_ref)
    row = lax.broadcasted_iota(jnp.int32, (2 * span, span), 0)
    column = lax.broadcasted_iota(jnp.int32, (2 * span, span), 1)

    def query_block(slot, carry):
        rows = pl.ds(pl.multiple_of(slot * span, span), span)
        place = slot_places[slot]
        low = key_low[slot]
        query = own_ref[rows, :head]
        grad = grad_ref[rows, :]
        first = start_ref[pl.ds(slot, 1), :]

        def key_pair(step, total):
            base = pl.multiple_of((low + 2 * step) * span, span)
            keys = pl.ds(base, 2 * span)
            key = key_ref[keys, :]
            seen = (row >= first - base) & (row - column <= place * span - base)
            sigma = jnp.where(seen, sigma_of(dense_t(key, query), length), 0.0)
            sum_value_ref[keys, :] += dense(sigma.astype(jnp.bfloat16), grad)
            grad_probs = dense_t(value_ref[keys, :], grad)
            grad_scores = (grad_probs * (sigma * (1.0 - sigma))).astype(jnp.bfloat16)
            sum_key_ref[keys, :] += dense(grad_scores, query)
            return total + lax.dot_general(
                grad_scores, key, (((0,), (0,)), ((), ())), preferred_element_type=jnp.float32
            )

        total = lax.fori_loop(
            0, (place - low) // 2 + 1, key_pair, jnp.zeros((span, head), jnp.float32)
        )
        grad_query_ref[rows, :] = total * factor
        return carry

    lax.fori_loop(0, own_slots, query_block, 0)
    for slot in range(2 * own_slots):
        target = grad_own_ref if slot < own_slots else grad_other_ref
        rows = slice((slot % own_slots) * span, (slot % own_slots + 1) * span)
        source = pl.ds(pl.multiple_of(slot_places[slot] * span, span), span)
        target[rows, :head] = (sum_key_ref[source, :] * factor).astype(target.dtype)
        target[rows, head:] = sum_value_ref[source, :].astype(target.dtype)


SHORT = pl.CostEstimate(flops=1, bytes_accessed=1, transcendentals=0)
SMALL = pl.BlockSpec(memory_space=pltpu.SMEM)
WHOLE = pl.BlockSpec(memory_space=pltpu.VMEM)


def attend_call(slot_places, key_low, own, other, start, span):
    rows = own.shape[0]
    return pl.pallas_call(
        functools.partial(attend_kernel, span=span),
        out_shape=jax.ShapeDtypeStruct((rows, HEAD_WIDTH), jnp.bfloat16),
        in_specs=[SMALL, SMALL, WHOLE, WHOLE, WHOLE],
        out_specs=WHOLE,
        scratch_shapes=[pltpu.VMEM((2 * rows + span, HEAD_WIDTH), jnp.bfloat16)] * 2,
        compiler_params=pltpu.CompilerParams(vmem_limit_bytes=8 << 20),
        cost_estimate=SHORT,
        name="attend",
    )(slot_places, key_low, own, other, start)


def attend_back_call(slot_places, key_low, own, other, start, grad, span):
    rows = own.shape[0]
    return pl.pallas_call(
        functools.partial(attend_back_kernel, span=span),
        out_shape=(
            jax.ShapeDtypeStruct((rows, HEAD_WIDTH), jnp.float32),
            jax.ShapeDtypeStruct((rows, 2 * HEAD_WIDTH), jnp.float32),
            jax.ShapeDtypeStruct((rows, 2 * HEAD_WIDTH), jnp.bfloat16),
        ),
        in_specs=[SMALL, SMALL, WHOLE, WHOLE, WHOLE, WHOLE],
        out_specs=(WHOLE, WHOLE, WHOLE),
        scratch_shapes=[pltpu.VMEM((2 * rows + span, HEAD_WIDTH), jnp.bfloat16)] * 2
        + [pltpu.VMEM((2 * rows + span, HEAD_WIDTH), jnp.float32)] * 2,
        compiler_params=pltpu.CompilerParams(vmem_limit_bytes=14 << 20),
        cost_estimate=SHORT,
        name="attend_back",
    )(slot_places, key_low, own, other, start, grad)


def call(kernel, outs, ins, scratch=(), scalars=0, grid=None, in_specs=None, out_specs=None, work=0, name=None, room=12):
    params = pltpu.CompilerParams(vmem_limit_bytes=room << 20)
    if grid is None:
        return pl.pallas_call(
            kernel,
            out_shape=tuple(outs),
            in_specs=[SMALL] * scalars + [WHOLE] * (len(ins) - scalars),
            out_specs=tuple([WHOLE] * len(outs)),
            scratch_shapes=list(scratch),
            compiler_params=params,
            cost_estimate=SHORT,
            name=name,
        )(*ins)
    return pl.pallas_call(
        kernel,
        out_shape=tuple(outs),
        grid_spec=pltpu.PrefetchScalarGridSpec(
            num_scalar_prefetch=scalars,
            grid=grid,
            in_specs=in_specs,
            out_specs=tuple(out_specs),
            scratch_shapes=list(scratch),
        ),
        compiler_params=params,
        cost_estimate=SHORT,
        name=name,
    )(*ins)


def made(shape, dtype):
    return jax.ShapeDtypeStruct(shape, dtype)


def norm_of(values):
    rows = values.astype(jnp.float32)
    scale = lax.rsqrt(jnp.mean(rows * rows, axis=-1, keepdims=True) + norm_eps)
    return scale, rows * scale


def norm_back(grad, gain, scale, unit):
    back = grad * gain
    return scale * (back - unit * jnp.mean(back * unit, axis=-1, keepdims=True))


def project_kernel(
    tokens_ref, gain_ref, live_ref, cosine_ref, sine_ref, query_ref, key_ref, value_ref, packed_ref, normed_ref
):
    head = HEAD_WIDTH
    rows = tokens_ref.shape[0]

    @pl.when(pl.program_id(0) == 0)
    def _():
        step = 128

        def piece(index, carry):
            at = pl.ds(pl.multiple_of(index * step, step), step)
            normed_ref[at, :] = (norm_of(tokens_ref[at, :])[1] * gain_ref[...]).astype(jnp.bfloat16)
            return carry

        lax.fori_loop(0, rows // step, piece, 0)

    normed = normed_ref[...]
    for index, weight in enumerate((query_ref, key_ref, value_ref)):
        both = dense(normed, weight[...])
        for which in range(2):
            values = both[:, which * head : (which + 1) * head]
            if index < 2:
                values = values * cosine_ref[...] + pltpu.roll(values, head // 2, 1) * sine_ref[...]
            else:
                values = jnp.where(live_ref[...] == 1, values, 0.0)
            packed_ref[which, :, index * head : (index + 1) * head] = values.astype(jnp.bfloat16)


def project_call(tokens, gain, live, cosine, sine, w_query, w_key, w_value):
    rows, width = tokens.shape
    heads = w_query.shape[1] // HEAD_WIDTH
    whole = lambda shape: pl.BlockSpec(shape, lambda h: (0, 0))
    weight = pl.BlockSpec((width, 2 * HEAD_WIDTH), lambda h: (0, h))
    w_query, w_key, w_value = [
        pltpu.with_memory_space_constraint(w, pltpu.HBM) for w in (w_query, w_key, w_value)
    ]
    return call(
        project_kernel,
        (made((heads, rows, 3 * HEAD_WIDTH), jnp.bfloat16), made((rows, width), jnp.bfloat16)),
        (tokens, gain, live, cosine, sine, w_query, w_key, w_value),
        grid=(heads // 2,),
        in_specs=[
            whole((rows, width)), whole((1, width)), whole((rows, 1)),
            whole((rows, HEAD_WIDTH)), whole((rows, HEAD_WIDTH)), weight, weight, weight,
        ],
        out_specs=[
            pl.BlockSpec((2, rows, 3 * HEAD_WIDTH), lambda h: (h, 0, 0)), whole((rows, width)),
        ],
        work=6 * rows * width * w_query.shape[1],
        room=32,
        name="project",
    )


def piece_at(own_tp, d, count):
    return lax.rem(own_tp + d, count)


def out_kernel(where_ref, tokens_ref, gain_ref, attended_ref, *refs):
    *weights, middle_ref, normed_ref = refs
    own_tp, core = where_ref[0], where_ref[1]
    count, part, _ = attended_ref.shape
    _, half, wide = weights[0].shape
    starts = (0, wide, middle_ref.shape[1])
    rows = tokens_ref[pl.ds(pl.multiple_of(own_tp * part, part), part), :].astype(jnp.float32)
    for piece in range(2):
        target = slice(starts[piece], starts[piece + 1])
        total = rows[:, target]
        for d in range(count):
            for which in range(2):
                side = core if which == 0 else 1 - core
                columns = pl.ds(pl.multiple_of(side * half, half), half)
                values = attended_ref[d, :, columns]
                total = total + dense(values, weights[2 * piece + which][d])
        middle_ref[:, target] = total
    normed_ref[...] = (norm_of(middle_ref[...])[1] * gain_ref[...]).astype(jnp.bfloat16)


def ffn_kernel(where_ref, *refs, chunk, sources, first):
    grad_act_ref, gate_ref, up_ref = refs[sources : sources + 3]
    act_ref, gate_pre_ref, up_pre_ref, normed_ref, *grads, total_ref = refs[
        sources + 3 + (0 if first else 4) :
    ]
    own_tp = where_ref[0]
    part = grads[0].shape[0]
    step = pl.program_id(0)

    @pl.when(step == 0)
    def _():
        if first:
            normed_ref[:part, :] = refs[0][...]
            normed_ref[part:, :] = jnp.where(from_above(own_tp, 1), refs[1][...], refs[2][...])
        elif chunk == 2:
            normed_ref[...] = jnp.where(from_above(own_tp, 2), refs[0][...], refs[1][...])
        else:
            inner = jnp.where(own_tp == 1, refs[0][...], refs[1][...])
            ends = jnp.where(own_tp == 0, refs[2][...], refs[3][...])
            normed_ref[...] = jnp.where(is_inner(own_tp), inner, ends)

    normed = normed_ref[...]
    gate = dense(normed, gate_ref[...])
    up = dense(normed, up_ref[...])
    sig = jax.nn.sigmoid(gate)
    grad_act = grad_act_ref[...]
    act_ref[...] = (gate * sig * up).astype(jnp.bfloat16)
    gate_pre = (grad_act * up * (sig * (1.0 + gate * (1.0 - sig)))).astype(jnp.bfloat16)
    up_pre = (grad_act * (gate * sig)).astype(jnp.bfloat16)
    gate_pre_ref[...] = gate_pre
    up_pre_ref[...] = up_pre
    term = dense_t(gate_pre, gate_ref[...]) + dense_t(up_pre, up_ref[...])

    @pl.when(step == 0)
    def _():
        total_ref[...] = term

    @pl.when(step > 0)
    def _():
        total_ref[...] += term

    @pl.when(step == pl.num_programs(0) - 1)
    def _():
        for index, grad_ref in enumerate(grads):
            rows = slice(index * part, (index + 1) * part)
            grad_ref[...] = total_ref[rows, :].astype(jnp.bfloat16)


def from_above(own_tp, chunk):
    return own_tp % (2 * chunk) < chunk


def is_inner(own_tp):
    return (own_tp == 1) | (own_tp == 2)


def ffn_call(where, chunk, sources, grad_act, w_gate, w_up, filled):
    part, width = sources[0].shape
    total, hidden = grad_act.shape
    wide = 512
    count = 2 if filled is None else 1
    rows = count * part
    whole = pl.BlockSpec((part, width), lambda f, w: (0, 0))
    weight = pl.BlockSpec((width, wide), lambda f, w: (0, f))
    block = pl.BlockSpec((rows, wide), lambda f, w: (chunk, f))
    low = made((total, hidden), jnp.bfloat16)
    w_gate, w_up = [pltpu.with_memory_space_constraint(w, pltpu.HBM) for w in (w_gate, w_up)]
    ins = [where, *sources, grad_act, w_gate, w_up]
    specs = [whole] * len(sources) + [block, weight, weight]
    aliases = {}
    if filled is not None:
        aliases = {len(ins) + i: i for i in range(4)}
        ins += list(filled)
        specs += [pl.BlockSpec(memory_space=pl.ANY)] * 4
    outs = pl.pallas_call(
        functools.partial(ffn_kernel, chunk=chunk, sources=len(sources), first=not aliases),
        out_shape=(low, low, low, made((total, width), jnp.bfloat16))
        + (made((part, width), jnp.bfloat16),) * count,
        grid_spec=pltpu.PrefetchScalarGridSpec(
            num_scalar_prefetch=1,
            grid=(hidden // wide,),
            in_specs=specs,
            out_specs=(
                block, block, block, pl.BlockSpec((rows, width), lambda f, w: (chunk, 0)),
            )
            + (whole,) * count,
            scratch_shapes=[pltpu.VMEM((rows, width), jnp.float32)],
        ),
        input_output_aliases=aliases,
        compiler_params=pltpu.CompilerParams(vmem_limit_bytes=28 << 20),
        cost_estimate=SHORT,
        name="ffn",
    )(*ins)
    return outs[:4], outs[4:]


def middle_kernel(where_ref, middle_ref, upstream_ref, gain_ref, *refs):
    terms, refs = refs[: refs[-2].shape[0]], refs[refs[-2].shape[0] :]
    *weights, low_ref, grad_ref, back_ref, gain_grad_ref = refs
    own_tp, core = where_ref[0], where_ref[1]
    count, part, _ = back_ref.shape
    _, half, wide = weights[0].shape
    scale, unit = norm_of(middle_ref[...])
    grad = sum([t[...].astype(jnp.float32) for t in terms[1:]], terms[0][...].astype(jnp.float32))
    gain_grad_ref[...] = jnp.sum(grad * unit, axis=0, keepdims=True)
    at = pl.ds(pl.multiple_of(own_tp * part, part), part)
    total = upstream_ref[at, :].astype(jnp.float32) + norm_back(grad, gain_ref[...], scale, unit)
    grad_ref[...] = total
    low = total.astype(jnp.bfloat16)
    low_ref[...] = low
    for d in range(count):
        for which in range(2):
            side = core if which == 0 else 1 - core
            columns = pl.ds(pl.multiple_of(side * half, half), half)
            values = dense_t(low[:, :wide], weights[which][d])
            values = values + dense_t(low[:, wide:], weights[2 + which][d])
            back_ref[d, :, columns] = values.astype(jnp.bfloat16)


def back_kernel(where_ref, back_ref, live_ref, tokens_ref, query_ref, key_ref, value_ref, low_ref, gain_ref, *refs):
    *outs, ordered_ref, unit_ref = refs
    head = HEAD_WIDTH
    heads = back_ref.shape[0]
    count = len(outs)
    part = outs[0].shape[0]
    own = heads * head
    step = pl.program_id(0)

    @pl.when(step == 0)
    def _():
        for d in range(count):
            at = pl.ds(pl.multiple_of(piece_at(where_ref[0], d, count) * part, part), part)
            rows = slice(d * part, (d + 1) * part)
            for index in range(3):
                low = jnp.concatenate(
                    [back_ref[h, at, index * head : (index + 1) * head] for h in range(heads)],
                    axis=-1,
                )
                if index == 2:
                    low = jnp.where(live_ref[at, :] == 1, low.astype(jnp.float32), 0.0)
                    low = low.astype(jnp.bfloat16)
                low_ref[at, index * own : (index + 1) * own] = low
                ordered_ref[rows, index * own : (index + 1) * own] = low
            unit = norm_of(tokens_ref[at, :])[1]
            for block in range(unit_ref.shape[0]):
                wide = unit_ref.shape[2]
                unit_ref[block, rows, :] = unit[:, block * wide : (block + 1) * wide]

    total = None
    for index, weight in enumerate((query_ref, key_ref, value_ref)):
        term = dense_t(ordered_ref[:, index * own : (index + 1) * own], weight[...])
        total = term if total is None else total + term
    gain_ref[...] = jnp.sum(total * unit_ref[step], axis=0, keepdims=True)
    for d in range(count):
        outs[d][...] = total[d * part : (d + 1) * part].astype(jnp.bfloat16)


def back_call(where, back_heads, live, tokens, weights, count):
    rows, width = tokens.shape
    own = weights[0].shape[1]
    part = rows // count
    wide = 512
    blocks = width // wide
    weights = [pltpu.with_memory_space_constraint(w, pltpu.HBM) for w in weights]
    whole = lambda x: pl.BlockSpec(x.shape, lambda f, w: (0,) * len(x.shape))
    return pl.pallas_call(
        back_kernel,
        out_shape=(made((rows, 3 * own), jnp.bfloat16), made((1, width), jnp.float32))
        + (made((part, width), jnp.bfloat16),) * count,
        grid_spec=pltpu.PrefetchScalarGridSpec(
            num_scalar_prefetch=1,
            grid=(blocks,),
            in_specs=[whole(back_heads), whole(live), whole(tokens)]
            + [pl.BlockSpec((wide, own), lambda f, w: (f, 0))] * 3,
            out_specs=(
                pl.BlockSpec((rows, 3 * own), lambda f, w: (0, 0)),
                pl.BlockSpec((1, wide), lambda f, w: (0, f)),
            )
            + (pl.BlockSpec((part, wide), lambda f, w: (0, f)),) * count,
            scratch_shapes=[
                pltpu.VMEM((rows, 3 * own), jnp.bfloat16),
                pltpu.VMEM((blocks, rows, wide), jnp.float32),
            ],
        ),
        compiler_params=pltpu.CompilerParams(vmem_limit_bytes=32 << 20),
        cost_estimate=SHORT,
        name="back",
    )(where, back_heads, live, tokens, *weights)


def tokens_kernel(
    where_ref, tokens_ref, gain_ref, grad_ref, gains_ref, middle_ref, branch_ref, own_ref, below_ref, above_ref, out_ref
):
    part = own_ref.shape[0]
    at = pl.ds(pl.multiple_of(where_ref[0] * part, part), part)
    scale, unit = norm_of(tokens_ref[at, :])
    grad = own_ref[...].astype(jnp.float32) + (
        below_ref[...].astype(jnp.float32) + above_ref[...].astype(jnp.float32)
    )
    total = grad_ref[...] + norm_back(grad, gain_ref[...], scale, unit)
    out_ref[:part, :] = total.astype(jnp.bfloat16)
    gains = gains_ref[...]
    high = gains.astype(jnp.bfloat16)
    low = (gains - high.astype(jnp.float32)).astype(jnp.bfloat16)
    wide = gains.shape[1]
    rows = out_ref.shape[0] - 2 * part
    middle = slice(part, part + rows)
    for index, values in enumerate((high, low)):
        out_ref[middle, index * wide : (index + 1) * wide] = jnp.broadcast_to(values, (rows, wide))
    out_ref[middle, 2 * wide :] = jnp.zeros((rows, out_ref.shape[1] - 2 * wide), jnp.bfloat16)
    layer = middle_ref[...] + branch_ref[...].astype(jnp.float32)
    out_ref[part + rows :, :] = layer.astype(jnp.bfloat16)


def join_kernel(where_ref, own_ref, *refs, part):
    *pieces, out_ref, gains_ref, layer_ref, terms_ref = refs
    count = len(pieces) // 2 + 1
    wide = gains_ref.shape[1]
    for d in range(count):
        place = piece_at(where_ref[0], d, count)
        values = own_ref[...] if d == 0 else pieces[d - 1][...] + pieces[2 * count - 2 - d][...]
        at = pl.ds(pl.multiple_of(place * part, part), part)
        out_ref[at, :] = values[:part].astype(jnp.float32)
        row = values[part : part + 8].astype(jnp.float32)
        terms_ref[place] = row[:, :wide] + row[:, wide : 2 * wide]
        layer_ref[at, :] = values[values.shape[0] - part :]
    total = terms_ref[0]
    for index in range(1, count):
        total = total + terms_ref[index]
    gains_ref[...] = total[:1]


def join(where, gathered, part, gains):
    own, above, below = gathered
    count = len(above) + 1
    width = own.shape[1]
    return call(
        functools.partial(join_kernel, part=part),
        (
            made((count * part, width), jnp.float32),
            made((1, gains), jnp.float32),
            made((count * part, width), jnp.bfloat16),
        ),
        (where, own, *above, *below),
        scratch=[pltpu.VMEM((count, 8, gains), jnp.float32)],
        scalars=1,
        name="join",
    )


def tie(*values):
    return lax.optimization_barrier(values)


def after(value, *others):
    return lax.optimization_barrier((value, *others))[0]


class Line:
    def __init__(self, axis, count):
        self.axis, self.count, self.at = axis, count, 0
        self.upward, self.downward = None, None

    def tie(self, *others):
        self.upward, self.downward, *others = tie(self.upward, self.downward, *others)
        return others[0] if len(others) == 1 else others

    def send(self, up, down, up_pairs, down_pairs):
        self.upward = lax.ppermute(up, self.axis, up_pairs)
        self.downward = lax.ppermute(down, self.axis, down_pairs)


class Gather(Line):
    def __init__(self, shard, axis, count):
        super().__init__(axis, count)
        self.own, self.above, self.below = shard, [], []

    def step(self):
        if self.at:
            self.keep()
        up, down = (self.upward, self.downward) if self.at else (self.own, self.own)
        self.at += 1
        at, count = self.at, self.count
        self.send(
            up,
            down,
            [(i, i + 1) for i in range(at - 1, count - 1)],
            [(i, i - 1) for i in range(1, count - at + 1)],
        )

    def keep(self):
        self.below.append(self.upward)
        self.above.append(self.downward)

    def result(self):
        while self.at < self.count - 1:
            self.step()
        self.keep()
        return self.own, self.above, self.below


def add_kernel(up_ref, got_up_ref, down_ref, got_down_ref, sum_up_ref, sum_down_ref):
    for part, got, total in (
        (up_ref, got_up_ref, sum_up_ref),
        (down_ref, got_down_ref, sum_down_ref),
    ):
        total[...] = (part[...].astype(jnp.float32) + got[...].astype(jnp.float32)).astype(
            jnp.bfloat16
        )


class Sum(Line):
    def __init__(self, parts, axis, count):
        super().__init__(axis, count)
        self.parts = parts

    def step(self):
        first = self.at == 0
        self.at += 1
        at, count = self.at, self.count
        up, down = self.parts[count - at], self.parts[at]
        if not first:
            outs = (made(up.shape, jnp.bfloat16),) * 2
            up, down = call(
                add_kernel, outs, (up, self.upward, down, self.downward), name="add"
            )
        self.send(
            up,
            down,
            [(i, i + 1) for i in range(0, at)],
            [(i, i - 1) for i in range(count - at, count)],
        )

    def result(self):
        while self.at < self.count - 1:
            self.step()
        return self.parts[0], self.upward, self.downward


def outer(left, right):
    return lax.dot_general(
        left, right, (((0,), (0,)), ((), ())), preferred_element_type=jnp.float32
    )


def chip_outer_kernel(where_ref, *refs, sides):
    del where_ref
    keep_x, sent_x, keep_y, sent_y = refs[-4:]
    step = pl.program_id(0)
    values = []
    for side in range(sides):
        left, left_other, right, right_other = refs[4 * side : 4 * side + 4]
        product = outer(left[...], right[...]) + outer(left_other[...], right_other[...])
        values.append(product.astype(jnp.bfloat16))
    values = values[0] if sides == 1 else jnp.concatenate(values, axis=-1)
    half = values.shape[1] // 2

    for target, part, places in (
        (keep_x, 0, (0, 1)),
        (sent_x, 0, (2, 3)),
        (keep_y, 1, (0, 3)),
        (sent_y, 1, (1, 2)),
    ):

        @pl.when((step == places[0]) | (step == places[1]))
        def _(target=target, part=part):
            target[0] = values[:, part * half : (part + 1) * half]


def chip_outer_call(where, pairs, seq_size, name, columns=1, column=0, into=None):
    rows, width = pairs[0][0].shape
    block = width // seq_size
    half = sum(pair[2].shape[1] for pair in pairs) // 2

    def left_index(k, w):
        chip = jnp.where(k == 0, 0, jnp.where(k == 1, 2, jnp.where(k == 2, 3, 1)))
        return 0, 2 * (w[2] ^ chip) + w[1]

    specs, ins = [], []
    for pair in pairs:
        wide = pl.BlockSpec(pair[2].shape, lambda k, w: (0, 0))
        specs += [pl.BlockSpec((rows, block), left_index)] * 2 + [wide, wide]
        ins += list(pair)
    aliases = {}
    if into is not None:
        aliases = {1 + len(ins) + i: i for i in range(4)}
        specs += [pl.BlockSpec(memory_space=pltpu.HBM)] * 4
        ins += list(into)

    def target(place):
        return pl.BlockSpec((1, block, half), lambda k, w: (place(k), 0, column))

    return pl.pallas_call(
        functools.partial(chip_outer_kernel, sides=len(pairs)),
        out_shape=(pltpu.HBM((2, block, columns * half), jnp.bfloat16),) * 4,
        grid_spec=pltpu.PrefetchScalarGridSpec(
            num_scalar_prefetch=1,
            grid=(4,),
            in_specs=specs,
            out_specs=(
                target(lambda k: jnp.minimum(k, 1)),
                target(lambda k: k // 3),
                target(lambda k: k // 3),
                target(lambda k: k // 2),
            ),
        ),
        input_output_aliases=aliases,
        compiler_params=pltpu.CompilerParams(vmem_limit_bytes=24 << 20),
        cost_estimate=SHORT,
        name=name,
    )(where, *ins)


class ChipSum:
    def __init__(self, arrays, seq_size):
        self.arrays, self.size = arrays, seq_size

    def over(self, values, side):
        return lax.ppermute(values, "seq", [(i, i ^ side) for i in range(self.size)])

    def first(self, *earlier):
        _, sent_x, _, sent_y = self.arrays
        if earlier:
            sent_x, sent_y = tie(sent_x, sent_y, *earlier)[:2]
        self.got_x, self.got_y = self.over(sent_x, 2), self.over(sent_y, 4)

    def tie(self, *others):
        self.got_x, self.got_y, *others = tie(self.got_x, self.got_y, *others)
        return others[0] if len(others) == 1 else others

    def second(self, *earlier):
        f32, bf16 = jnp.float32, jnp.bfloat16
        if earlier:
            self.got_x, self.got_y = tie(self.got_x, self.got_y, *earlier)[:2]
        keep_x, _, keep_y, _ = self.arrays
        through_x = (keep_x[1].astype(f32) + self.got_x[0].astype(f32)).astype(bf16)
        through_y = (keep_y[1].astype(f32) + self.got_y[1].astype(f32)).astype(bf16)
        self.last_x, self.last_y = self.over(through_x, 4), self.over(through_y, 2)

    def tie_last(self, *values):
        self.last_x, self.last_y, *values = tie(self.last_x, self.last_y, *values)
        return values

    def terms(self):
        keep_x, _, keep_y, _ = self.arrays
        return (keep_x, self.got_x, self.last_x), (keep_y, self.got_y, self.last_y)


def widen_kernel(*refs, terms, turned):
    f32 = jnp.float32
    values_refs, outs = refs[: len(terms)], refs[len(terms) :]
    column = 0
    for index, out_ref in enumerate(outs):
        wide = out_ref.shape[0] if turned[index] else out_ref.shape[1]
        columns = slice(column, column + wide)
        total = None
        for ref, place in zip(values_refs, terms):
            values = ref[:, columns] if place is None else ref[place, :, columns]
            total = values.astype(f32) if total is None else total + values.astype(f32)
        out_ref[...] = total.T if turned[index] else total
        column += wide


def widen(values, terms, widths, turned, name):
    rows = values[-1].shape[0]
    outs = [made((w, rows) if t else (rows, w), jnp.float32) for w, t in zip(widths, turned)]
    kernel = functools.partial(widen_kernel, terms=terms, turned=turned)
    return call(kernel, outs, tuple(values), name=name, room=24)


def widen_pair_kernel(*refs, turned):
    f32 = jnp.float32
    outs = refs[6:]
    for index, out_ref in enumerate(outs):
        half = (out_ref.shape[0] if turned[index] else out_ref.shape[1]) // 2
        columns = slice(index * half, (index + 1) * half)
        for way, (got_place, keep, got, last) in enumerate(((1, *refs[:3]), (0, *refs[3:6]))):
            total = keep[0, :, columns].astype(f32) + got[got_place, :, columns].astype(f32)
            total = total + last[:, columns].astype(f32)
            target = slice(way * half, (way + 1) * half)
            if turned[index]:
                out_ref[target, :] = total.T
            else:
                out_ref[:, target] = total


def widen_pair(values, width, turned, name):
    rows = values[2].shape[0]
    outs = [made((width, rows) if t else (rows, width), jnp.float32) for t in turned]
    kernel = functools.partial(widen_pair_kernel, turned=turned)
    return call(kernel, outs, tuple(values), name=name, room=24)


def matmul_kernel(where_ref, left_ref, right_ref, out_ref, *, turned, parts):
    product = (dense_t if turned else dense)(left_ref[...], right_ref[...]).astype(out_ref.dtype)
    if parts == 1:
        out_ref[...] = product
    part = product.shape[0] // parts
    for k in range(parts if parts > 1 else 0):
        place = where_ref[0] ^ k
        rows = pl.ds(pl.multiple_of(place * part, part), part)
        out_ref[rows, :] = product[k * part : (k + 1) * part]


def matmul_call(where, left, right, dtype, turned, name, parts=1):
    rows, depth = left.shape
    columns = right.shape[0 if turned else 1]
    wide = 512
    right = pltpu.with_memory_space_constraint(right, pltpu.HBM)
    if turned:
        right_spec = pl.BlockSpec((wide, depth), lambda f, w: (f, 0))
    else:
        right_spec = pl.BlockSpec((depth, wide), lambda f, w: (0, f))
    return pl.pallas_call(
        functools.partial(matmul_kernel, turned=turned, parts=parts),
        out_shape=made((rows, columns), dtype),
        grid_spec=pltpu.PrefetchScalarGridSpec(
            num_scalar_prefetch=1,
            grid=(columns // wide,),
            in_specs=[pl.BlockSpec((rows, depth), lambda f, w: (0, 0)), right_spec],
            out_specs=pl.BlockSpec((rows, wide), lambda f, w: (0, f)),
        ),
        compiler_params=pltpu.CompilerParams(vmem_limit_bytes=20 << 20),
        cost_estimate=SHORT,
        name=name,
    )(where, left, right)


def turn_kernel(query_ref, both_ref, other_ref, cosine_ref, sine_ref, out_ref):
    head = HEAD_WIDTH
    step = 256

    def piece(index, carry):
        rows = pl.ds(pl.multiple_of(index * step, step), step)
        both = both_ref[rows, :] + other_ref[rows, :].astype(jnp.float32)
        cosine, sine = cosine_ref[rows, :], sine_ref[rows, :]
        for place, values in ((0, query_ref[rows, :]), (1, both[:, :head])):
            values = values * cosine - pltpu.roll(values, head // 2, 1) * sine
            out_ref[rows, place * head : (place + 1) * head] = values.astype(jnp.bfloat16)
        out_ref[rows, 2 * head :] = both[:, head:].astype(jnp.bfloat16)
        return carry

    lax.fori_loop(0, query_ref.shape[0] // step, piece, 0)


def local_heads_apart(
    tokens,
    gain_attn,
    w_query,
    w_key,
    w_value,
    w_out,
    gain_ffn,
    w_gate,
    w_up,
    w_down,
    cotangent,
    doc_ids,
    valid,
    group_order,
    *,
    seq_size,
    tp_size,
):
    _, row_count, width = tokens.shape
    length = doc_ids.shape[1]
    groups = group_order.shape[1]
    span = length // groups
    head = HEAD_WIDTH
    heads = w_query.shape[1] // head
    own_width = heads * head
    hidden = w_gate.shape[1]
    chips = seq_size // 2
    part = row_count // tp_size
    block = width // seq_size
    bf16, f32, i32 = jnp.bfloat16, jnp.float32, jnp.int32
    same_core = [[2 * p + c for p in range(chips)] for c in range(2)]
    other_core = [(i, i ^ 1) for i in range(seq_size)]
    own_seq, own_tp = lax.axis_index("seq"), lax.axis_index("tp")
    core = own_seq % 2
    where = jnp.stack([own_tp, core, own_seq // 2]).astype(i32)
    tokens = tokens.reshape(row_count, width)
    upstream = cotangent.reshape(row_count, width)
    gain_attn, gain_ffn = gain_attn.reshape(1, width), gain_ffn.reshape(1, width)

    def swap(values):
        return lax.ppermute(values, "seq", other_core)

    def to_heads(values):
        return lax.all_to_all(values, "seq", 0, 0, axis_index_groups=same_core, tiled=True)

    def part_of(values, place):
        return lax.dynamic_slice_in_dim(values, place * part, part, 0)

    def reordered(values):
        return jnp.concatenate([part_of(values, own_tp ^ k) for k in range(tp_size)], axis=0)

    def across(values, k):
        return lax.ppermute(values, "tp", [(i, i ^ k) for i in range(tp_size)])

    half = own_width // 2
    most = width * 5 // 8
    w_half = lax.dynamic_slice_in_dim(w_out, core * half, half, 0)

    def gathered(columns):
        values = lax.all_gather(columns, "tp", axis=0, tiled=True)
        return values.reshape(tp_size, half, columns.shape[1])

    w_first = gathered(w_half[:, :most])
    w_second = gathered(w_half[:, most:])

    order = group_order[0]
    per_device = row_count // span

    def blocks_of(which):
        devices = 2 * jnp.arange(chips, dtype=i32) + which
        storage = (devices[:, None] * per_device + jnp.arange(per_device)[None, :]).reshape(-1)
        return jnp.take(order, storage)

    def places_of(block_ids):
        return (block_ids[:, None] * span + jnp.arange(span, dtype=i32)[None, :]).reshape(-1)

    own_blocks, other_blocks = blocks_of(core), blocks_of(1 - core)
    slot_places = jnp.concatenate([own_blocks, other_blocks])
    docs = doc_ids[0]
    first = jnp.sum(docs[None, :] < docs.reshape(groups, span)[:, :1], axis=1, dtype=i32)
    position = jnp.arange(length, dtype=i32).reshape(groups, span)
    change = jnp.where(docs != jnp.roll(docs, 1), jnp.arange(length, dtype=i32), 0)
    change = change.reshape(groups, span)
    start = jnp.max(
        jnp.where(position[:, None, :] <= position[:, :, None], change[:, None, :], 0), axis=2
    )
    start = jnp.maximum(start, first[:, None])
    start_q = jnp.take(start, own_blocks, axis=0)
    key_low = jnp.take(first, own_blocks) // span
    row_blocks = jnp.take(order, own_seq * per_device + jnp.arange(per_device, dtype=i32))
    live = jnp.take(valid.reshape(groups, span), row_blocks, axis=0).reshape(row_count, 1)
    cosine, sine = rope_tables(places_of(row_blocks), head)
    cosine = jnp.concatenate([cosine, cosine], axis=-1)
    sine = jnp.concatenate([-sine, sine], axis=-1)
    cosine_q, sine_q = rope_tables(places_of(own_blocks), head)
    cosine_q = jnp.concatenate([cosine_q, cosine_q], axis=-1)
    sine_q = jnp.concatenate([-sine_q, sine_q], axis=-1)

    packed, normed_attn = project_call(
        tokens, gain_attn, live, cosine, sine, w_query, w_key, w_value
    )
    mine = to_heads(packed).reshape(chips * row_count, 3 * head)
    upstream_rel = reordered(upstream)
    grad_act = matmul_call(where, upstream_rel, w_down, f32, True, "grad_act")
    upstream_pair = (upstream_rel, swap(upstream_rel))
    normed_attn_pair = (normed_attn, swap(normed_attn))
    mine, grad_act, cosine_q, sine_q = tie(mine, grad_act, cosine_q, sine_q)
    other = swap(mine[:, head:])

    attended = attend_call(slot_places, key_low, mine, other, start_q.reshape(-1, 1), span)
    attended, w_first = tie(attended, w_first)
    attended = to_heads(attended.reshape(chips, row_count, head))
    attended = attended.transpose(1, 0, 2).reshape(row_count, own_width)
    attended_part = lax.all_to_all(
        attended.reshape(tp_size, part, own_width), "tp", 0, 0, tiled=True
    )
    w_second = after(w_second, attended_part)
    out_weights = (w_first, swap(w_first), w_second, swap(w_second))
    middle, normed_part = call(
        out_kernel,
        (made((part, width), f32), made((part, width), bf16)),
        (where, tokens, gain_ffn, attended_part, *out_weights),
        scalars=1,
        work=2 * part * width * width,
        name="out",
    )

    line = Gather(normed_part, "tp", tp_size)
    line.step()
    line.step()
    above_1, below_1 = line.above[0], line.below[0]
    filled, (own_grad, grad_1) = ffn_call(
        where, 0, [normed_part, above_1, below_1], grad_act, w_gate, w_up, None
    )
    filled = line.tie(*filled)
    line.step()
    above_2, below_2 = line.above[1], line.below[1]
    filled, (grad_2,) = ffn_call(where, 2, [above_2, below_2], grad_act, w_gate, w_up, filled)
    *filled, grad_1, grad_2 = line.tie(*filled, grad_1, grad_2)
    grad_1, grad_2 = across(grad_1, 1), across(grad_2, 2)
    _, (_, _, above_3), (_, _, below_3) = line.result()
    filled, (grad_3,) = ffn_call(
        where, 3, [above_1, below_1, above_3, below_3], grad_act, w_gate, w_up, filled
    )
    grad_3 = across(grad_3, 3)
    activated, gate_pre, up_pre, normed_ffn = filled
    up_pre, grad_1, grad_2 = tie(up_pre, grad_1, grad_2)

    normed_pair = (normed_ffn, swap(normed_ffn))
    outer_ffn = functools.partial(
        chip_outer_call, where, seq_size=seq_size, name="ffn_outer"
    )
    gate_quad = (*normed_pair, gate_pre, swap(gate_pre))
    up_quad = (*normed_pair, up_pre, swap(up_pre))
    down_quad = (*upstream_pair, activated, swap(activated))
    gate_sum = ChipSum(outer_ffn([gate_quad]), seq_size)
    gate_sum.first()
    up_sum = ChipSum(outer_ffn([up_quad]), seq_size)
    up_sum.first()
    down_sum = ChipSum(outer_ffn([down_quad]), seq_size)
    grad_3, *down_sum.arrays = tie(grad_3, *down_sum.arrays)
    middle_low, grad_middle, grad_attended, gain_ffn_part = call(
        middle_kernel,
        (
            made((part, width), bf16),
            made((part, width), f32),
            made((tp_size, part, own_width), bf16),
            made((1, width), f32),
        ),
        (where, middle, upstream, gain_ffn, own_grad, grad_1, grad_2, grad_3, *out_weights),
        scalars=1,
        work=2 * part * width * width,
        name="middle",
    )
    grad_attended = lax.all_to_all(grad_attended, "tp", 0, 0, tiled=True)
    branch = matmul_call(where, after(activated, middle_low), w_down, bf16, False, "branch", tp_size)
    grad_attended, branch = up_sum.tie(*gate_sum.tie(grad_attended, branch))
    branch = after(branch, grad_attended)
    branch_part = lax.psum_scatter(branch, "tp", scatter_dimension=0, tiled=True)
    grad_attended = grad_attended.reshape(row_count, heads, head).transpose(1, 0, 2)
    grad_heads = to_heads(grad_attended).reshape(chips * row_count, head)
    grad_query, both, both_other = attend_back_call(
        slot_places, key_low, mine, other, start_q, grad_heads, span
    )
    other_term = swap(both_other)
    middle_all = lax.all_gather(after(middle_low, other_term), "tp", axis=0, tiled=True)
    packed_back = call(
        turn_kernel,
        (made((chips * row_count, 3 * head), bf16),),
        (grad_query, both, other_term, cosine_q, sine_q),
        name="turn",
    )[0].reshape(chips, row_count, 3 * head)
    back_heads = to_heads(packed_back)
    attended_pair = (attended, swap(attended))
    back_heads = after(back_heads, attended_pair[1], branch_part)
    low, gain_attn_part, *parts = back_call(
        where, back_heads, live, tokens, (w_query, w_key, w_value), tp_size
    )
    sums = Sum(parts, "tp", tp_size)
    sums.step()
    gains = jnp.concatenate([gain_attn_part, gain_ffn_part], axis=0)
    gains = gains.reshape(2, seq_size, block).transpose(1, 0, 2)
    gains = jnp.sum(lax.all_to_all(gains, "seq", 0, 0, tiled=True), axis=0).reshape(1, 2 * block)
    down_sum.first(low)
    down_sum.got_x, down_sum.got_y, low = sums.tie(down_sum.got_x, down_sum.got_y, low)
    sums.step()
    gains, low, middle_all = sums.tie(gains, low, middle_all)
    up_sum.second(low)
    sums.step()
    middle_pair = (middle_all, swap(middle_all))
    attn_grads = chip_outer_call(
        where,
        [(*middle_pair, *attended_pair), (*normed_attn_pair, low, swap(low))],
        seq_size,
        "attn_outer",
    )
    up_sum.last_x, up_sum.last_y, *attn_grads = sums.tie(
        up_sum.last_x, up_sum.last_y, *attn_grads
    )
    attn_sum = ChipSum(attn_grads, seq_size)
    tokens_part = call(
        tokens_kernel,
        (made((2 * part + 16, width), bf16),),
        (where, tokens, gain_attn, grad_middle, gains, middle, branch_part, *sums.result()),
        scalars=1,
        name="tokens",
    )[0]
    token_line = Gather(tokens_part, "tp", tp_size)
    token_line.step()
    attn_sum.first(tokens_part)
    attn_sum.got_x, attn_sum.got_y, low = token_line.tie(attn_sum.got_x, attn_sum.got_y, low)
    token_line.step()
    down_sum.second(low)
    gate_sum.second(low)
    (*last, low) = token_line.tie(
        down_sum.last_x, down_sum.last_y, gate_sum.last_x, gate_sum.last_y, low
    )
    down_sum.last_x, down_sum.last_y, gate_sum.last_x, gate_sum.last_y = last
    token_line.step()
    attn_sum.second(low)
    up_sum.last_x = after(up_sum.last_x, low)
    up_x, up_y = up_sum.terms()
    (grad_up,) = widen_pair([*up_x, *up_y], hidden, (False,), "widen_up")
    down_x, down_y = down_sum.terms()
    (grad_down,) = widen_pair([*down_x, *down_y], hidden, (True,), "widen_down")
    gate_x, gate_y = gate_sum.terms()
    (grad_gate,) = widen_pair([*gate_x, *gate_y], hidden, (False,), "widen_gate")
    terms_x, terms_y = attn_sum.terms()
    grad_out, grad_query = widen(
        terms_x, [0, 1, None], [own_width] * 2, (True, False), "widen_attn"
    )
    grad_key, grad_value = widen(
        terms_y, [0, 0, None], [own_width] * 2, (False, False), "widen_attn"
    )
    grad_out, grad_key, grad_gate, grad_up = token_line.tie(grad_out, grad_key, grad_gate, grad_up)
    grad_tokens, gains, layer_out = join(where, token_line.result(), part, 2 * block)
    gains = gains.reshape(2, block)

    return (
        layer_out.reshape(1, row_count, width),
        grad_tokens.reshape(1, row_count, width),
        gains[0],
        grad_query,
        grad_key,
        grad_value,
        grad_out,
        gains[1],
        grad_gate,
        grad_up,
        grad_down,
    )


def solution(mesh):
    placed = (
        P(None, "seq", None),
        P(),
        P(None, "tp"),
        P(None, "tp"),
        P(None, "tp"),
        P("tp", None),
        P(),
        P(None, "tp"),
        P(None, "tp"),
        P("tp", None),
        P(None, "seq", None),
        P(),
        P(),
        P(),
    )
    seq_size, tp_size = mesh.shape["seq"], mesh.shape["tp"]

    def local(*args):
        heads = args[2].shape[1] // HEAD_WIDTH
        if seq_size == 8 and tp_size == 4 and heads == 4 and args[0].shape[0] == 1:
            return local_heads_apart(*args, seq_size=seq_size, tp_size=tp_size)
        return local_general(*args)

    return jax.shard_map(
        local,
        mesh=mesh,
        in_specs=placed,
        out_specs=(
            P(None, "seq", None),
            P(None, "seq", None),
            P("seq"),
            P("seq", "tp"),
            P("seq", "tp"),
            P("seq", "tp"),
            P("tp", "seq"),
            P("seq"),
            P("seq", "tp"),
            P("seq", "tp"),
            P("tp", "seq"),
        ),
        check_vma=False,
    )
```

```python
import functools
import math

import jax
import jax.numpy as jnp
from jax import lax
from jax.experimental import pallas as pl
from jax.experimental.pallas import tpu as pltpu
from jax.sharding import PartitionSpec as P

HEAD_WIDTH = 128


norm_eps = 1e-05
rope_base = 10000.0


def rope_tables(places, head_size):
    half_size = head_size // 2
    freqs = rope_base ** (-jnp.arange(half_size, dtype=jnp.float32) * 2.0 / head_size)
    angles = places.astype(jnp.float32)[..., None] * freqs
    return (jnp.cos(angles), jnp.sin(angles))


def rotate(values, cosine, sine, forward):
    half_size = values.shape[-1] // 2
    first = values[..., :half_size]
    second = values[..., half_size:]
    cos_b = cosine[..., None, :]
    sin_b = sine[..., None, :]
    if forward:
        return jnp.concatenate(
            [first * cos_b - second * sin_b, second * cos_b + first * sin_b], axis=-1
        )
    return jnp.concatenate(
        [first * cos_b + second * sin_b, second * cos_b - first * sin_b], axis=-1
    )


def visible(place_q, doc_q, place_k, doc_k, live_k):
    allowed = (
        (place_k[None, :] <= place_q[:, None])
        & (doc_k[None, :] == doc_q[:, None])
        & (live_k[None, :] == 1)
    )
    return allowed.astype(jnp.float32)


def score_block(query_heads, key_heads, head_size, length):
    scores = jnp.einsum("qhe,khe->hqk", query_heads, key_heads, preferred_element_type=jnp.float32)
    return scores * (1.0 / math.sqrt(head_size)) - math.log(length)


def score_grads(query_heads, key_heads, value_heads, grad_heads, mask, head_size, length):
    sigma = jax.nn.sigmoid(score_block(query_heads, key_heads, head_size, length))
    weights = (sigma * mask).astype(jnp.bfloat16)
    grad_weights = jnp.einsum(
        "qhe,khe->hqk", grad_heads, value_heads, preferred_element_type=jnp.float32
    )
    grad_scores = (grad_weights * (sigma * (1.0 - sigma)) * mask).astype(jnp.bfloat16)
    return (weights, grad_scores)


def local_general(
    tokens,
    gain_attn,
    w_query,
    w_key,
    w_value,
    w_out,
    gain_ffn,
    w_gate,
    w_up,
    w_down,
    cotangent,
    doc_ids,
    valid,
    group_order,
):
    seq_count, row_count, model_width = tokens.shape
    length = doc_ids.shape[1]
    span = length // group_order.shape[1]
    head_size = HEAD_WIDTH
    local_width = w_query.shape[1]
    local_heads = local_width // head_size
    flat_rows = seq_count * row_count
    factor = 1.0 / math.sqrt(head_size)
    own_rows = lax.axis_index("seq") * row_count + jnp.arange(row_count, dtype=jnp.int32)
    all_rows = jnp.arange(length, dtype=jnp.int32)
    place_all = jnp.take(group_order, all_rows // span, axis=1) * span + (all_rows % span)[None, :]
    place_own = jnp.take(group_order, own_rows // span, axis=1) * span + (own_rows % span)[None, :]
    doc_all = jnp.take_along_axis(doc_ids, place_all, axis=1)
    live_all = jnp.take_along_axis(valid, place_all, axis=1)
    doc_own = jnp.take_along_axis(doc_ids, place_own, axis=1)
    cosine, sine = rope_tables(place_own, head_size)
    input_rows = tokens.astype(jnp.float32).reshape(flat_rows, model_width)
    scale_attn = lax.rsqrt(jnp.mean(input_rows * input_rows, axis=-1, keepdims=True) + norm_eps)
    unit_attn = input_rows * scale_attn
    normed_attn = (unit_attn * gain_attn).astype(jnp.bfloat16)

    def project(weight_matrix):
        return jnp.dot(normed_attn, weight_matrix, preferred_element_type=jnp.float32).reshape(
            seq_count, row_count, local_heads, head_size
        )

    query_rot = (
        rotate(project(w_query), cosine, sine, True)
        .astype(jnp.bfloat16)
        .reshape(seq_count, row_count, local_width)
    )
    key_rot = (
        rotate(project(w_key), cosine, sine, True)
        .astype(jnp.bfloat16)
        .reshape(seq_count, row_count, local_width)
    )
    value_low = (
        jnp.dot(normed_attn, w_value, preferred_element_type=jnp.float32)
        .astype(jnp.bfloat16)
        .reshape(seq_count, row_count, local_width)
    )
    key_all, value_all = (
        lax.all_gather(key_rot, "seq", axis=1, tiled=True),
        lax.all_gather(value_low, "seq", axis=1, tiled=True),
    )

    def attend(items):
        query_seq, key_seq, value_seq, place_q, doc_q, place_k, doc_k, live_k = items
        query_heads = query_seq.reshape(row_count, local_heads, head_size)
        key_heads = key_seq.reshape(length, local_heads, head_size)
        value_heads = value_seq.reshape(length, local_heads, head_size)
        mask = visible(place_q, doc_q, place_k, doc_k, live_k)
        weights = (
            jax.nn.sigmoid(score_block(query_heads, key_heads, head_size, length)) * mask
        ).astype(jnp.bfloat16)
        mixed = jnp.einsum("hqk,khe->qhe", weights, value_heads, preferred_element_type=jnp.float32)
        return mixed.astype(jnp.bfloat16).reshape(row_count, local_width)

    attention_output = lax.map(
        attend, (query_rot, key_all, value_all, place_own, doc_own, place_all, doc_all, live_all)
    )
    attended_flat = attention_output.reshape(flat_rows, local_width)
    branch_attn = lax.psum(jnp.dot(attended_flat, w_out, preferred_element_type=jnp.float32), "tp")
    hidden_rows = input_rows + branch_attn
    scale_ffn = lax.rsqrt(jnp.mean(hidden_rows * hidden_rows, axis=-1, keepdims=True) + norm_eps)
    unit_ffn = hidden_rows * scale_ffn
    normalized_feedforward = (unit_ffn * gain_ffn).astype(jnp.bfloat16)
    gate_rows = jnp.dot(normalized_feedforward, w_gate, preferred_element_type=jnp.float32)
    up_projected = jnp.dot(normalized_feedforward, w_up, preferred_element_type=jnp.float32)
    gate_sig = jax.nn.sigmoid(gate_rows)
    activation_rows = (gate_rows * gate_sig * up_projected).astype(jnp.bfloat16)
    branch_ffn = lax.psum(
        jnp.dot(activation_rows, w_down, preferred_element_type=jnp.float32).astype(jnp.bfloat16),
        "tp",
    ).astype(jnp.float32)
    layer_out = (
        (hidden_rows + branch_ffn).astype(jnp.bfloat16).reshape(seq_count, row_count, model_width)
    )
    upstream = cotangent.astype(jnp.float32).reshape(flat_rows, model_width)
    upstream_low = upstream.astype(jnp.bfloat16)
    grad_down = jnp.einsum(
        "tf,td->fd", activation_rows, upstream_low, preferred_element_type=jnp.float32
    )
    grad_act = jnp.einsum("td,fd->tf", upstream_low, w_down, preferred_element_type=jnp.float32)
    gate_pre = (grad_act * up_projected * (gate_sig * (1.0 + gate_rows * (1.0 - gate_sig)))).astype(
        jnp.bfloat16
    )
    up_pre = (grad_act * (gate_rows * gate_sig)).astype(jnp.bfloat16)
    grad_gate = jnp.einsum(
        "td,tf->df", normalized_feedforward, gate_pre, preferred_element_type=jnp.float32
    )
    grad_up = jnp.einsum(
        "td,tf->df", normalized_feedforward, up_pre, preferred_element_type=jnp.float32
    )
    normed_ffn_part = jnp.einsum(
        "tf,df->td", gate_pre, w_gate, preferred_element_type=jnp.float32
    ) + jnp.einsum("tf,df->td", up_pre, w_up, preferred_element_type=jnp.float32)
    grad_normed_ffn = lax.psum(normed_ffn_part, "tp")
    gain_ffn_part = jnp.sum(grad_normed_ffn * unit_ffn, axis=0)
    back_ffn = grad_normed_ffn * gain_ffn
    grad_middle = upstream + scale_ffn * (
        back_ffn - unit_ffn * jnp.mean(back_ffn * unit_ffn, axis=-1, keepdims=True)
    )
    middle_low = grad_middle.astype(jnp.bfloat16)
    grad_out = jnp.einsum(
        "te,td->ed", attended_flat, middle_low, preferred_element_type=jnp.float32
    )
    grad_attended = (
        jnp.einsum("td,ed->te", middle_low, w_out, preferred_element_type=jnp.float32)
        .astype(jnp.bfloat16)
        .reshape(seq_count, row_count, local_width)
    )
    key_back, value_back = (key_all, value_all)

    def attend_back(items):
        query_seq, key_seq, value_seq, grad_seq, place_q, doc_q, place_k, doc_k, live_k = items
        query_heads = query_seq.reshape(row_count, local_heads, head_size)
        key_heads = key_seq.reshape(length, local_heads, head_size)
        value_heads = value_seq.reshape(length, local_heads, head_size)
        grad_heads = grad_seq.reshape(row_count, local_heads, head_size)
        mask = visible(place_q, doc_q, place_k, doc_k, live_k)
        weights, grad_scores = score_grads(
            query_heads, key_heads, value_heads, grad_heads, mask, head_size, length
        )
        grad_value_seq = jnp.einsum(
            "hqk,qhe->khe", weights, grad_heads, preferred_element_type=jnp.float32
        )
        grad_query_seq = (
            jnp.einsum("hqk,khe->qhe", grad_scores, key_heads, preferred_element_type=jnp.float32)
            * factor
        )
        grad_key_seq = (
            jnp.einsum("hqk,qhe->khe", grad_scores, query_heads, preferred_element_type=jnp.float32)
            * factor
        )
        return (
            grad_query_seq,
            grad_key_seq.reshape(length, local_width),
            grad_value_seq.reshape(length, local_width),
        )

    grad_query_rot, grad_key_all, grad_value_all = lax.map(
        attend_back,
        (
            query_rot,
            key_back,
            value_back,
            grad_attended,
            place_own,
            doc_own,
            place_all,
            doc_all,
            live_all,
        ),
    )
    grad_key_rot, grad_value_own = (
        lax.psum_scatter(grad_key_all, "seq", scatter_dimension=1, tiled=True),
        lax.psum_scatter(grad_value_all, "seq", scatter_dimension=1, tiled=True),
    )
    query_low = (
        rotate(grad_query_rot, cosine, sine, False)
        .astype(jnp.bfloat16)
        .reshape(flat_rows, local_width)
    )
    key_low = (
        rotate(
            grad_key_rot.reshape(seq_count, row_count, local_heads, head_size), cosine, sine, False
        )
        .astype(jnp.bfloat16)
        .reshape(flat_rows, local_width)
    )
    value_grad_low = grad_value_own.astype(jnp.bfloat16).reshape(flat_rows, local_width)
    grad_query = jnp.einsum("td,te->de", normed_attn, query_low, preferred_element_type=jnp.float32)
    grad_key = jnp.einsum("td,te->de", normed_attn, key_low, preferred_element_type=jnp.float32)
    grad_value = jnp.einsum(
        "td,te->de", normed_attn, value_grad_low, preferred_element_type=jnp.float32
    )
    normed_attn_part = (
        jnp.einsum("te,de->td", query_low, w_query, preferred_element_type=jnp.float32)
        + jnp.einsum("te,de->td", key_low, w_key, preferred_element_type=jnp.float32)
        + jnp.einsum("te,de->td", value_grad_low, w_value, preferred_element_type=jnp.float32)
    )
    grad_normed_attn = lax.psum(normed_attn_part, "tp")
    gain_attn_part = jnp.sum(grad_normed_attn * unit_attn, axis=0)
    back_attn = grad_normed_attn * gain_attn
    grad_inputs = grad_middle + scale_attn * (
        back_attn - unit_attn * jnp.mean(back_attn * unit_attn, axis=-1, keepdims=True)
    )
    grad_tokens = grad_inputs.reshape(seq_count, row_count, model_width)
    (
        query_shard,
        key_shard,
        value_shard,
        out_shard,
        gain_attn_shard,
        gate_shard,
        up_shard,
        down_shard,
        gain_ffn_shard,
    ) = (
        lax.psum_scatter(grad_query, "seq", scatter_dimension=0, tiled=True),
        lax.psum_scatter(grad_key, "seq", scatter_dimension=0, tiled=True),
        lax.psum_scatter(grad_value, "seq", scatter_dimension=0, tiled=True),
        lax.psum_scatter(grad_out, "seq", scatter_dimension=1, tiled=True),
        lax.psum_scatter(gain_attn_part, "seq", scatter_dimension=0, tiled=True),
        lax.psum_scatter(grad_gate, "seq", scatter_dimension=0, tiled=True),
        lax.psum_scatter(grad_up, "seq", scatter_dimension=0, tiled=True),
        lax.psum_scatter(grad_down, "seq", scatter_dimension=1, tiled=True),
        lax.psum_scatter(gain_ffn_part, "seq", scatter_dimension=0, tiled=True),
    )
    return (
        layer_out,
        grad_tokens,
        gain_attn_shard,
        query_shard,
        key_shard,
        value_shard,
        out_shard,
        gain_ffn_shard,
        gate_shard,
        up_shard,
        down_shard,
    )


def dense(left, right):
    return jnp.dot(left, right, preferred_element_type=jnp.float32)


def dense_t(left, right):
    return lax.dot_general(
        left, right, (((1,), (1,)), ((), ())), preferred_element_type=jnp.float32
    )


def sigma_of(scores, length):
    return 1.0 / (1.0 + jnp.exp(math.log(length) - scores * (1.0 / math.sqrt(HEAD_WIDTH))))


def in_position_order(slot_places, own_ref, other_ref, first, span, scratch_refs):
    head = HEAD_WIDTH
    own_slots = own_ref.shape[0] // span
    for slot in range(2 * own_slots):
        source = own_ref if slot < own_slots else other_ref
        rows = slice((slot % own_slots) * span, (slot % own_slots + 1) * span)
        target = pl.ds(pl.multiple_of(slot_places[slot] * span, span), span)
        for index, scratch in enumerate(scratch_refs):
            columns = slice(first + index * head, first + (index + 1) * head)
            scratch[target, :] = source[rows, columns]
    for scratch in scratch_refs:
        scratch[2 * own_slots * span :, :] = jnp.zeros((span, head), scratch.dtype)


def attend_kernel(
    slot_places, key_low, own_ref, other_ref, start_ref, out_ref, key_ref, value_ref, *, span
):
    head = HEAD_WIDTH
    own_slots = own_ref.shape[0] // span
    length = 2 * own_ref.shape[0]
    in_position_order(slot_places, own_ref, other_ref, head, span, (key_ref, value_ref))
    row = lax.broadcasted_iota(jnp.int32, (span, 2 * span), 0)
    column = lax.broadcasted_iota(jnp.int32, (span, 2 * span), 1)

    def query_block(slot, carry):
        rows = pl.ds(pl.multiple_of(slot * span, span), span)
        place = slot_places[slot]
        low = key_low[slot]
        query = own_ref[rows, :head]
        first = start_ref[rows, :]

        def key_pair(step, total):
            base = pl.multiple_of((low + 2 * step) * span, span)
            keys = pl.ds(base, 2 * span)
            scores = dense_t(query, key_ref[keys, :])
            seen = (column >= first - base) & (column - row <= place * span - base)
            probs = jnp.where(seen, sigma_of(scores, length), 0.0).astype(jnp.bfloat16)
            return total + dense(probs, value_ref[keys, :])

        total = lax.fori_loop(
            0, (place - low) // 2 + 1, key_pair, jnp.zeros((span, head), jnp.float32)
        )
        out_ref[rows, :] = total.astype(jnp.bfloat16)
        return carry

    lax.fori_loop(0, own_slots, query_block, 0)


def attend_back_kernel(
    slot_places,
    key_low,
    own_ref,
    other_ref,
    start_ref,
    grad_ref,
    grad_query_ref,
    grad_own_ref,
    grad_other_ref,
    key_ref,
    value_ref,
    sum_key_ref,
    sum_value_ref,
    *,
    span,
):
    head = HEAD_WIDTH
    own_slots = own_ref.shape[0] // span
    length = 2 * own_ref.shape[0]
    factor = 1.0 / math.sqrt(head)
    in_position_order(slot_places, own_ref, other_ref, head, span, (key_ref, value_ref))
    sum_key_ref[...] = jnp.zeros_like(sum_key_ref)
    sum_value_ref[...] = jnp.zeros_like(sum_value_ref)
    row = lax.broadcasted_iota(jnp.int32, (2 * span, span), 0)
    column = lax.broadcasted_iota(jnp.int32, (2 * span, span), 1)

    def query_block(slot, carry):
        rows = pl.ds(pl.multiple_of(slot * span, span), span)
        place = slot_places[slot]
        low = key_low[slot]
        query = own_ref[rows, :head]
        grad = grad_ref[rows, :]
        first = start_ref[pl.ds(slot, 1), :]

        def key_pair(step, total):
            base = pl.multiple_of((low + 2 * step) * span, span)
            keys = pl.ds(base, 2 * span)
            key = key_ref[keys, :]
            seen = (row >= first - base) & (row - column <= place * span - base)
            sigma = jnp.where(seen, sigma_of(dense_t(key, query), length), 0.0)
            sum_value_ref[keys, :] += dense(sigma.astype(jnp.bfloat16), grad)
            grad_probs = dense_t(value_ref[keys, :], grad)
            grad_scores = (grad_probs * (sigma * (1.0 - sigma))).astype(jnp.bfloat16)
            sum_key_ref[keys, :] += dense(grad_scores, query)
            return total + lax.dot_general(
                grad_scores, key, (((0,), (0,)), ((), ())), preferred_element_type=jnp.float32
            )

        total = lax.fori_loop(
            0, (place - low) // 2 + 1, key_pair, jnp.zeros((span, head), jnp.float32)
        )
        grad_query_ref[rows, :] = total * factor
        return carry

    lax.fori_loop(0, own_slots, query_block, 0)
    for slot in range(2 * own_slots):
        target = grad_own_ref if slot < own_slots else grad_other_ref
        rows = slice((slot % own_slots) * span, (slot % own_slots + 1) * span)
        source = pl.ds(pl.multiple_of(slot_places[slot] * span, span), span)
        target[rows, :head] = (sum_key_ref[source, :] * factor).astype(target.dtype)
        target[rows, head:] = sum_value_ref[source, :].astype(target.dtype)


SHORT = pl.CostEstimate(flops=1, bytes_accessed=1, transcendentals=0)
SMALL = pl.BlockSpec(memory_space=pltpu.SMEM)
WHOLE = pl.BlockSpec(memory_space=pltpu.VMEM)


def attend_call(slot_places, key_low, own, other, start, span):
    rows = own.shape[0]
    return pl.pallas_call(
        functools.partial(attend_kernel, span=span),
        out_shape=jax.ShapeDtypeStruct((rows, HEAD_WIDTH), jnp.bfloat16),
        in_specs=[SMALL, SMALL, WHOLE, WHOLE, WHOLE],
        out_specs=WHOLE,
        scratch_shapes=[pltpu.VMEM((2 * rows + span, HEAD_WIDTH), jnp.bfloat16)] * 2,
        compiler_params=pltpu.CompilerParams(vmem_limit_bytes=8 << 20),
        cost_estimate=SHORT,
        name="attend",
    )(slot_places, key_low, own, other, start)


def attend_back_call(slot_places, key_low, own, other, start, grad, span):
    rows = own.shape[0]
    return pl.pallas_call(
        functools.partial(attend_back_kernel, span=span),
        out_shape=(
            jax.ShapeDtypeStruct((rows, HEAD_WIDTH), jnp.float32),
            jax.ShapeDtypeStruct((rows, 2 * HEAD_WIDTH), jnp.float32),
            jax.ShapeDtypeStruct((rows, 2 * HEAD_WIDTH), jnp.bfloat16),
        ),
        in_specs=[SMALL, SMALL, WHOLE, WHOLE, WHOLE, WHOLE],
        out_specs=(WHOLE, WHOLE, WHOLE),
        scratch_shapes=[pltpu.VMEM((2 * rows + span, HEAD_WIDTH), jnp.bfloat16)] * 2
        + [pltpu.VMEM((2 * rows + span, HEAD_WIDTH), jnp.float32)] * 2,
        compiler_params=pltpu.CompilerParams(vmem_limit_bytes=14 << 20),
        cost_estimate=SHORT,
        name="attend_back",
    )(slot_places, key_low, own, other, start, grad)


def call(kernel, outs, ins, scratch=(), scalars=0, grid=None, in_specs=None, out_specs=None, work=0, name=None, room=12):
    params = pltpu.CompilerParams(vmem_limit_bytes=room << 20)
    if grid is None:
        return pl.pallas_call(
            kernel,
            out_shape=tuple(outs),
            in_specs=[SMALL] * scalars + [WHOLE] * (len(ins) - scalars),
            out_specs=tuple([WHOLE] * len(outs)),
            scratch_shapes=list(scratch),
            compiler_params=params,
            cost_estimate=SHORT,
            name=name,
        )(*ins)
    return pl.pallas_call(
        kernel,
        out_shape=tuple(outs),
        grid_spec=pltpu.PrefetchScalarGridSpec(
            num_scalar_prefetch=scalars,
            grid=grid,
            in_specs=in_specs,
            out_specs=tuple(out_specs),
            scratch_shapes=list(scratch),
        ),
        compiler_params=params,
        cost_estimate=SHORT,
        name=name,
    )(*ins)


def made(shape, dtype):
    return jax.ShapeDtypeStruct(shape, dtype)


def norm_of(values):
    rows = values.astype(jnp.float32)
    scale = lax.rsqrt(jnp.mean(rows * rows, axis=-1, keepdims=True) + norm_eps)
    return scale, rows * scale


def norm_back(grad, gain, scale, unit):
    back = grad * gain
    return scale * (back - unit * jnp.mean(back * unit, axis=-1, keepdims=True))


def project_kernel(
    tokens_ref, gain_ref, live_ref, cosine_ref, sine_ref, query_ref, key_ref, value_ref, packed_ref, normed_ref
):
    head = HEAD_WIDTH
    rows = tokens_ref.shape[0]

    @pl.when(pl.program_id(0) == 0)
    def _():
        step = 128

        def piece(index, carry):
            at = pl.ds(pl.multiple_of(index * step, step), step)
            normed_ref[at, :] = (norm_of(tokens_ref[at, :])[1] * gain_ref[...]).astype(jnp.bfloat16)
            return carry

        lax.fori_loop(0, rows // step, piece, 0)

    normed = normed_ref[...]
    for index, weight in enumerate((query_ref, key_ref, value_ref)):
        both = dense(normed, weight[...])
        for which in range(2):
            values = both[:, which * head : (which + 1) * head]
            if index < 2:
                values = values * cosine_ref[...] + pltpu.roll(values, head // 2, 1) * sine_ref[...]
            else:
                values = jnp.where(live_ref[...] == 1, values, 0.0)
            packed_ref[which, :, index * head : (index + 1) * head] = values.astype(jnp.bfloat16)


def project_call(tokens, gain, live, cosine, sine, w_query, w_key, w_value):
    rows, width = tokens.shape
    heads = w_query.shape[1] // HEAD_WIDTH
    whole = lambda shape: pl.BlockSpec(shape, lambda h: (0, 0))
    weight = pl.BlockSpec((width, 2 * HEAD_WIDTH), lambda h: (0, h))
    w_query, w_key, w_value = [
        pltpu.with_memory_space_constraint(w, pltpu.HBM) for w in (w_query, w_key, w_value)
    ]
    return call(
        project_kernel,
        (made((heads, rows, 3 * HEAD_WIDTH), jnp.bfloat16), made((rows, width), jnp.bfloat16)),
        (tokens, gain, live, cosine, sine, w_query, w_key, w_value),
        grid=(heads // 2,),
        in_specs=[
            whole((rows, width)), whole((1, width)), whole((rows, 1)),
            whole((rows, HEAD_WIDTH)), whole((rows, HEAD_WIDTH)), weight, weight, weight,
        ],
        out_specs=[
            pl.BlockSpec((2, rows, 3 * HEAD_WIDTH), lambda h: (h, 0, 0)), whole((rows, width)),
        ],
        work=6 * rows * width * w_query.shape[1],
        room=32,
        name="project",
    )


def piece_at(own_tp, d, count):
    return lax.rem(own_tp + d, count)


def out_kernel(where_ref, tokens_ref, gain_ref, attended_ref, *refs):
    *weights, middle_ref, normed_ref = refs
    own_tp, core = where_ref[0], where_ref[1]
    count, part, _ = attended_ref.shape
    _, half, wide = weights[0].shape
    starts = (0, wide, middle_ref.shape[1])
    rows = tokens_ref[pl.ds(pl.multiple_of(own_tp * part, part), part), :].astype(jnp.float32)
    for piece in range(2):
        target = slice(starts[piece], starts[piece + 1])
        total = rows[:, target]
        for d in range(count):
            for which in range(2):
                side = core if which == 0 else 1 - core
                columns = pl.ds(pl.multiple_of(side * half, half), half)
                values = attended_ref[d, :, columns]
                total = total + dense(values, weights[2 * piece + which][d])
        middle_ref[:, target] = total
    normed_ref[...] = (norm_of(middle_ref[...])[1] * gain_ref[...]).astype(jnp.bfloat16)


def ffn_kernel(where_ref, *refs, chunk, sources, first):
    grad_act_ref, gate_ref, up_ref = refs[sources : sources + 3]
    act_ref, gate_pre_ref, up_pre_ref, normed_ref, *grads, total_ref = refs[
        sources + 3 + (0 if first else 4) :
    ]
    own_tp = where_ref[0]
    part = grads[0].shape[0]
    step = pl.program_id(0)

    @pl.when(step == 0)
    def _():
        if first:
            normed_ref[:part, :] = refs[0][...]
            normed_ref[part:, :] = jnp.where(from_above(own_tp, 1), refs[1][...], refs[2][...])
        elif chunk == 2:
            normed_ref[...] = jnp.where(from_above(own_tp, 2), refs[0][...], refs[1][...])
        else:
            inner = jnp.where(own_tp == 1, refs[0][...], refs[1][...])
            ends = jnp.where(own_tp == 0, refs[2][...], refs[3][...])
            normed_ref[...] = jnp.where(is_inner(own_tp), inner, ends)

    normed = normed_ref[...]
    gate = dense(normed, gate_ref[...])
    up = dense(normed, up_ref[...])
    sig = jax.nn.sigmoid(gate)
    grad_act = grad_act_ref[...]
    act_ref[...] = (gate * sig * up).astype(jnp.bfloat16)
    gate_pre = (grad_act * up * (sig * (1.0 + gate * (1.0 - sig)))).astype(jnp.bfloat16)
    up_pre = (grad_act * (gate * sig)).astype(jnp.bfloat16)
    gate_pre_ref[...] = gate_pre
    up_pre_ref[...] = up_pre
    term = dense_t(gate_pre, gate_ref[...]) + dense_t(up_pre, up_ref[...])

    @pl.when(step == 0)
    def _():
        total_ref[...] = term

    @pl.when(step > 0)
    def _():
        total_ref[...] += term

    @pl.when(step == pl.num_programs(0) - 1)
    def _():
        for index, grad_ref in enumerate(grads):
            rows = slice(index * part, (index + 1) * part)
            grad_ref[...] = total_ref[rows, :].astype(jnp.bfloat16)


def from_above(own_tp, chunk):
    return own_tp % (2 * chunk) < chunk


def is_inner(own_tp):
    return (own_tp == 1) | (own_tp == 2)


def ffn_call(where, chunk, sources, grad_act, w_gate, w_up, filled):
    part, width = sources[0].shape
    total, hidden = grad_act.shape
    wide = 512
    count = 2 if filled is None else 1
    rows = count * part
    whole = pl.BlockSpec((part, width), lambda f, w: (0, 0))
    weight = pl.BlockSpec((width, wide), lambda f, w: (0, f))
    block = pl.BlockSpec((rows, wide), lambda f, w: (chunk, f))
    low = made((total, hidden), jnp.bfloat16)
    w_gate, w_up = [pltpu.with_memory_space_constraint(w, pltpu.HBM) for w in (w_gate, w_up)]
    ins = [where, *sources, grad_act, w_gate, w_up]
    specs = [whole] * len(sources) + [block, weight, weight]
    aliases = {}
    if filled is not None:
        aliases = {len(ins) + i: i for i in range(4)}
        ins += list(filled)
        specs += [pl.BlockSpec(memory_space=pl.ANY)] * 4
    outs = pl.pallas_call(
        functools.partial(ffn_kernel, chunk=chunk, sources=len(sources), first=not aliases),
        out_shape=(low, low, low, made((total, width), jnp.bfloat16))
        + (made((part, width), jnp.bfloat16),) * count,
        grid_spec=pltpu.PrefetchScalarGridSpec(
            num_scalar_prefetch=1,
            grid=(hidden // wide,),
            in_specs=specs,
            out_specs=(
                block, block, block, pl.BlockSpec((rows, width), lambda f, w: (chunk, 0)),
            )
            + (whole,) * count,
            scratch_shapes=[pltpu.VMEM((rows, width), jnp.float32)],
        ),
        input_output_aliases=aliases,
        compiler_params=pltpu.CompilerParams(vmem_limit_bytes=28 << 20),
        cost_estimate=SHORT,
        name="ffn",
    )(*ins)
    return outs[:4], outs[4:]


def middle_kernel(where_ref, middle_ref, upstream_ref, gain_ref, *refs):
    terms, refs = refs[: refs[-2].shape[0]], refs[refs[-2].shape[0] :]
    *weights, low_ref, grad_ref, back_ref, gain_grad_ref = refs
    own_tp, core = where_ref[0], where_ref[1]
    count, part, _ = back_ref.shape
    _, half, wide = weights[0].shape
    scale, unit = norm_of(middle_ref[...])
    grad = sum([t[...].astype(jnp.float32) for t in terms[1:]], terms[0][...].astype(jnp.float32))
    gain_grad_ref[...] = jnp.sum(grad * unit, axis=0, keepdims=True)
    at = pl.ds(pl.multiple_of(own_tp * part, part), part)
    total = upstream_ref[at, :].astype(jnp.float32) + norm_back(grad, gain_ref[...], scale, unit)
    grad_ref[...] = total
    low = total.astype(jnp.bfloat16)
    low_ref[...] = low
    for d in range(count):
        for which in range(2):
            side = core if which == 0 else 1 - core
            columns = pl.ds(pl.multiple_of(side * half, half), half)
            values = dense_t(low[:, :wide], weights[which][d])
            values = values + dense_t(low[:, wide:], weights[2 + which][d])
            back_ref[d, :, columns] = values.astype(jnp.bfloat16)


def back_kernel(where_ref, back_ref, live_ref, tokens_ref, query_ref, key_ref, value_ref, low_ref, gain_ref, *refs):
    *outs, ordered_ref, unit_ref = refs
    head = HEAD_WIDTH
    heads = back_ref.shape[0]
    count = len(outs)
    part = outs[0].shape[0]
    own = heads * head
    step = pl.program_id(0)

    @pl.when(step == 0)
    def _():
        for d in range(count):
            at = pl.ds(pl.multiple_of(piece_at(where_ref[0], d, count) * part, part), part)
            rows = slice(d * part, (d + 1) * part)
            for index in range(3):
                low = jnp.concatenate(
                    [back_ref[h, at, index * head : (index + 1) * head] for h in range(heads)],
                    axis=-1,
                )
                if index == 2:
                    low = jnp.where(live_ref[at, :] == 1, low.astype(jnp.float32), 0.0)
                    low = low.astype(jnp.bfloat16)
                low_ref[at, index * own : (index + 1) * own] = low
                ordered_ref[rows, index * own : (index + 1) * own] = low
            unit = norm_of(tokens_ref[at, :])[1]
            for block in range(unit_ref.shape[0]):
                wide = unit_ref.shape[2]
                unit_ref[block, rows, :] = unit[:, block * wide : (block + 1) * wide]

    total = None
    for index, weight in enumerate((query_ref, key_ref, value_ref)):
        term = dense_t(ordered_ref[:, index * own : (index + 1) * own], weight[...])
        total = term if total is None else total + term
    gain_ref[...] = jnp.sum(total * unit_ref[step], axis=0, keepdims=True)
    for d in range(count):
        outs[d][...] = total[d * part : (d + 1) * part].astype(jnp.bfloat16)


def back_call(where, back_heads, live, tokens, weights, count):
    rows, width = tokens.shape
    own = weights[0].shape[1]
    part = rows // count
    wide = 512
    blocks = width // wide
    weights = [pltpu.with_memory_space_constraint(w, pltpu.HBM) for w in weights]
    whole = lambda x: pl.BlockSpec(x.shape, lambda f, w: (0,) * len(x.shape))
    return pl.pallas_call(
        back_kernel,
        out_shape=(made((rows, 3 * own), jnp.bfloat16), made((1, width), jnp.float32))
        + (made((part, width), jnp.bfloat16),) * count,
        grid_spec=pltpu.PrefetchScalarGridSpec(
            num_scalar_prefetch=1,
            grid=(blocks,),
            in_specs=[whole(back_heads), whole(live), whole(tokens)]
            + [pl.BlockSpec((wide, own), lambda f, w: (f, 0))] * 3,
            out_specs=(
                pl.BlockSpec((rows, 3 * own), lambda f, w: (0, 0)),
                pl.BlockSpec((1, wide), lambda f, w: (0, f)),
            )
            + (pl.BlockSpec((part, wide), lambda f, w: (0, f)),) * count,
            scratch_shapes=[
                pltpu.VMEM((rows, 3 * own), jnp.bfloat16),
                pltpu.VMEM((blocks, rows, wide), jnp.float32),
            ],
        ),
        compiler_params=pltpu.CompilerParams(vmem_limit_bytes=32 << 20),
        cost_estimate=SHORT,
        name="back",
    )(where, back_heads, live, tokens, *weights)


def tokens_kernel(
    where_ref, tokens_ref, gain_ref, grad_ref, gains_ref, middle_ref, branch_ref, own_ref, below_ref, above_ref, out_ref
):
    part = own_ref.shape[0]
    at = pl.ds(pl.multiple_of(where_ref[0] * part, part), part)
    scale, unit = norm_of(tokens_ref[at, :])
    grad = own_ref[...].astype(jnp.float32) + (
        below_ref[...].astype(jnp.float32) + above_ref[...].astype(jnp.float32)
    )
    total = grad_ref[...] + norm_back(grad, gain_ref[...], scale, unit)
    out_ref[:part, :] = total.astype(jnp.bfloat16)
    gains = gains_ref[...]
    high = gains.astype(jnp.bfloat16)
    low = (gains - high.astype(jnp.float32)).astype(jnp.bfloat16)
    wide = gains.shape[1]
    rows = out_ref.shape[0] - 2 * part
    middle = slice(part, part + rows)
    for index, values in enumerate((high, low)):
        out_ref[middle, index * wide : (index + 1) * wide] = jnp.broadcast_to(values, (rows, wide))
    out_ref[middle, 2 * wide :] = jnp.zeros((rows, out_ref.shape[1] - 2 * wide), jnp.bfloat16)
    layer = middle_ref[...] + branch_ref[...].astype(jnp.float32)
    out_ref[part + rows :, :] = layer.astype(jnp.bfloat16)


def join_kernel(where_ref, own_ref, *refs, part):
    *pieces, out_ref, gains_ref, layer_ref, terms_ref = refs
    count = len(pieces) // 2 + 1
    wide = gains_ref.shape[1]
    for d in range(count):
        place = piece_at(where_ref[0], d, count)
        values = own_ref[...] if d == 0 else pieces[d - 1][...] + pieces[2 * count - 2 - d][...]
        at = pl.ds(pl.multiple_of(place * part, part), part)
        out_ref[at, :] = values[:part].astype(jnp.float32)
        row = values[part : part + 8].astype(jnp.float32)
        terms_ref[place] = row[:, :wide] + row[:, wide : 2 * wide]
        layer_ref[at, :] = values[values.shape[0] - part :]
    total = terms_ref[0]
    for index in range(1, count):
        total = total + terms_ref[index]
    gains_ref[...] = total[:1]


def join(where, gathered, part, gains):
    own, above, below = gathered
    count = len(above) + 1
    width = own.shape[1]
    return call(
        functools.partial(join_kernel, part=part),
        (
            made((count * part, width), jnp.float32),
            made((1, gains), jnp.float32),
            made((count * part, width), jnp.bfloat16),
        ),
        (where, own, *above, *below),
        scratch=[pltpu.VMEM((count, 8, gains), jnp.float32)],
        scalars=1,
        name="join",
    )


def tie(*values):
    return lax.optimization_barrier(values)


def after(value, *others):
    return lax.optimization_barrier((value, *others))[0]


class Line:
    def __init__(self, axis, count):
        self.axis, self.count, self.at = axis, count, 0
        self.upward, self.downward = None, None

    def tie(self, *others):
        self.upward, self.downward, *others = tie(self.upward, self.downward, *others)
        return others[0] if len(others) == 1 else others

    def send(self, up, down, up_pairs, down_pairs):
        self.upward = lax.ppermute(up, self.axis, up_pairs)
        self.downward = lax.ppermute(down, self.axis, down_pairs)


class Gather(Line):
    def __init__(self, shard, axis, count):
        super().__init__(axis, count)
        self.own, self.above, self.below = shard, [], []

    def step(self):
        if self.at:
            self.keep()
        up, down = (self.upward, self.downward) if self.at else (self.own, self.own)
        self.at += 1
        at, count = self.at, self.count
        self.send(
            up,
            down,
            [(i, i + 1) for i in range(at - 1, count - 1)],
            [(i, i - 1) for i in range(1, count - at + 1)],
        )

    def keep(self):
        self.below.append(self.upward)
        self.above.append(self.downward)

    def result(self):
        while self.at < self.count - 1:
            self.step()
        self.keep()
        return self.own, self.above, self.below


def add_kernel(up_ref, got_up_ref, down_ref, got_down_ref, sum_up_ref, sum_down_ref):
    for part, got, total in (
        (up_ref, got_up_ref, sum_up_ref),
        (down_ref, got_down_ref, sum_down_ref),
    ):
        total[...] = (part[...].astype(jnp.float32) + got[...].astype(jnp.float32)).astype(
            jnp.bfloat16
        )


class Sum(Line):
    def __init__(self, parts, axis, count):
        super().__init__(axis, count)
        self.parts = parts

    def step(self):
        first = self.at == 0
        self.at += 1
        at, count = self.at, self.count
        up, down = self.parts[count - at], self.parts[at]
        if not first:
            outs = (made(up.shape, jnp.bfloat16),) * 2
            up, down = call(
                add_kernel, outs, (up, self.upward, down, self.downward), name="add"
            )
        self.send(
            up,
            down,
            [(i, i + 1) for i in range(0, at)],
            [(i, i - 1) for i in range(count - at, count)],
        )

    def result(self):
        while self.at < self.count - 1:
            self.step()
        return self.parts[0], self.upward, self.downward


def outer(left, right):
    return lax.dot_general(
        left, right, (((0,), (0,)), ((), ())), preferred_element_type=jnp.float32
    )


def chip_outer_kernel(where_ref, *refs, sides):
    del where_ref
    keep_x, sent_x, keep_y, sent_y = refs[-4:]
    step = pl.program_id(0)
    values = []
    for side in range(sides):
        left, left_other, right, right_other = refs[4 * side : 4 * side + 4]
        product = outer(left[...], right[...]) + outer(left_other[...], right_other[...])
        values.append(product.astype(jnp.bfloat16))
    values = values[0] if sides == 1 else jnp.concatenate(values, axis=-1)
    half = values.shape[1] // 2

    for target, part, places in (
        (keep_x, 0, (0, 1)),
        (sent_x, 0, (2, 3)),
        (keep_y, 1, (0, 3)),
        (sent_y, 1, (1, 2)),
    ):

        @pl.when((step == places[0]) | (step == places[1]))
        def _(target=target, part=part):
            target[0] = values[:, part * half : (part + 1) * half]


def chip_outer_call(where, pairs, seq_size, name, columns=1, column=0, into=None):
    rows, width = pairs[0][0].shape
    block = width // seq_size
    half = sum(pair[2].shape[1] for pair in pairs) // 2

    def left_index(k, w):
        chip = jnp.where(k == 0, 0, jnp.where(k == 1, 2, jnp.where(k == 2, 3, 1)))
        return 0, 2 * (w[2] ^ chip) + w[1]

    specs, ins = [], []
    for pair in pairs:
        wide = pl.BlockSpec(pair[2].shape, lambda k, w: (0, 0))
        specs += [pl.BlockSpec((rows, block), left_index)] * 2 + [wide, wide]
        ins += list(pair)
    aliases = {}
    if into is not None:
        aliases = {1 + len(ins) + i: i for i in range(4)}
        specs += [pl.BlockSpec(memory_space=pltpu.HBM)] * 4
        ins += list(into)

    def target(place):
        return pl.BlockSpec((1, block, half), lambda k, w: (place(k), 0, column))

    return pl.pallas_call(
        functools.partial(chip_outer_kernel, sides=len(pairs)),
        out_shape=(pltpu.HBM((2, block, columns * half), jnp.bfloat16),) * 4,
        grid_spec=pltpu.PrefetchScalarGridSpec(
            num_scalar_prefetch=1,
            grid=(4,),
            in_specs=specs,
            out_specs=(
                target(lambda k: jnp.minimum(k, 1)),
                target(lambda k: k // 3),
                target(lambda k: k // 3),
                target(lambda k: k // 2),
            ),
        ),
        input_output_aliases=aliases,
        compiler_params=pltpu.CompilerParams(vmem_limit_bytes=24 << 20),
        cost_estimate=SHORT,
        name=name,
    )(where, *ins)


class ChipSum:
    def __init__(self, arrays, seq_size):
        self.arrays, self.size = arrays, seq_size

    def over(self, values, side):
        return lax.ppermute(values, "seq", [(i, i ^ side) for i in range(self.size)])

    def first(self, *earlier):
        _, sent_x, _, sent_y = self.arrays
        if earlier:
            sent_x, sent_y = tie(sent_x, sent_y, *earlier)[:2]
        self.got_x, self.got_y = self.over(sent_x, 2), self.over(sent_y, 4)

    def tie(self, *others):
        self.got_x, self.got_y, *others = tie(self.got_x, self.got_y, *others)
        return others[0] if len(others) == 1 else others

    def second(self, *earlier):
        f32, bf16 = jnp.float32, jnp.bfloat16
        if earlier:
            self.got_x, self.got_y = tie(self.got_x, self.got_y, *earlier)[:2]
        keep_x, _, keep_y, _ = self.arrays
        through_x = (keep_x[1].astype(f32) + self.got_x[0].astype(f32)).astype(bf16)
        through_y = (keep_y[1].astype(f32) + self.got_y[1].astype(f32)).astype(bf16)
        self.last_x, self.last_y = self.over(through_x, 4), self.over(through_y, 2)

    def tie_last(self, *values):
        self.last_x, self.last_y, *values = tie(self.last_x, self.last_y, *values)
        return values

    def terms(self):
        keep_x, _, keep_y, _ = self.arrays
        return (keep_x, self.got_x, self.last_x), (keep_y, self.got_y, self.last_y)


def widen_kernel(*refs, terms, turned):
    f32 = jnp.float32
    values_refs, outs = refs[: len(terms)], refs[len(terms) :]
    column = 0
    for index, out_ref in enumerate(outs):
        wide = out_ref.shape[0] if turned[index] else out_ref.shape[1]
        columns = slice(column, column + wide)
        total = None
        for ref, place in zip(values_refs, terms):
            values = ref[:, columns] if place is None else ref[place, :, columns]
            total = values.astype(f32) if total is None else total + values.astype(f32)
        out_ref[...] = total.T if turned[index] else total
        column += wide


def widen(values, terms, widths, turned, name):
    rows = values[-1].shape[0]
    outs = [made((w, rows) if t else (rows, w), jnp.float32) for w, t in zip(widths, turned)]
    kernel = functools.partial(widen_kernel, terms=terms, turned=turned)
    return call(kernel, outs, tuple(values), name=name, room=24)


def widen_pair_kernel(*refs, turned):
    f32 = jnp.float32
    outs = refs[6:]
    for index, out_ref in enumerate(outs):
        half = (out_ref.shape[0] if turned[index] else out_ref.shape[1]) // 2
        columns = slice(index * half, (index + 1) * half)
        for way, (got_place, keep, got, last) in enumerate(((1, *refs[:3]), (0, *refs[3:6]))):
            total = keep[0, :, columns].astype(f32) + got[got_place, :, columns].astype(f32)
            total = total + last[:, columns].astype(f32)
            target = slice(way * half, (way + 1) * half)
            if turned[index]:
                out_ref[target, :] = total.T
            else:
                out_ref[:, target] = total


def widen_pair(values, width, turned, name):
    rows = values[2].shape[0]
    outs = [made((width, rows) if t else (rows, width), jnp.float32) for t in turned]
    kernel = functools.partial(widen_pair_kernel, turned=turned)
    return call(kernel, outs, tuple(values), name=name, room=24)


def matmul_kernel(where_ref, left_ref, right_ref, out_ref, *, turned, parts):
    product = (dense_t if turned else dense)(left_ref[...], right_ref[...]).astype(out_ref.dtype)
    if parts == 1:
        out_ref[...] = product
    part = product.shape[0] // parts
    for k in range(parts if parts > 1 else 0):
        place = where_ref[0] ^ k
        rows = pl.ds(pl.multiple_of(place * part, part), part)
        out_ref[rows, :] = product[k * part : (k + 1) * part]


def matmul_call(where, left, right, dtype, turned, name, parts=1):
    rows, depth = left.shape
    columns = right.shape[0 if turned else 1]
    wide = 512
    right = pltpu.with_memory_space_constraint(right, pltpu.HBM)
    if turned:
        right_spec = pl.BlockSpec((wide, depth), lambda f, w: (f, 0))
    else:
        right_spec = pl.BlockSpec((depth, wide), lambda f, w: (0, f))
    return pl.pallas_call(
        functools.partial(matmul_kernel, turned=turned, parts=parts),
        out_shape=made((rows, columns), dtype),
        grid_spec=pltpu.PrefetchScalarGridSpec(
            num_scalar_prefetch=1,
            grid=(columns // wide,),
            in_specs=[pl.BlockSpec((rows, depth), lambda f, w: (0, 0)), right_spec],
            out_specs=pl.BlockSpec((rows, wide), lambda f, w: (0, f)),
        ),
        compiler_params=pltpu.CompilerParams(vmem_limit_bytes=20 << 20),
        cost_estimate=SHORT,
        name=name,
    )(where, left, right)


def turn_kernel(query_ref, both_ref, other_ref, cosine_ref, sine_ref, out_ref):
    head = HEAD_WIDTH
    both = both_ref[...] + other_ref[...].astype(jnp.float32)
    cosine, sine = cosine_ref[...], sine_ref[...]
    for place, values in ((0, query_ref[...]), (1, both[:, :head])):
        values = values * cosine - pltpu.roll(values, head // 2, 1) * sine
        out_ref[:, place * head : (place + 1) * head] = values.astype(jnp.bfloat16)
    out_ref[:, 2 * head :] = both[:, head:].astype(jnp.bfloat16)


def turn_call(query, both, other, cosine, sine):
    rows, head = query.shape
    step = 256
    query, both, other, cosine, sine = [
        pltpu.with_memory_space_constraint(x, pltpu.HBM)
        for x in (query, both, other, cosine, sine)
    ]
    block = lambda x: pl.BlockSpec((step, x.shape[1]), lambda i: (i, 0))
    return pl.pallas_call(
        turn_kernel,
        out_shape=made((rows, 3 * head), jnp.bfloat16),
        grid=(rows // step,),
        in_specs=[block(x) for x in (query, both, other, cosine, sine)],
        out_specs=pl.BlockSpec((step, 3 * head), lambda i: (i, 0)),
        compiler_params=pltpu.CompilerParams(vmem_limit_bytes=12 << 20),
        cost_estimate=SHORT,
        name="turn",
    )(query, both, other, cosine, sine)


def local_heads_apart(
    tokens,
    gain_attn,
    w_query,
    w_key,
    w_value,
    w_out,
    gain_ffn,
    w_gate,
    w_up,
    w_down,
    cotangent,
    doc_ids,
    valid,
    group_order,
    *,
    seq_size,
    tp_size,
):
    _, row_count, width = tokens.shape
    length = doc_ids.shape[1]
    groups = group_order.shape[1]
    span = length // groups
    head = HEAD_WIDTH
    heads = w_query.shape[1] // head
    own_width = heads * head
    hidden = w_gate.shape[1]
    chips = seq_size // 2
    part = row_count // tp_size
    block = width // seq_size
    bf16, f32, i32 = jnp.bfloat16, jnp.float32, jnp.int32
    same_core = [[2 * p + c for p in range(chips)] for c in range(2)]
    other_core = [(i, i ^ 1) for i in range(seq_size)]
    own_seq, own_tp = lax.axis_index("seq"), lax.axis_index("tp")
    core = own_seq % 2
    where = jnp.stack([own_tp, core, own_seq // 2]).astype(i32)
    tokens = tokens.reshape(row_count, width)
    upstream = cotangent.reshape(row_count, width)
    gain_attn, gain_ffn = gain_attn.reshape(1, width), gain_ffn.reshape(1, width)

    def swap(values):
        return lax.ppermute(values, "seq", other_core)

    def to_heads(values):
        return lax.all_to_all(values, "seq", 0, 0, axis_index_groups=same_core, tiled=True)

    def part_of(values, place):
        return lax.dynamic_slice_in_dim(values, place * part, part, 0)

    def reordered(values):
        return jnp.concatenate([part_of(values, own_tp ^ k) for k in range(tp_size)], axis=0)

    def across(values, k):
        return lax.ppermute(values, "tp", [(i, i ^ k) for i in range(tp_size)])

    half = own_width // 2
    most = width * 5 // 8
    w_half = lax.dynamic_slice_in_dim(w_out, core * half, half, 0)

    def gathered(columns):
        values = lax.all_gather(columns, "tp", axis=0, tiled=True)
        return values.reshape(tp_size, half, columns.shape[1])

    w_first = gathered(w_half[:, :most])
    w_second = gathered(w_half[:, most:])

    order = group_order[0]
    per_device = row_count // span

    def blocks_of(which):
        devices = 2 * jnp.arange(chips, dtype=i32) + which
        storage = (devices[:, None] * per_device + jnp.arange(per_device)[None, :]).reshape(-1)
        return jnp.take(order, storage)

    def places_of(block_ids):
        return (block_ids[:, None] * span + jnp.arange(span, dtype=i32)[None, :]).reshape(-1)

    own_blocks, other_blocks = blocks_of(core), blocks_of(1 - core)
    slot_places = jnp.concatenate([own_blocks, other_blocks])
    docs = doc_ids[0]
    first = jnp.sum(docs[None, :] < docs.reshape(groups, span)[:, :1], axis=1, dtype=i32)
    position = jnp.arange(length, dtype=i32).reshape(groups, span)
    change = jnp.where(docs != jnp.roll(docs, 1), jnp.arange(length, dtype=i32), 0)
    change = change.reshape(groups, span)
    start = jnp.max(
        jnp.where(position[:, None, :] <= position[:, :, None], change[:, None, :], 0), axis=2
    )
    start = jnp.maximum(start, first[:, None])
    start_q = jnp.take(start, own_blocks, axis=0)
    key_low = jnp.take(first, own_blocks) // span
    row_blocks = jnp.take(order, own_seq * per_device + jnp.arange(per_device, dtype=i32))
    live = jnp.take(valid.reshape(groups, span), row_blocks, axis=0).reshape(row_count, 1)
    cosine, sine = rope_tables(places_of(row_blocks), head)
    cosine = jnp.concatenate([cosine, cosine], axis=-1)
    sine = jnp.concatenate([-sine, sine], axis=-1)
    cosine_q, sine_q = rope_tables(places_of(own_blocks), head)
    cosine_q = jnp.concatenate([cosine_q, cosine_q], axis=-1)
    sine_q = jnp.concatenate([-sine_q, sine_q], axis=-1)

    packed, normed_attn = project_call(
        tokens, gain_attn, live, cosine, sine, w_query, w_key, w_value
    )
    mine = to_heads(packed).reshape(chips * row_count, 3 * head)
    upstream_rel = reordered(upstream)
    grad_act = matmul_call(where, upstream_rel, w_down, f32, True, "grad_act")
    upstream_pair = (upstream_rel, swap(upstream_rel))
    normed_attn_pair = (normed_attn, swap(normed_attn))
    mine, grad_act, cosine_q, sine_q = tie(mine, grad_act, cosine_q, sine_q)
    other = swap(mine)

    attended = attend_call(slot_places, key_low, mine, other, start_q.reshape(-1, 1), span)
    attended, w_first = tie(attended, w_first)
    attended = to_heads(attended.reshape(chips, row_count, head))
    attended = attended.reshape(heads, row_count, head)
    attended = jnp.concatenate([attended[h] for h in range(heads)], axis=-1)
    attended_part = lax.all_to_all(
        attended.reshape(tp_size, part, own_width), "tp", 0, 0, tiled=True
    )
    w_second = after(w_second, attended_part)
    out_weights = (w_first, swap(w_first), w_second, swap(w_second))
    middle, normed_part = call(
        out_kernel,
        (made((part, width), f32), made((part, width), bf16)),
        (where, tokens, gain_ffn, attended_part, *out_weights),
        scalars=1,
        work=2 * part * width * width,
        name="out",
    )

    line = Gather(normed_part, "tp", tp_size)
    line.step()
    line.step()
    above_1, below_1 = line.above[0], line.below[0]
    filled, (own_grad, grad_1) = ffn_call(
        where, 0, [normed_part, above_1, below_1], grad_act, w_gate, w_up, None
    )
    filled = line.tie(*filled)
    line.step()
    above_2, below_2 = line.above[1], line.below[1]
    filled, (grad_2,) = ffn_call(where, 2, [above_2, below_2], grad_act, w_gate, w_up, filled)
    *filled, grad_1, grad_2 = line.tie(*filled, grad_1, grad_2)
    grad_1, grad_2 = across(grad_1, 1), across(grad_2, 2)
    _, (_, _, above_3), (_, _, below_3) = line.result()
    filled, (grad_3,) = ffn_call(
        where, 3, [above_1, below_1, above_3, below_3], grad_act, w_gate, w_up, filled
    )
    grad_3 = across(grad_3, 3)
    activated, gate_pre, up_pre, normed_ffn = filled
    up_pre, grad_1, grad_2 = tie(up_pre, grad_1, grad_2)

    normed_pair = (normed_ffn, swap(normed_ffn))
    outer_ffn = functools.partial(
        chip_outer_call, where, seq_size=seq_size, name="ffn_outer"
    )
    gate_quad = (*normed_pair, gate_pre, swap(gate_pre))
    up_quad = (*normed_pair, up_pre, swap(up_pre))
    down_quad = (*upstream_pair, activated, swap(activated))
    gate_sum = ChipSum(outer_ffn([gate_quad]), seq_size)
    gate_sum.first()
    up_sum = ChipSum(outer_ffn([up_quad]), seq_size)
    up_sum.first()
    down_sum = ChipSum(outer_ffn([down_quad]), seq_size)
    grad_3, *down_sum.arrays = tie(grad_3, *down_sum.arrays)
    middle_low, grad_middle, grad_attended, gain_ffn_part = call(
        middle_kernel,
        (
            made((part, width), bf16),
            made((part, width), f32),
            made((tp_size, part, own_width), bf16),
            made((1, width), f32),
        ),
        (where, middle, upstream, gain_ffn, own_grad, grad_1, grad_2, grad_3, *out_weights),
        scalars=1,
        work=2 * part * width * width,
        name="middle",
    )
    grad_attended = lax.all_to_all(grad_attended, "tp", 0, 0, tiled=True)
    branch = matmul_call(where, after(activated, middle_low), w_down, bf16, False, "branch", tp_size)
    grad_attended, branch = up_sum.tie(*gate_sum.tie(grad_attended, branch))
    branch = after(branch, grad_attended)
    branch_part = lax.psum_scatter(branch, "tp", scatter_dimension=0, tiled=True)
    grad_attended = grad_attended.reshape(row_count, own_width)
    grad_attended = jnp.stack(
        [grad_attended[:, h * head : (h + 1) * head] for h in range(heads)]
    )
    grad_heads = to_heads(grad_attended).reshape(chips * row_count, head)
    grad_query, both, both_other = attend_back_call(
        slot_places, key_low, mine, other, start_q, grad_heads, span
    )
    other_term = swap(both_other)
    middle_all = lax.all_gather(after(middle_low, other_term), "tp", axis=0, tiled=True)
    packed_back = turn_call(grad_query, both, other_term, cosine_q, sine_q)
    packed_back = packed_back.reshape(chips, row_count, 3 * head)
    back_heads = to_heads(packed_back)
    attended_pair = (attended, swap(attended))
    back_heads = after(back_heads, attended_pair[1], branch_part)
    low, gain_attn_part, *parts = back_call(
        where, back_heads, live, tokens, (w_query, w_key, w_value), tp_size
    )
    sums = Sum(parts, "tp", tp_size)
    sums.step()
    gains = jnp.concatenate([gain_attn_part, gain_ffn_part], axis=0)
    gains = gains.reshape(2, seq_size, block).transpose(1, 0, 2)
    gains = jnp.sum(lax.all_to_all(gains, "seq", 0, 0, tiled=True), axis=0).reshape(1, 2 * block)
    down_sum.first(low)
    down_sum.got_x, down_sum.got_y, low = sums.tie(down_sum.got_x, down_sum.got_y, low)
    sums.step()
    gains, low, middle_all = sums.tie(gains, low, middle_all)
    up_sum.second(low)
    sums.step()
    middle_pair = (middle_all, swap(middle_all))
    attn_grads = chip_outer_call(
        where,
        [(*middle_pair, *attended_pair), (*normed_attn_pair, low, swap(low))],
        seq_size,
        "attn_outer",
    )
    up_sum.last_x, up_sum.last_y, *attn_grads = sums.tie(
        up_sum.last_x, up_sum.last_y, *attn_grads
    )
    attn_sum = ChipSum(attn_grads, seq_size)
    tokens_part = call(
        tokens_kernel,
        (made((2 * part + 16, width), bf16),),
        (where, tokens, gain_attn, grad_middle, gains, middle, branch_part, *sums.result()),
        scalars=1,
        name="tokens",
    )[0]
    token_line = Gather(tokens_part, "tp", tp_size)
    token_line.step()
    attn_sum.first(tokens_part)
    attn_sum.got_x, attn_sum.got_y, low = token_line.tie(attn_sum.got_x, attn_sum.got_y, low)
    token_line.step()
    down_sum.second(low)
    gate_sum.second(low)
    (*last, low) = token_line.tie(
        down_sum.last_x, down_sum.last_y, gate_sum.last_x, gate_sum.last_y, low
    )
    down_sum.last_x, down_sum.last_y, gate_sum.last_x, gate_sum.last_y = last
    token_line.step()
    attn_sum.second(low)
    up_sum.last_x = after(up_sum.last_x, low)
    up_x, up_y = up_sum.terms()
    (grad_up,) = widen_pair([*up_x, *up_y], hidden, (False,), "widen_up")
    down_x, down_y = down_sum.terms()
    (grad_down,) = widen_pair([*down_x, *down_y], hidden, (True,), "widen_down")
    gate_x, gate_y = gate_sum.terms()
    (grad_gate,) = widen_pair([*gate_x, *gate_y], hidden, (False,), "widen_gate")
    terms_x, terms_y = attn_sum.terms()
    grad_out, grad_query = widen(
        terms_x, [0, 1, None], [own_width] * 2, (True, False), "widen_attn"
    )
    grad_key, grad_value = widen(
        terms_y, [0, 0, None], [own_width] * 2, (False, False), "widen_attn"
    )
    grad_out, grad_key, grad_gate, grad_up = token_line.tie(grad_out, grad_key, grad_gate, grad_up)
    grad_tokens, gains, layer_out = join(where, token_line.result(), part, 2 * block)
    gains = gains.reshape(2, block)

    return (
        layer_out.reshape(1, row_count, width),
        grad_tokens.reshape(1, row_count, width),
        gains[0],
        grad_query,
        grad_key,
        grad_value,
        grad_out,
        gains[1],
        grad_gate,
        grad_up,
        grad_down,
    )


def solution(mesh):
    placed = (
        P(None, "seq", None),
        P(),
        P(None, "tp"),
        P(None, "tp"),
        P(None, "tp"),
        P("tp", None),
        P(),
        P(None, "tp"),
        P(None, "tp"),
        P("tp", None),
        P(None, "seq", None),
        P(),
        P(),
        P(),
    )
    seq_size, tp_size = mesh.shape["seq"], mesh.shape["tp"]

    def local(*args):
        heads = args[2].shape[1] // HEAD_WIDTH
        if seq_size == 8 and tp_size == 4 and heads == 4 and args[0].shape[0] == 1:
            return local_heads_apart(*args, seq_size=seq_size, tp_size=tp_size)
        return local_general(*args)

    return jax.shard_map(
        local,
        mesh=mesh,
        in_specs=placed,
        out_specs=(
            P(None, "seq", None),
            P(None, "seq", None),
            P("seq"),
            P("seq", "tp"),
            P("seq", "tp"),
            P("seq", "tp"),
            P("tp", "seq"),
            P("seq"),
            P("seq", "tp"),
            P("seq", "tp"),
            P("tp", "seq"),
        ),
        check_vma=False,
    )
```

```python
import functools
import math

import jax
import jax.numpy as jnp
from jax import lax
from jax.experimental import pallas as pl
from jax.experimental.pallas import tpu as pltpu
from jax.sharding import PartitionSpec as P

HEAD_WIDTH = 128


norm_eps = 1e-05
rope_base = 10000.0


def rope_tables(places, head_size):
    half_size = head_size // 2
    freqs = rope_base ** (-jnp.arange(half_size, dtype=jnp.float32) * 2.0 / head_size)
    angles = places.astype(jnp.float32)[..., None] * freqs
    return (jnp.cos(angles), jnp.sin(angles))


def rotate(values, cosine, sine, forward):
    half_size = values.shape[-1] // 2
    first = values[..., :half_size]
    second = values[..., half_size:]
    cos_b = cosine[..., None, :]
    sin_b = sine[..., None, :]
    if forward:
        return jnp.concatenate(
            [first * cos_b - second * sin_b, second * cos_b + first * sin_b], axis=-1
        )
    return jnp.concatenate(
        [first * cos_b + second * sin_b, second * cos_b - first * sin_b], axis=-1
    )


def visible(place_q, doc_q, place_k, doc_k, live_k):
    allowed = (
        (place_k[None, :] <= place_q[:, None])
        & (doc_k[None, :] == doc_q[:, None])
        & (live_k[None, :] == 1)
    )
    return allowed.astype(jnp.float32)


def score_block(query_heads, key_heads, head_size, length):
    scores = jnp.einsum("qhe,khe->hqk", query_heads, key_heads, preferred_element_type=jnp.float32)
    return scores * (1.0 / math.sqrt(head_size)) - math.log(length)


def score_grads(query_heads, key_heads, value_heads, grad_heads, mask, head_size, length):
    sigma = jax.nn.sigmoid(score_block(query_heads, key_heads, head_size, length))
    weights = (sigma * mask).astype(jnp.bfloat16)
    grad_weights = jnp.einsum(
        "qhe,khe->hqk", grad_heads, value_heads, preferred_element_type=jnp.float32
    )
    grad_scores = (grad_weights * (sigma * (1.0 - sigma)) * mask).astype(jnp.bfloat16)
    return (weights, grad_scores)


def local_general(
    tokens,
    gain_attn,
    w_query,
    w_key,
    w_value,
    w_out,
    gain_ffn,
    w_gate,
    w_up,
    w_down,
    cotangent,
    doc_ids,
    valid,
    group_order,
):
    seq_count, row_count, model_width = tokens.shape
    length = doc_ids.shape[1]
    span = length // group_order.shape[1]
    head_size = HEAD_WIDTH
    local_width = w_query.shape[1]
    local_heads = local_width // head_size
    flat_rows = seq_count * row_count
    factor = 1.0 / math.sqrt(head_size)
    own_rows = lax.axis_index("seq") * row_count + jnp.arange(row_count, dtype=jnp.int32)
    all_rows = jnp.arange(length, dtype=jnp.int32)
    place_all = jnp.take(group_order, all_rows // span, axis=1) * span + (all_rows % span)[None, :]
    place_own = jnp.take(group_order, own_rows // span, axis=1) * span + (own_rows % span)[None, :]
    doc_all = jnp.take_along_axis(doc_ids, place_all, axis=1)
    live_all = jnp.take_along_axis(valid, place_all, axis=1)
    doc_own = jnp.take_along_axis(doc_ids, place_own, axis=1)
    cosine, sine = rope_tables(place_own, head_size)
    input_rows = tokens.astype(jnp.float32).reshape(flat_rows, model_width)
    scale_attn = lax.rsqrt(jnp.mean(input_rows * input_rows, axis=-1, keepdims=True) + norm_eps)
    unit_attn = input_rows * scale_attn
    normed_attn = (unit_attn * gain_attn).astype(jnp.bfloat16)

    def project(weight_matrix):
        return jnp.dot(normed_attn, weight_matrix, preferred_element_type=jnp.float32).reshape(
            seq_count, row_count, local_heads, head_size
        )

    query_rot = (
        rotate(project(w_query), cosine, sine, True)
        .astype(jnp.bfloat16)
        .reshape(seq_count, row_count, local_width)
    )
    key_rot = (
        rotate(project(w_key), cosine, sine, True)
        .astype(jnp.bfloat16)
        .reshape(seq_count, row_count, local_width)
    )
    value_low = (
        jnp.dot(normed_attn, w_value, preferred_element_type=jnp.float32)
        .astype(jnp.bfloat16)
        .reshape(seq_count, row_count, local_width)
    )
    key_all, value_all = (
        lax.all_gather(key_rot, "seq", axis=1, tiled=True),
        lax.all_gather(value_low, "seq", axis=1, tiled=True),
    )

    def attend(items):
        query_seq, key_seq, value_seq, place_q, doc_q, place_k, doc_k, live_k = items
        query_heads = query_seq.reshape(row_count, local_heads, head_size)
        key_heads = key_seq.reshape(length, local_heads, head_size)
        value_heads = value_seq.reshape(length, local_heads, head_size)
        mask = visible(place_q, doc_q, place_k, doc_k, live_k)
        weights = (
            jax.nn.sigmoid(score_block(query_heads, key_heads, head_size, length)) * mask
        ).astype(jnp.bfloat16)
        mixed = jnp.einsum("hqk,khe->qhe", weights, value_heads, preferred_element_type=jnp.float32)
        return mixed.astype(jnp.bfloat16).reshape(row_count, local_width)

    attention_output = lax.map(
        attend, (query_rot, key_all, value_all, place_own, doc_own, place_all, doc_all, live_all)
    )
    attended_flat = attention_output.reshape(flat_rows, local_width)
    branch_attn = lax.psum(jnp.dot(attended_flat, w_out, preferred_element_type=jnp.float32), "tp")
    hidden_rows = input_rows + branch_attn
    scale_ffn = lax.rsqrt(jnp.mean(hidden_rows * hidden_rows, axis=-1, keepdims=True) + norm_eps)
    unit_ffn = hidden_rows * scale_ffn
    normalized_feedforward = (unit_ffn * gain_ffn).astype(jnp.bfloat16)
    gate_rows = jnp.dot(normalized_feedforward, w_gate, preferred_element_type=jnp.float32)
    up_projected = jnp.dot(normalized_feedforward, w_up, preferred_element_type=jnp.float32)
    gate_sig = jax.nn.sigmoid(gate_rows)
    activation_rows = (gate_rows * gate_sig * up_projected).astype(jnp.bfloat16)
    branch_ffn = lax.psum(
        jnp.dot(activation_rows, w_down, preferred_element_type=jnp.float32).astype(jnp.bfloat16),
        "tp",
    ).astype(jnp.float32)
    layer_out = (
        (hidden_rows + branch_ffn).astype(jnp.bfloat16).reshape(seq_count, row_count, model_width)
    )
    upstream = cotangent.astype(jnp.float32).reshape(flat_rows, model_width)
    upstream_low = upstream.astype(jnp.bfloat16)
    grad_down = jnp.einsum(
        "tf,td->fd", activation_rows, upstream_low, preferred_element_type=jnp.float32
    )
    grad_act = jnp.einsum("td,fd->tf", upstream_low, w_down, preferred_element_type=jnp.float32)
    gate_pre = (grad_act * up_projected * (gate_sig * (1.0 + gate_rows * (1.0 - gate_sig)))).astype(
        jnp.bfloat16
    )
    up_pre = (grad_act * (gate_rows * gate_sig)).astype(jnp.bfloat16)
    grad_gate = jnp.einsum(
        "td,tf->df", normalized_feedforward, gate_pre, preferred_element_type=jnp.float32
    )
    grad_up = jnp.einsum(
        "td,tf->df", normalized_feedforward, up_pre, preferred_element_type=jnp.float32
    )
    normed_ffn_part = jnp.einsum(
        "tf,df->td", gate_pre, w_gate, preferred_element_type=jnp.float32
    ) + jnp.einsum("tf,df->td", up_pre, w_up, preferred_element_type=jnp.float32)
    grad_normed_ffn = lax.psum(normed_ffn_part, "tp")
    gain_ffn_part = jnp.sum(grad_normed_ffn * unit_ffn, axis=0)
    back_ffn = grad_normed_ffn * gain_ffn
    grad_middle = upstream + scale_ffn * (
        back_ffn - unit_ffn * jnp.mean(back_ffn * unit_ffn, axis=-1, keepdims=True)
    )
    middle_low = grad_middle.astype(jnp.bfloat16)
    grad_out = jnp.einsum(
        "te,td->ed", attended_flat, middle_low, preferred_element_type=jnp.float32
    )
    grad_attended = (
        jnp.einsum("td,ed->te", middle_low, w_out, preferred_element_type=jnp.float32)
        .astype(jnp.bfloat16)
        .reshape(seq_count, row_count, local_width)
    )
    key_back, value_back = (key_all, value_all)

    def attend_back(items):
        query_seq, key_seq, value_seq, grad_seq, place_q, doc_q, place_k, doc_k, live_k = items
        query_heads = query_seq.reshape(row_count, local_heads, head_size)
        key_heads = key_seq.reshape(length, local_heads, head_size)
        value_heads = value_seq.reshape(length, local_heads, head_size)
        grad_heads = grad_seq.reshape(row_count, local_heads, head_size)
        mask = visible(place_q, doc_q, place_k, doc_k, live_k)
        weights, grad_scores = score_grads(
            query_heads, key_heads, value_heads, grad_heads, mask, head_size, length
        )
        grad_value_seq = jnp.einsum(
            "hqk,qhe->khe", weights, grad_heads, preferred_element_type=jnp.float32
        )
        grad_query_seq = (
            jnp.einsum("hqk,khe->qhe", grad_scores, key_heads, preferred_element_type=jnp.float32)
            * factor
        )
        grad_key_seq = (
            jnp.einsum("hqk,qhe->khe", grad_scores, query_heads, preferred_element_type=jnp.float32)
            * factor
        )
        return (
            grad_query_seq,
            grad_key_seq.reshape(length, local_width),
            grad_value_seq.reshape(length, local_width),
        )

    grad_query_rot, grad_key_all, grad_value_all = lax.map(
        attend_back,
        (
            query_rot,
            key_back,
            value_back,
            grad_attended,
            place_own,
            doc_own,
            place_all,
            doc_all,
            live_all,
        ),
    )
    grad_key_rot, grad_value_own = (
        lax.psum_scatter(grad_key_all, "seq", scatter_dimension=1, tiled=True),
        lax.psum_scatter(grad_value_all, "seq", scatter_dimension=1, tiled=True),
    )
    query_low = (
        rotate(grad_query_rot, cosine, sine, False)
        .astype(jnp.bfloat16)
        .reshape(flat_rows, local_width)
    )
    key_low = (
        rotate(
            grad_key_rot.reshape(seq_count, row_count, local_heads, head_size), cosine, sine, False
        )
        .astype(jnp.bfloat16)
        .reshape(flat_rows, local_width)
    )
    value_grad_low = grad_value_own.astype(jnp.bfloat16).reshape(flat_rows, local_width)
    grad_query = jnp.einsum("td,te->de", normed_attn, query_low, preferred_element_type=jnp.float32)
    grad_key = jnp.einsum("td,te->de", normed_attn, key_low, preferred_element_type=jnp.float32)
    grad_value = jnp.einsum(
        "td,te->de", normed_attn, value_grad_low, preferred_element_type=jnp.float32
    )
    normed_attn_part = (
        jnp.einsum("te,de->td", query_low, w_query, preferred_element_type=jnp.float32)
        + jnp.einsum("te,de->td", key_low, w_key, preferred_element_type=jnp.float32)
        + jnp.einsum("te,de->td", value_grad_low, w_value, preferred_element_type=jnp.float32)
    )
    grad_normed_attn = lax.psum(normed_attn_part, "tp")
    gain_attn_part = jnp.sum(grad_normed_attn * unit_attn, axis=0)
    back_attn = grad_normed_attn * gain_attn
    grad_inputs = grad_middle + scale_attn * (
        back_attn - unit_attn * jnp.mean(back_attn * unit_attn, axis=-1, keepdims=True)
    )
    grad_tokens = grad_inputs.reshape(seq_count, row_count, model_width)
    (
        query_shard,
        key_shard,
        value_shard,
        out_shard,
        gain_attn_shard,
        gate_shard,
        up_shard,
        down_shard,
        gain_ffn_shard,
    ) = (
        lax.psum_scatter(grad_query, "seq", scatter_dimension=0, tiled=True),
        lax.psum_scatter(grad_key, "seq", scatter_dimension=0, tiled=True),
        lax.psum_scatter(grad_value, "seq", scatter_dimension=0, tiled=True),
        lax.psum_scatter(grad_out, "seq", scatter_dimension=1, tiled=True),
        lax.psum_scatter(gain_attn_part, "seq", scatter_dimension=0, tiled=True),
        lax.psum_scatter(grad_gate, "seq", scatter_dimension=0, tiled=True),
        lax.psum_scatter(grad_up, "seq", scatter_dimension=0, tiled=True),
        lax.psum_scatter(grad_down, "seq", scatter_dimension=1, tiled=True),
        lax.psum_scatter(gain_ffn_part, "seq", scatter_dimension=0, tiled=True),
    )
    return (
        layer_out,
        grad_tokens,
        gain_attn_shard,
        query_shard,
        key_shard,
        value_shard,
        out_shard,
        gain_ffn_shard,
        gate_shard,
        up_shard,
        down_shard,
    )


def dense(left, right):
    return jnp.dot(left, right, preferred_element_type=jnp.float32)


def dense_t(left, right):
    return lax.dot_general(
        left, right, (((1,), (1,)), ((), ())), preferred_element_type=jnp.float32
    )


def sigma_of(scores, length):
    return 1.0 / (1.0 + jnp.exp(math.log(length) - scores * (1.0 / math.sqrt(HEAD_WIDTH))))


def in_position_order(slot_places, own_ref, other_ref, first, span, scratch_refs):
    head = HEAD_WIDTH
    own_slots = own_ref.shape[0] // span
    for slot in range(2 * own_slots):
        source = own_ref if slot < own_slots else other_ref
        rows = slice((slot % own_slots) * span, (slot % own_slots + 1) * span)
        target = pl.ds(pl.multiple_of(slot_places[slot] * span, span), span)
        for index, scratch in enumerate(scratch_refs):
            columns = slice(first + index * head, first + (index + 1) * head)
            scratch[target, :] = source[rows, columns]
    for scratch in scratch_refs:
        scratch[2 * own_slots * span :, :] = jnp.zeros((span, head), scratch.dtype)


def attend_kernel(
    slot_places, key_low, own_ref, other_ref, start_ref, out_ref, key_ref, value_ref, *, span
):
    head = HEAD_WIDTH
    own_slots = own_ref.shape[0] // span
    length = 2 * own_ref.shape[0]
    in_position_order(slot_places, own_ref, other_ref, head, span, (key_ref, value_ref))
    row = lax.broadcasted_iota(jnp.int32, (span, 2 * span), 0)
    column = lax.broadcasted_iota(jnp.int32, (span, 2 * span), 1)

    def query_block(slot, carry):
        rows = pl.ds(pl.multiple_of(slot * span, span), span)
        place = slot_places[slot]
        low = key_low[slot]
        query = own_ref[rows, :head]
        first = start_ref[rows, :]

        def key_pair(step, total):
            base = pl.multiple_of((low + 2 * step) * span, span)
            keys = pl.ds(base, 2 * span)
            scores = dense_t(query, key_ref[keys, :])
            seen = (column >= first - base) & (column - row <= place * span - base)
            probs = jnp.where(seen, sigma_of(scores, length), 0.0).astype(jnp.bfloat16)
            return total + dense(probs, value_ref[keys, :])

        total = lax.fori_loop(
            0, (place - low) // 2 + 1, key_pair, jnp.zeros((span, head), jnp.float32)
        )
        out_ref[rows, :] = total.astype(jnp.bfloat16)
        return carry

    lax.fori_loop(0, own_slots, query_block, 0)


def attend_back_kernel(
    slot_places,
    key_low,
    own_ref,
    other_ref,
    start_ref,
    grad_ref,
    grad_query_ref,
    grad_own_ref,
    grad_other_ref,
    key_ref,
    value_ref,
    sum_key_ref,
    sum_value_ref,
    *,
    span,
):
    head = HEAD_WIDTH
    own_slots = own_ref.shape[0] // span
    length = 2 * own_ref.shape[0]
    factor = 1.0 / math.sqrt(head)
    in_position_order(slot_places, own_ref, other_ref, head, span, (key_ref, value_ref))
    sum_key_ref[...] = jnp.zeros_like(sum_key_ref)
    sum_value_ref[...] = jnp.zeros_like(sum_value_ref)
    row = lax.broadcasted_iota(jnp.int32, (2 * span, span), 0)
    column = lax.broadcasted_iota(jnp.int32, (2 * span, span), 1)

    def query_block(slot, carry):
        rows = pl.ds(pl.multiple_of(slot * span, span), span)
        place = slot_places[slot]
        low = key_low[slot]
        query = own_ref[rows, :head]
        grad = grad_ref[rows, :]
        first = start_ref[pl.ds(slot, 1), :]

        def key_pair(step, total):
            base = pl.multiple_of((low + 2 * step) * span, span)
            keys = pl.ds(base, 2 * span)
            key = key_ref[keys, :]
            seen = (row >= first - base) & (row - column <= place * span - base)
            sigma = jnp.where(seen, sigma_of(dense_t(key, query), length), 0.0)
            sum_value_ref[keys, :] += dense(sigma.astype(jnp.bfloat16), grad)
            grad_probs = dense_t(value_ref[keys, :], grad)
            grad_scores = (grad_probs * (sigma * (1.0 - sigma))).astype(jnp.bfloat16)
            sum_key_ref[keys, :] += dense(grad_scores, query)
            return total + lax.dot_general(
                grad_scores, key, (((0,), (0,)), ((), ())), preferred_element_type=jnp.float32
            )

        total = lax.fori_loop(
            0, (place - low) // 2 + 1, key_pair, jnp.zeros((span, head), jnp.float32)
        )
        grad_query_ref[rows, :] = total * factor
        return carry

    lax.fori_loop(0, own_slots, query_block, 0)
    for slot in range(2 * own_slots):
        target = grad_own_ref if slot < own_slots else grad_other_ref
        rows = slice((slot % own_slots) * span, (slot % own_slots + 1) * span)
        source = pl.ds(pl.multiple_of(slot_places[slot] * span, span), span)
        target[rows, :head] = (sum_key_ref[source, :] * factor).astype(target.dtype)
        target[rows, head:] = sum_value_ref[source, :].astype(target.dtype)


SHORT = pl.CostEstimate(flops=1, bytes_accessed=1, transcendentals=0)
SMALL = pl.BlockSpec(memory_space=pltpu.SMEM)
WHOLE = pl.BlockSpec(memory_space=pltpu.VMEM)


def attend_call(slot_places, key_low, own, other, start, span):
    rows = own.shape[0]
    return pl.pallas_call(
        functools.partial(attend_kernel, span=span),
        out_shape=jax.ShapeDtypeStruct((rows, HEAD_WIDTH), jnp.bfloat16),
        in_specs=[SMALL, SMALL, WHOLE, WHOLE, WHOLE],
        out_specs=WHOLE,
        scratch_shapes=[pltpu.VMEM((2 * rows + span, HEAD_WIDTH), jnp.bfloat16)] * 2,
        compiler_params=pltpu.CompilerParams(vmem_limit_bytes=8 << 20),
        cost_estimate=SHORT,
        name="attend",
    )(slot_places, key_low, own, other, start)


def attend_back_call(slot_places, key_low, own, other, start, grad, span):
    rows = own.shape[0]
    return pl.pallas_call(
        functools.partial(attend_back_kernel, span=span),
        out_shape=(
            jax.ShapeDtypeStruct((rows, HEAD_WIDTH), jnp.float32),
            jax.ShapeDtypeStruct((rows, 2 * HEAD_WIDTH), jnp.float32),
            jax.ShapeDtypeStruct((rows, 2 * HEAD_WIDTH), jnp.bfloat16),
        ),
        in_specs=[SMALL, SMALL, WHOLE, WHOLE, WHOLE, WHOLE],
        out_specs=(WHOLE, WHOLE, WHOLE),
        scratch_shapes=[pltpu.VMEM((2 * rows + span, HEAD_WIDTH), jnp.bfloat16)] * 2
        + [pltpu.VMEM((2 * rows + span, HEAD_WIDTH), jnp.float32)] * 2,
        compiler_params=pltpu.CompilerParams(vmem_limit_bytes=14 << 20),
        cost_estimate=SHORT,
        name="attend_back",
    )(slot_places, key_low, own, other, start, grad)


def call(kernel, outs, ins, scratch=(), scalars=0, grid=None, in_specs=None, out_specs=None, work=0, name=None, room=12):
    params = pltpu.CompilerParams(vmem_limit_bytes=room << 20)
    if grid is None:
        return pl.pallas_call(
            kernel,
            out_shape=tuple(outs),
            in_specs=[SMALL] * scalars + [WHOLE] * (len(ins) - scalars),
            out_specs=tuple([WHOLE] * len(outs)),
            scratch_shapes=list(scratch),
            compiler_params=params,
            cost_estimate=SHORT,
            name=name,
        )(*ins)
    return pl.pallas_call(
        kernel,
        out_shape=tuple(outs),
        grid_spec=pltpu.PrefetchScalarGridSpec(
            num_scalar_prefetch=scalars,
            grid=grid,
            in_specs=in_specs,
            out_specs=tuple(out_specs),
            scratch_shapes=list(scratch),
        ),
        compiler_params=params,
        cost_estimate=SHORT,
        name=name,
    )(*ins)


def made(shape, dtype):
    return jax.ShapeDtypeStruct(shape, dtype)


def norm_of(values):
    rows = values.astype(jnp.float32)
    scale = lax.rsqrt(jnp.mean(rows * rows, axis=-1, keepdims=True) + norm_eps)
    return scale, rows * scale


def norm_back(grad, gain, scale, unit):
    back = grad * gain
    return scale * (back - unit * jnp.mean(back * unit, axis=-1, keepdims=True))


def project_kernel(
    tokens_ref, gain_ref, live_ref, cosine_ref, sine_ref, query_ref, key_ref, value_ref, packed_ref, normed_ref
):
    head = HEAD_WIDTH
    rows = tokens_ref.shape[0]

    @pl.when(pl.program_id(0) == 0)
    def _():
        step = 128

        def piece(index, carry):
            at = pl.ds(pl.multiple_of(index * step, step), step)
            normed_ref[at, :] = (norm_of(tokens_ref[at, :])[1] * gain_ref[...]).astype(jnp.bfloat16)
            return carry

        lax.fori_loop(0, rows // step, piece, 0)

    normed = normed_ref[...]
    for index, weight in enumerate((query_ref, key_ref, value_ref)):
        both = dense(normed, weight[...])
        for which in range(2):
            values = both[:, which * head : (which + 1) * head]
            if index < 2:
                values = values * cosine_ref[...] + pltpu.roll(values, head // 2, 1) * sine_ref[...]
            else:
                values = jnp.where(live_ref[...] == 1, values, 0.0)
            packed_ref[which, :, index * head : (index + 1) * head] = values.astype(jnp.bfloat16)


def project_call(tokens, gain, live, cosine, sine, w_query, w_key, w_value):
    rows, width = tokens.shape
    heads = w_query.shape[1] // HEAD_WIDTH
    whole = lambda shape: pl.BlockSpec(shape, lambda h: (0, 0))
    weight = pl.BlockSpec((width, 2 * HEAD_WIDTH), lambda h: (0, h))
    w_query, w_key, w_value = [
        pltpu.with_memory_space_constraint(w, pltpu.HBM) for w in (w_query, w_key, w_value)
    ]
    return call(
        project_kernel,
        (made((heads, rows, 3 * HEAD_WIDTH), jnp.bfloat16), made((rows, width), jnp.bfloat16)),
        (tokens, gain, live, cosine, sine, w_query, w_key, w_value),
        grid=(heads // 2,),
        in_specs=[
            whole((rows, width)), whole((1, width)), whole((rows, 1)),
            whole((rows, HEAD_WIDTH)), whole((rows, HEAD_WIDTH)), weight, weight, weight,
        ],
        out_specs=[
            pl.BlockSpec((2, rows, 3 * HEAD_WIDTH), lambda h: (h, 0, 0)), whole((rows, width)),
        ],
        work=6 * rows * width * w_query.shape[1],
        room=32,
        name="project",
    )


def piece_at(own_tp, d, count):
    return lax.rem(own_tp + d, count)


def out_kernel(where_ref, tokens_ref, gain_ref, attended_ref, *refs):
    *weights, middle_ref, normed_ref = refs
    own_tp, core = where_ref[0], where_ref[1]
    part, width = middle_ref.shape
    _, half, wide = weights[0].shape
    starts = (0, wide, width)
    step = pl.program_id(0)

    @pl.when(step == 0)
    def _():
        rows = pl.ds(pl.multiple_of(own_tp * part, part), part)
        middle_ref[...] = tokens_ref[rows, :].astype(jnp.float32)

    for piece in range(2):
        target = slice(starts[piece], starts[piece + 1])
        total = middle_ref[:, target]
        for which in range(2):
            side = core if which == 0 else 1 - core
            columns = pl.ds(pl.multiple_of(side * half, half), half)
            total = total + dense(attended_ref[0, :, columns], weights[2 * piece + which][0])
        middle_ref[:, target] = total

    @pl.when(step == pl.num_programs(0) - 1)
    def _():
        normed_ref[...] = (norm_of(middle_ref[...])[1] * gain_ref[...]).astype(jnp.bfloat16)


def out_call(where, tokens, gain, attended, weights):
    rows, width = tokens.shape
    count, part, own = attended.shape
    weights = [pltpu.with_memory_space_constraint(w, pltpu.HBM) for w in weights]
    whole = lambda shape: pl.BlockSpec(shape, lambda d, w: (0, 0))
    group = lambda x: pl.BlockSpec((1, *x.shape[1:]), lambda d, w: (d, 0, 0))
    return call(
        out_kernel,
        (made((part, width), jnp.float32), made((part, width), jnp.bfloat16)),
        (where, tokens, gain, attended, *weights),
        scalars=1,
        grid=(count,),
        in_specs=[whole((rows, width)), whole((1, width)), group(attended)]
        + [group(w) for w in weights],
        out_specs=[whole((part, width))] * 2,
        room=24,
        name="out",
    )


def ffn_kernel(where_ref, *refs, chunk, sources, first):
    grad_act_ref, gate_ref, up_ref = refs[sources : sources + 3]
    act_ref, gate_pre_ref, up_pre_ref, normed_ref, *grads, total_ref = refs[
        sources + 3 + (0 if first else 4) :
    ]
    own_tp = where_ref[0]
    part = grads[0].shape[0]
    step = pl.program_id(0)

    @pl.when(step == 0)
    def _():
        if first:
            normed_ref[:part, :] = refs[0][...]
            normed_ref[part:, :] = jnp.where(from_above(own_tp, 1), refs[1][...], refs[2][...])
        elif chunk == 2:
            normed_ref[...] = jnp.where(from_above(own_tp, 2), refs[0][...], refs[1][...])
        else:
            inner = jnp.where(own_tp == 1, refs[0][...], refs[1][...])
            ends = jnp.where(own_tp == 0, refs[2][...], refs[3][...])
            normed_ref[...] = jnp.where(is_inner(own_tp), inner, ends)

    normed = normed_ref[...]
    gate = dense(normed, gate_ref[...])
    up = dense(normed, up_ref[...])
    sig = jax.nn.sigmoid(gate)
    grad_act = grad_act_ref[...]
    act_ref[...] = (gate * sig * up).astype(jnp.bfloat16)
    gate_pre = (grad_act * up * (sig * (1.0 + gate * (1.0 - sig)))).astype(jnp.bfloat16)
    up_pre = (grad_act * (gate * sig)).astype(jnp.bfloat16)
    gate_pre_ref[...] = gate_pre
    up_pre_ref[...] = up_pre
    term = dense_t(gate_pre, gate_ref[...]) + dense_t(up_pre, up_ref[...])

    @pl.when(step == 0)
    def _():
        total_ref[...] = term

    @pl.when(step > 0)
    def _():
        total_ref[...] += term

    @pl.when(step == pl.num_programs(0) - 1)
    def _():
        for index, grad_ref in enumerate(grads):
            rows = slice(index * part, (index + 1) * part)
            grad_ref[...] = total_ref[rows, :].astype(jnp.bfloat16)


def from_above(own_tp, chunk):
    return own_tp % (2 * chunk) < chunk


def is_inner(own_tp):
    return (own_tp == 1) | (own_tp == 2)


def ffn_call(where, chunk, sources, grad_act, w_gate, w_up, filled):
    part, width = sources[0].shape
    total, hidden = grad_act.shape
    wide = 512
    count = 2 if filled is None else 1
    rows = count * part
    whole = pl.BlockSpec((part, width), lambda f, w: (0, 0))
    weight = pl.BlockSpec((width, wide), lambda f, w: (0, f))
    block = pl.BlockSpec((rows, wide), lambda f, w: (chunk, f))
    low = made((total, hidden), jnp.bfloat16)
    w_gate, w_up = [pltpu.with_memory_space_constraint(w, pltpu.HBM) for w in (w_gate, w_up)]
    ins = [where, *sources, grad_act, w_gate, w_up]
    specs = [whole] * len(sources) + [block, weight, weight]
    aliases = {}
    if filled is not None:
        aliases = {len(ins) + i: i for i in range(4)}
        ins += list(filled)
        specs += [pl.BlockSpec(memory_space=pl.ANY)] * 4
    outs = pl.pallas_call(
        functools.partial(ffn_kernel, chunk=chunk, sources=len(sources), first=not aliases),
        out_shape=(low, low, low, made((total, width), jnp.bfloat16))
        + (made((part, width), jnp.bfloat16),) * count,
        grid_spec=pltpu.PrefetchScalarGridSpec(
            num_scalar_prefetch=1,
            grid=(hidden // wide,),
            in_specs=specs,
            out_specs=(
                block, block, block, pl.BlockSpec((rows, width), lambda f, w: (chunk, 0)),
            )
            + (whole,) * count,
            scratch_shapes=[pltpu.VMEM((rows, width), jnp.float32)],
        ),
        input_output_aliases=aliases,
        compiler_params=pltpu.CompilerParams(vmem_limit_bytes=28 << 20),
        cost_estimate=SHORT,
        name="ffn",
    )(*ins)
    return outs[:4], outs[4:]


def middle_kernel(where_ref, middle_ref, upstream_ref, gain_ref, *refs):
    terms, refs = refs[: refs[-2].shape[0]], refs[refs[-2].shape[0] :]
    *weights, low_ref, grad_ref, back_ref, gain_grad_ref = refs
    own_tp, core = where_ref[0], where_ref[1]
    count, part, _ = back_ref.shape
    _, half, wide = weights[0].shape
    scale, unit = norm_of(middle_ref[...])
    grad = sum([t[...].astype(jnp.float32) for t in terms[1:]], terms[0][...].astype(jnp.float32))
    gain_grad_ref[...] = jnp.sum(grad * unit, axis=0, keepdims=True)
    at = pl.ds(pl.multiple_of(own_tp * part, part), part)
    total = upstream_ref[at, :].astype(jnp.float32) + norm_back(grad, gain_ref[...], scale, unit)
    grad_ref[...] = total
    low = total.astype(jnp.bfloat16)
    low_ref[...] = low
    for d in range(count):
        for which in range(2):
            side = core if which == 0 else 1 - core
            columns = pl.ds(pl.multiple_of(side * half, half), half)
            values = dense_t(low[:, :wide], weights[which][d])
            values = values + dense_t(low[:, wide:], weights[2 + which][d])
            back_ref[d, :, columns] = values.astype(jnp.bfloat16)


def back_kernel(where_ref, back_ref, live_ref, tokens_ref, query_ref, key_ref, value_ref, low_ref, gain_ref, *refs):
    *outs, ordered_ref, unit_ref = refs
    head = HEAD_WIDTH
    heads = back_ref.shape[0]
    count = len(outs)
    part = outs[0].shape[0]
    own = heads * head
    step = pl.program_id(0)

    @pl.when(step == 0)
    def _():
        for d in range(count):
            at = pl.ds(pl.multiple_of(piece_at(where_ref[0], d, count) * part, part), part)
            rows = slice(d * part, (d + 1) * part)
            for index in range(3):
                low = jnp.concatenate(
                    [back_ref[h, at, index * head : (index + 1) * head] for h in range(heads)],
                    axis=-1,
                )
                if index == 2:
                    low = jnp.where(live_ref[at, :] == 1, low.astype(jnp.float32), 0.0)
                    low = low.astype(jnp.bfloat16)
                low_ref[at, index * own : (index + 1) * own] = low
                ordered_ref[rows, index * own : (index + 1) * own] = low
            unit = norm_of(tokens_ref[at, :])[1]
            for block in range(unit_ref.shape[0]):
                wide = unit_ref.shape[2]
                unit_ref[block, rows, :] = unit[:, block * wide : (block + 1) * wide]

    total = None
    for index, weight in enumerate((query_ref, key_ref, value_ref)):
        term = dense_t(ordered_ref[:, index * own : (index + 1) * own], weight[...])
        total = term if total is None else total + term
    gain_ref[...] = jnp.sum(total * unit_ref[step], axis=0, keepdims=True)
    for d in range(count):
        outs[d][...] = total[d * part : (d + 1) * part].astype(jnp.bfloat16)


def back_call(where, back_heads, live, tokens, weights, count):
    rows, width = tokens.shape
    own = weights[0].shape[1]
    part = rows // count
    wide = 512
    blocks = width // wide
    weights = [pltpu.with_memory_space_constraint(w, pltpu.HBM) for w in weights]
    whole = lambda x: pl.BlockSpec(x.shape, lambda f, w: (0,) * len(x.shape))
    return pl.pallas_call(
        back_kernel,
        out_shape=(made((rows, 3 * own), jnp.bfloat16), made((1, width), jnp.float32))
        + (made((part, width), jnp.bfloat16),) * count,
        grid_spec=pltpu.PrefetchScalarGridSpec(
            num_scalar_prefetch=1,
            grid=(blocks,),
            in_specs=[whole(back_heads), whole(live), whole(tokens)]
            + [pl.BlockSpec((wide, own), lambda f, w: (f, 0))] * 3,
            out_specs=(
                pl.BlockSpec((rows, 3 * own), lambda f, w: (0, 0)),
                pl.BlockSpec((1, wide), lambda f, w: (0, f)),
            )
            + (pl.BlockSpec((part, wide), lambda f, w: (0, f)),) * count,
            scratch_shapes=[
                pltpu.VMEM((rows, 3 * own), jnp.bfloat16),
                pltpu.VMEM((blocks, rows, wide), jnp.float32),
            ],
        ),
        compiler_params=pltpu.CompilerParams(vmem_limit_bytes=32 << 20),
        cost_estimate=SHORT,
        name="back",
    )(where, back_heads, live, tokens, *weights)


def tokens_kernel(
    where_ref, tokens_ref, gain_ref, grad_ref, gains_ref, middle_ref, branch_ref, own_ref, below_ref, above_ref, out_ref
):
    part = own_ref.shape[0]
    at = pl.ds(pl.multiple_of(where_ref[0] * part, part), part)
    scale, unit = norm_of(tokens_ref[at, :])
    grad = own_ref[...].astype(jnp.float32) + (
        below_ref[...].astype(jnp.float32) + above_ref[...].astype(jnp.float32)
    )
    total = grad_ref[...] + norm_back(grad, gain_ref[...], scale, unit)
    out_ref[:part, :] = total.astype(jnp.bfloat16)
    gains = gains_ref[...]
    high = gains.astype(jnp.bfloat16)
    low = (gains - high.astype(jnp.float32)).astype(jnp.bfloat16)
    wide = gains.shape[1]
    rows = out_ref.shape[0] - 2 * part
    middle = slice(part, part + rows)
    for index, values in enumerate((high, low)):
        out_ref[middle, index * wide : (index + 1) * wide] = jnp.broadcast_to(values, (rows, wide))
    out_ref[middle, 2 * wide :] = jnp.zeros((rows, out_ref.shape[1] - 2 * wide), jnp.bfloat16)
    layer = middle_ref[...] + branch_ref[...].astype(jnp.float32)
    out_ref[part + rows :, :] = layer.astype(jnp.bfloat16)


def join_kernel(where_ref, own_ref, *refs, part):
    *pieces, out_ref, gains_ref, layer_ref, terms_ref = refs
    count = len(pieces) // 2 + 1
    wide = gains_ref.shape[1]
    for d in range(count):
        place = piece_at(where_ref[0], d, count)
        values = own_ref[...] if d == 0 else pieces[d - 1][...] + pieces[2 * count - 2 - d][...]
        at = pl.ds(pl.multiple_of(place * part, part), part)
        out_ref[at, :] = values[:part].astype(jnp.float32)
        row = values[part : part + 8].astype(jnp.float32)
        terms_ref[place] = row[:, :wide] + row[:, wide : 2 * wide]
        layer_ref[at, :] = values[values.shape[0] - part :]
    total = terms_ref[0]
    for index in range(1, count):
        total = total + terms_ref[index]
    gains_ref[...] = total[:1]


def join(where, gathered, part, gains):
    own, above, below = gathered
    count = len(above) + 1
    width = own.shape[1]
    return call(
        functools.partial(join_kernel, part=part),
        (
            made((count * part, width), jnp.float32),
            made((1, gains), jnp.float32),
            made((count * part, width), jnp.bfloat16),
        ),
        (where, own, *above, *below),
        scratch=[pltpu.VMEM((count, 8, gains), jnp.float32)],
        scalars=1,
        name="join",
    )


def tie(*values):
    return lax.optimization_barrier(values)


def after(value, *others):
    return lax.optimization_barrier((value, *others))[0]


class Line:
    def __init__(self, axis, count):
        self.axis, self.count, self.at = axis, count, 0
        self.upward, self.downward = None, None

    def tie(self, *others):
        self.upward, self.downward, *others = tie(self.upward, self.downward, *others)
        return others[0] if len(others) == 1 else others

    def send(self, up, down, up_pairs, down_pairs):
        self.upward = lax.ppermute(up, self.axis, up_pairs)
        self.downward = lax.ppermute(down, self.axis, down_pairs)


class Gather(Line):
    def __init__(self, shard, axis, count):
        super().__init__(axis, count)
        self.own, self.above, self.below = shard, [], []

    def step(self):
        if self.at:
            self.keep()
        up, down = (self.upward, self.downward) if self.at else (self.own, self.own)
        self.at += 1
        at, count = self.at, self.count
        self.send(
            up,
            down,
            [(i, i + 1) for i in range(at - 1, count - 1)],
            [(i, i - 1) for i in range(1, count - at + 1)],
        )

    def keep(self):
        self.below.append(self.upward)
        self.above.append(self.downward)

    def result(self):
        while self.at < self.count - 1:
            self.step()
        self.keep()
        return self.own, self.above, self.below


def add_kernel(up_ref, got_up_ref, down_ref, got_down_ref, sum_up_ref, sum_down_ref):
    for part, got, total in (
        (up_ref, got_up_ref, sum_up_ref),
        (down_ref, got_down_ref, sum_down_ref),
    ):
        total[...] = (part[...].astype(jnp.float32) + got[...].astype(jnp.float32)).astype(
            jnp.bfloat16
        )


class Sum(Line):
    def __init__(self, parts, axis, count):
        super().__init__(axis, count)
        self.parts = parts

    def step(self):
        first = self.at == 0
        self.at += 1
        at, count = self.at, self.count
        up, down = self.parts[count - at], self.parts[at]
        if not first:
            outs = (made(up.shape, jnp.bfloat16),) * 2
            up, down = call(
                add_kernel, outs, (up, self.upward, down, self.downward), name="add"
            )
        self.send(
            up,
            down,
            [(i, i + 1) for i in range(0, at)],
            [(i, i - 1) for i in range(count - at, count)],
        )

    def result(self):
        while self.at < self.count - 1:
            self.step()
        return self.parts[0], self.upward, self.downward


def outer(left, right):
    return lax.dot_general(
        left, right, (((0,), (0,)), ((), ())), preferred_element_type=jnp.float32
    )


def chip_outer_kernel(where_ref, *refs, sides):
    del where_ref
    keep_x, sent_x, keep_y, sent_y = refs[-4:]
    step = pl.program_id(0)
    values = []
    for side in range(sides):
        left, left_other, right, right_other = refs[4 * side : 4 * side + 4]
        product = outer(left[...], right[...]) + outer(left_other[...], right_other[...])
        values.append(product.astype(jnp.bfloat16))
    values = values[0] if sides == 1 else jnp.concatenate(values, axis=-1)
    half = values.shape[1] // 2

    for target, part, places in (
        (keep_x, 0, (0, 1)),
        (sent_x, 0, (2, 3)),
        (keep_y, 1, (0, 3)),
        (sent_y, 1, (1, 2)),
    ):

        @pl.when((step == places[0]) | (step == places[1]))
        def _(target=target, part=part):
            target[0] = values[:, part * half : (part + 1) * half]


def chip_outer_call(where, pairs, seq_size, name, columns=1, column=0, into=None):
    rows, width = pairs[0][0].shape
    block = width // seq_size
    half = sum(pair[2].shape[1] for pair in pairs) // 2

    def left_index(k, w):
        chip = jnp.where(k == 0, 0, jnp.where(k == 1, 2, jnp.where(k == 2, 3, 1)))
        return 0, 2 * (w[2] ^ chip) + w[1]

    specs, ins = [], []
    for pair in pairs:
        wide = pl.BlockSpec(pair[2].shape, lambda k, w: (0, 0))
        specs += [pl.BlockSpec((rows, block), left_index)] * 2 + [wide, wide]
        ins += list(pair)
    aliases = {}
    if into is not None:
        aliases = {1 + len(ins) + i: i for i in range(4)}
        specs += [pl.BlockSpec(memory_space=pltpu.HBM)] * 4
        ins += list(into)

    def target(place):
        return pl.BlockSpec((1, block, half), lambda k, w: (place(k), 0, column))

    return pl.pallas_call(
        functools.partial(chip_outer_kernel, sides=len(pairs)),
        out_shape=(pltpu.HBM((2, block, columns * half), jnp.bfloat16),) * 4,
        grid_spec=pltpu.PrefetchScalarGridSpec(
            num_scalar_prefetch=1,
            grid=(4,),
            in_specs=specs,
            out_specs=(
                target(lambda k: jnp.minimum(k, 1)),
                target(lambda k: k // 3),
                target(lambda k: k // 3),
                target(lambda k: k // 2),
            ),
        ),
        input_output_aliases=aliases,
        compiler_params=pltpu.CompilerParams(vmem_limit_bytes=24 << 20),
        cost_estimate=SHORT,
        name=name,
    )(where, *ins)


class ChipSum:
    def __init__(self, arrays, seq_size):
        self.arrays, self.size = arrays, seq_size

    def over(self, values, side):
        return lax.ppermute(values, "seq", [(i, i ^ side) for i in range(self.size)])

    def first(self, *earlier):
        _, sent_x, _, sent_y = self.arrays
        if earlier:
            sent_x, sent_y = tie(sent_x, sent_y, *earlier)[:2]
        self.got_x, self.got_y = self.over(sent_x, 2), self.over(sent_y, 4)

    def tie(self, *others):
        self.got_x, self.got_y, *others = tie(self.got_x, self.got_y, *others)
        return others[0] if len(others) == 1 else others

    def second(self, *earlier):
        f32, bf16 = jnp.float32, jnp.bfloat16
        if earlier:
            self.got_x, self.got_y = tie(self.got_x, self.got_y, *earlier)[:2]
        keep_x, _, keep_y, _ = self.arrays
        through_x = (keep_x[1].astype(f32) + self.got_x[0].astype(f32)).astype(bf16)
        through_y = (keep_y[1].astype(f32) + self.got_y[1].astype(f32)).astype(bf16)
        self.last_x, self.last_y = self.over(through_x, 4), self.over(through_y, 2)

    def tie_last(self, *values):
        self.last_x, self.last_y, *values = tie(self.last_x, self.last_y, *values)
        return values

    def terms(self):
        keep_x, _, keep_y, _ = self.arrays
        return (keep_x, self.got_x, self.last_x), (keep_y, self.got_y, self.last_y)


def widen_kernel(*refs, terms, turned):
    f32 = jnp.float32
    values_refs, outs = refs[: len(terms)], refs[len(terms) :]
    column = 0
    for index, out_ref in enumerate(outs):
        wide = out_ref.shape[0] if turned[index] else out_ref.shape[1]
        columns = slice(column, column + wide)
        total = None
        for ref, place in zip(values_refs, terms):
            values = ref[:, columns] if place is None else ref[place, :, columns]
            total = values.astype(f32) if total is None else total + values.astype(f32)
        out_ref[...] = total.T if turned[index] else total
        column += wide


def widen(values, terms, widths, turned, name):
    rows = values[-1].shape[0]
    outs = [made((w, rows) if t else (rows, w), jnp.float32) for w, t in zip(widths, turned)]
    kernel = functools.partial(widen_kernel, terms=terms, turned=turned)
    return call(kernel, outs, tuple(values), name=name, room=24)


def widen_pair_kernel(*refs, turned):
    f32 = jnp.float32
    outs = refs[6:]
    for index, out_ref in enumerate(outs):
        half = (out_ref.shape[0] if turned[index] else out_ref.shape[1]) // 2
        columns = slice(index * half, (index + 1) * half)
        for way, (got_place, keep, got, last) in enumerate(((1, *refs[:3]), (0, *refs[3:6]))):
            total = keep[0, :, columns].astype(f32) + got[got_place, :, columns].astype(f32)
            total = total + last[:, columns].astype(f32)
            target = slice(way * half, (way + 1) * half)
            if turned[index]:
                out_ref[target, :] = total.T
            else:
                out_ref[:, target] = total


def widen_pair(values, width, turned, name):
    rows = values[2].shape[0]
    outs = [made((width, rows) if t else (rows, width), jnp.float32) for t in turned]
    kernel = functools.partial(widen_pair_kernel, turned=turned)
    return call(kernel, outs, tuple(values), name=name, room=24)


def matmul_kernel(where_ref, left_ref, right_ref, out_ref, *, turned, parts):
    product = (dense_t if turned else dense)(left_ref[...], right_ref[...]).astype(out_ref.dtype)
    if parts == 1:
        out_ref[...] = product
    part = product.shape[0] // parts
    for k in range(parts if parts > 1 else 0):
        place = where_ref[0] ^ k
        rows = pl.ds(pl.multiple_of(place * part, part), part)
        out_ref[rows, :] = product[k * part : (k + 1) * part]


def matmul_call(where, left, right, dtype, turned, name, parts=1):
    rows, depth = left.shape
    columns = right.shape[0 if turned else 1]
    wide = 512
    right = pltpu.with_memory_space_constraint(right, pltpu.HBM)
    if turned:
        right_spec = pl.BlockSpec((wide, depth), lambda f, w: (f, 0))
    else:
        right_spec = pl.BlockSpec((depth, wide), lambda f, w: (0, f))
    return pl.pallas_call(
        functools.partial(matmul_kernel, turned=turned, parts=parts),
        out_shape=made((rows, columns), dtype),
        grid_spec=pltpu.PrefetchScalarGridSpec(
            num_scalar_prefetch=1,
            grid=(columns // wide,),
            in_specs=[pl.BlockSpec((rows, depth), lambda f, w: (0, 0)), right_spec],
            out_specs=pl.BlockSpec((rows, wide), lambda f, w: (0, f)),
        ),
        compiler_params=pltpu.CompilerParams(vmem_limit_bytes=20 << 20),
        cost_estimate=SHORT,
        name=name,
    )(where, left, right)


def turn_kernel(query_ref, both_ref, other_ref, cosine_ref, sine_ref, out_ref):
    head = HEAD_WIDTH
    both = both_ref[...] + other_ref[...].astype(jnp.float32)
    cosine, sine = cosine_ref[...], sine_ref[...]
    for place, values in ((0, query_ref[...]), (1, both[:, :head])):
        values = values * cosine - pltpu.roll(values, head // 2, 1) * sine
        out_ref[:, place * head : (place + 1) * head] = values.astype(jnp.bfloat16)
    out_ref[:, 2 * head :] = both[:, head:].astype(jnp.bfloat16)


def turn_call(query, both, other, cosine, sine):
    rows, head = query.shape
    step = 256
    query, both, other, cosine, sine = [
        pltpu.with_memory_space_constraint(x, pltpu.HBM)
        for x in (query, both, other, cosine, sine)
    ]
    block = lambda x: pl.BlockSpec((step, x.shape[1]), lambda i: (i, 0))
    return pl.pallas_call(
        turn_kernel,
        out_shape=made((rows, 3 * head), jnp.bfloat16),
        grid=(rows // step,),
        in_specs=[block(x) for x in (query, both, other, cosine, sine)],
        out_specs=pl.BlockSpec((step, 3 * head), lambda i: (i, 0)),
        compiler_params=pltpu.CompilerParams(vmem_limit_bytes=12 << 20),
        cost_estimate=SHORT,
        name="turn",
    )(query, both, other, cosine, sine)


def local_heads_apart(
    tokens,
    gain_attn,
    w_query,
    w_key,
    w_value,
    w_out,
    gain_ffn,
    w_gate,
    w_up,
    w_down,
    cotangent,
    doc_ids,
    valid,
    group_order,
    *,
    seq_size,
    tp_size,
):
    _, row_count, width = tokens.shape
    length = doc_ids.shape[1]
    groups = group_order.shape[1]
    span = length // groups
    head = HEAD_WIDTH
    heads = w_query.shape[1] // head
    own_width = heads * head
    hidden = w_gate.shape[1]
    chips = seq_size // 2
    part = row_count // tp_size
    block = width // seq_size
    bf16, f32, i32 = jnp.bfloat16, jnp.float32, jnp.int32
    same_core = [[2 * p + c for p in range(chips)] for c in range(2)]
    other_core = [(i, i ^ 1) for i in range(seq_size)]
    own_seq, own_tp = lax.axis_index("seq"), lax.axis_index("tp")
    core = own_seq % 2
    where = jnp.stack([own_tp, core, own_seq // 2]).astype(i32)
    tokens = tokens.reshape(row_count, width)
    upstream = cotangent.reshape(row_count, width)
    gain_attn, gain_ffn = gain_attn.reshape(1, width), gain_ffn.reshape(1, width)

    def swap(values):
        return lax.ppermute(values, "seq", other_core)

    def to_heads(values):
        return lax.all_to_all(values, "seq", 0, 0, axis_index_groups=same_core, tiled=True)

    def part_of(values, place):
        return lax.dynamic_slice_in_dim(values, place * part, part, 0)

    def reordered(values):
        return jnp.concatenate([part_of(values, own_tp ^ k) for k in range(tp_size)], axis=0)

    def across(values, k):
        return lax.ppermute(values, "tp", [(i, i ^ k) for i in range(tp_size)])

    half = own_width // 2
    most = width * 5 // 8
    w_half = lax.dynamic_slice_in_dim(w_out, core * half, half, 0)

    def gathered(columns):
        values = lax.all_gather(columns, "tp", axis=0, tiled=True)
        return values.reshape(tp_size, half, columns.shape[1])

    w_first = gathered(w_half[:, :most])
    w_second = gathered(w_half[:, most:])

    order = group_order[0]
    per_device = row_count // span

    def blocks_of(which):
        devices = 2 * jnp.arange(chips, dtype=i32) + which
        storage = (devices[:, None] * per_device + jnp.arange(per_device)[None, :]).reshape(-1)
        return jnp.take(order, storage)

    def places_of(block_ids):
        return (block_ids[:, None] * span + jnp.arange(span, dtype=i32)[None, :]).reshape(-1)

    own_blocks, other_blocks = blocks_of(core), blocks_of(1 - core)
    slot_places = jnp.concatenate([own_blocks, other_blocks])
    docs = doc_ids[0]
    first = jnp.sum(docs[None, :] < docs.reshape(groups, span)[:, :1], axis=1, dtype=i32)
    position = jnp.arange(length, dtype=i32).reshape(groups, span)
    change = jnp.where(docs != jnp.roll(docs, 1), jnp.arange(length, dtype=i32), 0)
    change = change.reshape(groups, span)
    start = jnp.max(
        jnp.where(position[:, None, :] <= position[:, :, None], change[:, None, :], 0), axis=2
    )
    start = jnp.maximum(start, first[:, None])
    start_q = jnp.take(start, own_blocks, axis=0)
    key_low = jnp.take(first, own_blocks) // span
    row_blocks = jnp.take(order, own_seq * per_device + jnp.arange(per_device, dtype=i32))
    live = jnp.take(valid.reshape(groups, span), row_blocks, axis=0).reshape(row_count, 1)
    cosine, sine = rope_tables(places_of(row_blocks), head)
    cosine = jnp.concatenate([cosine, cosine], axis=-1)
    sine = jnp.concatenate([-sine, sine], axis=-1)
    cosine_q, sine_q = rope_tables(places_of(own_blocks), head)
    cosine_q = jnp.concatenate([cosine_q, cosine_q], axis=-1)
    sine_q = jnp.concatenate([-sine_q, sine_q], axis=-1)

    packed, normed_attn = project_call(
        tokens, gain_attn, live, cosine, sine, w_query, w_key, w_value
    )
    mine = to_heads(packed).reshape(chips * row_count, 3 * head)
    upstream_rel = reordered(upstream)
    grad_act = matmul_call(where, upstream_rel, w_down, f32, True, "grad_act")
    upstream_pair = (upstream_rel, swap(upstream_rel))
    normed_attn_pair = (normed_attn, swap(normed_attn))
    mine, grad_act, cosine_q, sine_q = tie(mine, grad_act, cosine_q, sine_q)
    other = swap(mine)

    attended = attend_call(slot_places, key_low, mine, other, start_q.reshape(-1, 1), span)
    attended, w_first = tie(attended, w_first)
    attended = to_heads(attended.reshape(chips, row_count, head))
    attended = attended.reshape(heads, row_count, head)
    attended = jnp.concatenate([attended[h] for h in range(heads)], axis=-1)
    attended_part = lax.all_to_all(
        attended.reshape(tp_size, part, own_width), "tp", 0, 0, tiled=True
    )
    w_second = after(w_second, attended_part)
    out_weights = (w_first, swap(w_first), w_second, swap(w_second))
    middle, normed_part = out_call(where, tokens, gain_ffn, attended_part, out_weights)

    line = Gather(normed_part, "tp", tp_size)
    line.step()
    line.step()
    above_1, below_1 = line.above[0], line.below[0]
    filled, (own_grad, grad_1) = ffn_call(
        where, 0, [normed_part, above_1, below_1], grad_act, w_gate, w_up, None
    )
    filled = line.tie(*filled)
    line.step()
    above_2, below_2 = line.above[1], line.below[1]
    filled, (grad_2,) = ffn_call(where, 2, [above_2, below_2], grad_act, w_gate, w_up, filled)
    *filled, grad_1, grad_2 = line.tie(*filled, grad_1, grad_2)
    grad_1, grad_2 = across(grad_1, 1), across(grad_2, 2)
    _, (_, _, above_3), (_, _, below_3) = line.result()
    filled, (grad_3,) = ffn_call(
        where, 3, [above_1, below_1, above_3, below_3], grad_act, w_gate, w_up, filled
    )
    grad_3 = across(grad_3, 3)
    activated, gate_pre, up_pre, normed_ffn = filled
    up_pre, grad_1, grad_2 = tie(up_pre, grad_1, grad_2)

    normed_pair = (normed_ffn, swap(normed_ffn))
    outer_ffn = functools.partial(
        chip_outer_call, where, seq_size=seq_size, name="ffn_outer"
    )
    gate_quad = (*normed_pair, gate_pre, swap(gate_pre))
    up_quad = (*normed_pair, up_pre, swap(up_pre))
    down_quad = (*upstream_pair, activated, swap(activated))
    gate_sum = ChipSum(outer_ffn([gate_quad]), seq_size)
    gate_sum.first()
    up_sum = ChipSum(outer_ffn([up_quad]), seq_size)
    up_sum.first()
    down_sum = ChipSum(outer_ffn([down_quad]), seq_size)
    grad_3, *down_sum.arrays = tie(grad_3, *down_sum.arrays)
    middle_low, grad_middle, grad_attended, gain_ffn_part = call(
        middle_kernel,
        (
            made((part, width), bf16),
            made((part, width), f32),
            made((tp_size, part, own_width), bf16),
            made((1, width), f32),
        ),
        (where, middle, upstream, gain_ffn, own_grad, grad_1, grad_2, grad_3, *out_weights),
        scalars=1,
        work=2 * part * width * width,
        name="middle",
    )
    grad_attended = lax.all_to_all(grad_attended, "tp", 0, 0, tiled=True)
    branch = matmul_call(where, after(activated, middle_low), w_down, bf16, False, "branch", tp_size)
    grad_attended, branch = up_sum.tie(*gate_sum.tie(grad_attended, branch))
    branch = after(branch, grad_attended)
    branch_part = lax.psum_scatter(branch, "tp", scatter_dimension=0, tiled=True)
    grad_attended = grad_attended.reshape(row_count, own_width)
    grad_attended = jnp.stack(
        [grad_attended[:, h * head : (h + 1) * head] for h in range(heads)]
    )
    grad_heads = to_heads(grad_attended).reshape(chips * row_count, head)
    grad_query, both, both_other = attend_back_call(
        slot_places, key_low, mine, other, start_q, grad_heads, span
    )
    other_term = swap(both_other)
    middle_all = lax.all_gather(after(middle_low, other_term), "tp", axis=0, tiled=True)
    packed_back = turn_call(grad_query, both, other_term, cosine_q, sine_q)
    packed_back = packed_back.reshape(chips, row_count, 3 * head)
    back_heads = to_heads(packed_back)
    attended_pair = (attended, swap(attended))
    back_heads = after(back_heads, attended_pair[1], branch_part)
    low, gain_attn_part, *parts = back_call(
        where, back_heads, live, tokens, (w_query, w_key, w_value), tp_size
    )
    sums = Sum(parts, "tp", tp_size)
    sums.step()
    gains = jnp.concatenate([gain_attn_part, gain_ffn_part], axis=0)
    gains = gains.reshape(2, seq_size, block).transpose(1, 0, 2)
    gains = jnp.sum(lax.all_to_all(gains, "seq", 0, 0, tiled=True), axis=0).reshape(1, 2 * block)
    down_sum.first(low)
    down_sum.got_x, down_sum.got_y, low = sums.tie(down_sum.got_x, down_sum.got_y, low)
    sums.step()
    gains, low, middle_all = sums.tie(gains, low, middle_all)
    up_sum.second(low)
    sums.step()
    middle_pair = (middle_all, swap(middle_all))
    attn_grads = chip_outer_call(
        where,
        [(*middle_pair, *attended_pair), (*normed_attn_pair, low, swap(low))],
        seq_size,
        "attn_outer",
    )
    up_sum.last_x, up_sum.last_y, *attn_grads = sums.tie(
        up_sum.last_x, up_sum.last_y, *attn_grads
    )
    attn_sum = ChipSum(attn_grads, seq_size)
    tokens_part = call(
        tokens_kernel,
        (made((2 * part + 16, width), bf16),),
        (where, tokens, gain_attn, grad_middle, gains, middle, branch_part, *sums.result()),
        scalars=1,
        name="tokens",
    )[0]
    token_line = Gather(tokens_part, "tp", tp_size)
    token_line.step()
    attn_sum.first(tokens_part)
    attn_sum.got_x, attn_sum.got_y, low = token_line.tie(attn_sum.got_x, attn_sum.got_y, low)
    token_line.step()
    down_sum.second(low)
    gate_sum.second(low)
    (*last, low) = token_line.tie(
        down_sum.last_x, down_sum.last_y, gate_sum.last_x, gate_sum.last_y, low
    )
    down_sum.last_x, down_sum.last_y, gate_sum.last_x, gate_sum.last_y = last
    token_line.step()
    attn_sum.second(low)
    up_sum.last_x = after(up_sum.last_x, low)
    up_x, up_y = up_sum.terms()
    (grad_up,) = widen_pair([*up_x, *up_y], hidden, (False,), "widen_up")
    down_x, down_y = down_sum.terms()
    (grad_down,) = widen_pair([*down_x, *down_y], hidden, (True,), "widen_down")
    gate_x, gate_y = gate_sum.terms()
    (grad_gate,) = widen_pair([*gate_x, *gate_y], hidden, (False,), "widen_gate")
    terms_x, terms_y = attn_sum.terms()
    grad_out, grad_query = widen(
        terms_x, [0, 1, None], [own_width] * 2, (True, False), "widen_attn"
    )
    grad_key, grad_value = widen(
        terms_y, [0, 0, None], [own_width] * 2, (False, False), "widen_attn"
    )
    grad_out, grad_key, grad_gate, grad_up = token_line.tie(grad_out, grad_key, grad_gate, grad_up)
    grad_tokens, gains, layer_out = join(where, token_line.result(), part, 2 * block)
    gains = gains.reshape(2, block)

    return (
        layer_out.reshape(1, row_count, width),
        grad_tokens.reshape(1, row_count, width),
        gains[0],
        grad_query,
        grad_key,
        grad_value,
        grad_out,
        gains[1],
        grad_gate,
        grad_up,
        grad_down,
    )


def solution(mesh):
    placed = (
        P(None, "seq", None),
        P(),
        P(None, "tp"),
        P(None, "tp"),
        P(None, "tp"),
        P("tp", None),
        P(),
        P(None, "tp"),
        P(None, "tp"),
        P("tp", None),
        P(None, "seq", None),
        P(),
        P(),
        P(),
    )
    seq_size, tp_size = mesh.shape["seq"], mesh.shape["tp"]

    def local(*args):
        heads = args[2].shape[1] // HEAD_WIDTH
        if seq_size == 8 and tp_size == 4 and heads == 4 and args[0].shape[0] == 1:
            return local_heads_apart(*args, seq_size=seq_size, tp_size=tp_size)
        return local_general(*args)

    return jax.shard_map(
        local,
        mesh=mesh,
        in_specs=placed,
        out_specs=(
            P(None, "seq", None),
            P(None, "seq", None),
            P("seq"),
            P("seq", "tp"),
            P("seq", "tp"),
            P("seq", "tp"),
            P("tp", "seq"),
            P("seq"),
            P("seq", "tp"),
            P("seq", "tp"),
            P("tp", "seq"),
        ),
        check_vma=False,
    )
```

```python
import functools
import math

import jax
import jax.numpy as jnp
from jax import lax
from jax.experimental import pallas as pl
from jax.experimental.pallas import tpu as pltpu
from jax.sharding import PartitionSpec as P

HEAD_WIDTH = 128


norm_eps = 1e-05
rope_base = 10000.0


def rope_tables(places, head_size):
    half_size = head_size // 2
    freqs = rope_base ** (-jnp.arange(half_size, dtype=jnp.float32) * 2.0 / head_size)
    angles = places.astype(jnp.float32)[..., None] * freqs
    return (jnp.cos(angles), jnp.sin(angles))


def rotate(values, cosine, sine, forward):
    half_size = values.shape[-1] // 2
    first = values[..., :half_size]
    second = values[..., half_size:]
    cos_b = cosine[..., None, :]
    sin_b = sine[..., None, :]
    if forward:
        return jnp.concatenate(
            [first * cos_b - second * sin_b, second * cos_b + first * sin_b], axis=-1
        )
    return jnp.concatenate(
        [first * cos_b + second * sin_b, second * cos_b - first * sin_b], axis=-1
    )


def visible(place_q, doc_q, place_k, doc_k, live_k):
    allowed = (
        (place_k[None, :] <= place_q[:, None])
        & (doc_k[None, :] == doc_q[:, None])
        & (live_k[None, :] == 1)
    )
    return allowed.astype(jnp.float32)


def score_block(query_heads, key_heads, head_size, length):
    scores = jnp.einsum("qhe,khe->hqk", query_heads, key_heads, preferred_element_type=jnp.float32)
    return scores * (1.0 / math.sqrt(head_size)) - math.log(length)


def score_grads(query_heads, key_heads, value_heads, grad_heads, mask, head_size, length):
    sigma = jax.nn.sigmoid(score_block(query_heads, key_heads, head_size, length))
    weights = (sigma * mask).astype(jnp.bfloat16)
    grad_weights = jnp.einsum(
        "qhe,khe->hqk", grad_heads, value_heads, preferred_element_type=jnp.float32
    )
    grad_scores = (grad_weights * (sigma * (1.0 - sigma)) * mask).astype(jnp.bfloat16)
    return (weights, grad_scores)


def local_general(
    tokens,
    gain_attn,
    w_query,
    w_key,
    w_value,
    w_out,
    gain_ffn,
    w_gate,
    w_up,
    w_down,
    cotangent,
    doc_ids,
    valid,
    group_order,
):
    seq_count, row_count, model_width = tokens.shape
    length = doc_ids.shape[1]
    span = length // group_order.shape[1]
    head_size = HEAD_WIDTH
    local_width = w_query.shape[1]
    local_heads = local_width // head_size
    flat_rows = seq_count * row_count
    factor = 1.0 / math.sqrt(head_size)
    own_rows = lax.axis_index("seq") * row_count + jnp.arange(row_count, dtype=jnp.int32)
    all_rows = jnp.arange(length, dtype=jnp.int32)
    place_all = jnp.take(group_order, all_rows // span, axis=1) * span + (all_rows % span)[None, :]
    place_own = jnp.take(group_order, own_rows // span, axis=1) * span + (own_rows % span)[None, :]
    doc_all = jnp.take_along_axis(doc_ids, place_all, axis=1)
    live_all = jnp.take_along_axis(valid, place_all, axis=1)
    doc_own = jnp.take_along_axis(doc_ids, place_own, axis=1)
    cosine, sine = rope_tables(place_own, head_size)
    input_rows = tokens.astype(jnp.float32).reshape(flat_rows, model_width)
    scale_attn = lax.rsqrt(jnp.mean(input_rows * input_rows, axis=-1, keepdims=True) + norm_eps)
    unit_attn = input_rows * scale_attn
    normed_attn = (unit_attn * gain_attn).astype(jnp.bfloat16)

    def project(weight_matrix):
        return jnp.dot(normed_attn, weight_matrix, preferred_element_type=jnp.float32).reshape(
            seq_count, row_count, local_heads, head_size
        )

    query_rot = (
        rotate(project(w_query), cosine, sine, True)
        .astype(jnp.bfloat16)
        .reshape(seq_count, row_count, local_width)
    )
    key_rot = (
        rotate(project(w_key), cosine, sine, True)
        .astype(jnp.bfloat16)
        .reshape(seq_count, row_count, local_width)
    )
    value_low = (
        jnp.dot(normed_attn, w_value, preferred_element_type=jnp.float32)
        .astype(jnp.bfloat16)
        .reshape(seq_count, row_count, local_width)
    )
    key_all, value_all = (
        lax.all_gather(key_rot, "seq", axis=1, tiled=True),
        lax.all_gather(value_low, "seq", axis=1, tiled=True),
    )

    def attend(items):
        query_seq, key_seq, value_seq, place_q, doc_q, place_k, doc_k, live_k = items
        query_heads = query_seq.reshape(row_count, local_heads, head_size)
        key_heads = key_seq.reshape(length, local_heads, head_size)
        value_heads = value_seq.reshape(length, local_heads, head_size)
        mask = visible(place_q, doc_q, place_k, doc_k, live_k)
        weights = (
            jax.nn.sigmoid(score_block(query_heads, key_heads, head_size, length)) * mask
        ).astype(jnp.bfloat16)
        mixed = jnp.einsum("hqk,khe->qhe", weights, value_heads, preferred_element_type=jnp.float32)
        return mixed.astype(jnp.bfloat16).reshape(row_count, local_width)

    attention_output = lax.map(
        attend, (query_rot, key_all, value_all, place_own, doc_own, place_all, doc_all, live_all)
    )
    attended_flat = attention_output.reshape(flat_rows, local_width)
    branch_attn = lax.psum(jnp.dot(attended_flat, w_out, preferred_element_type=jnp.float32), "tp")
    hidden_rows = input_rows + branch_attn
    scale_ffn = lax.rsqrt(jnp.mean(hidden_rows * hidden_rows, axis=-1, keepdims=True) + norm_eps)
    unit_ffn = hidden_rows * scale_ffn
    normalized_feedforward = (unit_ffn * gain_ffn).astype(jnp.bfloat16)
    gate_rows = jnp.dot(normalized_feedforward, w_gate, preferred_element_type=jnp.float32)
    up_projected = jnp.dot(normalized_feedforward, w_up, preferred_element_type=jnp.float32)
    gate_sig = jax.nn.sigmoid(gate_rows)
    activation_rows = (gate_rows * gate_sig * up_projected).astype(jnp.bfloat16)
    branch_ffn = lax.psum(
        jnp.dot(activation_rows, w_down, preferred_element_type=jnp.float32).astype(jnp.bfloat16),
        "tp",
    ).astype(jnp.float32)
    layer_out = (
        (hidden_rows + branch_ffn).astype(jnp.bfloat16).reshape(seq_count, row_count, model_width)
    )
    upstream = cotangent.astype(jnp.float32).reshape(flat_rows, model_width)
    upstream_low = upstream.astype(jnp.bfloat16)
    grad_down = jnp.einsum(
        "tf,td->fd", activation_rows, upstream_low, preferred_element_type=jnp.float32
    )
    grad_act = jnp.einsum("td,fd->tf", upstream_low, w_down, preferred_element_type=jnp.float32)
    gate_pre = (grad_act * up_projected * (gate_sig * (1.0 + gate_rows * (1.0 - gate_sig)))).astype(
        jnp.bfloat16
    )
    up_pre = (grad_act * (gate_rows * gate_sig)).astype(jnp.bfloat16)
    grad_gate = jnp.einsum(
        "td,tf->df", normalized_feedforward, gate_pre, preferred_element_type=jnp.float32
    )
    grad_up = jnp.einsum(
        "td,tf->df", normalized_feedforward, up_pre, preferred_element_type=jnp.float32
    )
    normed_ffn_part = jnp.einsum(
        "tf,df->td", gate_pre, w_gate, preferred_element_type=jnp.float32
    ) + jnp.einsum("tf,df->td", up_pre, w_up, preferred_element_type=jnp.float32)
    grad_normed_ffn = lax.psum(normed_ffn_part, "tp")
    gain_ffn_part = jnp.sum(grad_normed_ffn * unit_ffn, axis=0)
    back_ffn = grad_normed_ffn * gain_ffn
    grad_middle = upstream + scale_ffn * (
        back_ffn - unit_ffn * jnp.mean(back_ffn * unit_ffn, axis=-1, keepdims=True)
    )
    middle_low = grad_middle.astype(jnp.bfloat16)
    grad_out = jnp.einsum(
        "te,td->ed", attended_flat, middle_low, preferred_element_type=jnp.float32
    )
    grad_attended = (
        jnp.einsum("td,ed->te", middle_low, w_out, preferred_element_type=jnp.float32)
        .astype(jnp.bfloat16)
        .reshape(seq_count, row_count, local_width)
    )
    key_back, value_back = (key_all, value_all)

    def attend_back(items):
        query_seq, key_seq, value_seq, grad_seq, place_q, doc_q, place_k, doc_k, live_k = items
        query_heads = query_seq.reshape(row_count, local_heads, head_size)
        key_heads = key_seq.reshape(length, local_heads, head_size)
        value_heads = value_seq.reshape(length, local_heads, head_size)
        grad_heads = grad_seq.reshape(row_count, local_heads, head_size)
        mask = visible(place_q, doc_q, place_k, doc_k, live_k)
        weights, grad_scores = score_grads(
            query_heads, key_heads, value_heads, grad_heads, mask, head_size, length
        )
        grad_value_seq = jnp.einsum(
            "hqk,qhe->khe", weights, grad_heads, preferred_element_type=jnp.float32
        )
        grad_query_seq = (
            jnp.einsum("hqk,khe->qhe", grad_scores, key_heads, preferred_element_type=jnp.float32)
            * factor
        )
        grad_key_seq = (
            jnp.einsum("hqk,qhe->khe", grad_scores, query_heads, preferred_element_type=jnp.float32)
            * factor
        )
        return (
            grad_query_seq,
            grad_key_seq.reshape(length, local_width),
            grad_value_seq.reshape(length, local_width),
        )

    grad_query_rot, grad_key_all, grad_value_all = lax.map(
        attend_back,
        (
            query_rot,
            key_back,
            value_back,
            grad_attended,
            place_own,
            doc_own,
            place_all,
            doc_all,
            live_all,
        ),
    )
    grad_key_rot, grad_value_own = (
        lax.psum_scatter(grad_key_all, "seq", scatter_dimension=1, tiled=True),
        lax.psum_scatter(grad_value_all, "seq", scatter_dimension=1, tiled=True),
    )
    query_low = (
        rotate(grad_query_rot, cosine, sine, False)
        .astype(jnp.bfloat16)
        .reshape(flat_rows, local_width)
    )
    key_low = (
        rotate(
            grad_key_rot.reshape(seq_count, row_count, local_heads, head_size), cosine, sine, False
        )
        .astype(jnp.bfloat16)
        .reshape(flat_rows, local_width)
    )
    value_grad_low = grad_value_own.astype(jnp.bfloat16).reshape(flat_rows, local_width)
    grad_query = jnp.einsum("td,te->de", normed_attn, query_low, preferred_element_type=jnp.float32)
    grad_key = jnp.einsum("td,te->de", normed_attn, key_low, preferred_element_type=jnp.float32)
    grad_value = jnp.einsum(
        "td,te->de", normed_attn, value_grad_low, preferred_element_type=jnp.float32
    )
    normed_attn_part = (
        jnp.einsum("te,de->td", query_low, w_query, preferred_element_type=jnp.float32)
        + jnp.einsum("te,de->td", key_low, w_key, preferred_element_type=jnp.float32)
        + jnp.einsum("te,de->td", value_grad_low, w_value, preferred_element_type=jnp.float32)
    )
    grad_normed_attn = lax.psum(normed_attn_part, "tp")
    gain_attn_part = jnp.sum(grad_normed_attn * unit_attn, axis=0)
    back_attn = grad_normed_attn * gain_attn
    grad_inputs = grad_middle + scale_attn * (
        back_attn - unit_attn * jnp.mean(back_attn * unit_attn, axis=-1, keepdims=True)
    )
    grad_tokens = grad_inputs.reshape(seq_count, row_count, model_width)
    (
        query_shard,
        key_shard,
        value_shard,
        out_shard,
        gain_attn_shard,
        gate_shard,
        up_shard,
        down_shard,
        gain_ffn_shard,
    ) = (
        lax.psum_scatter(grad_query, "seq", scatter_dimension=0, tiled=True),
        lax.psum_scatter(grad_key, "seq", scatter_dimension=0, tiled=True),
        lax.psum_scatter(grad_value, "seq", scatter_dimension=0, tiled=True),
        lax.psum_scatter(grad_out, "seq", scatter_dimension=1, tiled=True),
        lax.psum_scatter(gain_attn_part, "seq", scatter_dimension=0, tiled=True),
        lax.psum_scatter(grad_gate, "seq", scatter_dimension=0, tiled=True),
        lax.psum_scatter(grad_up, "seq", scatter_dimension=0, tiled=True),
        lax.psum_scatter(grad_down, "seq", scatter_dimension=1, tiled=True),
        lax.psum_scatter(gain_ffn_part, "seq", scatter_dimension=0, tiled=True),
    )
    return (
        layer_out,
        grad_tokens,
        gain_attn_shard,
        query_shard,
        key_shard,
        value_shard,
        out_shard,
        gain_ffn_shard,
        gate_shard,
        up_shard,
        down_shard,
    )


def dense(left, right):
    return jnp.dot(left, right, preferred_element_type=jnp.float32)


def dense_t(left, right):
    return lax.dot_general(
        left, right, (((1,), (1,)), ((), ())), preferred_element_type=jnp.float32
    )


def sigma_of(scores, length):
    return 1.0 / (1.0 + jnp.exp(math.log(length) - scores * (1.0 / math.sqrt(HEAD_WIDTH))))


def in_position_order(slot_places, own_ref, other_ref, first, span, scratch_refs):
    head = HEAD_WIDTH
    own_slots = own_ref.shape[0] // span
    for slot in range(2 * own_slots):
        source = own_ref if slot < own_slots else other_ref
        rows = slice((slot % own_slots) * span, (slot % own_slots + 1) * span)
        target = pl.ds(pl.multiple_of(slot_places[slot] * span, span), span)
        for index, scratch in enumerate(scratch_refs):
            columns = slice(first + index * head, first + (index + 1) * head)
            scratch[target, :] = source[rows, columns]
    for scratch in scratch_refs:
        scratch[2 * own_slots * span :, :] = jnp.zeros((span, head), scratch.dtype)


def attend_kernel(
    slot_places, key_low, own_ref, other_ref, start_ref, out_ref, key_ref, value_ref, *, span
):
    head = HEAD_WIDTH
    own_slots = own_ref.shape[0] // span
    length = 2 * own_ref.shape[0]
    in_position_order(slot_places, own_ref, other_ref, head, span, (key_ref, value_ref))
    row = lax.broadcasted_iota(jnp.int32, (span, 2 * span), 0)
    column = lax.broadcasted_iota(jnp.int32, (span, 2 * span), 1)

    def query_block(slot, carry):
        rows = pl.ds(pl.multiple_of(slot * span, span), span)
        place = slot_places[slot]
        low = key_low[slot]
        query = own_ref[rows, :head]
        first = start_ref[rows, :]

        def key_pair(step, total):
            base = pl.multiple_of((low + 2 * step) * span, span)
            keys = pl.ds(base, 2 * span)
            scores = dense_t(query, key_ref[keys, :])
            seen = (column >= first - base) & (column - row <= place * span - base)
            probs = jnp.where(seen, sigma_of(scores, length), 0.0).astype(jnp.bfloat16)
            return total + dense(probs, value_ref[keys, :])

        total = lax.fori_loop(
            0, (place - low) // 2 + 1, key_pair, jnp.zeros((span, head), jnp.float32)
        )
        out_ref[rows, :] = total.astype(jnp.bfloat16)
        return carry

    lax.fori_loop(0, own_slots, query_block, 0)


def attend_back_kernel(
    slot_places,
    key_low,
    own_ref,
    other_ref,
    start_ref,
    grad_ref,
    grad_query_ref,
    grad_own_ref,
    grad_other_ref,
    key_ref,
    value_ref,
    sum_key_ref,
    sum_value_ref,
    *,
    span,
):
    head = HEAD_WIDTH
    own_slots = own_ref.shape[0] // span
    length = 2 * own_ref.shape[0]
    factor = 1.0 / math.sqrt(head)
    in_position_order(slot_places, own_ref, other_ref, head, span, (key_ref, value_ref))
    sum_key_ref[...] = jnp.zeros_like(sum_key_ref)
    sum_value_ref[...] = jnp.zeros_like(sum_value_ref)
    row = lax.broadcasted_iota(jnp.int32, (2 * span, span), 0)
    column = lax.broadcasted_iota(jnp.int32, (2 * span, span), 1)

    def query_block(slot, carry):
        rows = pl.ds(pl.multiple_of(slot * span, span), span)
        place = slot_places[slot]
        low = key_low[slot]
        query = own_ref[rows, :head]
        grad = grad_ref[rows, :]
        first = start_ref[pl.ds(slot, 1), :]

        def key_pair(step, total):
            base = pl.multiple_of((low + 2 * step) * span, span)
            keys = pl.ds(base, 2 * span)
            key = key_ref[keys, :]
            seen = (row >= first - base) & (row - column <= place * span - base)
            sigma = jnp.where(seen, sigma_of(dense_t(key, query), length), 0.0)
            sum_value_ref[keys, :] += dense(sigma.astype(jnp.bfloat16), grad)
            grad_probs = dense_t(value_ref[keys, :], grad)
            grad_scores = (grad_probs * (sigma * (1.0 - sigma))).astype(jnp.bfloat16)
            sum_key_ref[keys, :] += dense(grad_scores, query)
            return total + lax.dot_general(
                grad_scores, key, (((0,), (0,)), ((), ())), preferred_element_type=jnp.float32
            )

        total = lax.fori_loop(
            0, (place - low) // 2 + 1, key_pair, jnp.zeros((span, head), jnp.float32)
        )
        grad_query_ref[rows, :] = total * factor
        return carry

    lax.fori_loop(0, own_slots, query_block, 0)
    for slot in range(2 * own_slots):
        target = grad_own_ref if slot < own_slots else grad_other_ref
        rows = slice((slot % own_slots) * span, (slot % own_slots + 1) * span)
        source = pl.ds(pl.multiple_of(slot_places[slot] * span, span), span)
        target[rows, :head] = (sum_key_ref[source, :] * factor).astype(target.dtype)
        target[rows, head:] = sum_value_ref[source, :].astype(target.dtype)


SHORT = pl.CostEstimate(flops=1, bytes_accessed=1, transcendentals=0)
SMALL = pl.BlockSpec(memory_space=pltpu.SMEM)
WHOLE = pl.BlockSpec(memory_space=pltpu.VMEM)


def attend_call(slot_places, key_low, own, other, start, span):
    rows = own.shape[0]
    return pl.pallas_call(
        functools.partial(attend_kernel, span=span),
        out_shape=jax.ShapeDtypeStruct((rows, HEAD_WIDTH), jnp.bfloat16),
        in_specs=[SMALL, SMALL, WHOLE, WHOLE, WHOLE],
        out_specs=WHOLE,
        scratch_shapes=[pltpu.VMEM((2 * rows + span, HEAD_WIDTH), jnp.bfloat16)] * 2,
        compiler_params=pltpu.CompilerParams(vmem_limit_bytes=8 << 20),
        cost_estimate=SHORT,
        name="attend",
    )(slot_places, key_low, own, other, start)


def attend_back_call(slot_places, key_low, own, other, start, grad, span):
    rows = own.shape[0]
    return pl.pallas_call(
        functools.partial(attend_back_kernel, span=span),
        out_shape=(
            jax.ShapeDtypeStruct((rows, HEAD_WIDTH), jnp.float32),
            jax.ShapeDtypeStruct((rows, 2 * HEAD_WIDTH), jnp.float32),
            jax.ShapeDtypeStruct((rows, 2 * HEAD_WIDTH), jnp.bfloat16),
        ),
        in_specs=[SMALL, SMALL, WHOLE, WHOLE, WHOLE, WHOLE],
        out_specs=(WHOLE, WHOLE, WHOLE),
        scratch_shapes=[pltpu.VMEM((2 * rows + span, HEAD_WIDTH), jnp.bfloat16)] * 2
        + [pltpu.VMEM((2 * rows + span, HEAD_WIDTH), jnp.float32)] * 2,
        compiler_params=pltpu.CompilerParams(vmem_limit_bytes=14 << 20),
        cost_estimate=SHORT,
        name="attend_back",
    )(slot_places, key_low, own, other, start, grad)


def call(kernel, outs, ins, scratch=(), scalars=0, grid=None, in_specs=None, out_specs=None, work=0, name=None, room=12):
    params = pltpu.CompilerParams(vmem_limit_bytes=room << 20)
    if grid is None:
        return pl.pallas_call(
            kernel,
            out_shape=tuple(outs),
            in_specs=[SMALL] * scalars + [WHOLE] * (len(ins) - scalars),
            out_specs=tuple([WHOLE] * len(outs)),
            scratch_shapes=list(scratch),
            compiler_params=params,
            cost_estimate=SHORT,
            name=name,
        )(*ins)
    return pl.pallas_call(
        kernel,
        out_shape=tuple(outs),
        grid_spec=pltpu.PrefetchScalarGridSpec(
            num_scalar_prefetch=scalars,
            grid=grid,
            in_specs=in_specs,
            out_specs=tuple(out_specs),
            scratch_shapes=list(scratch),
        ),
        compiler_params=params,
        cost_estimate=SHORT,
        name=name,
    )(*ins)


def made(shape, dtype):
    return jax.ShapeDtypeStruct(shape, dtype)


def norm_of(values):
    rows = values.astype(jnp.float32)
    scale = lax.rsqrt(jnp.mean(rows * rows, axis=-1, keepdims=True) + norm_eps)
    return scale, rows * scale


def norm_back(grad, gain, scale, unit):
    back = grad * gain
    return scale * (back - unit * jnp.mean(back * unit, axis=-1, keepdims=True))


def project_kernel(
    tokens_ref, gain_ref, live_ref, cosine_ref, sine_ref, query_ref, key_ref, value_ref, packed_ref, normed_ref
):
    head = HEAD_WIDTH
    rows = tokens_ref.shape[0]

    @pl.when(pl.program_id(0) == 0)
    def _():
        step = 128

        def piece(index, carry):
            at = pl.ds(pl.multiple_of(index * step, step), step)
            normed_ref[at, :] = (norm_of(tokens_ref[at, :])[1] * gain_ref[...]).astype(jnp.bfloat16)
            return carry

        lax.fori_loop(0, rows // step, piece, 0)

    normed = normed_ref[...]
    for index, weight in enumerate((query_ref, key_ref, value_ref)):
        both = dense(normed, weight[...])
        for which in range(2):
            values = both[:, which * head : (which + 1) * head]
            if index < 2:
                values = values * cosine_ref[...] + pltpu.roll(values, head // 2, 1) * sine_ref[...]
            else:
                values = jnp.where(live_ref[...] == 1, values, 0.0)
            packed_ref[which, :, index * head : (index + 1) * head] = values.astype(jnp.bfloat16)


def project_call(tokens, gain, live, cosine, sine, w_query, w_key, w_value):
    rows, width = tokens.shape
    heads = w_query.shape[1] // HEAD_WIDTH
    whole = lambda shape: pl.BlockSpec(shape, lambda h: (0, 0))
    weight = pl.BlockSpec((width, 2 * HEAD_WIDTH), lambda h: (0, h))
    w_query, w_key, w_value = [
        pltpu.with_memory_space_constraint(w, pltpu.HBM) for w in (w_query, w_key, w_value)
    ]
    return call(
        project_kernel,
        (made((heads, rows, 3 * HEAD_WIDTH), jnp.bfloat16), made((rows, width), jnp.bfloat16)),
        (tokens, gain, live, cosine, sine, w_query, w_key, w_value),
        grid=(heads // 2,),
        in_specs=[
            whole((rows, width)), whole((1, width)), whole((rows, 1)),
            whole((rows, HEAD_WIDTH)), whole((rows, HEAD_WIDTH)), weight, weight, weight,
        ],
        out_specs=[
            pl.BlockSpec((2, rows, 3 * HEAD_WIDTH), lambda h: (h, 0, 0)), whole((rows, width)),
        ],
        work=6 * rows * width * w_query.shape[1],
        room=32,
        name="project",
    )


def piece_at(own_tp, d, count):
    return lax.rem(own_tp + d, count)


def out_kernel(where_ref, tokens_ref, gain_ref, attended_ref, *refs):
    *weights, middle_ref, normed_ref = refs
    own_tp, core = where_ref[0], where_ref[1]
    part, width = middle_ref.shape
    _, half, wide = weights[0].shape
    starts = (0, wide, width)
    step = pl.program_id(0)

    @pl.when(step == 0)
    def _():
        rows = pl.ds(pl.multiple_of(own_tp * part, part), part)
        middle_ref[...] = tokens_ref[rows, :].astype(jnp.float32)

    for piece in range(2):
        target = slice(starts[piece], starts[piece + 1])
        total = middle_ref[:, target]
        for which in range(2):
            side = core if which == 0 else 1 - core
            columns = pl.ds(pl.multiple_of(side * half, half), half)
            total = total + dense(attended_ref[0, :, columns], weights[2 * piece + which][0])
        middle_ref[:, target] = total

    @pl.when(step == pl.num_programs(0) - 1)
    def _():
        normed_ref[...] = (norm_of(middle_ref[...])[1] * gain_ref[...]).astype(jnp.bfloat16)


def out_call(where, tokens, gain, attended, weights):
    rows, width = tokens.shape
    count, part, own = attended.shape
    weights = [pltpu.with_memory_space_constraint(w, pltpu.HBM) for w in weights]
    whole = lambda shape: pl.BlockSpec(shape, lambda d, w: (0, 0))
    group = lambda x: pl.BlockSpec((1, *x.shape[1:]), lambda d, w: (d, 0, 0))
    return call(
        out_kernel,
        (made((part, width), jnp.float32), made((part, width), jnp.bfloat16)),
        (where, tokens, gain, attended, *weights),
        scalars=1,
        grid=(count,),
        in_specs=[whole((rows, width)), whole((1, width)), group(attended)]
        + [group(w) for w in weights],
        out_specs=[whole((part, width))] * 2,
        room=24,
        name="out",
    )


def ffn_kernel(where_ref, *refs, chunk, sources, first):
    grad_act_ref, gate_ref, up_ref = refs[sources : sources + 3]
    act_ref, gate_pre_ref, up_pre_ref, normed_ref, *grads, total_ref = refs[
        sources + 3 + (0 if first else 4) :
    ]
    own_tp = where_ref[0]
    part = grads[0].shape[0]
    step = pl.program_id(0)

    @pl.when(step == 0)
    def _():
        if first:
            normed_ref[:part, :] = refs[0][...]
            normed_ref[part:, :] = jnp.where(from_above(own_tp, 1), refs[1][...], refs[2][...])
        elif chunk == 2:
            normed_ref[...] = jnp.where(from_above(own_tp, 2), refs[0][...], refs[1][...])
        else:
            inner = jnp.where(own_tp == 1, refs[0][...], refs[1][...])
            ends = jnp.where(own_tp == 0, refs[2][...], refs[3][...])
            normed_ref[...] = jnp.where(is_inner(own_tp), inner, ends)

    normed = normed_ref[...]
    gate = dense(normed, gate_ref[...])
    up = dense(normed, up_ref[...])
    sig = jax.nn.sigmoid(gate)
    grad_act = grad_act_ref[...]
    act_ref[...] = (gate * sig * up).astype(jnp.bfloat16)
    gate_pre = (grad_act * up * (sig * (1.0 + gate * (1.0 - sig)))).astype(jnp.bfloat16)
    up_pre = (grad_act * (gate * sig)).astype(jnp.bfloat16)
    gate_pre_ref[...] = gate_pre
    up_pre_ref[...] = up_pre
    term = dense_t(gate_pre, gate_ref[...]) + dense_t(up_pre, up_ref[...])

    @pl.when(step == 0)
    def _():
        total_ref[...] = term

    @pl.when(step > 0)
    def _():
        total_ref[...] += term

    @pl.when(step == pl.num_programs(0) - 1)
    def _():
        for index, grad_ref in enumerate(grads):
            rows = slice(index * part, (index + 1) * part)
            grad_ref[...] = total_ref[rows, :].astype(jnp.bfloat16)


def from_above(own_tp, chunk):
    return own_tp % (2 * chunk) < chunk


def is_inner(own_tp):
    return (own_tp == 1) | (own_tp == 2)


def ffn_call(where, chunk, sources, grad_act, w_gate, w_up, filled):
    part, width = sources[0].shape
    total, hidden = grad_act.shape
    wide = 512
    count = 2 if filled is None else 1
    rows = count * part
    whole = pl.BlockSpec((part, width), lambda f, w: (0, 0))
    weight = pl.BlockSpec((width, wide), lambda f, w: (0, f))
    block = pl.BlockSpec((rows, wide), lambda f, w: (chunk, f))
    low = made((total, hidden), jnp.bfloat16)
    w_gate, w_up = [pltpu.with_memory_space_constraint(w, pltpu.HBM) for w in (w_gate, w_up)]
    ins = [where, *sources, grad_act, w_gate, w_up]
    specs = [whole] * len(sources) + [block, weight, weight]
    aliases = {}
    if filled is not None:
        aliases = {len(ins) + i: i for i in range(4)}
        ins += list(filled)
        specs += [pl.BlockSpec(memory_space=pl.ANY)] * 4
    outs = pl.pallas_call(
        functools.partial(ffn_kernel, chunk=chunk, sources=len(sources), first=not aliases),
        out_shape=(low, low, low, made((total, width), jnp.bfloat16))
        + (made((part, width), jnp.bfloat16),) * count,
        grid_spec=pltpu.PrefetchScalarGridSpec(
            num_scalar_prefetch=1,
            grid=(hidden // wide,),
            in_specs=specs,
            out_specs=(
                block, block, block, pl.BlockSpec((rows, width), lambda f, w: (chunk, 0)),
            )
            + (whole,) * count,
            scratch_shapes=[pltpu.VMEM((rows, width), jnp.float32)],
        ),
        input_output_aliases=aliases,
        compiler_params=pltpu.CompilerParams(vmem_limit_bytes=28 << 20),
        cost_estimate=SHORT,
        name="ffn",
    )(*ins)
    return outs[:4], outs[4:]


def middle_kernel(where_ref, middle_ref, upstream_ref, gain_ref, *refs):
    terms, refs = refs[: refs[-2].shape[0]], refs[refs[-2].shape[0] :]
    *weights, low_ref, grad_ref, back_ref, gain_grad_ref = refs
    own_tp, core = where_ref[0], where_ref[1]
    count, part, _ = back_ref.shape
    _, half, wide = weights[0].shape
    scale, unit = norm_of(middle_ref[...])
    grad = sum([t[...].astype(jnp.float32) for t in terms[1:]], terms[0][...].astype(jnp.float32))
    gain_grad_ref[...] = jnp.sum(grad * unit, axis=0, keepdims=True)
    at = pl.ds(pl.multiple_of(own_tp * part, part), part)
    total = upstream_ref[at, :].astype(jnp.float32) + norm_back(grad, gain_ref[...], scale, unit)
    grad_ref[...] = total
    low = total.astype(jnp.bfloat16)
    low_ref[...] = low
    for d in range(count):
        for which in range(2):
            side = core if which == 0 else 1 - core
            columns = pl.ds(pl.multiple_of(side * half, half), half)
            values = dense_t(low[:, :wide], weights[which][d])
            values = values + dense_t(low[:, wide:], weights[2 + which][d])
            back_ref[d, :, columns] = values.astype(jnp.bfloat16)


def back_kernel(where_ref, back_ref, live_ref, tokens_ref, query_ref, key_ref, value_ref, low_ref, gain_ref, *refs):
    *outs, ordered_ref, unit_ref = refs
    head = HEAD_WIDTH
    heads = back_ref.shape[0]
    count = len(outs)
    part = outs[0].shape[0]
    own = heads * head
    step = pl.program_id(0)

    @pl.when(step == 0)
    def _():
        for d in range(count):
            at = pl.ds(pl.multiple_of(piece_at(where_ref[0], d, count) * part, part), part)
            rows = slice(d * part, (d + 1) * part)
            for index in range(3):
                low = jnp.concatenate(
                    [back_ref[h, at, index * head : (index + 1) * head] for h in range(heads)],
                    axis=-1,
                )
                if index == 2:
                    low = jnp.where(live_ref[at, :] == 1, low.astype(jnp.float32), 0.0)
                    low = low.astype(jnp.bfloat16)
                low_ref[at, index * own : (index + 1) * own] = low
                ordered_ref[rows, index * own : (index + 1) * own] = low
            unit = norm_of(tokens_ref[at, :])[1]
            for block in range(unit_ref.shape[0]):
                wide = unit_ref.shape[2]
                unit_ref[block, rows, :] = unit[:, block * wide : (block + 1) * wide]

    total = None
    for index, weight in enumerate((query_ref, key_ref, value_ref)):
        term = dense_t(ordered_ref[:, index * own : (index + 1) * own], weight[...])
        total = term if total is None else total + term
    gain_ref[...] = jnp.sum(total * unit_ref[step], axis=0, keepdims=True)
    for d in range(count):
        outs[d][...] = total[d * part : (d + 1) * part].astype(jnp.bfloat16)


def back_call(where, back_heads, live, tokens, weights, count):
    rows, width = tokens.shape
    own = weights[0].shape[1]
    part = rows // count
    wide = 512
    blocks = width // wide
    weights = [pltpu.with_memory_space_constraint(w, pltpu.HBM) for w in weights]
    whole = lambda x: pl.BlockSpec(x.shape, lambda f, w: (0,) * len(x.shape))
    return pl.pallas_call(
        back_kernel,
        out_shape=(made((rows, 3 * own), jnp.bfloat16), made((1, width), jnp.float32))
        + (made((part, width), jnp.bfloat16),) * count,
        grid_spec=pltpu.PrefetchScalarGridSpec(
            num_scalar_prefetch=1,
            grid=(blocks,),
            in_specs=[whole(back_heads), whole(live), whole(tokens)]
            + [pl.BlockSpec((wide, own), lambda f, w: (f, 0))] * 3,
            out_specs=(
                pl.BlockSpec((rows, 3 * own), lambda f, w: (0, 0)),
                pl.BlockSpec((1, wide), lambda f, w: (0, f)),
            )
            + (pl.BlockSpec((part, wide), lambda f, w: (0, f)),) * count,
            scratch_shapes=[
                pltpu.VMEM((rows, 3 * own), jnp.bfloat16),
                pltpu.VMEM((blocks, rows, wide), jnp.float32),
            ],
        ),
        compiler_params=pltpu.CompilerParams(vmem_limit_bytes=32 << 20),
        cost_estimate=SHORT,
        name="back",
    )(where, back_heads, live, tokens, *weights)


def tokens_kernel(
    where_ref, tokens_ref, gain_ref, grad_ref, gains_ref, middle_ref, branch_ref, own_ref, below_ref, above_ref, out_ref
):
    part = own_ref.shape[0]
    at = pl.ds(pl.multiple_of(where_ref[0] * part, part), part)
    scale, unit = norm_of(tokens_ref[at, :])
    grad = own_ref[...].astype(jnp.float32) + (
        below_ref[...].astype(jnp.float32) + above_ref[...].astype(jnp.float32)
    )
    total = grad_ref[...] + norm_back(grad, gain_ref[...], scale, unit)
    out_ref[:part, :] = total.astype(jnp.bfloat16)
    gains = gains_ref[...]
    high = gains.astype(jnp.bfloat16)
    low = (gains - high.astype(jnp.float32)).astype(jnp.bfloat16)
    wide = gains.shape[1]
    rows = out_ref.shape[0] - 2 * part
    middle = slice(part, part + rows)
    for index, values in enumerate((high, low)):
        out_ref[middle, index * wide : (index + 1) * wide] = jnp.broadcast_to(values, (rows, wide))
    out_ref[middle, 2 * wide :] = jnp.zeros((rows, out_ref.shape[1] - 2 * wide), jnp.bfloat16)
    layer = middle_ref[...] + branch_ref[...].astype(jnp.float32)
    out_ref[part + rows :, :] = layer.astype(jnp.bfloat16)


def join_kernel(where_ref, own_ref, *refs, part):
    *pieces, out_ref, gains_ref, layer_ref, terms_ref = refs
    count = len(pieces) // 2 + 1
    wide = gains_ref.shape[1]
    for d in range(count):
        place = piece_at(where_ref[0], d, count)
        values = own_ref[...] if d == 0 else pieces[d - 1][...] + pieces[2 * count - 2 - d][...]
        at = pl.ds(pl.multiple_of(place * part, part), part)
        out_ref[at, :] = values[:part].astype(jnp.float32)
        row = values[part : part + 8].astype(jnp.float32)
        terms_ref[place] = row[:, :wide] + row[:, wide : 2 * wide]
        layer_ref[at, :] = values[values.shape[0] - part :]
    total = terms_ref[0]
    for index in range(1, count):
        total = total + terms_ref[index]
    gains_ref[...] = total[:1]


def join(where, gathered, part, gains):
    own, above, below = gathered
    count = len(above) + 1
    width = own.shape[1]
    return call(
        functools.partial(join_kernel, part=part),
        (
            made((count * part, width), jnp.float32),
            made((1, gains), jnp.float32),
            made((count * part, width), jnp.bfloat16),
        ),
        (where, own, *above, *below),
        scratch=[pltpu.VMEM((count, 8, gains), jnp.float32)],
        scalars=1,
        name="join",
    )


def tie(*values):
    return lax.optimization_barrier(values)


def after(value, *others):
    return lax.optimization_barrier((value, *others))[0]


class Line:
    def __init__(self, axis, count):
        self.axis, self.count, self.at = axis, count, 0
        self.upward, self.downward = None, None

    def tie(self, *others):
        self.upward, self.downward, *others = tie(self.upward, self.downward, *others)
        return others[0] if len(others) == 1 else others

    def send(self, up, down, up_pairs, down_pairs):
        self.upward = lax.ppermute(up, self.axis, up_pairs)
        self.downward = lax.ppermute(down, self.axis, down_pairs)


class Gather(Line):
    def __init__(self, shard, axis, count):
        super().__init__(axis, count)
        self.own, self.above, self.below = shard, [], []

    def step(self):
        if self.at:
            self.keep()
        up, down = (self.upward, self.downward) if self.at else (self.own, self.own)
        self.at += 1
        at, count = self.at, self.count
        self.send(
            up,
            down,
            [(i, i + 1) for i in range(at - 1, count - 1)],
            [(i, i - 1) for i in range(1, count - at + 1)],
        )

    def keep(self):
        self.below.append(self.upward)
        self.above.append(self.downward)

    def result(self):
        while self.at < self.count - 1:
            self.step()
        self.keep()
        return self.own, self.above, self.below


def add_kernel(up_ref, got_up_ref, down_ref, got_down_ref, sum_up_ref, sum_down_ref):
    for part, got, total in (
        (up_ref, got_up_ref, sum_up_ref),
        (down_ref, got_down_ref, sum_down_ref),
    ):
        total[...] = (part[...].astype(jnp.float32) + got[...].astype(jnp.float32)).astype(
            jnp.bfloat16
        )


class Sum(Line):
    def __init__(self, parts, axis, count):
        super().__init__(axis, count)
        self.parts = parts

    def step(self):
        first = self.at == 0
        self.at += 1
        at, count = self.at, self.count
        up, down = self.parts[count - at], self.parts[at]
        if not first:
            outs = (made(up.shape, jnp.bfloat16),) * 2
            up, down = call(
                add_kernel, outs, (up, self.upward, down, self.downward), name="add"
            )
        self.send(
            up,
            down,
            [(i, i + 1) for i in range(0, at)],
            [(i, i - 1) for i in range(count - at, count)],
        )

    def result(self):
        while self.at < self.count - 1:
            self.step()
        return self.parts[0], self.upward, self.downward


def outer(left, right):
    return lax.dot_general(
        left, right, (((0,), (0,)), ((), ())), preferred_element_type=jnp.float32
    )


def chip_outer_kernel(where_ref, *refs, sides):
    del where_ref
    keep_x, sent_x, keep_y, sent_y = refs[-4:]
    step = pl.program_id(0)
    values = []
    for side in range(sides):
        left, left_other, right, right_other = refs[4 * side : 4 * side + 4]
        product = outer(left[...], right[...]) + outer(left_other[...], right_other[...])
        values.append(product.astype(jnp.bfloat16))
    values = values[0] if sides == 1 else jnp.concatenate(values, axis=-1)
    half = values.shape[1] // 2

    for target, part, places in (
        (keep_x, 0, (0, 1)),
        (sent_x, 0, (2, 3)),
        (keep_y, 1, (0, 3)),
        (sent_y, 1, (1, 2)),
    ):

        @pl.when((step == places[0]) | (step == places[1]))
        def _(target=target, part=part):
            target[0] = values[:, part * half : (part + 1) * half]


def chip_outer_call(where, pairs, seq_size, name, columns=1, column=0, into=None):
    rows, width = pairs[0][0].shape
    block = width // seq_size
    half = sum(pair[2].shape[1] for pair in pairs) // 2

    def left_index(k, w):
        chip = jnp.where(k == 0, 0, jnp.where(k == 1, 2, jnp.where(k == 2, 3, 1)))
        return 0, 2 * (w[2] ^ chip) + w[1]

    specs, ins = [], []
    for pair in pairs:
        wide = pl.BlockSpec(pair[2].shape, lambda k, w: (0, 0))
        specs += [pl.BlockSpec((rows, block), left_index)] * 2 + [wide, wide]
        ins += list(pair)
    aliases = {}
    if into is not None:
        aliases = {1 + len(ins) + i: i for i in range(4)}
        specs += [pl.BlockSpec(memory_space=pltpu.HBM)] * 4
        ins += list(into)

    def target(place):
        return pl.BlockSpec((1, block, half), lambda k, w: (place(k), 0, column))

    return pl.pallas_call(
        functools.partial(chip_outer_kernel, sides=len(pairs)),
        out_shape=(pltpu.HBM((2, block, columns * half), jnp.bfloat16),) * 4,
        grid_spec=pltpu.PrefetchScalarGridSpec(
            num_scalar_prefetch=1,
            grid=(4,),
            in_specs=specs,
            out_specs=(
                target(lambda k: jnp.minimum(k, 1)),
                target(lambda k: k // 3),
                target(lambda k: k // 3),
                target(lambda k: k // 2),
            ),
        ),
        input_output_aliases=aliases,
        compiler_params=pltpu.CompilerParams(vmem_limit_bytes=24 << 20),
        cost_estimate=SHORT,
        name=name,
    )(where, *ins)


class ChipSum:
    def __init__(self, arrays, seq_size):
        self.arrays, self.size = arrays, seq_size

    def over(self, values, side):
        return lax.ppermute(values, "seq", [(i, i ^ side) for i in range(self.size)])

    def first(self, *earlier):
        _, sent_x, _, sent_y = self.arrays
        if earlier:
            sent_x, sent_y = tie(sent_x, sent_y, *earlier)[:2]
        self.got_x, self.got_y = self.over(sent_x, 2), self.over(sent_y, 4)

    def tie(self, *others):
        self.got_x, self.got_y, *others = tie(self.got_x, self.got_y, *others)
        return others[0] if len(others) == 1 else others

    def second(self, *earlier):
        f32, bf16 = jnp.float32, jnp.bfloat16
        if earlier:
            self.got_x, self.got_y = tie(self.got_x, self.got_y, *earlier)[:2]
        keep_x, _, keep_y, _ = self.arrays
        through_x = (keep_x[1].astype(f32) + self.got_x[0].astype(f32)).astype(bf16)
        through_y = (keep_y[1].astype(f32) + self.got_y[1].astype(f32)).astype(bf16)
        self.last_x, self.last_y = self.over(through_x, 4), self.over(through_y, 2)

    def tie_last(self, *values):
        self.last_x, self.last_y, *values = tie(self.last_x, self.last_y, *values)
        return values

    def terms(self):
        keep_x, _, keep_y, _ = self.arrays
        return (keep_x, self.got_x, self.last_x), (keep_y, self.got_y, self.last_y)


def widen_kernel(*refs, terms, turned):
    f32 = jnp.float32
    values_refs, outs = refs[: len(terms)], refs[len(terms) :]
    column = 0
    for index, out_ref in enumerate(outs):
        wide = out_ref.shape[0] if turned[index] else out_ref.shape[1]
        columns = slice(column, column + wide)
        total = None
        for ref, place in zip(values_refs, terms):
            values = ref[:, columns] if place is None else ref[place, :, columns]
            total = values.astype(f32) if total is None else total + values.astype(f32)
        out_ref[...] = total.T if turned[index] else total
        column += wide


def widen(values, terms, widths, turned, name):
    rows = values[-1].shape[0]
    outs = [made((w, rows) if t else (rows, w), jnp.float32) for w, t in zip(widths, turned)]
    kernel = functools.partial(widen_kernel, terms=terms, turned=turned)
    return call(kernel, outs, tuple(values), name=name, room=24)


def widen_pair_kernel(*refs, turned):
    f32 = jnp.float32
    outs = refs[6:]
    for index, out_ref in enumerate(outs):
        half = (out_ref.shape[0] if turned[index] else out_ref.shape[1]) // 2
        columns = slice(index * half, (index + 1) * half)
        for way, (got_place, keep, got, last) in enumerate(((1, *refs[:3]), (0, *refs[3:6]))):
            total = keep[0, :, columns].astype(f32) + got[got_place, :, columns].astype(f32)
            total = total + last[:, columns].astype(f32)
            target = slice(way * half, (way + 1) * half)
            if turned[index]:
                out_ref[target, :] = total.T
            else:
                out_ref[:, target] = total


def widen_pair(values, width, turned, name):
    rows = values[2].shape[0]
    outs = [made((width, rows) if t else (rows, width), jnp.float32) for t in turned]
    kernel = functools.partial(widen_pair_kernel, turned=turned)
    return call(kernel, outs, tuple(values), name=name, room=24)


def matmul_kernel(where_ref, left_ref, right_ref, out_ref, *, turned, parts):
    product = (dense_t if turned else dense)(left_ref[...], right_ref[...]).astype(out_ref.dtype)
    if parts == 1:
        out_ref[...] = product
    part = product.shape[0] // parts
    for k in range(parts if parts > 1 else 0):
        place = where_ref[0] ^ k
        rows = pl.ds(pl.multiple_of(place * part, part), part)
        out_ref[rows, :] = product[k * part : (k + 1) * part]


def matmul_call(where, left, right, dtype, turned, name, parts=1):
    rows, depth = left.shape
    columns = right.shape[0 if turned else 1]
    wide = 512
    right = pltpu.with_memory_space_constraint(right, pltpu.HBM)
    if turned:
        right_spec = pl.BlockSpec((wide, depth), lambda f, w: (f, 0))
    else:
        right_spec = pl.BlockSpec((depth, wide), lambda f, w: (0, f))
    return pl.pallas_call(
        functools.partial(matmul_kernel, turned=turned, parts=parts),
        out_shape=made((rows, columns), dtype),
        grid_spec=pltpu.PrefetchScalarGridSpec(
            num_scalar_prefetch=1,
            grid=(columns // wide,),
            in_specs=[pl.BlockSpec((rows, depth), lambda f, w: (0, 0)), right_spec],
            out_specs=pl.BlockSpec((rows, wide), lambda f, w: (0, f)),
        ),
        compiler_params=pltpu.CompilerParams(vmem_limit_bytes=20 << 20),
        cost_estimate=SHORT,
        name=name,
    )(where, left, right)


def turn_kernel(query_ref, both_ref, other_ref, cosine_ref, sine_ref, out_ref):
    head = HEAD_WIDTH
    both = both_ref[...] + other_ref[...].astype(jnp.float32)
    cosine, sine = cosine_ref[...], sine_ref[...]
    for place, values in ((0, query_ref[...]), (1, both[:, :head])):
        values = values * cosine - pltpu.roll(values, head // 2, 1) * sine
        out_ref[:, place * head : (place + 1) * head] = values.astype(jnp.bfloat16)
    out_ref[:, 2 * head :] = both[:, head:].astype(jnp.bfloat16)


def turn_call(query, both, other, cosine, sine):
    rows, head = query.shape
    step = 256
    query, both, other, cosine, sine = [
        pltpu.with_memory_space_constraint(x, pltpu.HBM)
        for x in (query, both, other, cosine, sine)
    ]
    block = lambda x: pl.BlockSpec((step, x.shape[1]), lambda i: (i, 0))
    return pl.pallas_call(
        turn_kernel,
        out_shape=made((rows, 3 * head), jnp.bfloat16),
        grid=(rows // step,),
        in_specs=[block(x) for x in (query, both, other, cosine, sine)],
        out_specs=pl.BlockSpec((step, 3 * head), lambda i: (i, 0)),
        compiler_params=pltpu.CompilerParams(vmem_limit_bytes=12 << 20),
        cost_estimate=SHORT,
        name="turn",
    )(query, both, other, cosine, sine)


def local_heads_apart(
    tokens,
    gain_attn,
    w_query,
    w_key,
    w_value,
    w_out,
    gain_ffn,
    w_gate,
    w_up,
    w_down,
    cotangent,
    doc_ids,
    valid,
    group_order,
    *,
    seq_size,
    tp_size,
):
    _, row_count, width = tokens.shape
    length = doc_ids.shape[1]
    groups = group_order.shape[1]
    span = length // groups
    head = HEAD_WIDTH
    heads = w_query.shape[1] // head
    own_width = heads * head
    hidden = w_gate.shape[1]
    chips = seq_size // 2
    part = row_count // tp_size
    block = width // seq_size
    bf16, f32, i32 = jnp.bfloat16, jnp.float32, jnp.int32
    same_core = [[2 * p + c for p in range(chips)] for c in range(2)]
    other_core = [(i, i ^ 1) for i in range(seq_size)]
    own_seq, own_tp = lax.axis_index("seq"), lax.axis_index("tp")
    core = own_seq % 2
    where = jnp.stack([own_tp, core, own_seq // 2]).astype(i32)
    tokens = tokens.reshape(row_count, width)
    upstream = cotangent.reshape(row_count, width)
    gain_attn, gain_ffn = gain_attn.reshape(1, width), gain_ffn.reshape(1, width)

    def swap(values):
        return lax.ppermute(values, "seq", other_core)

    def to_heads(values):
        return lax.all_to_all(values, "seq", 0, 0, axis_index_groups=same_core, tiled=True)

    def part_of(values, place):
        return lax.dynamic_slice_in_dim(values, place * part, part, 0)

    def reordered(values):
        return jnp.concatenate([part_of(values, own_tp ^ k) for k in range(tp_size)], axis=0)

    def across(values, k):
        return lax.ppermute(values, "tp", [(i, i ^ k) for i in range(tp_size)])

    half = own_width // 2
    most = width * 5 // 8
    w_half = lax.dynamic_slice_in_dim(w_out, core * half, half, 0)

    def gathered(columns):
        values = lax.all_gather(columns, "tp", axis=0, tiled=True)
        return values.reshape(tp_size, half, columns.shape[1])

    w_first = gathered(w_half[:, :most])
    w_second = gathered(w_half[:, most:])

    order = group_order[0]
    per_device = row_count // span

    def blocks_of(which):
        devices = 2 * jnp.arange(chips, dtype=i32) + which
        storage = (devices[:, None] * per_device + jnp.arange(per_device)[None, :]).reshape(-1)
        return jnp.take(order, storage)

    def places_of(block_ids):
        return (block_ids[:, None] * span + jnp.arange(span, dtype=i32)[None, :]).reshape(-1)

    own_blocks, other_blocks = blocks_of(core), blocks_of(1 - core)
    slot_places = jnp.concatenate([own_blocks, other_blocks])
    docs = doc_ids[0]
    first = jnp.sum(docs[None, :] < docs.reshape(groups, span)[:, :1], axis=1, dtype=i32)
    position = jnp.arange(length, dtype=i32).reshape(groups, span)
    change = jnp.where(docs != jnp.roll(docs, 1), jnp.arange(length, dtype=i32), 0)
    change = change.reshape(groups, span)
    start = jnp.max(
        jnp.where(position[:, None, :] <= position[:, :, None], change[:, None, :], 0), axis=2
    )
    start = jnp.maximum(start, first[:, None])
    start_q = jnp.take(start, own_blocks, axis=0)
    key_low = jnp.take(first, own_blocks) // span
    row_blocks = jnp.take(order, own_seq * per_device + jnp.arange(per_device, dtype=i32))
    live = jnp.take(valid.reshape(groups, span), row_blocks, axis=0).reshape(row_count, 1)
    cosine, sine = rope_tables(places_of(row_blocks), head)
    cosine = jnp.concatenate([cosine, cosine], axis=-1)
    sine = jnp.concatenate([-sine, sine], axis=-1)
    cosine_q, sine_q = rope_tables(places_of(own_blocks), head)
    cosine_q = jnp.concatenate([cosine_q, cosine_q], axis=-1)
    sine_q = jnp.concatenate([-sine_q, sine_q], axis=-1)

    packed, normed_attn = project_call(
        tokens, gain_attn, live, cosine, sine, w_query, w_key, w_value
    )
    mine = to_heads(packed).reshape(chips * row_count, 3 * head)
    upstream_rel = reordered(upstream)
    grad_act = matmul_call(where, upstream_rel, w_down, f32, True, "grad_act")
    upstream_pair = (upstream_rel, swap(upstream_rel))
    normed_attn_pair = (normed_attn, swap(normed_attn))
    mine, grad_act, cosine_q, sine_q = tie(mine, grad_act, cosine_q, sine_q)
    other = swap(mine)

    attended = attend_call(slot_places, key_low, mine, other, start_q.reshape(-1, 1), span)
    attended, w_first = tie(attended, w_first)
    attended = to_heads(attended.reshape(chips, row_count, head))
    attended = attended.reshape(heads, row_count, head)
    attended = jnp.concatenate([attended[h] for h in range(heads)], axis=-1)
    attended_part = lax.all_to_all(
        attended.reshape(tp_size, part, own_width), "tp", 0, 0, tiled=True
    )
    w_second = after(w_second, attended_part)
    out_weights = (w_first, swap(w_first), w_second, swap(w_second))
    middle, normed_part = out_call(where, tokens, gain_ffn, attended_part, out_weights)

    line = Gather(normed_part, "tp", tp_size)
    line.step()
    line.step()
    above_1, below_1 = line.above[0], line.below[0]
    filled, (own_grad, grad_1) = ffn_call(
        where, 0, [normed_part, above_1, below_1], grad_act, w_gate, w_up, None
    )
    filled = line.tie(*filled)
    line.step()
    above_2, below_2 = line.above[1], line.below[1]
    filled, (grad_2,) = ffn_call(where, 2, [above_2, below_2], grad_act, w_gate, w_up, filled)
    *filled, grad_1, grad_2 = line.tie(*filled, grad_1, grad_2)
    grad_1, grad_2 = across(grad_1, 1), across(grad_2, 2)
    _, (_, _, above_3), (_, _, below_3) = line.result()
    filled, (grad_3,) = ffn_call(
        where, 3, [above_1, below_1, above_3, below_3], grad_act, w_gate, w_up, filled
    )
    grad_3 = across(grad_3, 3)
    activated, gate_pre, up_pre, normed_ffn = filled
    up_pre, grad_1, grad_2 = tie(up_pre, grad_1, grad_2)

    normed_pair = (normed_ffn, swap(normed_ffn))
    outer_ffn = functools.partial(
        chip_outer_call, where, seq_size=seq_size, name="ffn_outer"
    )
    gate_quad = (*normed_pair, gate_pre, swap(gate_pre))
    up_quad = (*normed_pair, up_pre, swap(up_pre))
    down_quad = (*upstream_pair, activated, swap(activated))
    gate_sum = ChipSum(outer_ffn([gate_quad]), seq_size)
    gate_sum.first()
    up_sum = ChipSum(outer_ffn([up_quad]), seq_size)
    up_sum.first()
    grad_3 = after(grad_3, up_sum.arrays[0])
    middle_low, grad_middle, grad_attended, gain_ffn_part = call(
        middle_kernel,
        (
            made((part, width), bf16),
            made((part, width), f32),
            made((tp_size, part, own_width), bf16),
            made((1, width), f32),
        ),
        (where, middle, upstream, gain_ffn, own_grad, grad_1, grad_2, grad_3, *out_weights),
        scalars=1,
        work=2 * part * width * width,
        name="middle",
    )
    grad_attended = lax.all_to_all(grad_attended, "tp", 0, 0, tiled=True)
    branch = matmul_call(where, after(activated, middle_low), w_down, bf16, False, "branch", tp_size)
    down_quad = (after(down_quad[0], middle_low), *down_quad[1:])
    down_sum = ChipSum(outer_ffn([down_quad]), seq_size)
    grad_attended, branch, *down_sum.arrays = up_sum.tie(
        *gate_sum.tie(grad_attended, branch, *down_sum.arrays)
    )
    branch = after(branch, grad_attended)
    branch_part = lax.psum_scatter(branch, "tp", scatter_dimension=0, tiled=True)
    grad_attended = grad_attended.reshape(row_count, own_width)
    grad_attended = jnp.stack(
        [grad_attended[:, h * head : (h + 1) * head] for h in range(heads)]
    )
    grad_heads = to_heads(grad_attended).reshape(chips * row_count, head)
    grad_query, both, both_other = attend_back_call(
        slot_places, key_low, mine, other, start_q, grad_heads, span
    )
    other_term = swap(both_other)
    middle_all = lax.all_gather(after(middle_low, other_term), "tp", axis=0, tiled=True)
    packed_back = turn_call(grad_query, both, other_term, cosine_q, sine_q)
    packed_back = packed_back.reshape(chips, row_count, 3 * head)
    back_heads = to_heads(packed_back)
    attended_pair = (attended, swap(attended))
    back_heads = after(back_heads, attended_pair[1], branch_part)
    low, gain_attn_part, *parts = back_call(
        where, back_heads, live, tokens, (w_query, w_key, w_value), tp_size
    )
    sums = Sum(parts, "tp", tp_size)
    sums.step()
    gains = jnp.concatenate([gain_attn_part, gain_ffn_part], axis=0)
    gains = gains.reshape(2, seq_size, block).transpose(1, 0, 2)
    gains = jnp.sum(lax.all_to_all(gains, "seq", 0, 0, tiled=True), axis=0).reshape(1, 2 * block)
    down_sum.first(low)
    down_sum.got_x, down_sum.got_y, low = sums.tie(down_sum.got_x, down_sum.got_y, low)
    sums.step()
    gains, low, middle_all = sums.tie(gains, low, middle_all)
    up_sum.second(low)
    sums.step()
    middle_pair = (middle_all, swap(middle_all))
    attn_grads = chip_outer_call(
        where,
        [(*middle_pair, *attended_pair), (*normed_attn_pair, low, swap(low))],
        seq_size,
        "attn_outer",
    )
    up_sum.last_x, up_sum.last_y, *attn_grads = sums.tie(
        up_sum.last_x, up_sum.last_y, *attn_grads
    )
    attn_sum = ChipSum(attn_grads, seq_size)
    tokens_part = call(
        tokens_kernel,
        (made((2 * part + 16, width), bf16),),
        (where, tokens, gain_attn, grad_middle, gains, middle, branch_part, *sums.result()),
        scalars=1,
        name="tokens",
    )[0]
    token_line = Gather(tokens_part, "tp", tp_size)
    token_line.step()
    attn_sum.first(tokens_part)
    attn_sum.got_x, attn_sum.got_y, low = token_line.tie(attn_sum.got_x, attn_sum.got_y, low)
    token_line.step()
    down_sum.second(low)
    gate_sum.second(low)
    (*last, low) = token_line.tie(
        down_sum.last_x, down_sum.last_y, gate_sum.last_x, gate_sum.last_y, low
    )
    down_sum.last_x, down_sum.last_y, gate_sum.last_x, gate_sum.last_y = last
    token_line.step()
    attn_sum.second(low)
    up_sum.last_x = after(up_sum.last_x, low)
    up_x, up_y = up_sum.terms()
    (grad_up,) = widen_pair([*up_x, *up_y], hidden, (False,), "widen_up")
    down_x, down_y = down_sum.terms()
    (grad_down,) = widen_pair([*down_x, *down_y], hidden, (True,), "widen_down")
    gate_x, gate_y = gate_sum.terms()
    (grad_gate,) = widen_pair([*gate_x, *gate_y], hidden, (False,), "widen_gate")
    terms_x, terms_y = attn_sum.terms()
    grad_out, grad_query = widen(
        terms_x, [0, 1, None], [own_width] * 2, (True, False), "widen_attn"
    )
    grad_key, grad_value = widen(
        terms_y, [0, 0, None], [own_width] * 2, (False, False), "widen_attn"
    )
    grad_out, grad_key, grad_gate, grad_up = token_line.tie(grad_out, grad_key, grad_gate, grad_up)
    grad_tokens, gains, layer_out = join(where, token_line.result(), part, 2 * block)
    gains = gains.reshape(2, block)

    return (
        layer_out.reshape(1, row_count, width),
        grad_tokens.reshape(1, row_count, width),
        gains[0],
        grad_query,
        grad_key,
        grad_value,
        grad_out,
        gains[1],
        grad_gate,
        grad_up,
        grad_down,
    )


def solution(mesh):
    placed = (
        P(None, "seq", None),
        P(),
        P(None, "tp"),
        P(None, "tp"),
        P(None, "tp"),
        P("tp", None),
        P(),
        P(None, "tp"),
        P(None, "tp"),
        P("tp", None),
        P(None, "seq", None),
        P(),
        P(),
        P(),
    )
    seq_size, tp_size = mesh.shape["seq"], mesh.shape["tp"]

    def local(*args):
        heads = args[2].shape[1] // HEAD_WIDTH
        if seq_size == 8 and tp_size == 4 and heads == 4 and args[0].shape[0] == 1:
            return local_heads_apart(*args, seq_size=seq_size, tp_size=tp_size)
        return local_general(*args)

    return jax.shard_map(
        local,
        mesh=mesh,
        in_specs=placed,
        out_specs=(
            P(None, "seq", None),
            P(None, "seq", None),
            P("seq"),
            P("seq", "tp"),
            P("seq", "tp"),
            P("seq", "tp"),
            P("tp", "seq"),
            P("seq"),
            P("seq", "tp"),
            P("seq", "tp"),
            P("tp", "seq"),
        ),
        check_vma=False,
    )
```
